32 devices in a mesh: seq: 4 (over x, core), dp: 8 (over z, y).
Axes of the slice: x: 2, y: 2, z: 4, core: 2. Of those that a mesh axis runs over, the one named last changes fastest.
Arguments:
- tokens: bfloat16 [8, 1280, 960], P('dp', 'seq'), may hold values from -6 to 6
- seg_ids: int32 [8, 1280], P('dp', 'seq'), may hold values from 0 to 4, as said below
- positions: int32 [8, 1280], P('dp', 'seq'), may hold values from 0 to 1279, as said below
- attn_gain: float32 [960], replicated, may hold values from 0.25 to 1.75
- w_query: bfloat16 [960, 960], replicated, may hold values from -0.1875 to 0.1875
- w_key: bfloat16 [960, 320], replicated, may hold values from -0.1875 to 0.1875
- w_value: bfloat16 [960, 320], replicated, may hold values from -0.1875 to 0.1875
- w_out: bfloat16 [960, 960], replicated, may hold values from -0.5 to 0.5
- ffn_gain: float32 [960], replicated, may hold values from 0.25 to 1.75
- w_gate: bfloat16 [960, 2560], P(None, 'seq'), may hold values from -0.1875 to 0.1875
- w_up: bfloat16 [960, 2560], P(None, 'seq'), may hold values from -0.1875 to 0.1875
- w_down: bfloat16 [2560, 960], P('seq'), may hold values from -0.125 to 0.125
- cotangent: bfloat16 [8, 1280, 960], P('dp', 'seq'), may hold values from -6 to 6
Outputs:
- output: bfloat16 [8, 1280, 960], P('dp', 'seq')
- input_grad: float32 [8, 1280, 960], P('dp', 'seq')
- attn_gain_grad: float32 [960], P('dp')
- w_query_grad: float32 [960, 960], P('dp')
- w_key_grad: float32 [960, 320], P('dp')
- w_value_grad: float32 [960, 320], P('dp')
- w_out_grad: float32 [960, 960], P('dp')
- ffn_gain_grad: float32 [960], P('dp')
- w_gate_grad: float32 [960, 2560], P('dp', 'seq')
- w_up_grad: float32 [960, 2560], P('dp', 'seq')
- w_down_grad: float32 [2560, 960], P('seq', 'dp')
The draws below stay inside these ranges and needn't reach their ends.
Inputs may be any that keep to these rules, and one draw needn't show every extreme that they name: `seg_ids`: within a row the ids start at 0 and never fall. `positions`: A token's position counts the tokens before it in its document (0 at a document's first token).
All inputs are finite; a program needn't handle non-finite values.
Results may differ from the reference program's by a relative error of at most 0.025.
Values may be sent and summed in bfloat16 or wider, within the bound.
A program may use at most 256 MiB of HBM per device.

```python
import jax
import jax.numpy as jnp
from jax import lax

D = 960
HEADS = 15
KV_HEADS = 5
HEAD_DIM = 64
FF = 2560
LEN = 1280
DOCS = 5
ROWS = 8


def doc_layout(key):
    row_keys = jax.random.split(jax.random.fold_in(key, 7), ROWS)

    def row_bounds(row_key):
        picked = jax.random.permutation(row_key, LEN - 1)[:DOCS - 1] + 1
        return jnp.sort(picked)
    bounds = jax.vmap(row_bounds)(row_keys)
    bounds = bounds.at[0].set(LEN)
    token_place = jnp.arange(LEN)
    passed = bounds[:, None, :] <= token_place[None, :, None]
    segment = jnp.sum(passed.astype(jnp.int32), axis=2)
    doc_start = jnp.max(jnp.where(passed, bounds[:, None, :], 0), axis=2)
    return (segment.astype(jnp.int32), (token_place[None, :] - doc_start).astype(jnp.int32))


def draw_seg_ids(key, part):
    return doc_layout(key)[0]


def draw_positions(key, part):
    return doc_layout(key)[1]


def level_of(stream_key, shape, shards, smallest, high):
    level, own = 1.0, jax.random.fold_in(stream_key, 6)
    for position, shards_of in shards:
        steps = jnp.exp(jax.random.uniform(jax.random.fold_in(own, position), (shards_of,), jnp.float32, smallest / len(shards), high / len(shards)))
        level = level * jnp.repeat(steps, shape[position] // shards_of).reshape([-1 if axis == position else 1 for axis in range(len(shape))])
    return level


def bell_draw(own_key, dims, scale, limit, cuts=(), kind=jnp.bfloat16):
    array = jax.random.normal(own_key, dims, jnp.float32) * scale
    if len(cuts) > 0:
        array = level_of(own_key, dims, cuts, -0.22, 0.18) * array
    return jnp.clip(array, min=-limit, max=limit).astype(kind)


def setup_inputs(seed: int = 0) -> dict:
    key_list = jax.random.split(jax.random.key(seed), 14)
    return {
        "tokens": bell_draw(key_list[0], (ROWS, LEN, D), 1.0, 6.0, ((0, 8), (1, 4))),
        "seg_ids": draw_seg_ids(jax.random.fold_in(key_list[13], 71), 0),
        "positions": draw_positions(jax.random.fold_in(key_list[13], 71), 0),
        "attn_gain": jnp.clip(1.0 + 0.15 * jax.random.normal(key_list[3], (D,), jnp.float32), 0.25, 1.75),
        "w_query": bell_draw(key_list[4], (D, HEADS * HEAD_DIM), D ** -0.5, 0.1875),
        "w_key": bell_draw(key_list[5], (D, KV_HEADS * HEAD_DIM), D ** -0.5, 0.1875),
        "w_value": bell_draw(key_list[6], (D, KV_HEADS * HEAD_DIM), D ** -0.5, 0.1875),
        "w_out": bell_draw(key_list[7], (HEADS * HEAD_DIM, D), (HEADS * HEAD_DIM // 8) ** -0.5, 0.5),
        "ffn_gain": jnp.clip(1.0 + 0.15 * jax.random.normal(key_list[8], (D,), jnp.float32), 0.25, 1.75),
        "w_gate": bell_draw(key_list[9], (D, FF), D ** -0.5, 0.1875, ((1, 4),)),
        "w_up": bell_draw(key_list[10], (D, FF), D ** -0.5, 0.1875, ((1, 4),)),
        "w_down": bell_draw(key_list[11], (FF, D), FF ** -0.5, 0.125, ((0, 4),)),
        "cotangent": bell_draw(key_list[12], (ROWS, LEN, D), 1.0, 6.0, ((0, 8), (1, 4))),
    }


EPSILON = 1e-05
THETA = 10000.0
MASKED = -1e+30
HIGHEST = lax.Precision.HIGHEST

@jax.custom_vjp
def low(v):
    return lax.optimization_barrier(v.astype(jnp.bfloat16)).astype(jnp.float32)

@jax.custom_vjp
def low_back(v):
    return v

def low_keep(v):
    return (low(v), None)

def low_pass(kept, grad):
    return (grad,)

def back_keep(v):
    return (v, None)

def back_low(kept, grad):
    return (low(grad),)
low.defvjp(low_keep, low_pass)
low_back.defvjp(back_keep, back_low)

def rope_tables(positions):
    half_dim = HEAD_DIM // 2
    frequency = THETA ** (-(jnp.arange(half_dim, dtype=jnp.float32) * 2.0 / HEAD_DIM))
    angles = positions.astype(jnp.float32)[..., None] * frequency
    return (jnp.cos(angles), jnp.sin(angles))

def rotate(values, cos_table, sin_table):
    half_dim = values.shape[-1] // 2
    first_half = values[..., :half_dim]
    second_half = values[..., half_dim:]
    cos_head = cos_table[..., None, :]
    sin_head = sin_table[..., None, :]
    return jnp.concatenate([first_half * cos_head - second_half * sin_head, second_half * cos_head + first_half * sin_head], axis=-1)

def rms_norm(residual, gain_vec):
    return residual * lax.rsqrt(lax.optimization_barrier(jnp.mean(residual * residual, axis=-1, keepdims=True)) + EPSILON) * gain_vec

def block(residual, allowed, cos_table, sin_table, weights):
    attn_gain, w_query, w_key, w_value, w_out, ffn_gain, w_gate, w_up, w_down = weights
    length = residual.shape[0]
    groups = HEADS // KV_HEADS
    normed = low(rms_norm(residual, attn_gain))
    query_pre = low_back(jnp.dot(normed, w_query, precision=HIGHEST))
    key_pre = low_back(jnp.dot(normed, w_key, precision=HIGHEST))
    value_pre = low_back(jnp.dot(normed, w_value, precision=HIGHEST))
    queries = low(rotate(query_pre.reshape(length, HEADS, HEAD_DIM), cos_table, sin_table))
    keys_all = low(rotate(key_pre.reshape(length, KV_HEADS, HEAD_DIM), cos_table, sin_table))
    values_all = low(value_pre.reshape(length, KV_HEADS, HEAD_DIM))
    grouped = queries.reshape(length, KV_HEADS, groups, HEAD_DIM)
    raw_scores = jnp.einsum('qkgd,tkd->kgqt', grouped, keys_all, precision=HIGHEST)
    scores = low_back(raw_scores * HEAD_DIM ** (-0.5))
    scores = jnp.where(allowed, scores, MASKED)
    weights_soft = low(jax.nn.softmax(scores, axis=-1))
    mixed_heads = jnp.einsum('kgqt,tkd->qkgd', weights_soft, values_all, precision=HIGHEST)
    mixed_heads = low(low_back(mixed_heads.reshape(length, HEADS * HEAD_DIM)))
    after_attn = residual + low_back(jnp.dot(mixed_heads, w_out, precision=HIGHEST))
    normed_two = low(rms_norm(after_attn, ffn_gain))
    gate_pre = low_back(jnp.dot(normed_two, w_gate, precision=HIGHEST))
    up_pre = low_back(jnp.dot(normed_two, w_up, precision=HIGHEST))
    hidden = low(jax.nn.silu(gate_pre) * up_pre)
    return after_attn + low_back(jnp.dot(hidden, w_down, precision=HIGHEST))

def reference(tokens, seg_ids, positions, attn_gain, w_query, w_key, w_value, w_out, ffn_gain, w_gate, w_up, w_down, cotangent):
    weights = tuple((weight.astype(jnp.float32) for weight in (attn_gain, w_query, w_key, w_value, w_out, ffn_gain, w_gate, w_up, w_down)))
    token_place = jnp.arange(LEN)

    def row_step(totals, inputs):
        token_row, segment_row, position_row, cotangent_row = inputs
        cos_table, sin_table = rope_tables(position_row)
        allowed = (segment_row[:, None] == segment_row[None, :]) & (token_place[None, :] <= token_place[:, None])

        def forward(initial, params):
            residual = initial
            for repeat in range(2):
                residual = block(residual, allowed, cos_table, sin_table, params)
            return residual
        result, pullback = jax.vjp(forward, token_row.astype(jnp.float32), weights)
        row_grad, weight_grads = pullback(cotangent_row.astype(jnp.float32))
        totals = jax.tree.map(jnp.add, totals, weight_grads)
        return (totals, (result.astype(jnp.bfloat16), row_grad))
    zero_grads = jax.tree.map(jnp.zeros_like, weights)
    totals, (output, input_grad) = lax.scan(row_step, zero_grads, (tokens, seg_ids, positions, cotangent))
    return (output, input_grad, totals[0], totals[1], totals[2], totals[3], totals[4], totals[5], totals[6], totals[7], totals[8])
```

```python
import functools

import jax
import jax.numpy as jnp
from jax import lax
from jax.experimental import pallas as pl
from jax.experimental.pallas import tpu as pltpu
from jax.sharding import PartitionSpec as P

MESH_ID = pl.DeviceIdType.MESH

HEADS = 15
KV_HEADS = 5
HEAD_DIM = 64


EPSILON = 1e-05
THETA = 10000.0
MASKED = -1e30


def rope_tables(positions):
    half_dim = HEAD_DIM // 2
    frequency = THETA ** (-(jnp.arange(half_dim, dtype=jnp.float32) * 2.0 / HEAD_DIM))
    angles = positions.astype(jnp.float32)[..., None] * frequency
    return (jnp.cos(angles), jnp.sin(angles))


def rotate(values, cos_table, sin_table):
    half_dim = values.shape[-1] // 2
    first_half = values[..., :half_dim]
    second_half = values[..., half_dim:]
    cos_head = cos_table[..., None, :]
    sin_head = sin_table[..., None, :]
    return jnp.concatenate(
        [
            first_half * cos_head - second_half * sin_head,
            second_half * cos_head + first_half * sin_head,
        ],
        axis=-1,
    )


def norm_forward(residual, gain_vec):
    inverse = lax.rsqrt(jnp.mean(residual * residual, axis=-1, keepdims=True) + EPSILON)
    return ((residual * inverse * gain_vec).astype(jnp.bfloat16), inverse)


def norm_backward(residual, inverse, gain_vec, upstream):
    weighted = upstream * gain_vec
    inner_mean = jnp.mean(weighted * residual, axis=-1, keepdims=True)
    residual_grad = inverse * weighted - residual * (inverse * inverse * inverse) * inner_mean
    gain_grad = jnp.sum(upstream * residual * inverse, axis=(0, 1))
    return (residual_grad, gain_grad)


def masked_scores(queries, keys_all, allowed):
    raw_scores = jnp.einsum("qkgd,tkd->kgqt", queries, keys_all, preferred_element_type=jnp.float32)
    return jnp.where(allowed[None, None], raw_scores * HEAD_DIM ** (-0.5), MASKED)


def row_attend(operands):
    queries, keys_all, values_all, allowed = operands
    scores = masked_scores(queries, keys_all, allowed)
    row_max = jnp.max(scores, axis=-1, keepdims=True)
    shifted = jnp.exp(scores - row_max)
    row_total = jnp.sum(shifted, axis=-1, keepdims=True)
    probs_low = (shifted / row_total).astype(jnp.bfloat16)
    mixed_heads = jnp.einsum(
        "kgqt,tkd->qkgd", probs_low, values_all, preferred_element_type=jnp.float32
    )
    return (mixed_heads, row_max + jnp.log(row_total))


def row_backward(operands):
    queries, keys_all, values_all, allowed, log_total, mixed_grad = operands
    scores = masked_scores(queries, keys_all, allowed)
    weights_soft = jnp.exp(scores - log_total)
    probs_grad = jnp.einsum(
        "qkgd,tkd->kgqt", mixed_grad, values_all, preferred_element_type=jnp.float32
    )
    row_delta = jnp.sum(probs_grad * weights_soft, axis=-1, keepdims=True)
    score_grad = (weights_soft * (probs_grad - row_delta)).astype(jnp.bfloat16)
    score_scale = HEAD_DIM ** (-0.5)
    query_grad = (
        jnp.einsum("kgqt,tkd->qkgd", score_grad, keys_all, preferred_element_type=jnp.float32)
        * score_scale
    )
    key_grad = (
        jnp.einsum("kgqt,qkgd->tkd", score_grad, queries, preferred_element_type=jnp.float32)
        * score_scale
    )
    value_grad = jnp.einsum(
        "kgqt,qkgd->tkd",
        weights_soft.astype(jnp.bfloat16),
        mixed_grad,
        preferred_element_type=jnp.float32,
    )
    return (query_grad, key_grad, value_grad)


def device(seq_pos, dp_pos):
    return {"seq": seq_pos, "dp": dp_pos}


def send(src, dst, send_sem, recv_sem, target):
    copy = pltpu.make_async_remote_copy(
        src_ref=src,
        dst_ref=dst,
        send_sem=send_sem,
        recv_sem=recv_sem,
        device_id=target,
        device_id_type=MESH_ID,
    )
    copy.start()
    return copy


def greet(targets):
    barrier = pltpu.get_barrier_semaphore()
    for target in targets:
        pl.semaphore_signal(barrier, inc=1, device_id=target, device_id_type=MESH_ID)
    pl.semaphore_wait(barrier, len(targets))


def reduce_kernel(
    attn_ref, ffn_ref, gain_ref,
    attn_out, ffn_out, gain_out,
    core_send, core_recv, x_send, x_recv, own,
    y_send, y_recv, z_send, z_recv, g_recv, share_low,
    send_sem, recv_sem,
):
    seq, dp = lax.axis_index("seq"), lax.axis_index("dp")
    core, chip_x = lax.rem(seq, 2), lax.div(seq, 2)
    row_y, row_z = lax.rem(dp, 2), lax.div(dp, 2)
    mate = device(seq + 1 - 2 * core, dp)
    x_mate = device(lax.rem(seq + 2, 4), dp)
    y_mate = device(seq, dp + 1 - 2 * row_y)
    z_of = [lax.rem(row_z + k, 4) for k in range(1, 4)]
    z_mates = [device(seq, z * 2 + row_y) for z in z_of]
    greet([mate, x_mate, y_mate] + z_mates)
    low = jnp.bfloat16

    def y_start(index, load):
        for z in range(4):
            y_send[index, z] = load(2 * z + 1 - row_y).astype(low)
        return send(y_send.at[index], y_recv.at[index], send_sem.at[index], recv_sem.at[index], y_mate)

    def z_start(index, load):
        copies = []
        for k in range(3):
            z = z_of[k]
            z_send[index, k] = (load(2 * z + row_y) + y_recv[index, z].astype(jnp.float32)).astype(low)
            sem = 4 + 3 * index + k
            copies.append(
                send(z_send.at[index, k], z_recv.at[index, k], send_sem.at[sem], recv_sem.at[sem], z_mates[k])
            )
        return copies

    def z_finish(index, load, copies):
        total = load(2 * row_z + row_y) + y_recv[index, row_z].astype(jnp.float32)
        for k in range(3):
            copies[k].wait()
            total = total + z_recv[index, k].astype(jnp.float32)
        return total

    gain_out[...] = gain_ref[...]
    hops = [mate, x_mate, y_mate, device(seq, lax.rem(dp + 4, 8)), device(seq, dp + 2 - 4 * lax.rem(row_z, 2))]

    def gain_start(hop):
        sem = 22 + hop
        return send(gain_ref if hop == 0 else gain_out, g_recv.at[hop], send_sem.at[sem], recv_sem.at[sem], hops[hop])

    for half in range(2):
        core_send[half] = attn_ref[2 * half + 1 - core].astype(low)
    core_copy = send(core_send, core_recv, send_sem.at[16], recv_sem.at[16], mate)
    gain_copy = gain_start(0)
    ffn_load = lambda m: (lambda j: ffn_ref[m, j])
    y_copies = [y_start(m, ffn_load(m)) for m in range(3)]
    core_copy.wait()
    x_send[...] = (
        attn_ref[2 * (1 - chip_x) + core] + core_recv[1 - chip_x].astype(jnp.float32)
    ).astype(low)
    x_copy = send(x_send, x_recv, send_sem.at[17], recv_sem.at[17], x_mate)
    own[...] = attn_ref[seq] + core_recv[chip_x].astype(jnp.float32)
    for hop in range(5):
        gain_copy.wait()
        gain_out[...] += g_recv[hop]
        if hop < 4:
            gain_copy = gain_start(hop + 1)
    z_copies = []
    for m in range(3):
        y_copies[m].wait()
        z_copies.append(z_start(m, ffn_load(m)))
    x_copy.wait()
    own[...] += x_recv[...].astype(jnp.float32)
    own_load = lambda j: own[j]
    y_copy = y_start(3, own_load)
    for m in range(3):
        ffn_out[m] = z_finish(m, ffn_load(m), z_copies[m])
    y_copy.wait()
    z_copy = z_start(3, own_load)
    share_low[seq] = z_finish(3, own_load, z_copy).astype(low)
    to_mate = send(share_low.at[seq], share_low.at[seq], send_sem.at[18], recv_sem.at[18], mate)
    to_x = send(share_low.at[seq], share_low.at[seq], send_sem.at[19], recv_sem.at[19], x_mate)
    to_x.wait()
    far = lax.rem(seq + 2, 4)
    onward = send(share_low.at[far], share_low.at[far], send_sem.at[20], recv_sem.at[20], mate)
    to_mate.wait()
    onward.wait()
    attn_out[...] = share_low[...].astype(jnp.float32)


def reduce_grads(attn_grads, ffn_grads, gain_grads):
    share, cols = attn_grads.shape[2:]
    low, full = jnp.bfloat16, jnp.float32
    vmem = pl.BlockSpec(memory_space=pltpu.VMEM)
    return pl.pallas_call(
        reduce_kernel,
        out_shape=(
            jax.ShapeDtypeStruct((4, share, cols), full),
            jax.ShapeDtypeStruct((3, share, cols), full),
            jax.ShapeDtypeStruct(gain_grads.shape, full),
        ),
        in_specs=[vmem] * 3,
        out_specs=(vmem, vmem, vmem),
        scratch_shapes=[
            pltpu.VMEM((2, 8, share, cols), low),
            pltpu.VMEM((2, 8, share, cols), low),
            pltpu.VMEM((8, share, cols), low),
            pltpu.VMEM((8, share, cols), low),
            pltpu.VMEM((8, share, cols), full),
            pltpu.VMEM((4, 4, share, cols), low),
            pltpu.VMEM((4, 4, share, cols), low),
            pltpu.VMEM((4, 3, share, cols), low),
            pltpu.VMEM((4, 3, share, cols), low),
            pltpu.VMEM((5,) + gain_grads.shape, full),
            pltpu.VMEM((4, share, cols), low),
            pltpu.SemaphoreType.DMA((27,)),
            pltpu.SemaphoreType.DMA((27,)),
        ],
        compiler_params=pltpu.CompilerParams(
            collective_id=0, has_side_effects=True, vmem_limit_bytes=60 * 1024 * 1024
        ),
        name="reduce_grads",
    )(attn_grads, ffn_grads, gain_grads)


def on_device(
    tokens,
    seg_ids,
    positions,
    attn_gain,
    w_query,
    w_key,
    w_value,
    w_out,
    ffn_gain,
    w_gate,
    w_up,
    w_down,
    cotangent,
):
    row_count, shard_len, model_width = tokens.shape
    row_len = shard_len * lax.axis_size("seq")
    groups = HEADS // KV_HEADS
    kv_width = KV_HEADS * HEAD_DIM
    doc_all = lax.all_gather(seg_ids, "seq", axis=1, tiled=True)
    query_place = lax.axis_index("seq") * shard_len + jnp.arange(shard_len, dtype=jnp.int32)
    key_place = jnp.arange(row_len, dtype=jnp.int32)
    allowed = (seg_ids[:, :, None] == doc_all[:, None, :]) & (
        key_place[None, None, :] <= query_place[None, :, None]
    )
    cos_table, sin_table = rope_tables(positions)
    gate_mat, up_mat, down_mat = w_gate, w_up, w_down
    residual = tokens.astype(jnp.float32)
    kept_runs = []
    for repeat in range(2):
        normed, attn_inverse = norm_forward(residual, attn_gain)
        query_pre = jnp.einsum("rcd,de->rce", normed, w_query, preferred_element_type=jnp.float32)
        key_pre = jnp.einsum("rcd,de->rce", normed, w_key, preferred_element_type=jnp.float32)
        value_pre = jnp.einsum("rcd,de->rce", normed, w_value, preferred_element_type=jnp.float32)
        queries = rotate(
            query_pre.reshape(row_count, shard_len, HEADS, HEAD_DIM), cos_table, sin_table
        ).astype(jnp.bfloat16)
        keys_local = rotate(
            key_pre.reshape(row_count, shard_len, KV_HEADS, HEAD_DIM), cos_table, sin_table
        ).astype(jnp.bfloat16)
        joined = jnp.concatenate(
            [keys_local.reshape(row_count, shard_len, kv_width), value_pre.astype(jnp.bfloat16)],
            axis=-1,
        )
        joined_all = lax.all_gather(joined, "seq", axis=1, tiled=True)
        keys_all = joined_all[..., :kv_width].reshape(row_count, row_len, KV_HEADS, HEAD_DIM)
        values_all = joined_all[..., kv_width:].reshape(row_count, row_len, KV_HEADS, HEAD_DIM)
        grouped = queries.reshape(row_count, shard_len, KV_HEADS, groups, HEAD_DIM)
        mixed_heads, log_total = lax.map(row_attend, (grouped, keys_all, values_all, allowed))
        mixed_low = mixed_heads.reshape(row_count, shard_len, HEADS * HEAD_DIM).astype(jnp.bfloat16)
        after_attn = residual + jnp.einsum(
            "rce,ed->rcd", mixed_low, w_out, preferred_element_type=jnp.float32
        )
        normed_two, ffn_inverse = norm_forward(after_attn, ffn_gain)
        normed_two = lax.all_gather(normed_two, "seq", axis=1, tiled=True)
        gate_pre = jnp.einsum(
            "rtd,df->rtf", normed_two, gate_mat, preferred_element_type=jnp.float32
        )
        up_pre = jnp.einsum("rtd,df->rtf", normed_two, up_mat, preferred_element_type=jnp.float32)
        ffn_hidden = (jax.nn.silu(gate_pre) * up_pre).astype(jnp.bfloat16)
        partial_sum = jnp.einsum(
            "rtf,fd->rtd", ffn_hidden, down_mat, preferred_element_type=jnp.float32
        )
        partial_sum = lax.psum_scatter(
            partial_sum.astype(jnp.bfloat16), "seq", scatter_dimension=1, tiled=True
        ).astype(jnp.float32)
        normed_rows, gate_pre, up_pre, ffn_out = (normed_two, gate_pre, up_pre, partial_sum)
        kept_runs.append(
            (
                residual,
                normed,
                attn_inverse,
                grouped,
                keys_all,
                values_all,
                log_total,
                mixed_low,
                after_attn,
                ffn_inverse,
                normed_rows,
                gate_pre,
                up_pre,
            )
        )
        residual = after_attn + ffn_out
    output = residual.astype(jnp.bfloat16)
    attn_gain_grad = jnp.zeros(attn_gain.shape, jnp.float32)
    ffn_gain_grad = jnp.zeros(ffn_gain.shape, jnp.float32)
    w_query_grad = jnp.zeros(w_query.shape, jnp.float32)
    w_key_grad = jnp.zeros(w_key.shape, jnp.float32)
    w_value_grad = jnp.zeros(w_value.shape, jnp.float32)
    w_out_grad = jnp.zeros(w_out.shape, jnp.float32)
    w_gate_grad = jnp.zeros(gate_mat.shape, jnp.float32)
    w_up_grad = jnp.zeros(up_mat.shape, jnp.float32)
    w_down_grad = jnp.zeros(down_mat.shape[::-1], jnp.float32)
    upstream = cotangent.astype(jnp.float32)
    for repeat in (1, 0):
        (
            residual,
            normed,
            attn_inverse,
            grouped,
            keys_all,
            values_all,
            log_total,
            mixed_low,
            after_attn,
            ffn_inverse,
            normed_rows,
            gate_pre,
            up_pre,
        ) = kept_runs[repeat]
        ffn_grad = lax.all_gather(upstream.astype(jnp.bfloat16), "seq", axis=1, tiled=True)
        sigmoid_gate = jax.nn.sigmoid(gate_pre)
        silu_gate = jax.nn.silu(gate_pre)
        hidden = (silu_gate * up_pre).astype(jnp.bfloat16)
        w_down_grad = w_down_grad + jnp.einsum(
            "rtf,rtd->df", hidden, ffn_grad, preferred_element_type=jnp.float32
        )
        hidden_grad = jnp.einsum(
            "rtd,fd->rtf", ffn_grad, down_mat, preferred_element_type=jnp.float32
        )
        gate_grad = (
            hidden_grad * up_pre * sigmoid_gate * (1.0 + gate_pre * (1.0 - sigmoid_gate))
        ).astype(jnp.bfloat16)
        up_grad = (hidden_grad * silu_gate).astype(jnp.bfloat16)
        w_gate_grad = w_gate_grad + jnp.einsum(
            "rtd,rtf->df", normed_rows, gate_grad, preferred_element_type=jnp.float32
        )
        w_up_grad = w_up_grad + jnp.einsum(
            "rtd,rtf->df", normed_rows, up_grad, preferred_element_type=jnp.float32
        )
        normed_two_grad = jnp.einsum(
            "rtf,df->rtd", gate_grad, gate_mat, preferred_element_type=jnp.float32
        ) + jnp.einsum("rtf,df->rtd", up_grad, up_mat, preferred_element_type=jnp.float32)
        normed_two_grad = lax.psum_scatter(
            normed_two_grad.astype(jnp.bfloat16), "seq", scatter_dimension=1, tiled=True
        ).astype(jnp.float32)
        after_grad, gain_two = norm_backward(after_attn, ffn_inverse, ffn_gain, normed_two_grad)
        after_grad = after_grad + upstream
        ffn_gain_grad = ffn_gain_grad + gain_two
        attn_grad = after_grad.astype(jnp.bfloat16)
        w_out_grad = w_out_grad + jnp.einsum(
            "rce,rcd->ed", mixed_low, attn_grad, preferred_element_type=jnp.float32
        )
        mixed_grad = jnp.einsum(
            "rcd,ed->rce", attn_grad, w_out, preferred_element_type=jnp.float32
        ).astype(jnp.bfloat16)
        mixed_grad = mixed_grad.reshape(row_count, shard_len, KV_HEADS, groups, HEAD_DIM)
        query_grad, key_grad, value_grad = lax.map(
            row_backward, (grouped, keys_all, values_all, allowed, log_total, mixed_grad)
        )
        joined_grad = jnp.concatenate(
            [
                key_grad.reshape(row_count, row_len, kv_width),
                value_grad.reshape(row_count, row_len, kv_width),
            ],
            axis=-1,
        )
        local_grad = lax.psum_scatter(
            joined_grad.astype(jnp.bfloat16), "seq", scatter_dimension=1, tiled=True
        ).astype(jnp.float32)
        key_back = rotate(
            local_grad[..., :kv_width].reshape(row_count, shard_len, KV_HEADS, HEAD_DIM),
            cos_table,
            -sin_table,
        )
        key_back = key_back.reshape(row_count, shard_len, kv_width).astype(jnp.bfloat16)
        value_back = local_grad[..., kv_width:].astype(jnp.bfloat16)
        query_back = rotate(
            query_grad.reshape(row_count, shard_len, HEADS, HEAD_DIM), cos_table, -sin_table
        )
        query_back = query_back.reshape(row_count, shard_len, HEADS * HEAD_DIM).astype(jnp.bfloat16)
        w_query_grad = w_query_grad + jnp.einsum(
            "rcd,rce->de", normed, query_back, preferred_element_type=jnp.float32
        )
        w_key_grad = w_key_grad + jnp.einsum(
            "rcd,rce->de", normed, key_back, preferred_element_type=jnp.float32
        )
        w_value_grad = w_value_grad + jnp.einsum(
            "rcd,rce->de", normed, value_back, preferred_element_type=jnp.float32
        )
        normed_grad = jnp.einsum(
            "rce,de->rcd", query_back, w_query, preferred_element_type=jnp.float32
        )
        normed_grad = normed_grad + jnp.einsum(
            "rce,de->rcd", key_back, w_key, preferred_element_type=jnp.float32
        )
        normed_grad = normed_grad + jnp.einsum(
            "rce,de->rcd", value_back, w_value, preferred_element_type=jnp.float32
        )
        residual_grad, gain_one = norm_backward(residual, attn_inverse, attn_gain, normed_grad)
        attn_gain_grad = attn_gain_grad + gain_one
        upstream = residual_grad + after_grad
    if lax.axis_size("dp") == 8 and lax.axis_size("seq") == 4 and model_width % 64 == 0:
        share = model_width // 8
        attn_grads = jnp.concatenate([w_query_grad, w_key_grad, w_value_grad, w_out_grad], axis=1)
        attn_grads = attn_grads.reshape(8, share, 4, -1).transpose(2, 0, 1, 3)
        ffn_grads = jnp.stack([w_gate_grad, w_up_grad, w_down_grad]).reshape(3, 8, share, -1)
        gain_grads = jnp.stack([attn_gain_grad, ffn_gain_grad]).reshape(2, 8, share).transpose(1, 0, 2)
        gain_grads = jnp.pad(gain_grads, ((0, 0), (0, 6), (0, 128 - share)))
        attn_share, ffn_share, gain_share = reduce_grads(attn_grads, ffn_grads, gain_grads)
        attn_share = attn_share.transpose(1, 0, 2).reshape(share, -1)
        own_gains = lax.dynamic_index_in_dim(gain_share, lax.axis_index("dp"), 0, keepdims=False)
        q_end = w_query.shape[1]
        k_end = q_end + w_key.shape[1]
        v_end = k_end + w_value.shape[1]
        return (
            output,
            upstream,
            own_gains[0, :share],
            attn_share[:, :q_end],
            attn_share[:, q_end:k_end],
            attn_share[:, k_end:v_end],
            attn_share[:, v_end:],
            own_gains[1, :share],
            ffn_share[0],
            ffn_share[1],
            ffn_share[2].T,
        )

    def over_rows(grad):
        low_grad = grad.astype(jnp.bfloat16)
        return lax.psum_scatter(low_grad, "dp", scatter_dimension=0, tiled=True).astype(jnp.float32)

    def over_all(grad):
        return lax.psum(over_rows(grad).astype(jnp.bfloat16), "seq").astype(jnp.float32)

    return (
        output,
        upstream,
        over_all(attn_gain_grad),
        over_all(w_query_grad),
        over_all(w_key_grad),
        over_all(w_value_grad),
        over_all(w_out_grad),
        over_all(ffn_gain_grad),
        over_rows(w_gate_grad),
        over_rows(w_up_grad),
        over_rows(w_down_grad).T,
    )


def solution(mesh):
    in_specs = (
        P("dp", "seq", None),
        P("dp", "seq"),
        P("dp", "seq"),
        P(),
        P(),
        P(),
        P(),
        P(),
        P(),
        P(None, "seq"),
        P(None, "seq"),
        P("seq", None),
        P("dp", "seq", None),
    )
    out_specs = (
        P("dp", "seq", None),
        P("dp", "seq", None),
        P("dp"),
        P("dp", None),
        P("dp", None),
        P("dp", None),
        P("dp", None),
        P("dp"),
        P("dp", "seq"),
        P("dp", "seq"),
        P("seq", "dp"),
    )
    return jax.shard_map(
        on_device, mesh=mesh, in_specs=in_specs, out_specs=out_specs, check_vma=False
    )
```

```python
import functools

import jax
import jax.numpy as jnp
from jax import lax
from jax.experimental import pallas as pl
from jax.experimental.pallas import tpu as pltpu
from jax.sharding import PartitionSpec as P

MESH_ID = pl.DeviceIdType.MESH
HEADS = 15
KV_HEADS = 5
GROUP = 3
HEAD_DIM = 64
EPSILON = 1e-05
THETA = 10000.0
CHUNKS = 2
MASKED = -1e30
LOW = jnp.bfloat16
FULL = jnp.float32
SCALE = HEAD_DIM ** (-0.5)
NT = (((1,), (1,)), ((), ()))
TN = (((0,), (0,)), ((), ()))


def device(seq_pos, dp_pos):
    return {"seq": seq_pos, "dp": dp_pos}


def send(src, dst, send_sem, recv_sem, target):
    copy = pltpu.make_async_remote_copy(
        src_ref=src,
        dst_ref=dst,
        send_sem=send_sem,
        recv_sem=recv_sem,
        device_id=target,
        device_id_type=MESH_ID,
    )
    copy.start()
    return copy


def greet(targets):
    barrier = pltpu.get_barrier_semaphore()
    for target in targets:
        pl.semaphore_signal(barrier, inc=1, device_id=target, device_id_type=MESH_ID)
    pl.semaphore_wait(barrier, len(targets))


def dot(left, right, dims=None):
    if dims is None:
        return jnp.dot(left, right, preferred_element_type=FULL)
    return lax.dot_general(left, right, dims, preferred_element_type=FULL)


def inverse_rms(value):
    return lax.rsqrt(jnp.mean(value * value, axis=-1, keepdims=True) + EPSILON)


def swap_halves(value):
    lane = lax.broadcasted_iota(jnp.int32, value.shape, 1)
    first = lax.rem(lane, HEAD_DIM) < HEAD_DIM // 2
    return jnp.where(first, pltpu.roll(value, 96, 1), pltpu.roll(value, 32, 1))


def attn_forward_kernel(
    res_ref, gains_ref, w_kvq_ref, w_out_ref, trig_ref, place_ref,
    normed_out, q_out, kv_out, log_out, mixed_out, after_out, normed_two_out,
    peak, total, acc, send_sem, recv_sem,
):
    seq, dp = lax.axis_index("seq"), lax.axis_index("dp")
    core, chip_x = lax.rem(seq, 2), lax.div(seq, 2)
    mate_seq, far_seq = seq + 1 - 2 * core, lax.rem(seq + 2, 4)
    mate, x_mate = device(mate_seq, dp), device(far_seq, dp)
    length = res_ref.shape[0]
    stacked = GROUP * length
    residual = res_ref[...]
    normed_out[...] = (residual * inverse_rms(residual) * gains_ref[0:1, :]).astype(LOW)
    kv_width = 2 * KV_HEADS * HEAD_DIM
    kv_pre = dot(normed_out[...], w_kvq_ref[:, :kv_width])
    for g in range(KV_HEADS):
        part = kv_pre[:, g * 128 : (g + 1) * 128]
        turned = part * trig_ref[2] + swap_halves(part) * trig_ref[3]
        kv_out[seq, :, g * 128 : (g + 1) * 128] = turned.astype(LOW)
    greet([mate, x_mate])
    own_kv = kv_out.at[seq]
    to_mate = send(own_kv, own_kv, send_sem.at[0], recv_sem.at[0], mate)
    to_x = send(own_kv, own_kv, send_sem.at[1], recv_sem.at[1], x_mate)
    q_pre = dot(normed_out[...], w_kvq_ref[:, kv_width:])
    lane = lax.broadcasted_iota(jnp.int32, (length, 128), 1)
    for pair in range((HEADS + 1) // 2):
        width = min(128, HEADS * HEAD_DIM - pair * 128)
        part = q_pre[:, pair * 128 : pair * 128 + width]
        if width < 128:
            part = jnp.concatenate([part, part], axis=1)
        turned = (part * trig_ref[0] + swap_halves(part) * trig_ref[1]) * SCALE
        q_out[2 * pair] = jnp.where(lane < HEAD_DIM, turned, 0.0).astype(LOW)
        if width == 128:
            q_out[2 * pair + 1] = jnp.where(lane < HEAD_DIM, pltpu.roll(turned, 64, 1), 0.0).astype(LOW)

    start, place = place_ref[0:1, :], place_ref[1:2, :]

    def attend(block, g, first):
        kv_g = kv_out[block, :, pl.ds(pl.multiple_of(g * 128, 128), 128)]
        q_g = q_out[pl.ds(3 * g, 3)].reshape(stacked, 128)
        scores = dot(kv_g, q_g, NT)
        key = lax.broadcasted_iota(jnp.int32, (length, stacked), 0) + block * length
        allowed = key >= start
        if first:
            allowed = allowed & (key <= place)
        scores = jnp.where(allowed, scores, MASKED)
        here = jnp.max(scores, axis=0, keepdims=True)
        if first:
            new_peak = here
        else:
            new_peak = jnp.maximum(peak[g], here)
        weights = jnp.exp(scores - new_peak)
        row_total = jnp.sum(weights, axis=0, keepdims=True)
        mix = dot(kv_g, weights.astype(LOW), TN)[HEAD_DIM:]
        if not first:
            fade = jnp.exp(peak[g] - new_peak)
            row_total = row_total + fade * total[g]
            mix = mix + fade * acc[g]
        peak[g], total[g], acc[g] = new_peak, row_total, mix

    @pl.loop(0, KV_HEADS)
    def _(g):
        attend(seq, g, True)

    to_mate.wait()

    @pl.when(core == 1)
    def _():
        @pl.loop(0, KV_HEADS)
        def _(g):
            attend(mate_seq, g, False)

    to_x.wait()
    far_kv = kv_out.at[far_seq]
    onward = send(far_kv, far_kv, send_sem.at[2], recv_sem.at[2], mate)

    @pl.when(chip_x == 1)
    def _():
        @pl.loop(0, KV_HEADS)
        def _(g):
            attend(far_seq, g, False)

    onward.wait()

    @pl.when(chip_x == 1)
    def _():
        @pl.loop(0, KV_HEADS)
        def _(g):
            attend(lax.rem(mate_seq + 2, 4), g, False)

    for g in range(KV_HEADS):
        heads = (acc[g] / total[g]).T.astype(LOW)
        log_out[g] = peak[g] + jnp.log(total[g])
        for i in range(GROUP):
            h = GROUP * g + i
            mixed_out[:, h * HEAD_DIM : (h + 1) * HEAD_DIM] = heads[i * length : (i + 1) * length]
    after = residual + dot(mixed_out[...], w_out_ref[...])
    after_out[...] = after
    normed_two_out[...] = (after * inverse_rms(after) * gains_ref[1:2, :]).astype(LOW)


VMEM = pl.BlockSpec(memory_space=pltpu.VMEM)


def attn_forward(residual, gains, w_kvq, w_out, trig, place):
    length, width = residual.shape
    kv_width = 2 * KV_HEADS * HEAD_DIM
    shapes = (
        ((length, width), LOW),
        ((HEADS, length, 128), LOW),
        ((4, length, kv_width), LOW),
        ((KV_HEADS, 1, GROUP * length), FULL),
        ((length, HEADS * HEAD_DIM), LOW),
        ((length, width), FULL),
        ((length, width), LOW),
    )
    return pl.pallas_call(
        attn_forward_kernel,
        out_shape=tuple(jax.ShapeDtypeStruct(*s) for s in shapes),
        in_specs=[VMEM] * 6,
        out_specs=(VMEM,) * len(shapes),
        scratch_shapes=[
            pltpu.VMEM((KV_HEADS, 1, GROUP * length), FULL),
            pltpu.VMEM((KV_HEADS, 1, GROUP * length), FULL),
            pltpu.VMEM((KV_HEADS, HEAD_DIM, GROUP * length), FULL),
            pltpu.SemaphoreType.DMA((3,)),
            pltpu.SemaphoreType.DMA((3,)),
        ],
        compiler_params=pltpu.CompilerParams(
            collective_id=1, has_side_effects=True, vmem_limit_bytes=60 * 1024 * 1024
        ),
        name="attn_forward",
    )(residual, gains, w_kvq, w_out, trig, place)


def prepare(positions, w_query, w_key, w_value):
    length = positions.shape[0]
    frequency = THETA ** (-(jnp.arange(HEAD_DIM // 2, dtype=FULL) * 2.0 / HEAD_DIM))
    angles = positions.astype(FULL)[:, None] * frequency
    cos, sin = jnp.cos(angles), jnp.sin(angles)
    one, none = jnp.ones((length, HEAD_DIM), FULL), jnp.zeros((length, HEAD_DIM), FULL)
    trig = jnp.stack(
        [
            jnp.concatenate([cos, cos, cos, cos], 1),
            jnp.concatenate([-sin, sin, -sin, sin], 1),
            jnp.concatenate([cos, cos, one], 1),
            jnp.concatenate([-sin, sin, none], 1),
        ]
    )
    width = w_key.shape[0]
    pairs = jnp.stack([w_key.reshape(width, KV_HEADS, HEAD_DIM), w_value.reshape(width, KV_HEADS, HEAD_DIM)], axis=2)
    w_kvq = jnp.concatenate([pairs.reshape(width, -1), w_query], axis=1)
    own = lax.axis_index("seq") * length + jnp.arange(length, dtype=jnp.int32)
    place = jnp.stack([jnp.tile(own - positions, GROUP), jnp.tile(own, GROUP)])
    place = jnp.pad(place, ((0, 6), (0, 0)))
    return trig, w_kvq, place


def ffn_forward_kernel(
    after_ref, normed_ref, w_gate_ref, w_up_ref, w_down_ref,
    res_out, rows_out, gate_out, up_out,
    mate_send, mate_recv, x_send, x_recv, own_far,
    send_sem, recv_sem,
):
    seq, dp = lax.axis_index("seq"), lax.axis_index("dp")
    core = lax.rem(seq, 2)
    mate_seq, far_seq = seq + 1 - 2 * core, lax.rem(seq + 2, 4)
    far_mate = lax.rem(mate_seq + 2, 4)
    mate, x_mate = device(mate_seq, dp), device(far_seq, dp)
    length = after_ref.shape[0]
    step = length // CHUNKS
    greet([mate, x_mate])
    part = lambda k: pl.ds(k * step, step)

    def hop(index, src, dst, target):
        return send(src, dst, send_sem.at[index], recv_sem.at[index], target)

    rows_out[seq] = normed_ref[...]
    own_rows = lambda k: rows_out.at[seq, part(k)]
    far_rows = lambda k: rows_out.at[far_seq, part(k)]
    to_x = [hop(k, own_rows(k), own_rows(k), x_mate) for k in range(CHUNKS)]
    to_mate = hop(CHUNKS, rows_out.at[seq], rows_out.at[seq], mate)
    base = CHUNKS + 1

    def ffn(quarter, rows):
        block = rows_out[quarter, rows]
        gate = dot(block, w_gate_ref[...])
        up = dot(block, w_up_ref[...])
        gate_out[quarter, rows] = gate.astype(LOW)
        up_out[quarter, rows] = up.astype(LOW)
        hidden = (gate * jax.nn.sigmoid(gate) * up).astype(LOW)
        return dot(hidden, w_down_ref[...])

    everything = pl.ds(0, length)
    res_out[...] = after_ref[...] + ffn(seq, everything)
    to_mate.wait()
    mate_send[0] = ffn(mate_seq, everything).astype(LOW)
    back = hop(base, mate_send.at[0], mate_recv.at[0], mate)
    onward = []
    for k in range(CHUNKS):
        to_x[k].wait()
        onward.append(hop(base + 1 + k, far_rows(k), far_rows(k), mate))
        own_far[part(k)] = ffn(far_seq, part(k))
        onward[k].wait()
        mate_send[1, part(k)] = ffn(far_mate, part(k)).astype(LOW)
        joint = hop(base + 1 + CHUNKS + k, mate_send.at[1, part(k)], mate_recv.at[1, part(k)], mate)
        joint.wait()
        x_send[part(k)] = (own_far[part(k)] + mate_recv[1, part(k)].astype(FULL)).astype(LOW)
        onward.append(
            hop(base + 1 + 2 * CHUNKS + k, x_send.at[part(k)], x_recv.at[part(k)], x_mate)
        )
        onward[k], onward[-1] = onward[-1], onward[k]
        onward.pop()
    back.wait()
    res_out[...] += mate_recv[0].astype(FULL)
    for k in range(CHUNKS):
        onward[k].wait()
        res_out[part(k)] += x_recv[part(k)].astype(FULL)


def ffn_forward(after, normed_two, w_gate, w_up, w_down):
    length, width = after.shape
    hidden = w_gate.shape[1]
    shapes = (
        ((length, width), FULL),
        ((4, length, width), LOW),
        ((4, length, hidden), LOW),
        ((4, length, hidden), LOW),
    )
    sems = 3 * CHUNKS + CHUNKS + 2
    return pl.pallas_call(
        ffn_forward_kernel,
        out_shape=tuple(jax.ShapeDtypeStruct(*s) for s in shapes),
        in_specs=[VMEM] * 5,
        out_specs=(VMEM,) * len(shapes),
        scratch_shapes=[
            pltpu.VMEM((2, length, width), LOW),
            pltpu.VMEM((2, length, width), LOW),
            pltpu.VMEM((length, width), LOW),
            pltpu.VMEM((length, width), LOW),
            pltpu.VMEM((length, width), FULL),
            pltpu.SemaphoreType.DMA((sems,)),
            pltpu.SemaphoreType.DMA((sems,)),
        ],
        compiler_params=pltpu.CompilerParams(
            collective_id=2, has_side_effects=True, vmem_limit_bytes=60 * 1024 * 1024
        ),
        name="ffn_forward",
    )(after, normed_two, w_gate, w_up, w_down)


def norm_back(value, gain, grad):
    inverse = inverse_rms(value)
    weighted = grad * gain
    inner = jnp.mean(weighted * value, axis=-1, keepdims=True)
    back = inverse * weighted - value * (inverse * inverse * inverse) * inner
    return back, jnp.sum(grad * value * inverse, axis=0, keepdims=True)


def ffn_backward_kernel(
    up_ref, after_ref, gains_ref, rows_ref, gate_ref, upp_ref, w_gate_ref, w_up_ref, w_down_ref, *rest
):
    (prev_ref,) = rest[:-14] if len(rest) == 15 else (None,)
    (
        grad_out, gain_out, weight_out,
        low_all, gate_grad, up_grad, hidden,
        mate_send, mate_recv, x_send, x_recv, own_far,
        send_sem, recv_sem,
    ) = rest[-14:]
    seq, dp = lax.axis_index("seq"), lax.axis_index("dp")
    core, chip_x = lax.rem(seq, 2), lax.div(seq, 2)
    mate_seq, far_seq = seq + 1 - 2 * core, lax.rem(seq + 2, 4)
    far_mate = lax.rem(mate_seq + 2, 4)
    mate, x_mate = device(mate_seq, dp), device(far_seq, dp)
    length, width = up_ref.shape
    step = length // CHUNKS
    greet([mate, x_mate])
    part = lambda k: pl.ds(k * step, step)

    def hop(index, src, dst, target):
        return send(src, dst, send_sem.at[index], recv_sem.at[index], target)

    low_all[seq] = up_ref[...].astype(LOW)
    own_rows = lambda k: low_all.at[seq, part(k)]
    far_rows = lambda k: low_all.at[far_seq, part(k)]
    to_x = [hop(k, own_rows(k), own_rows(k), x_mate) for k in range(CHUNKS)]
    to_mate = hop(CHUNKS, low_all.at[seq], low_all.at[seq], mate)
    base = CHUNKS + 1

    def ffn(quarter, rows):
        hidden_grad = dot(low_all[quarter, rows], w_down_ref[...], NT)
        gate = gate_ref[quarter, rows].astype(FULL)
        up = upp_ref[quarter, rows].astype(FULL)
        bend = jax.nn.sigmoid(gate)
        silu = gate * bend
        hidden[quarter, rows] = (silu * up).astype(LOW)
        gate_low = (hidden_grad * up * bend * (1.0 + gate * (1.0 - bend))).astype(LOW)
        up_low = (hidden_grad * silu).astype(LOW)
        gate_grad[quarter, rows] = gate_low
        up_grad[quarter, rows] = up_low
        return dot(gate_low, w_gate_ref[...], NT) + dot(up_low, w_up_ref[...], NT)

    def weights(first_quarter, first):
        pair = lambda ref: ref[pl.ds(first_quarter, 2)].reshape(2 * length, ref.shape[2])
        rows, low = pair(rows_ref), pair(low_all)
        for i, (left, right) in enumerate(
            ((rows, pair(gate_grad)), (rows, pair(up_grad)), (low, pair(hidden)))
        ):
            term = dot(left, right, TN)
            if not first:
                term = term + weight_out[i]
            elif prev_ref is not None:
                term = term + prev_ref[i]
            weight_out[i] = term

    everything = pl.ds(0, length)
    grad_out[...] = ffn(seq, everything)
    to_mate.wait()
    mate_send[0] = ffn(mate_seq, everything).astype(LOW)
    back = hop(base, mate_send.at[0], mate_recv.at[0], mate)
    last = []
    for k in range(CHUNKS):
        to_x[k].wait()
        onward = hop(base + 1 + k, far_rows(k), far_rows(k), mate)
        own_far[part(k)] = ffn(far_seq, part(k))
        onward.wait()
        mate_send[1, part(k)] = ffn(far_mate, part(k)).astype(LOW)
        joint = hop(base + 1 + CHUNKS + k, mate_send.at[1, part(k)], mate_recv.at[1, part(k)], mate)
        joint.wait()
        x_send[part(k)] = (own_far[part(k)] + mate_recv[1, part(k)].astype(FULL)).astype(LOW)
        last.append(hop(base + 1 + 2 * CHUNKS + k, x_send.at[part(k)], x_recv.at[part(k)], x_mate))
        if k == 0:
            weights(2 * chip_x, True)
    weights(2 - 2 * chip_x, False)
    back.wait()
    total = grad_out[...] + mate_recv[0].astype(FULL)
    for k in range(CHUNKS):
        last[k].wait()
    total = total + x_recv[...].astype(FULL)
    sent_back, gain_term = norm_back(after_ref[...], gains_ref[1:2, :], total)
    grad_out[...] = up_ref[...] + sent_back
    gain_out[...] = jnp.broadcast_to(gain_term, gain_out.shape)


def ffn_backward(upstream, after, gains, rows_all, gate_all, up_all, w_gate, w_up, w_down, prev=None):
    length, width = after.shape
    hidden = w_gate.shape[1]
    shapes = (
        ((length, width), FULL),
        ((8, width), FULL),
        ((3, width, hidden), FULL),
    )
    sems = 3 * CHUNKS + CHUNKS + 2
    args = (upstream, after, gains, rows_all, gate_all, up_all, w_gate, w_up, w_down)
    if prev is not None:
        args = args + (prev,)
    return pl.pallas_call(
        ffn_backward_kernel,
        out_shape=tuple(jax.ShapeDtypeStruct(*s) for s in shapes),
        in_specs=[VMEM] * len(args),
        out_specs=(VMEM,) * len(shapes),
        scratch_shapes=[
            pltpu.VMEM((4, length, width), LOW),
            pltpu.VMEM((4, length, hidden), LOW),
            pltpu.VMEM((4, length, hidden), LOW),
            pltpu.VMEM((4, length, hidden), LOW),
            pltpu.VMEM((2, length, width), LOW),
            pltpu.VMEM((2, length, width), LOW),
            pltpu.VMEM((length, width), LOW),
            pltpu.VMEM((length, width), LOW),
            pltpu.VMEM((length, width), FULL),
            pltpu.SemaphoreType.DMA((sems,)),
            pltpu.SemaphoreType.DMA((sems,)),
        ],
        compiler_params=pltpu.CompilerParams(
            collective_id=3 if prev is None else 4, has_side_effects=True, vmem_limit_bytes=60 * 1024 * 1024
        ),
        name="ffn_backward",
    )(*args)


def attn_backward_kernel(
    after_grad_ref, res_ref, normed_ref, gains_ref, q_ref, kv_ref, log_ref, mixed_ref,
    w_kvq_ref, w_out_ref, trig_ref, place_ref, *rest
):
    (prev_ref,) = rest[:-12] if len(rest) == 13 else (None,)
    (
        grad_out, gain_out, weight_out,
        mixed_grad, delta, kv_grad, query_grad, back,
        grad_send, grad_recv,
        send_sem, recv_sem,
    ) = rest[-12:]
    seq, dp = lax.axis_index("seq"), lax.axis_index("dp")
    core, chip_x = lax.rem(seq, 2), lax.div(seq, 2)
    mate_seq, far_seq = seq + 1 - 2 * core, lax.rem(seq + 2, 4)
    far_mate = lax.rem(mate_seq + 2, 4)
    mate, x_mate = device(mate_seq, dp), device(far_seq, dp)
    length, width = res_ref.shape
    stacked = GROUP * length
    kv_width = 2 * KV_HEADS * HEAD_DIM
    greet([mate, x_mate])

    def hop(index, src, dst, target):
        return send(src, dst, send_sem.at[index], recv_sem.at[index], target)

    low_grad = after_grad_ref[...].astype(LOW)
    mixed_back = dot(low_grad, w_out_ref[...], NT)
    lane = lax.broadcasted_iota(jnp.int32, (length, 128), 1)
    for pair in range((HEADS + 1) // 2):
        span = min(128, HEADS * HEAD_DIM - pair * 128)
        part = mixed_back[:, pair * 128 : pair * 128 + span]
        if span < 128:
            part = jnp.concatenate([part, part], axis=1)
        else:
            mixed_grad[2 * pair + 1] = jnp.where(lane >= HEAD_DIM, part, 0.0).astype(LOW)
        mixed_grad[2 * pair] = jnp.where(lane >= HEAD_DIM, pltpu.roll(part, 64, 1), 0.0).astype(LOW)
    product = mixed_back.astype(LOW).astype(FULL) * mixed_ref[...].astype(FULL)
    high = product.astype(LOW)
    rest_low = (product - high.astype(FULL)).astype(LOW)
    head = lax.broadcasted_iota(jnp.int32, (16, HEADS * HEAD_DIM), 0)
    column = lax.broadcasted_iota(jnp.int32, (16, HEADS * HEAD_DIM), 1)
    pick = jnp.where(lax.div(column, HEAD_DIM) == head, 1.0, 0.0).astype(LOW)
    sums = dot(pick, high, NT) + dot(pick, rest_low, NT)
    for g in range(KV_HEADS):
        delta[g] = jnp.concatenate([sums[3 * g + i : 3 * g + i + 1] for i in range(GROUP)], axis=1)
    query_grad[...] = jnp.zeros_like(query_grad)

    start, place = place_ref[0:1, :], place_ref[1:2, :]

    def attend(block, g, diagonal):
        columns = pl.ds(pl.multiple_of(g * 128, 128), 128)
        kv_g = kv_ref[block, :, columns]
        q_g = q_ref[pl.ds(3 * g, 3)].reshape(stacked, 128)
        out_g = mixed_grad[pl.ds(3 * g, 3)].reshape(stacked, 128)
        scores = dot(kv_g, q_g, NT)
        key = lax.broadcasted_iota(jnp.int32, (length, stacked), 0) + block * length
        allowed = key >= start
        if diagonal:
            allowed = allowed & (key <= place)
        weights = jnp.where(allowed, jnp.exp(scores - log_ref[g]), 0.0)
        probs_grad = dot(kv_g, out_g, NT)
        score_grad = (weights * (probs_grad - delta[g])).astype(LOW)
        kv_grad[block, :, columns] = dot(weights.astype(LOW), out_g) + dot(score_grad, q_g)
        query_grad[g] += dot(kv_g, score_grad, TN)[:HEAD_DIM]

    def attend_all(block, condition, diagonal=False):
        @pl.when(condition)
        def _():
            @pl.loop(0, KV_HEADS)
            def _(g):
                attend(block, g, diagonal)

        if not diagonal:
            @pl.when(jnp.logical_not(condition))
            def _():
                kv_grad[block] = jnp.zeros_like(kv_grad[block])

    right = chip_x == 1
    attend_all(far_mate, right)
    grad_send[0] = kv_grad[far_mate].astype(LOW)
    joint = hop(0, grad_send.at[0], grad_recv.at[0], mate)
    attend_all(far_seq, right)
    joint.wait()
    grad_send[1] = (kv_grad[far_seq] + grad_recv[0].astype(FULL)).astype(LOW)
    across = hop(1, grad_send.at[1], grad_recv.at[1], x_mate)
    attend_all(mate_seq, core == 1)
    grad_send[2] = kv_grad[mate_seq].astype(LOW)
    beside = hop(2, grad_send.at[2], grad_recv.at[2], mate)
    attend_all(seq, seq >= 0, True)

    for g in range(KV_HEADS):
        heads = query_grad[g].T * SCALE
        for i in range(GROUP):
            h = GROUP * g + i
            part = heads[i * length : (i + 1) * length]
            part = jnp.concatenate([part, part], axis=1)
            turned = part * trig_ref[0] - swap_halves(part) * trig_ref[1]
            at = kv_width + h * HEAD_DIM
            back[:, at : at + HEAD_DIM] = turned[:, :HEAD_DIM].astype(LOW)

    def weight(block, at, left, right):
        columns = slice(at, at + right.shape[1])
        term = dot(left, right, TN)
        weight_out[block, :, columns] = term if prev_ref is None else term + prev_ref[block, :, columns]

    third = width // 3
    cut = kv_width + 2 * third
    weight(2, 0, mixed_ref[...], low_grad[:, : 2 * third])
    weight(3, third, mixed_ref[...], low_grad[:, 2 * third :])
    weight(1, 0, normed_ref[...], back[:, kv_width:cut])
    weight(3, 0, normed_ref[...], back[:, cut:])
    normed_grad = dot(back[:, kv_width:], w_kvq_ref[:, kv_width:], NT)

    across.wait()
    beside.wait()
    own = kv_grad[seq] + grad_recv[1].astype(FULL) + grad_recv[2].astype(FULL)
    for g in range(KV_HEADS):
        part = own[:, g * 128 : (g + 1) * 128]
        back[:, g * 128 : (g + 1) * 128] = (part * trig_ref[2] - swap_halves(part) * trig_ref[3]).astype(LOW)
    weight(0, 0, normed_ref[...], back[:, :kv_width])
    normed_grad = normed_grad + dot(back[:, :kv_width], w_kvq_ref[:, :kv_width], NT)
    sent_back, gain_term = norm_back(res_ref[...], gains_ref[0:1, :], normed_grad)
    grad_out[...] = after_grad_ref[...] + sent_back
    gain_out[...] = jnp.broadcast_to(gain_term, gain_out.shape)


def attn_backward(
    after_grad, residual, normed, gains, q, kv, log_total, mixed, w_kvq, w_out, trig, place, prev=None
):
    length, width = residual.shape
    kv_width = 2 * KV_HEADS * HEAD_DIM
    args = (after_grad, residual, normed, gains, q, kv, log_total, mixed, w_kvq, w_out, trig, place)
    if prev is not None:
        args = args + (prev,)
    shapes = (
        ((length, width), FULL),
        ((8, width), FULL),
        ((4, width, kv_width), FULL),
    )
    return pl.pallas_call(
        attn_backward_kernel,
        out_shape=tuple(jax.ShapeDtypeStruct(*s) for s in shapes),
        in_specs=[VMEM] * len(args),
        out_specs=(VMEM,) * len(shapes),
        scratch_shapes=[
            pltpu.VMEM((HEADS, length, 128), LOW),
            pltpu.VMEM((KV_HEADS, 1, GROUP * length), FULL),
            pltpu.VMEM((4, length, kv_width), FULL),
            pltpu.VMEM((KV_HEADS, HEAD_DIM, GROUP * length), FULL),
            pltpu.VMEM((length, kv_width + width), LOW),
            pltpu.VMEM((3, length, kv_width), LOW),
            pltpu.VMEM((3, length, kv_width), LOW),
            pltpu.SemaphoreType.DMA((3,)),
            pltpu.SemaphoreType.DMA((3,)),
        ],
        compiler_params=pltpu.CompilerParams(
            collective_id=5 if prev is None else 6, has_side_effects=True, vmem_limit_bytes=60 * 1024 * 1024
        ),
        name="attn_backward",
    )(*args)


def reduce_kernel(
    attn_ref, ffn_ref, gain_ref,
    attn_out, ffn_out, gain_out,
    core_send, core_recv, x_send, x_recv, own,
    y_send, y_recv, z_send, z_recv, g_recv, share_low,
    send_sem, recv_sem,
):
    seq, dp = lax.axis_index("seq"), lax.axis_index("dp")
    core, chip_x = lax.rem(seq, 2), lax.div(seq, 2)
    row_y, row_z = lax.rem(dp, 2), lax.div(dp, 2)
    mate = device(seq + 1 - 2 * core, dp)
    x_mate = device(lax.rem(seq + 2, 4), dp)
    y_mate = device(seq, dp + 1 - 2 * row_y)
    z_of = [lax.rem(row_z + k, 4) for k in range(1, 4)]
    z_mates = [device(seq, z * 2 + row_y) for z in z_of]
    greet([mate, x_mate, y_mate] + z_mates)
    low = jnp.bfloat16

    def y_start(index, load):
        for z in range(4):
            y_send[index, z] = load(2 * z + 1 - row_y).astype(low)
        return send(y_send.at[index], y_recv.at[index], send_sem.at[index], recv_sem.at[index], y_mate)

    def z_start(index, load):
        copies = []
        for k in range(3):
            z = z_of[k]
            z_send[index, k] = (load(2 * z + row_y) + y_recv[index, z].astype(jnp.float32)).astype(low)
            sem = 4 + 3 * index + k
            copies.append(
                send(z_send.at[index, k], z_recv.at[index, k], send_sem.at[sem], recv_sem.at[sem], z_mates[k])
            )
        return copies

    def z_finish(index, load, copies):
        total = load(2 * row_z + row_y) + y_recv[index, row_z].astype(jnp.float32)
        for k in range(3):
            copies[k].wait()
            total = total + z_recv[index, k].astype(jnp.float32)
        return total

    gain_out[...] = gain_ref[...]
    hops = [mate, x_mate, y_mate, device(seq, lax.rem(dp + 4, 8)), device(seq, dp + 2 - 4 * lax.rem(row_z, 2))]

    def gain_start(hop):
        sem = 22 + hop
        return send(gain_ref if hop == 0 else gain_out, g_recv.at[hop], send_sem.at[sem], recv_sem.at[sem], hops[hop])

    for half in range(2):
        core_send[half] = attn_ref[2 * half + 1 - core].astype(low)
    core_copy = send(core_send, core_recv, send_sem.at[16], recv_sem.at[16], mate)
    gain_copy = gain_start(0)
    ffn_load = lambda m: (lambda j: ffn_ref[m, j])
    y_copies = [y_start(m, ffn_load(m)) for m in range(3)]
    core_copy.wait()
    x_send[...] = (
        attn_ref[2 * (1 - chip_x) + core] + core_recv[1 - chip_x].astype(jnp.float32)
    ).astype(low)
    x_copy = send(x_send, x_recv, send_sem.at[17], recv_sem.at[17], x_mate)
    own[...] = attn_ref[seq] + core_recv[chip_x].astype(jnp.float32)
    for hop in range(5):
        gain_copy.wait()
        gain_out[...] += g_recv[hop]
        if hop < 4:
            gain_copy = gain_start(hop + 1)
    z_copies = []
    for m in range(3):
        y_copies[m].wait()
        z_copies.append(z_start(m, ffn_load(m)))
    x_copy.wait()
    own[...] += x_recv[...].astype(jnp.float32)
    own_load = lambda j: own[j]
    y_copy = y_start(3, own_load)
    for m in range(3):
        ffn_out[m] = z_finish(m, ffn_load(m), z_copies[m])
    y_copy.wait()
    z_copy = z_start(3, own_load)
    share_low[seq] = z_finish(3, own_load, z_copy).astype(low)
    to_mate = send(share_low.at[seq], share_low.at[seq], send_sem.at[18], recv_sem.at[18], mate)
    to_x = send(share_low.at[seq], share_low.at[seq], send_sem.at[19], recv_sem.at[19], x_mate)
    to_x.wait()
    far = lax.rem(seq + 2, 4)
    onward = send(share_low.at[far], share_low.at[far], send_sem.at[20], recv_sem.at[20], mate)
    to_mate.wait()
    onward.wait()
    attn_out[...] = share_low[...].astype(jnp.float32)


def reduce_grads(attn_grads, ffn_grads, gain_grads):
    share, cols = attn_grads.shape[2:]
    low, full = jnp.bfloat16, jnp.float32
    vmem = pl.BlockSpec(memory_space=pltpu.VMEM)
    return pl.pallas_call(
        reduce_kernel,
        out_shape=(
            jax.ShapeDtypeStruct((4, share, cols), full),
            jax.ShapeDtypeStruct((3, share, cols), full),
            jax.ShapeDtypeStruct(gain_grads.shape, full),
        ),
        in_specs=[vmem] * 3,
        out_specs=(vmem, vmem, vmem),
        scratch_shapes=[
            pltpu.VMEM((2, 8, share, cols), low),
            pltpu.VMEM((2, 8, share, cols), low),
            pltpu.VMEM((8, share, cols), low),
            pltpu.VMEM((8, share, cols), low),
            pltpu.VMEM((8, share, cols), full),
            pltpu.VMEM((4, 4, share, cols), low),
            pltpu.VMEM((4, 4, share, cols), low),
            pltpu.VMEM((4, 3, share, cols), low),
            pltpu.VMEM((4, 3, share, cols), low),
            pltpu.VMEM((5,) + gain_grads.shape, full),
            pltpu.VMEM((4, share, cols), low),
            pltpu.SemaphoreType.DMA((27,)),
            pltpu.SemaphoreType.DMA((27,)),
        ],
        compiler_params=pltpu.CompilerParams(
            collective_id=0, has_side_effects=True, vmem_limit_bytes=60 * 1024 * 1024
        ),
        name="reduce_grads",
    )(attn_grads, ffn_grads, gain_grads)


def unpack(grads):
    rows, columns = grads.shape[1:]
    pairs = grads[0].reshape(rows, KV_HEADS, 2, HEAD_DIM)
    half = columns // 2
    return (
        jnp.concatenate([grads[1], grads[3][:, :half]], axis=1),
        pairs[:, :, 0].reshape(rows, -1),
        pairs[:, :, 1].reshape(rows, -1),
        jnp.concatenate([grads[2], grads[3][:, half:]], axis=1),
    )


def on_device(
    tokens,
    seg_ids,
    positions,
    attn_gain,
    w_query,
    w_key,
    w_value,
    w_out,
    ffn_gain,
    w_gate,
    w_up,
    w_down,
    cotangent,
):
    width = tokens.shape[2]
    trig, w_kvq, place = prepare(positions[0], w_query, w_key, w_value)
    gains = jnp.pad(jnp.stack([attn_gain, ffn_gain]), ((0, 6), (0, 0)))
    residual = tokens[0].astype(FULL)
    kept = []
    for repeat in range(2):
        normed, q, kv, log_total, mixed, after, normed_two = attn_forward(
            residual, gains, w_kvq, w_out, trig, place
        )
        result, rows_all, gate_all, up_all = ffn_forward(after, normed_two, w_gate, w_up, w_down)
        kept.append((residual, normed, q, kv, log_total, mixed, after, rows_all, gate_all, up_all))
        residual = result
    output = residual.astype(LOW)
    upstream = cotangent[0].astype(FULL)
    ffn_grads, attn_grads, gain_terms = None, None, []
    for repeat in (1, 0):
        residual, normed, q, kv, log_total, mixed, after, rows_all, gate_all, up_all = kept[repeat]
        after_grad, ffn_gain_term, ffn_grads = ffn_backward(
            upstream, after, gains, rows_all, gate_all, up_all, w_gate, w_up, w_down, ffn_grads
        )
        upstream, attn_gain_term, attn_grads = attn_backward(
            after_grad, residual, normed, gains, q, kv, log_total, mixed, w_kvq, w_out, trig, place, attn_grads
        )
        gain_terms.append(jnp.stack([attn_gain_term[0], ffn_gain_term[0]]))
    gain_grads = gain_terms[0] + gain_terms[1]
    if lax.axis_size("dp") == 8 and width % 64 == 0:
        share = width // 8
        own = gain_grads.reshape(2, 8, share).transpose(1, 0, 2)
        own = jnp.pad(own, ((0, 0), (0, 6), (0, 128 - share)))
        attn_share, ffn_share, gain_share = reduce_grads(
            attn_grads.reshape(4, 8, share, -1), ffn_grads.reshape(3, 8, share, -1), own
        )
        own_gains = lax.dynamic_index_in_dim(gain_share, lax.axis_index("dp"), 0, keepdims=False)[:2, :share]
    else:

        def over_rows(grads, dim):
            grads = lax.psum_scatter(grads.astype(LOW), "dp", scatter_dimension=dim, tiled=True)
            return grads.astype(FULL)

        def over_all(grads, dim):
            return lax.psum(over_rows(grads, dim).astype(LOW), "seq").astype(FULL)

        attn_share = over_all(attn_grads, 1)
        ffn_share = over_rows(ffn_grads, 1)
        own_gains = over_all(gain_grads, 1)
    query_share, key_share, value_share, out_share = unpack(attn_share)
    return (
        output[None],
        upstream[None],
        own_gains[0],
        query_share,
        key_share,
        value_share,
        out_share,
        own_gains[1],
        ffn_share[0],
        ffn_share[1],
        ffn_share[2].T,
    )


def solution(mesh):
    in_specs = (
        P("dp", "seq", None),
        P("dp", "seq"),
        P("dp", "seq"),
        P(),
        P(),
        P(),
        P(),
        P(),
        P(),
        P(None, "seq"),
        P(None, "seq"),
        P("seq", None),
        P("dp", "seq", None),
    )
    out_specs = (
        P("dp", "seq", None),
        P("dp", "seq", None),
        P("dp"),
        P("dp", None),
        P("dp", None),
        P("dp", None),
        P("dp", None),
        P("dp"),
        P("dp", "seq"),
        P("dp", "seq"),
        P("seq", "dp"),
    )
    return jax.shard_map(
        on_device, mesh=mesh, in_specs=in_specs, out_specs=out_specs, check_vma=False
    )
```

```python
import functools

import jax
import jax.numpy as jnp
from jax import lax
from jax.experimental import pallas as pl
from jax.experimental.pallas import tpu as pltpu
from jax.sharding import PartitionSpec as P

MESH_ID = pl.DeviceIdType.MESH
HEADS = 15
KV_HEADS = 5
GROUP = 3
HEAD_DIM = 64
EPSILON = 1e-05
THETA = 10000.0
CHUNKS = 2
SHARES = 8
ROWS_PAD = 32
MASKED = -1e30
LOW = jnp.bfloat16
FULL = jnp.float32
SCALE = HEAD_DIM ** (-0.5)
NT = (((1,), (1,)), ((), ()))
TN = (((0,), (0,)), ((), ()))


def device(seq_pos, dp_pos):
    return {"seq": seq_pos, "dp": dp_pos}


def send(src, dst, send_sem, recv_sem, target):
    copy = pltpu.make_async_remote_copy(
        src_ref=src,
        dst_ref=dst,
        send_sem=send_sem,
        recv_sem=recv_sem,
        device_id=target,
        device_id_type=MESH_ID,
    )
    copy.start()
    return copy


def greet(targets):
    barrier = pltpu.get_barrier_semaphore()
    for target in targets:
        pl.semaphore_signal(barrier, inc=1, device_id=target, device_id_type=MESH_ID)
    pl.semaphore_wait(barrier, len(targets))


def dot(left, right, dims=None):
    if dims is None:
        return jnp.dot(left, right, preferred_element_type=FULL)
    return lax.dot_general(left, right, dims, preferred_element_type=FULL)


def inverse_rms(value):
    return lax.rsqrt(jnp.mean(value * value, axis=-1, keepdims=True) + EPSILON)


def swap_halves(value):
    lane = lax.broadcasted_iota(jnp.int32, value.shape, 1)
    first = lax.rem(lane, HEAD_DIM) < HEAD_DIM // 2
    return jnp.where(first, pltpu.roll(value, 96, 1), pltpu.roll(value, 32, 1))


def attn_forward_kernel(
    res_ref, gains_ref, w_kvq_ref, w_out_ref, trig_ref, place_ref,
    normed_out, q_out, kv_out, log_out, mixed_out, after_out, normed_two_out,
    peak, total, acc, send_sem, recv_sem,
):
    seq, dp = lax.axis_index("seq"), lax.axis_index("dp")
    core, chip_x = lax.rem(seq, 2), lax.div(seq, 2)
    mate_seq, far_seq = seq + 1 - 2 * core, lax.rem(seq + 2, 4)
    mate, x_mate = device(mate_seq, dp), device(far_seq, dp)
    length = res_ref.shape[0]
    stacked = GROUP * length
    residual = res_ref[...]
    normed_out[...] = (residual * inverse_rms(residual) * gains_ref[0:1, :]).astype(LOW)
    kv_width = 2 * KV_HEADS * HEAD_DIM
    kv_pre = dot(normed_out[...], w_kvq_ref[:, :kv_width])
    for g in range(KV_HEADS):
        part = kv_pre[:, g * 128 : (g + 1) * 128]
        turned = part * trig_ref[2] + swap_halves(part) * trig_ref[3]
        kv_out[seq, :, g * 128 : (g + 1) * 128] = turned.astype(LOW)
    greet([mate, x_mate])
    own_kv = kv_out.at[seq]
    to_mate = send(own_kv, own_kv, send_sem.at[0], recv_sem.at[0], mate)
    to_x = send(own_kv, own_kv, send_sem.at[1], recv_sem.at[1], x_mate)
    q_pre = dot(normed_out[...], w_kvq_ref[:, kv_width:])
    lane = lax.broadcasted_iota(jnp.int32, (length, 128), 1)
    for pair in range((HEADS + 1) // 2):
        width = min(128, HEADS * HEAD_DIM - pair * 128)
        part = q_pre[:, pair * 128 : pair * 128 + width]
        if width < 128:
            part = jnp.concatenate([part, part], axis=1)
        turned = (part * trig_ref[0] + swap_halves(part) * trig_ref[1]) * SCALE
        q_out[2 * pair] = jnp.where(lane < HEAD_DIM, turned, 0.0).astype(LOW)
        if width == 128:
            q_out[2 * pair + 1] = jnp.where(lane < HEAD_DIM, pltpu.roll(turned, 64, 1), 0.0).astype(LOW)

    start, place = place_ref[0:1, :], place_ref[1:2, :]

    def attend(block, g, first):
        kv_g = kv_out[block, :, pl.ds(pl.multiple_of(g * 128, 128), 128)]
        q_g = q_out[pl.ds(3 * g, 3)].reshape(stacked, 128)
        scores = dot(kv_g, q_g, NT)
        key = lax.broadcasted_iota(jnp.int32, (length, stacked), 0) + block * length
        allowed = key >= start
        if first:
            allowed = allowed & (key <= place)
        scores = jnp.where(allowed, scores, MASKED)
        here = jnp.max(scores, axis=0, keepdims=True)
        if first:
            new_peak = here
        else:
            new_peak = jnp.maximum(peak[g], here)
        weights = jnp.exp(scores - new_peak)
        row_total = jnp.sum(weights, axis=0, keepdims=True)
        mix = dot(kv_g, weights.astype(LOW), TN)[HEAD_DIM:]
        if not first:
            fade = jnp.exp(peak[g] - new_peak)
            row_total = row_total + fade * total[g]
            mix = mix + fade * acc[g]
        peak[g], total[g], acc[g] = new_peak, row_total, mix

    @pl.loop(0, KV_HEADS)
    def _(g):
        attend(seq, g, True)

    to_mate.wait()

    @pl.when(core == 1)
    def _():
        @pl.loop(0, KV_HEADS)
        def _(g):
            attend(mate_seq, g, False)

    to_x.wait()
    far_kv = kv_out.at[far_seq]
    onward = send(far_kv, far_kv, send_sem.at[2], recv_sem.at[2], mate)

    @pl.when(chip_x == 1)
    def _():
        @pl.loop(0, KV_HEADS)
        def _(g):
            attend(far_seq, g, False)

    onward.wait()

    @pl.when(chip_x == 1)
    def _():
        @pl.loop(0, KV_HEADS)
        def _(g):
            attend(lax.rem(mate_seq + 2, 4), g, False)

    for g in range(KV_HEADS):
        heads = (acc[g] / total[g]).T.astype(LOW)
        log_out[g] = peak[g] + jnp.log(total[g])
        for i in range(GROUP):
            h = GROUP * g + i
            mixed_out[:, h * HEAD_DIM : (h + 1) * HEAD_DIM] = heads[i * length : (i + 1) * length]
    after = residual + dot(mixed_out[...], w_out_ref[...])
    after_out[...] = after
    normed_two_out[...] = (after * inverse_rms(after) * gains_ref[1:2, :]).astype(LOW)


VMEM = pl.BlockSpec(memory_space=pltpu.VMEM)


def attn_forward(residual, gains, w_kvq, w_out, trig, place):
    length, width = residual.shape
    kv_width = 2 * KV_HEADS * HEAD_DIM
    shapes = (
        ((length, width), LOW),
        ((HEADS, length, 128), LOW),
        ((4, length, kv_width), LOW),
        ((KV_HEADS, 1, GROUP * length), FULL),
        ((length, HEADS * HEAD_DIM), LOW),
        ((length, width), FULL),
        ((length, width), LOW),
    )
    return pl.pallas_call(
        attn_forward_kernel,
        out_shape=tuple(jax.ShapeDtypeStruct(*s) for s in shapes),
        in_specs=[VMEM] * 6,
        out_specs=(VMEM,) * len(shapes),
        scratch_shapes=[
            pltpu.VMEM((KV_HEADS, 1, GROUP * length), FULL),
            pltpu.VMEM((KV_HEADS, 1, GROUP * length), FULL),
            pltpu.VMEM((KV_HEADS, HEAD_DIM, GROUP * length), FULL),
            pltpu.SemaphoreType.DMA((3,)),
            pltpu.SemaphoreType.DMA((3,)),
        ],
        compiler_params=pltpu.CompilerParams(
            collective_id=1, has_side_effects=True, vmem_limit_bytes=60 * 1024 * 1024
        ),
        name="attn_forward",
    )(residual, gains, w_kvq, w_out, trig, place)


def prepare(positions, w_query, w_key, w_value):
    length = positions.shape[0]
    frequency = THETA ** (-(jnp.arange(HEAD_DIM // 2, dtype=FULL) * 2.0 / HEAD_DIM))
    angles = positions.astype(FULL)[:, None] * frequency
    cos, sin = jnp.cos(angles), jnp.sin(angles)
    one, none = jnp.ones((length, HEAD_DIM), FULL), jnp.zeros((length, HEAD_DIM), FULL)
    trig = jnp.stack(
        [
            jnp.concatenate([cos, cos, cos, cos], 1),
            jnp.concatenate([-sin, sin, -sin, sin], 1),
            jnp.concatenate([cos, cos, one], 1),
            jnp.concatenate([-sin, sin, none], 1),
        ]
    )
    width = w_key.shape[0]
    pairs = jnp.stack([w_key.reshape(width, KV_HEADS, HEAD_DIM), w_value.reshape(width, KV_HEADS, HEAD_DIM)], axis=2)
    w_kvq = jnp.concatenate([pairs.reshape(width, -1), w_query], axis=1)
    own = lax.axis_index("seq") * length + jnp.arange(length, dtype=jnp.int32)
    place = jnp.stack([jnp.tile(own - positions, GROUP), jnp.tile(own, GROUP)])
    place = jnp.pad(place, ((0, 6), (0, 0)))
    return trig, w_kvq, place


def ffn_forward_kernel(
    after_ref, normed_ref, w_gate_ref, w_up_ref, w_down_ref,
    res_out, rows_out, gate_out, up_out,
    mate_send, mate_recv, x_send, x_recv, own_far,
    send_sem, recv_sem,
):
    seq, dp = lax.axis_index("seq"), lax.axis_index("dp")
    core = lax.rem(seq, 2)
    mate_seq, far_seq = seq + 1 - 2 * core, lax.rem(seq + 2, 4)
    far_mate = lax.rem(mate_seq + 2, 4)
    mate, x_mate = device(mate_seq, dp), device(far_seq, dp)
    length = after_ref.shape[0]
    step = length // CHUNKS
    greet([mate, x_mate])
    part = lambda k: pl.ds(k * step, step)

    def hop(index, src, dst, target):
        return send(src, dst, send_sem.at[index], recv_sem.at[index], target)

    rows_out[seq] = normed_ref[...]
    own_rows = lambda k: rows_out.at[seq, part(k)]
    far_rows = lambda k: rows_out.at[far_seq, part(k)]
    to_x = [hop(k, own_rows(k), own_rows(k), x_mate) for k in range(CHUNKS)]
    to_mate = hop(CHUNKS, rows_out.at[seq], rows_out.at[seq], mate)
    base = CHUNKS + 1

    def ffn(quarter, rows):
        block = rows_out[quarter, rows]
        gate = dot(block, w_gate_ref[...])
        up = dot(block, w_up_ref[...])
        gate_out[quarter, rows] = gate.astype(LOW)
        up_out[quarter, rows] = up.astype(LOW)
        hidden = (gate * jax.nn.sigmoid(gate) * up).astype(LOW)
        return dot(hidden, w_down_ref[...])

    everything = pl.ds(0, length)
    res_out[...] = after_ref[...] + ffn(seq, everything)
    to_mate.wait()
    mate_send[0] = ffn(mate_seq, everything).astype(LOW)
    back = hop(base, mate_send.at[0], mate_recv.at[0], mate)
    onward = []
    for k in range(CHUNKS):
        to_x[k].wait()
        onward.append(hop(base + 1 + k, far_rows(k), far_rows(k), mate))
        own_far[part(k)] = ffn(far_seq, part(k))
        onward[k].wait()
        mate_send[1, part(k)] = ffn(far_mate, part(k)).astype(LOW)
        joint = hop(base + 1 + CHUNKS + k, mate_send.at[1, part(k)], mate_recv.at[1, part(k)], mate)
        joint.wait()
        x_send[part(k)] = (own_far[part(k)] + mate_recv[1, part(k)].astype(FULL)).astype(LOW)
        onward.append(
            hop(base + 1 + 2 * CHUNKS + k, x_send.at[part(k)], x_recv.at[part(k)], x_mate)
        )
        onward[k], onward[-1] = onward[-1], onward[k]
        onward.pop()
    back.wait()
    res_out[...] += mate_recv[0].astype(FULL)
    for k in range(CHUNKS):
        onward[k].wait()
        res_out[part(k)] += x_recv[part(k)].astype(FULL)


def ffn_forward(after, normed_two, w_gate, w_up, w_down):
    length, width = after.shape
    hidden = w_gate.shape[1]
    shapes = (
        ((length, width), FULL),
        ((4, length, width), LOW),
        ((4, length, hidden), LOW),
        ((4, length, hidden), LOW),
    )
    sems = 3 * CHUNKS + CHUNKS + 2
    return pl.pallas_call(
        ffn_forward_kernel,
        out_shape=tuple(jax.ShapeDtypeStruct(*s) for s in shapes),
        in_specs=[VMEM] * 5,
        out_specs=(VMEM,) * len(shapes),
        scratch_shapes=[
            pltpu.VMEM((2, length, width), LOW),
            pltpu.VMEM((2, length, width), LOW),
            pltpu.VMEM((length, width), LOW),
            pltpu.VMEM((length, width), LOW),
            pltpu.VMEM((length, width), FULL),
            pltpu.SemaphoreType.DMA((sems,)),
            pltpu.SemaphoreType.DMA((sems,)),
        ],
        compiler_params=pltpu.CompilerParams(
            collective_id=2, has_side_effects=True, vmem_limit_bytes=60 * 1024 * 1024
        ),
        name="ffn_forward",
    )(after, normed_two, w_gate, w_up, w_down)


def norm_back(value, gain, grad):
    inverse = inverse_rms(value)
    weighted = grad * gain
    inner = jnp.mean(weighted * value, axis=-1, keepdims=True)
    back = inverse * weighted - value * (inverse * inverse * inverse) * inner
    return back, jnp.sum(grad * value * inverse, axis=0, keepdims=True)


def ffn_backward_kernel(
    up_ref, after_ref, gains_ref, rows_ref, gate_ref, upp_ref, w_gate_ref, w_up_ref, w_down_ref, *rest
):
    (prev_ref,) = rest[:-15] if len(rest) == 16 else (None,)
    (
        grad_out, gain_out, weight_out,
        weight_sum, low_all, gate_grad, up_grad, hidden,
        mate_send, mate_recv, x_send, x_recv, own_far,
        send_sem, recv_sem,
    ) = rest[-15:]
    seq, dp = lax.axis_index("seq"), lax.axis_index("dp")
    core, chip_x = lax.rem(seq, 2), lax.div(seq, 2)
    mate_seq, far_seq = seq + 1 - 2 * core, lax.rem(seq + 2, 4)
    far_mate = lax.rem(mate_seq + 2, 4)
    mate, x_mate = device(mate_seq, dp), device(far_seq, dp)
    length, width = up_ref.shape
    step = length // CHUNKS
    greet([mate, x_mate])
    part = lambda k: pl.ds(k * step, step)

    def hop(index, src, dst, target):
        return send(src, dst, send_sem.at[index], recv_sem.at[index], target)

    low_all[seq] = up_ref[...].astype(LOW)
    own_rows = lambda k: low_all.at[seq, part(k)]
    far_rows = lambda k: low_all.at[far_seq, part(k)]
    to_x = [hop(k, own_rows(k), own_rows(k), x_mate) for k in range(CHUNKS)]
    to_mate = hop(CHUNKS, low_all.at[seq], low_all.at[seq], mate)
    base = CHUNKS + 1

    def ffn(quarter, rows):
        hidden_grad = dot(low_all[quarter, rows], w_down_ref[...], NT)
        gate = gate_ref[quarter, rows].astype(FULL)
        up = upp_ref[quarter, rows].astype(FULL)
        bend = jax.nn.sigmoid(gate)
        silu = gate * bend
        hidden[quarter, rows] = (silu * up).astype(LOW)
        gate_low = (hidden_grad * up * bend * (1.0 + gate * (1.0 - bend))).astype(LOW)
        up_low = (hidden_grad * silu).astype(LOW)
        gate_grad[quarter, rows] = gate_low
        up_grad[quarter, rows] = up_low
        return dot(gate_low, w_gate_ref[...], NT) + dot(up_low, w_up_ref[...], NT)

    def weights(first_quarter, first):
        pair = lambda ref: ref[pl.ds(first_quarter, 2)].reshape(2 * length, ref.shape[2])
        rows, low = pair(rows_ref), pair(low_all)
        for i, (left, right) in enumerate(
            ((rows, pair(gate_grad)), (rows, pair(up_grad)), (low, pair(hidden)))
        ):
            term = dot(left, right, TN)
            if not first:
                weight_out[i] = (term + weight_sum[i]).astype(LOW)
            elif prev_ref is not None:
                weight_sum[i] = term + prev_ref[i].astype(FULL)
            else:
                weight_sum[i] = term

    everything = pl.ds(0, length)
    grad_out[...] = ffn(seq, everything)
    to_mate.wait()
    mate_send[0] = ffn(mate_seq, everything).astype(LOW)
    back = hop(base, mate_send.at[0], mate_recv.at[0], mate)
    last = []
    for k in range(CHUNKS):
        to_x[k].wait()
        onward = hop(base + 1 + k, far_rows(k), far_rows(k), mate)
        own_far[part(k)] = ffn(far_seq, part(k))
        onward.wait()
        mate_send[1, part(k)] = ffn(far_mate, part(k)).astype(LOW)
        joint = hop(base + 1 + CHUNKS + k, mate_send.at[1, part(k)], mate_recv.at[1, part(k)], mate)
        joint.wait()
        x_send[part(k)] = (own_far[part(k)] + mate_recv[1, part(k)].astype(FULL)).astype(LOW)
        last.append(hop(base + 1 + 2 * CHUNKS + k, x_send.at[part(k)], x_recv.at[part(k)], x_mate))
        if k == 0:
            weights(2 * chip_x, True)
    weights(2 - 2 * chip_x, False)
    back.wait()
    total = grad_out[...] + mate_recv[0].astype(FULL)
    for k in range(CHUNKS):
        last[k].wait()
    total = total + x_recv[...].astype(FULL)
    sent_back, gain_term = norm_back(after_ref[...], gains_ref[1:2, :], total)
    grad_out[...] = up_ref[...] + sent_back
    gain_out[...] = jnp.broadcast_to(gain_term, gain_out.shape)


def ffn_backward(upstream, after, gains, rows_all, gate_all, up_all, w_gate, w_up, w_down, prev=None):
    length, width = after.shape
    hidden = w_gate.shape[1]
    shapes = (
        ((length, width), FULL),
        ((8, width), FULL),
        ((3, width, hidden), LOW),
    )
    sems = 3 * CHUNKS + CHUNKS + 2
    args = (upstream, after, gains, rows_all, gate_all, up_all, w_gate, w_up, w_down)
    if prev is not None:
        args = args + (prev,)
    return pl.pallas_call(
        ffn_backward_kernel,
        out_shape=tuple(jax.ShapeDtypeStruct(*s) for s in shapes),
        in_specs=[VMEM] * len(args),
        out_specs=(VMEM,) * len(shapes),
        scratch_shapes=[
            pltpu.VMEM((3, width, hidden), FULL),
            pltpu.VMEM((4, length, width), LOW),
            pltpu.VMEM((4, length, hidden), LOW),
            pltpu.VMEM((4, length, hidden), LOW),
            pltpu.VMEM((4, length, hidden), LOW),
            pltpu.VMEM((2, length, width), LOW),
            pltpu.VMEM((2, length, width), LOW),
            pltpu.VMEM((length, width), LOW),
            pltpu.VMEM((length, width), LOW),
            pltpu.VMEM((length, width), FULL),
            pltpu.SemaphoreType.DMA((sems,)),
            pltpu.SemaphoreType.DMA((sems,)),
        ],
        compiler_params=pltpu.CompilerParams(
            collective_id=3 if prev is None else 4, has_side_effects=True, vmem_limit_bytes=60 * 1024 * 1024
        ),
        name="ffn_backward",
    )(*args)


class Hops:
    def __init__(self, send_sem, recv_sem):
        self.send_sem, self.recv_sem, self.used = send_sem, recv_sem, 0

    def __call__(self, src, dst, target):
        index, self.used = self.used, self.used + 1
        return send(src, dst, self.send_sem.at[index], self.recv_sem.at[index], target)


def attn_backward_kernel(
    last, after_grad_ref, res_ref, normed_ref, gains_ref, q_ref, kv_ref, log_ref, mixed_ref,
    w_kvq_ref, w_out_ref, trig_ref, place_ref, *rest
):
    if last:
        prev, ffn_ref, gain_ref = rest[:3], rest[3], rest[4]
        grad_out, gain_out, ffn_out, share_outs = rest[5], rest[6], rest[7], rest[8:11]
        rest = rest[11:]
    else:
        prev = (None, None, None)
        grad_out, gain_out = rest[:2]
        parts = rest[2:5]
        rest = rest[5:]
    mixed_grad, delta, kv_grad, query_grad, back, grad_send, grad_recv, send_sem, recv_sem = rest[:9]
    hop = Hops(send_sem, recv_sem)
    seq, dp = lax.axis_index("seq"), lax.axis_index("dp")
    core, chip_x = lax.rem(seq, 2), lax.div(seq, 2)
    mate_seq, far_seq = seq + 1 - 2 * core, lax.rem(seq + 2, 4)
    far_mate = lax.rem(mate_seq + 2, 4)
    mate, x_mate = device(mate_seq, dp), device(far_seq, dp)
    length, width = res_ref.shape
    stacked = GROUP * length
    kv_width = 2 * KV_HEADS * HEAD_DIM
    if last:
        parts = rest[9:12]
        f_y_recv, f_z_send, f_z_recv, gain_recv = rest[12:16]
        buffers = [rest[16 + 8 * i : 24 + 8 * i] for i in range(3)]
        row_y, row_z = lax.rem(dp, 2), lax.div(dp, 2)
        y_mate = device(seq, dp + 1 - 2 * row_y)
        z_of = [lax.rem(row_z + k, 4) for k in range(1, 4)]
        z_mates = [device(seq, z * 2 + row_y) for z in z_of]
        greet([mate, x_mate, y_mate] + z_mates)
        f_y = [hop(ffn_ref.at[m, :, 1 - row_y], f_y_recv.at[m], y_mate) for m in range(3)]
    else:
        greet([mate, x_mate])

    def f_z_start(m):
        f_y[m].wait()
        copies = []
        for k in range(3):
            joint = ffn_ref[m, z_of[k], row_y].astype(FULL) + f_y_recv[m, z_of[k]].astype(FULL)
            f_z_send[m, k] = joint.astype(LOW)
            copies.append(hop(f_z_send.at[m, k], f_z_recv.at[m, k], z_mates[k]))
        return copies

    def f_z_finish(m, copies):
        total = ffn_ref[m, row_z, row_y].astype(FULL) + f_y_recv[m, row_z].astype(FULL)
        for k in range(3):
            copies[k].wait()
            total = total + f_z_recv[m, k].astype(FULL)
        ffn_out[m] = total

    quarter = lambda x, c: pl.ds(pl.multiple_of(64 * x + ROWS_PAD * c, ROWS_PAD), ROWS_PAD)

    def core_start(i):
        core_recv = buffers[i][0]
        return [hop(parts[i].at[:, quarter(x, 1 - core)], core_recv.at[x], mate) for x in range(2)]

    def x_start(i, copies):
        core_recv, x_send, x_recv = buffers[i][:3]
        for copy in copies:
            copy.wait()
        joint = parts[i][:, quarter(1 - chip_x, core)].astype(FULL) + core_recv[1 - chip_x].astype(FULL)
        x_send[...] = joint.astype(LOW)
        return hop(x_send, x_recv, x_mate)

    def y_start(i, copy):
        core_recv, x_send, x_recv, own, y_recv = buffers[i][:5]
        joint = parts[i][:, quarter(chip_x, core)].astype(FULL) + core_recv[chip_x].astype(FULL)
        copy.wait()
        own[...] = (joint + x_recv[...].astype(FULL)).astype(LOW).reshape(own.shape)
        return hop(own.at[:, 1 - row_y], y_recv, y_mate)

    def z_start(i, copy):
        own, y_recv, z_send, z_recv = buffers[i][3:7]
        copy.wait()
        copies = []
        for k in range(3):
            z_send[k] = (own[z_of[k], row_y].astype(FULL) + y_recv[z_of[k]].astype(FULL)).astype(LOW)
            copies.append(hop(z_send.at[k], z_recv.at[k], z_mates[k]))
        return copies

    def share_start(i, copies):
        own, y_recv, z_send, z_recv, gathered = buffers[i][3:8]
        total = own[row_z, row_y].astype(FULL) + y_recv[row_z].astype(FULL)
        for k in range(3):
            copies[k].wait()
            total = total + z_recv[k].astype(FULL)
        gathered[seq] = total.astype(LOW)
        mine = gathered.at[seq]
        return hop(mine, mine, x_mate), hop(mine, mine, mate)

    def share_pass(i, copies):
        gathered = buffers[i][7]
        copies[0].wait()
        theirs = gathered.at[far_seq]
        return hop(theirs, theirs, mate), copies[1]

    def share_finish(i, copies):
        gathered = buffers[i][7]
        for copy in copies:
            copy.wait()
        for s in range(4):
            share_outs[i][s * ROWS_PAD : (s + 1) * ROWS_PAD] = gathered[s].astype(FULL)

    def weight(i, left, right):
        term = dot(left, right, TN)
        share = width // SHARES
        for j in range(SHARES):
            rows = term[j * share : (j + 1) * share]
            if prev[i] is not None:
                rows = rows + prev[i][j, :share].astype(FULL)
            parts[i][j, :share] = rows.astype(LOW)

    low_grad = after_grad_ref[...].astype(LOW)
    mixed_back = dot(low_grad, w_out_ref[...], NT)
    lane = lax.broadcasted_iota(jnp.int32, (length, 128), 1)
    for pair in range((HEADS + 1) // 2):
        span = min(128, HEADS * HEAD_DIM - pair * 128)
        part = mixed_back[:, pair * 128 : pair * 128 + span]
        if span < 128:
            part = jnp.concatenate([part, part], axis=1)
        else:
            mixed_grad[2 * pair + 1] = jnp.where(lane >= HEAD_DIM, part, 0.0).astype(LOW)
        mixed_grad[2 * pair] = jnp.where(lane >= HEAD_DIM, pltpu.roll(part, 64, 1), 0.0).astype(LOW)
    product = mixed_back.astype(LOW).astype(FULL) * mixed_ref[...].astype(FULL)
    high = product.astype(LOW)
    rest_low = (product - high.astype(FULL)).astype(LOW)
    head = lax.broadcasted_iota(jnp.int32, (16, HEADS * HEAD_DIM), 0)
    column = lax.broadcasted_iota(jnp.int32, (16, HEADS * HEAD_DIM), 1)
    pick = jnp.where(lax.div(column, HEAD_DIM) == head, 1.0, 0.0).astype(LOW)
    sums = dot(pick, high, NT) + dot(pick, rest_low, NT)
    for g in range(KV_HEADS):
        delta[g] = jnp.concatenate([sums[3 * g + i : 3 * g + i + 1] for i in range(GROUP)], axis=1)
    query_grad[...] = jnp.zeros_like(query_grad)
    weight(0, mixed_ref[...], low_grad)
    if last:
        o_core = core_start(0)

    start, place = place_ref[0:1, :], place_ref[1:2, :]

    def attend(block, g, diagonal):
        columns = pl.ds(pl.multiple_of(g * 128, 128), 128)
        kv_g = kv_ref[block, :, columns]
        q_g = q_ref[pl.ds(3 * g, 3)].reshape(stacked, 128)
        out_g = mixed_grad[pl.ds(3 * g, 3)].reshape(stacked, 128)
        scores = dot(kv_g, q_g, NT)
        key = lax.broadcasted_iota(jnp.int32, (length, stacked), 0) + block * length
        allowed = key >= start
        if diagonal:
            allowed = allowed & (key <= place)
        weights = jnp.where(allowed, jnp.exp(scores - log_ref[g]), 0.0)
        probs_grad = dot(kv_g, out_g, NT)
        score_grad = (weights * (probs_grad - delta[g])).astype(LOW)
        kv_grad[block, :, columns] = dot(weights.astype(LOW), out_g) + dot(score_grad, q_g)
        query_grad[g] += dot(kv_g, score_grad, TN)[:HEAD_DIM]

    def attend_all(block, condition, diagonal=False):
        @pl.when(condition)
        def _():
            @pl.loop(0, KV_HEADS)
            def _(g):
                attend(block, g, diagonal)

        if not diagonal:
            @pl.when(jnp.logical_not(condition))
            def _():
                kv_grad[block] = jnp.zeros_like(kv_grad[block])

    right = chip_x == 1
    attend_all(far_mate, right)
    grad_send[0] = kv_grad[far_mate].astype(LOW)
    joint = hop(grad_send.at[0], grad_recv.at[0], mate)
    attend_all(far_seq, right)
    joint.wait()
    grad_send[1] = (kv_grad[far_seq] + grad_recv[0].astype(FULL)).astype(LOW)
    across = hop(grad_send.at[1], grad_recv.at[1], x_mate)
    if last:
        o_x = x_start(0, o_core)
        f_z = [f_z_start(0)]
    attend_all(mate_seq, core == 1)
    grad_send[2] = kv_grad[mate_seq].astype(LOW)
    beside = hop(grad_send.at[2], grad_recv.at[2], mate)
    if last:
        f_z.append(f_z_start(1))
    attend_all(seq, seq >= 0, True)

    for g in range(KV_HEADS):
        heads = query_grad[g].T * SCALE
        for i in range(GROUP):
            h = GROUP * g + i
            part = heads[i * length : (i + 1) * length]
            part = jnp.concatenate([part, part], axis=1)
            turned = part * trig_ref[0] - swap_halves(part) * trig_ref[1]
            at = kv_width + h * HEAD_DIM
            back[:, at : at + HEAD_DIM] = turned[:, :HEAD_DIM].astype(LOW)
    weight(1, normed_ref[...], back[:, kv_width:])
    if last:
        q_core = core_start(1)
        o_y = y_start(0, o_x)
        f_z.append(f_z_start(2))
    normed_grad = dot(back[:, kv_width:], w_kvq_ref[:, kv_width:], NT)
    if last:
        q_x = x_start(1, q_core)

    across.wait()
    beside.wait()
    own = kv_grad[seq] + grad_recv[1].astype(FULL) + grad_recv[2].astype(FULL)
    for g in range(KV_HEADS):
        part = own[:, g * 128 : (g + 1) * 128]
        back[:, g * 128 : (g + 1) * 128] = (part * trig_ref[2] - swap_halves(part) * trig_ref[3]).astype(LOW)
    weight(2, normed_ref[...], back[:, :kv_width])
    if last:
        kv_core = core_start(2)
    normed_grad = normed_grad + dot(back[:, :kv_width], w_kvq_ref[:, :kv_width], NT)
    sent_back, gain_term = norm_back(res_ref[...], gains_ref[0:1, :], normed_grad)
    grad_out[...] = after_grad_ref[...] + sent_back
    if not last:
        gain_out[...] = jnp.broadcast_to(gain_term, gain_out.shape)
        return

    row = lax.broadcasted_iota(jnp.int32, gain_out.shape, 0)
    gain_out[...] = gain_ref[...] + jnp.where(row == 0, gain_term, 0.0)
    partners = [
        mate, x_mate, y_mate, device(seq, lax.rem(dp + 4, 8)), device(seq, dp + 2 - 4 * lax.rem(row_z, 2))
    ]
    gain_hop = lambda n: hop(gain_out, gain_recv.at[n], partners[n])

    def gain_add(n, copy):
        copy.wait()
        gain_out[...] += gain_recv[n]

    kv_x = x_start(2, kv_core)
    gain_copy = gain_hop(0)
    o_z = z_start(0, o_y)
    gain_add(0, gain_copy)
    gain_copy = gain_hop(1)
    q_y = y_start(1, q_x)
    gain_add(1, gain_copy)
    gain_copy = gain_hop(2)
    f_z_finish(0, f_z[0])
    f_z_finish(1, f_z[1])
    gain_add(2, gain_copy)
    gain_copy = gain_hop(3)
    kv_y = y_start(2, kv_x)
    q_z = z_start(1, q_y)
    gain_add(3, gain_copy)
    gain_copy = gain_hop(4)
    f_z_finish(2, f_z[2])
    o_s = share_start(0, o_z)
    kv_z = z_start(2, kv_y)
    o_s = share_pass(0, o_s)
    q_s = share_start(1, q_z)
    gain_add(4, gain_copy)
    kv_s = share_start(2, kv_z)
    q_s = share_pass(1, q_s)
    share_finish(0, o_s)
    kv_s = share_pass(2, kv_s)
    share_finish(1, q_s)
    share_finish(2, kv_s)


def attn_backward(after_grad, residual, normed, gains, q, kv, log_total, mixed, w_kvq, w_out, trig, place, final=None):
    length, width = residual.shape
    kv_width = 2 * KV_HEADS * HEAD_DIM
    last = final is not None
    args = (after_grad, residual, normed, gains, q, kv, log_total, mixed, w_kvq, w_out, trig, place)
    shapes = (((length, width), FULL), ((8, width), FULL))
    sizes = (width, width, kv_width)
    part_shapes = [((SHARES, 4 * ROWS_PAD, c), LOW) for c in sizes]
    scratch = [
        pltpu.VMEM((HEADS, length, 128), LOW),
        pltpu.VMEM((KV_HEADS, 1, GROUP * length), FULL),
        pltpu.VMEM((4, length, kv_width), FULL),
        pltpu.VMEM((KV_HEADS, HEAD_DIM, GROUP * length), FULL),
        pltpu.VMEM((length, kv_width + width), LOW),
        pltpu.VMEM((3, length, kv_width), LOW),
        pltpu.VMEM((3, length, kv_width), LOW),
    ]
    hops = 3
    if last:
        share, hidden = final[3].shape[3:]
        args = args + tuple(final)
        shapes = shapes + (((3, share, hidden), FULL),) + tuple(((4 * ROWS_PAD, c), FULL) for c in sizes)
        hops = 3 + 3 + 9 + 5 + 3 * (2 + 1 + 1 + 3 + 3)
        scratch += [pltpu.SemaphoreType.DMA((hops,))] * 2
        scratch += [pltpu.VMEM(*s) for s in part_shapes]
        scratch += [
            pltpu.VMEM((3, 4, share, hidden), LOW),
            pltpu.VMEM((3, 3, share, hidden), LOW),
            pltpu.VMEM((3, 3, share, hidden), LOW),
            pltpu.VMEM((5, 8, width), FULL),
        ]
        for c in sizes:
            scratch += [
                pltpu.VMEM((2, SHARES, ROWS_PAD, c), LOW),
                pltpu.VMEM((SHARES, ROWS_PAD, c), LOW),
                pltpu.VMEM((SHARES, ROWS_PAD, c), LOW),
                pltpu.VMEM((4, 2, ROWS_PAD, c), LOW),
                pltpu.VMEM((4, ROWS_PAD, c), LOW),
                pltpu.VMEM((3, ROWS_PAD, c), LOW),
                pltpu.VMEM((3, ROWS_PAD, c), LOW),
                pltpu.VMEM((4, ROWS_PAD, c), LOW),
            ]
    else:
        shapes = shapes + tuple(part_shapes)
        scratch += [pltpu.SemaphoreType.DMA((hops,))] * 2
    return pl.pallas_call(
        functools.partial(attn_backward_kernel, last),
        out_shape=tuple(jax.ShapeDtypeStruct(*s) for s in shapes),
        in_specs=[VMEM] * len(args),
        out_specs=(VMEM,) * len(shapes),
        scratch_shapes=scratch,
        compiler_params=pltpu.CompilerParams(
            collective_id=6 if last else 5, has_side_effects=True, vmem_limit_bytes=60 * 1024 * 1024
        ),
        name="attn_backward_last" if last else "attn_backward",
    )(*args)


def split_pairs(grads):
    rows = grads.shape[0]
    pairs = grads.reshape(rows, KV_HEADS, 2, HEAD_DIM)
    return pairs[:, :, 0].reshape(rows, -1), pairs[:, :, 1].reshape(rows, -1)


def on_device(
    tokens,
    seg_ids,
    positions,
    attn_gain,
    w_query,
    w_key,
    w_value,
    w_out,
    ffn_gain,
    w_gate,
    w_up,
    w_down,
    cotangent,
):
    width = tokens.shape[2]
    trig, w_kvq, place = prepare(positions[0], w_query, w_key, w_value)
    gains = jnp.pad(jnp.stack([attn_gain, ffn_gain]), ((0, 6), (0, 0)))
    residual = tokens[0].astype(FULL)
    kept = []
    for repeat in range(2):
        normed, q, kv, log_total, mixed, after, normed_two = attn_forward(
            residual, gains, w_kvq, w_out, trig, place
        )
        result, rows_all, gate_all, up_all = ffn_forward(after, normed_two, w_gate, w_up, w_down)
        kept.append((residual, normed, q, kv, log_total, mixed, after, rows_all, gate_all, up_all))
        residual = result
    output = residual.astype(LOW)
    upstream = cotangent[0].astype(FULL)
    share = width // SHARES
    ffn_grads, parts, gain_grads = None, None, None
    whole = lax.axis_size("dp") != SHARES
    for repeat in (1, 0):
        residual, normed, q, kv, log_total, mixed, after, rows_all, gate_all, up_all = kept[repeat]
        after_grad, ffn_gain_term, ffn_grads = ffn_backward(
            upstream, after, gains, rows_all, gate_all, up_all, w_gate, w_up, w_down, ffn_grads
        )
        args = (after_grad, residual, normed, gains, q, kv, log_total, mixed, w_kvq, w_out, trig, place)
        if repeat == 1:
            upstream, attn_gain_term, *parts = attn_backward(*args)
            gain_grads = jnp.stack([attn_gain_term[0], ffn_gain_term[0]])
        elif whole:
            upstream, attn_gain_term, *terms = attn_backward(*args)
            gain_grads = gain_grads + jnp.stack([attn_gain_term[0], ffn_gain_term[0]])
            parts = [part.astype(FULL) + term.astype(FULL) for part, term in zip(parts, terms)]
        else:
            gain_grads = gain_grads + jnp.stack([jnp.zeros_like(attn_gain), ffn_gain_term[0]])
            final = (*parts, ffn_grads.reshape(3, SHARES // 2, 2, share, -1), jnp.pad(gain_grads, ((0, 6), (0, 0))))
            upstream, gain_all, ffn_share, *shares = attn_backward(*args, final)
    if whole:

        def over_rows(grads, dim):
            grads = lax.psum_scatter(grads.astype(LOW), "dp", scatter_dimension=dim, tiled=True)
            return grads.astype(FULL)

        def over_all(grads, dim):
            return lax.psum(over_rows(grads, dim).astype(LOW), "seq").astype(FULL)

        shares = [over_all(part[:, :share].reshape(width, -1), 0) for part in parts]
        ffn_share = over_rows(ffn_grads, 1)
        own_gains = over_all(gain_grads, 1)
    else:
        shares = [part[:share] for part in shares]
        own_gains = lax.dynamic_slice_in_dim(gain_all, lax.axis_index("dp") * share, share, axis=1)
    key_share, value_share = split_pairs(shares[2])
    return (
        output[None],
        upstream[None],
        own_gains[0],
        shares[1],
        key_share,
        value_share,
        shares[0],
        own_gains[1],
        ffn_share[0],
        ffn_share[1],
        ffn_share[2].T,
    )


def solution(mesh):
    in_specs = (
        P("dp", "seq", None),
        P("dp", "seq"),
        P("dp", "seq"),
        P(),
        P(),
        P(),
        P(),
        P(),
        P(),
        P(None, "seq"),
        P(None, "seq"),
        P("seq", None),
        P("dp", "seq", None),
    )
    out_specs = (
        P("dp", "seq", None),
        P("dp", "seq", None),
        P("dp"),
        P("dp", None),
        P("dp", None),
        P("dp", None),
        P("dp", None),
        P("dp"),
        P("dp", "seq"),
        P("dp", "seq"),
        P("seq", "dp"),
    )
    return jax.shard_map(
        on_device, mesh=mesh, in_specs=in_specs, out_specs=out_specs, check_vma=False
    )
```

```python
import functools

import jax
import jax.numpy as jnp
from jax import lax
from jax.experimental import pallas as pl
from jax.experimental.pallas import tpu as pltpu
from jax.sharding import PartitionSpec as P

MESH_ID = pl.DeviceIdType.MESH
HEADS = 15
KV_HEADS = 5
GROUP = 3
HEAD_DIM = 64
EPSILON = 1e-05
THETA = 10000.0
CHUNKS = 2
SHARES = 8
ROWS_PAD = 32
PIECE = 128
MASKED = -1e30
LOW = jnp.bfloat16
FULL = jnp.float32
SCALE = HEAD_DIM ** (-0.5)
NT = (((1,), (1,)), ((), ()))
TN = (((0,), (0,)), ((), ()))


def device(seq_pos, dp_pos):
    return {"seq": seq_pos, "dp": dp_pos}


def send(src, dst, send_sem, recv_sem, target):
    copy = pltpu.make_async_remote_copy(
        src_ref=src,
        dst_ref=dst,
        send_sem=send_sem,
        recv_sem=recv_sem,
        device_id=target,
        device_id_type=MESH_ID,
    )
    copy.start()
    return copy


class Hops:
    def __init__(self, send_sem, recv_sem):
        self.send_sem, self.recv_sem, self.used = send_sem, recv_sem, 0

    def __call__(self, src, dst, target):
        index, self.used = self.used, self.used + 1
        return send(src, dst, self.send_sem.at[index], self.recv_sem.at[index], target)


def greet(targets):
    barrier = pltpu.get_barrier_semaphore()
    for target in targets:
        pl.semaphore_signal(barrier, inc=1, device_id=target, device_id_type=MESH_ID)
    pl.semaphore_wait(barrier, len(targets))


def dot(left, right, dims=None):
    if dims is None:
        return jnp.dot(left, right, preferred_element_type=FULL)
    return lax.dot_general(left, right, dims, preferred_element_type=FULL)


def cost(microseconds):
    return pl.CostEstimate(flops=int(microseconds * 1.15e9), bytes_accessed=1 << 20, transcendentals=0)


def inverse_rms(value):
    return lax.rsqrt(jnp.mean(value * value, axis=-1, keepdims=True) + EPSILON)


def swap_halves(value):
    lane = lax.broadcasted_iota(jnp.int32, value.shape, 1)
    first = lax.rem(lane, HEAD_DIM) < HEAD_DIM // 2
    return jnp.where(first, pltpu.roll(value, 96, 1), pltpu.roll(value, 32, 1))


def attn_forward_kernel(
    extra, res_ref, gains_ref, w_kvq_ref, w_out_ref, trig_ref, place_ref, *rest
):
    if extra:
        extra_ref, extra_out = rest[0], rest[8]
        rest = rest[1:8] + rest[9:]
    (
        normed_out, q_out, kv_out, log_out, mixed_out, after_out, normed_two_out,
        peak, total, acc, send_sem, recv_sem,
    ) = rest[:12]
    seq, dp = lax.axis_index("seq"), lax.axis_index("dp")
    core, chip_x = lax.rem(seq, 2), lax.div(seq, 2)
    mate_seq, far_seq = seq + 1 - 2 * core, lax.rem(seq + 2, 4)
    mate, x_mate = device(mate_seq, dp), device(far_seq, dp)
    length = res_ref.shape[0]
    stacked = GROUP * length
    residual = res_ref[...]
    normed_out[...] = (residual * inverse_rms(residual) * gains_ref[0:1, :]).astype(LOW)
    kv_width = 2 * KV_HEADS * HEAD_DIM
    kv_pre = dot(normed_out[...], w_kvq_ref[:, :kv_width])
    for g in range(KV_HEADS):
        part = kv_pre[:, g * 128 : (g + 1) * 128]
        turned = part * trig_ref[2] + swap_halves(part) * trig_ref[3]
        kv_out[seq, :, g * 128 : (g + 1) * 128] = turned.astype(LOW)
    greet([mate, x_mate])
    own_kv = kv_out.at[seq]
    to_mate = send(own_kv, own_kv, send_sem.at[0], recv_sem.at[0], mate)
    to_x = send(own_kv, own_kv, send_sem.at[1], recv_sem.at[1], x_mate)
    q_pre = dot(normed_out[...], w_kvq_ref[:, kv_width:])
    lane = lax.broadcasted_iota(jnp.int32, (length, 128), 1)
    for pair in range((HEADS + 1) // 2):
        width = min(128, HEADS * HEAD_DIM - pair * 128)
        part = q_pre[:, pair * 128 : pair * 128 + width]
        if width < 128:
            part = jnp.concatenate([part, part], axis=1)
        turned = (part * trig_ref[0] + swap_halves(part) * trig_ref[1]) * SCALE
        q_out[2 * pair] = jnp.where(lane < HEAD_DIM, turned, 0.0).astype(LOW)
        if width == 128:
            q_out[2 * pair + 1] = jnp.where(lane < HEAD_DIM, pltpu.roll(turned, 64, 1), 0.0).astype(LOW)

    start, place = place_ref[0:1, :], place_ref[1:2, :]

    def attend(block, g, first):
        kv_g = kv_out[block, :, pl.ds(pl.multiple_of(g * 128, 128), 128)]
        q_g = q_out[pl.ds(3 * g, 3)].reshape(stacked, 128)
        scores = dot(kv_g, q_g, NT)
        key = lax.broadcasted_iota(jnp.int32, (length, stacked), 0) + block * length
        allowed = key >= start
        if first:
            allowed = allowed & (key <= place)
        scores = jnp.where(allowed, scores, MASKED)
        here = jnp.max(scores, axis=0, keepdims=True)
        if first:
            new_peak = here
        else:
            new_peak = jnp.maximum(peak[g], here)
        weights = jnp.exp(scores - new_peak)
        row_total = jnp.sum(weights, axis=0, keepdims=True)
        mix = dot(kv_g, weights.astype(LOW), TN)[HEAD_DIM:]
        if not first:
            fade = jnp.exp(peak[g] - new_peak)
            row_total = row_total + fade * total[g]
            mix = mix + fade * acc[g]
        peak[g], total[g], acc[g] = new_peak, row_total, mix

    @pl.loop(0, KV_HEADS)
    def _(g):
        attend(seq, g, True)

    to_mate.wait()

    @pl.when(core == 1)
    def _():
        @pl.loop(0, KV_HEADS)
        def _(g):
            attend(mate_seq, g, False)

    to_x.wait()
    far_kv = kv_out.at[far_seq]
    onward = send(far_kv, far_kv, send_sem.at[2], recv_sem.at[2], mate)
    if extra:
        mine, theirs = extra_out.at[seq], extra_out.at[far_seq]
        keep = pltpu.make_async_copy(extra_ref, mine, rest[12])
        keep.start()
        extra_x = send(extra_ref, mine, send_sem.at[3], recv_sem.at[3], x_mate)
        extra_mate = send(extra_ref, mine, send_sem.at[4], recv_sem.at[4], mate)

    @pl.when(chip_x == 1)
    def _():
        @pl.loop(0, KV_HEADS)
        def _(g):
            attend(far_seq, g, False)

    onward.wait()

    @pl.when(chip_x == 1)
    def _():
        @pl.loop(0, KV_HEADS)
        def _(g):
            attend(lax.rem(mate_seq + 2, 4), g, False)

    for g in range(KV_HEADS):
        heads = (acc[g] / total[g]).T.astype(LOW)
        log_out[g] = peak[g] + jnp.log(total[g])
        for i in range(GROUP):
            h = GROUP * g + i
            mixed_out[:, h * HEAD_DIM : (h + 1) * HEAD_DIM] = heads[i * length : (i + 1) * length]
    after = residual + dot(mixed_out[...], w_out_ref[...])
    after_out[...] = after
    normed_two_out[...] = (after * inverse_rms(after) * gains_ref[1:2, :]).astype(LOW)
    if extra:
        extra_x.wait()
        extra_onward = send(theirs, theirs, send_sem.at[5], recv_sem.at[5], mate)
        keep.wait()
        extra_mate.wait()
        extra_onward.wait()


VMEM = pl.BlockSpec(memory_space=pltpu.VMEM)
ANYWHERE = pl.BlockSpec(memory_space=pl.ANY)


def attn_forward(residual, gains, w_kvq, w_out, trig, place, extra=None):
    length, width = residual.shape
    kv_width = 2 * KV_HEADS * HEAD_DIM
    shapes = (
        ((length, width), LOW),
        ((HEADS, length, 128), LOW),
        ((4, length, kv_width), LOW),
        ((KV_HEADS, 1, GROUP * length), FULL),
        ((length, HEADS * HEAD_DIM), LOW),
        ((length, width), FULL),
        ((length, width), LOW),
    )
    args = (residual, gains, w_kvq, w_out, trig, place)
    in_specs, out_specs, extra_scratch, hops = [VMEM] * 6, (VMEM,) * 7, [], 3
    if extra is not None:
        args, in_specs, out_specs = args + (extra,), in_specs + [ANYWHERE], out_specs + (ANYWHERE,)
        shapes = shapes + (((4,) + extra.shape, extra.dtype),)
        extra_scratch, hops = [pltpu.SemaphoreType.DMA], 6
    return pl.pallas_call(
        functools.partial(attn_forward_kernel, extra is not None),
        out_shape=tuple(jax.ShapeDtypeStruct(*s) for s in shapes),
        in_specs=in_specs,
        out_specs=out_specs,
        scratch_shapes=[
            pltpu.VMEM((KV_HEADS, 1, GROUP * length), FULL),
            pltpu.VMEM((KV_HEADS, 1, GROUP * length), FULL),
            pltpu.VMEM((KV_HEADS, HEAD_DIM, GROUP * length), FULL),
            pltpu.SemaphoreType.DMA((hops,)),
            pltpu.SemaphoreType.DMA((hops,)),
        ]
        + extra_scratch,
        compiler_params=pltpu.CompilerParams(
            collective_id=1 if extra is None else 0, has_side_effects=True, vmem_limit_bytes=60 * 1024 * 1024
        ),
        cost_estimate=cost(25),
        name="attn_forward",
    )(*args)


def prepare(positions, w_query, w_key, w_value):
    length = positions.shape[0]
    frequency = THETA ** (-(jnp.arange(HEAD_DIM // 2, dtype=FULL) * 2.0 / HEAD_DIM))
    angles = positions.astype(FULL)[:, None] * frequency
    cos, sin = jnp.cos(angles), jnp.sin(angles)
    one, none = jnp.ones((length, HEAD_DIM), FULL), jnp.zeros((length, HEAD_DIM), FULL)
    trig = jnp.stack(
        [
            jnp.concatenate([cos, cos, cos, cos], 1),
            jnp.concatenate([-sin, sin, -sin, sin], 1),
            jnp.concatenate([cos, cos, one], 1),
            jnp.concatenate([-sin, sin, none], 1),
        ]
    )
    width = w_key.shape[0]
    pairs = jnp.stack([w_key.reshape(width, KV_HEADS, HEAD_DIM), w_value.reshape(width, KV_HEADS, HEAD_DIM)], axis=2)
    w_kvq = jnp.concatenate([pairs.reshape(width, -1), w_query], axis=1)
    own = lax.axis_index("seq") * length + jnp.arange(length, dtype=jnp.int32)
    place = jnp.stack([jnp.tile(own - positions, GROUP), jnp.tile(own, GROUP)])
    place = jnp.pad(place, ((0, 6), (0, 0)))
    return trig, w_kvq, place


def ffn_forward_kernel(
    after_ref, normed_ref, w_gate_ref, w_up_ref, w_down_ref,
    res_out, rows_out,
    mate_send, mate_recv, x_send, x_recv, own_far,
    send_sem, recv_sem,
):
    seq, dp = lax.axis_index("seq"), lax.axis_index("dp")
    core = lax.rem(seq, 2)
    mate_seq, far_seq = seq + 1 - 2 * core, lax.rem(seq + 2, 4)
    far_mate = lax.rem(mate_seq + 2, 4)
    mate, x_mate = device(mate_seq, dp), device(far_seq, dp)
    length = after_ref.shape[0]
    step = length // CHUNKS
    greet([mate, x_mate])
    part = lambda k: pl.ds(k * step, step)

    def hop(index, src, dst, target):
        return send(src, dst, send_sem.at[index], recv_sem.at[index], target)

    rows_out[seq] = normed_ref[...]
    own_rows = lambda k: rows_out.at[seq, part(k)]
    far_rows = lambda k: rows_out.at[far_seq, part(k)]
    to_x = [hop(k, own_rows(k), own_rows(k), x_mate) for k in range(CHUNKS)]
    to_mate = hop(CHUNKS, rows_out.at[seq], rows_out.at[seq], mate)
    base = CHUNKS + 1

    def ffn(quarter, rows):
        block = rows_out[quarter, rows]
        gate = dot(block, w_gate_ref[...])
        up = dot(block, w_up_ref[...])
        hidden = (gate * jax.nn.sigmoid(gate) * up).astype(LOW)
        return dot(hidden, w_down_ref[...], NT)

    everything = pl.ds(0, length)
    res_out[...] = after_ref[...] + ffn(seq, everything)
    to_mate.wait()
    mate_send[0] = ffn(mate_seq, everything).astype(LOW)
    back = hop(base, mate_send.at[0], mate_recv.at[0], mate)
    onward = []
    for k in range(CHUNKS):
        to_x[k].wait()
        onward.append(hop(base + 1 + k, far_rows(k), far_rows(k), mate))
        own_far[part(k)] = ffn(far_seq, part(k))
        onward[k].wait()
        mate_send[1, part(k)] = ffn(far_mate, part(k)).astype(LOW)
        joint = hop(base + 1 + CHUNKS + k, mate_send.at[1, part(k)], mate_recv.at[1, part(k)], mate)
        joint.wait()
        x_send[part(k)] = (own_far[part(k)] + mate_recv[1, part(k)].astype(FULL)).astype(LOW)
        onward.append(
            hop(base + 1 + 2 * CHUNKS + k, x_send.at[part(k)], x_recv.at[part(k)], x_mate)
        )
        onward[k], onward[-1] = onward[-1], onward[k]
        onward.pop()
    back.wait()
    res_out[...] += mate_recv[0].astype(FULL)
    for k in range(CHUNKS):
        onward[k].wait()
        res_out[part(k)] += x_recv[part(k)].astype(FULL)


def ffn_forward(after, normed_two, w_gate, w_up, w_down):
    length, width = after.shape
    shapes = (
        ((length, width), FULL),
        ((4, length, width), LOW),
    )
    sems = 3 * CHUNKS + CHUNKS + 2
    return pl.pallas_call(
        ffn_forward_kernel,
        out_shape=tuple(jax.ShapeDtypeStruct(*s) for s in shapes),
        in_specs=[VMEM] * 5,
        out_specs=(VMEM,) * len(shapes),
        scratch_shapes=[
            pltpu.VMEM((2, length, width), LOW),
            pltpu.VMEM((2, length, width), LOW),
            pltpu.VMEM((length, width), LOW),
            pltpu.VMEM((length, width), LOW),
            pltpu.VMEM((length, width), FULL),
            pltpu.SemaphoreType.DMA((sems,)),
            pltpu.SemaphoreType.DMA((sems,)),
        ],
        compiler_params=pltpu.CompilerParams(
            collective_id=2, has_side_effects=True, vmem_limit_bytes=60 * 1024 * 1024
        ),
        cost_estimate=cost(36),
        name="ffn_forward",
    )(after, normed_two, w_gate, w_up, w_down)


def norm_back(value, gain, grad):
    inverse = inverse_rms(value)
    weighted = grad * gain
    inner = jnp.mean(weighted * value, axis=-1, keepdims=True)
    back = inverse * weighted - value * (inverse * inverse * inverse) * inner
    return back, jnp.sum(grad * value * inverse, axis=0, keepdims=True)


def ffn_all_kernel(second, up_ref, after_ref, gains_ref, own_ref, still_refs, gate_ref, upw_ref, down_ref, far_ref, *rest):
    if second:
        result_out, prev_ref = rest[0], None
        rest = rest[1:]
    else:
        prev_ref, rest = rest[0], rest[1:]
    (
        grad_out, gain_out, weight_out,
        w_in, w_down, still_ref, moved, in_grad, in_temp, hidden, back,
        load_sem, send_sem, recv_sem,
    ) = rest
    hop = Hops(send_sem, recv_sem)
    seq, dp = lax.axis_index("seq"), lax.axis_index("dp")
    core = lax.rem(seq, 2)
    mate_seq, far_seq = seq + 1 - 2 * core, lax.rem(seq + 2, 4)
    far_mate = lax.rem(mate_seq + 2, 4)
    mate, x_mate = device(mate_seq, dp), device(far_seq, dp)
    length, width = up_ref.shape
    units = gate_ref.shape[1]
    whole = pl.ds(0, width)

    def slots(w, rows):
        return w_in.at[w, rows, :units], w_in.at[w, rows, units:], w_down.at[w, rows]

    loads = []

    def load(src, dst):
        loads.append(pltpu.make_async_copy(src, dst, load_sem.at[len(loads)]))
        loads[-1].start()

    for src, dst in zip((gate_ref, upw_ref, down_ref), slots(0, whole)):
        load(src, dst)
    moved[seq] = own_ref[...].astype(LOW)
    at = 0
    for ref in still_refs:
        load(ref, still_ref.at[:, pl.ds(at, ref.shape[1])])
        at += ref.shape[1]
    far_from = len(loads)
    for d in range(SHARES):
        at = min(d * PIECE, width - PIECE)
        rows = min(PIECE, width - PIECE - at) if d == SHARES - 2 else PIECE
        for i, dst in enumerate(slots(2, pl.ds(at, rows))):
            load(far_ref.at[d, pl.ds(i * PIECE, rows)], dst)
    greet([mate, x_mate])
    mine, theirs = moved.at[seq], moved.at[far_seq]
    to_x = hop(mine, mine, x_mate)
    to_mate = hop(mine, mine, mate)
    beside = [hop(src, dst, mate) for src, dst in zip((gate_ref, upw_ref, down_ref), slots(1, whole))]
    rows_ref, low_ref = (moved, still_ref) if second else (still_ref, moved)

    def halves(quarter, w, grads):
        both = dot(rows_ref[quarter], w_in[w])
        gate, up = both[:, :units], both[:, units:]
        bend = jax.nn.sigmoid(gate)
        silu = gate * bend
        hidden_grad = dot(low_ref[quarter], w_down[w])
        grads[:, :units] = (hidden_grad * up * bend * (1.0 + gate * (1.0 - bend))).astype(LOW)
        grads[:, units:] = (hidden_grad * silu).astype(LOW)
        return (silu * up).astype(LOW)

    for copy in loads[:far_from]:
        copy.wait()
    hidden[seq] = halves(seq, 0, in_grad.at[seq])
    back[...] = dot(in_grad[seq], w_in[0], NT)
    if second:
        grad_out[...] = after_ref[...] + dot(hidden[seq], w_down[0], NT)
    for copy in loads[far_from:]:
        copy.wait()
    across = [hop(w_in.at[2], w_in.at[3], mate), hop(w_down.at[2], w_down.at[3], mate)]
    for copy in beside:
        copy.wait()

    @pl.loop(1, 4)
    def _(w):
        @pl.when(w == 3)
        def _():
            for copy in across:
                copy.wait()

        act = halves(seq, w, in_temp)
        back[...] += dot(in_temp[...], w_in[w], NT)
        if second:
            grad_out[...] += dot(act, w_down[w], NT)

    if second:
        result_out[...] = grad_out[...].astype(LOW)
    sent_back, gain_term = norm_back(after_ref[...], gains_ref[1:2, :], back[...])
    grad_out[...] = up_ref[...].astype(FULL) + sent_back
    gain_out[...] = jnp.broadcast_to(gain_term, gain_out.shape)

    to_mate.wait()
    to_x.wait()
    onward = hop(theirs, theirs, mate)

    @pl.loop(0, 3)
    def _(i):
        @pl.when(i == 2)
        def _():
            onward.wait()

        quarter = jnp.where(i == 0, mate_seq, jnp.where(i == 1, far_seq, far_mate))
        hidden[quarter] = halves(quarter, 0, in_grad.at[quarter])

    flat = lambda ref: ref[...].reshape(4 * length, ref.shape[2])

    def finish(i, term):
        if prev_ref is not None:
            term = term + prev_ref[i].astype(FULL)
        weight_out[i] = term.astype(LOW)

    both = dot(flat(rows_ref), flat(in_grad), TN)
    finish(0, both[:, :units])
    finish(1, both[:, units:])
    finish(2, dot(flat(low_ref), flat(hidden), TN))


def ffn_all_call(stills, second, *refs):
    return ffn_all_kernel(second, *refs[:4], refs[4 : 4 + stills], *refs[4 + stills :])


def ffn_all(second, upstream, after, gains, own, stills, weights, far, prev=None):
    length, width = after.shape
    units = weights[0].shape[1]
    shapes = (
        ((length, width), FULL),
        ((8, width), FULL),
        ((3, width, units), LOW),
    )
    if second:
        shapes = (((length, width), LOW),) + shapes
    args = (upstream, after, gains, own) + tuple(stills) + tuple(weights) + (far,)
    specs = [VMEM] * 4 + [ANYWHERE] * (len(stills) + 4)
    if not second:
        args, specs = args + (prev,), specs + [VMEM]
    return pl.pallas_call(
        functools.partial(ffn_all_call, len(stills), second),
        out_shape=tuple(jax.ShapeDtypeStruct(*s) for s in shapes),
        in_specs=specs,
        out_specs=(VMEM,) * len(shapes),
        scratch_shapes=[
            pltpu.VMEM((4, width, 2 * units), LOW),
            pltpu.VMEM((4, width, units), LOW),
            pltpu.VMEM((4, length, width), LOW),
            pltpu.VMEM((4, length, width), LOW),
            pltpu.VMEM((4, length, 2 * units), LOW),
            pltpu.VMEM((length, 2 * units), LOW),
            pltpu.VMEM((4, length, units), LOW),
            pltpu.VMEM((length, width), FULL),
            pltpu.SemaphoreType.DMA((3 + len(stills) + 3 * SHARES,)),
            pltpu.SemaphoreType.DMA((8,)),
            pltpu.SemaphoreType.DMA((8,)),
        ],
        compiler_params=pltpu.CompilerParams(
            collective_id=3 if second else 4, has_side_effects=True, vmem_limit_bytes=60 * 1024 * 1024
        ),
        cost_estimate=cost(30),
        name="ffn_second" if second else "ffn_first_backward",
    )(*args)


def attn_backward_kernel(
    last, after_grad_ref, res_ref, normed_ref, gains_ref, q_ref, kv_ref, log_ref, mixed_ref,
    w_kvq_ref, w_out_ref, trig_ref, place_ref, *rest
):
    if last:
        prev, ffn_ref, gain_ref = rest[:3], rest[3], rest[4]
        grad_out, gain_out, ffn_out, share_outs = rest[5], rest[6], rest[7], rest[8:11]
        rest = rest[11:]
    else:
        prev = (None, None, None)
        grad_out, gain_out = rest[:2]
        parts = rest[2:5]
        rest = rest[5:]
    mixed_grad, delta, kv_grad, query_grad, back, grad_send, grad_recv, send_sem, recv_sem = rest[:9]
    hop = Hops(send_sem, recv_sem)
    seq, dp = lax.axis_index("seq"), lax.axis_index("dp")
    core, chip_x = lax.rem(seq, 2), lax.div(seq, 2)
    mate_seq, far_seq = seq + 1 - 2 * core, lax.rem(seq + 2, 4)
    far_mate = lax.rem(mate_seq + 2, 4)
    mate, x_mate = device(mate_seq, dp), device(far_seq, dp)
    length, width = res_ref.shape
    stacked = GROUP * length
    kv_width = 2 * KV_HEADS * HEAD_DIM
    if last:
        parts = rest[9:12]
        f_y_recv, f_z_send, f_z_recv, gain_recv = rest[12:16]
        buffers = [rest[16 + 8 * i : 24 + 8 * i] for i in range(3)]
        row_y, row_z = lax.rem(dp, 2), lax.div(dp, 2)
        y_mate = device(seq, dp + 1 - 2 * row_y)
        z_of = [lax.rem(row_z + k, 4) for k in range(1, 4)]
        z_mates = [device(seq, z * 2 + row_y) for z in z_of]
        greet([mate, x_mate, y_mate] + z_mates)
        f_y = [hop(ffn_ref.at[m, :, 1 - row_y], f_y_recv.at[m], y_mate) for m in range(3)]
    else:
        greet([mate, x_mate])

    def f_z_start(m):
        f_y[m].wait()
        copies = []
        for k in range(3):
            joint = ffn_ref[m, z_of[k], row_y].astype(FULL) + f_y_recv[m, z_of[k]].astype(FULL)
            f_z_send[m, k] = joint.astype(LOW)
            copies.append(hop(f_z_send.at[m, k], f_z_recv.at[m, k], z_mates[k]))
        return copies

    def f_z_finish(m, copies):
        total = ffn_ref[m, row_z, row_y].astype(FULL) + f_y_recv[m, row_z].astype(FULL)
        for k in range(3):
            copies[k].wait()
            total = total + f_z_recv[m, k].astype(FULL)
        ffn_out[m] = total

    quarter = lambda x, c: pl.ds(pl.multiple_of(64 * x + ROWS_PAD * c, ROWS_PAD), ROWS_PAD)

    def core_start(i):
        core_recv = buffers[i][0]
        return [hop(parts[i].at[:, quarter(x, 1 - core)], core_recv.at[x], mate) for x in range(2)]

    def x_start(i, copies):
        core_recv, x_send, x_recv = buffers[i][:3]
        for copy in copies:
            copy.wait()
        joint = parts[i][:, quarter(1 - chip_x, core)].astype(FULL) + core_recv[1 - chip_x].astype(FULL)
        x_send[...] = joint.astype(LOW)
        return hop(x_send, x_recv, x_mate)

    def y_start(i, copy):
        core_recv, x_send, x_recv, own, y_recv = buffers[i][:5]
        joint = parts[i][:, quarter(chip_x, core)].astype(FULL) + core_recv[chip_x].astype(FULL)
        copy.wait()
        own[...] = (joint + x_recv[...].astype(FULL)).astype(LOW).reshape(own.shape)
        return hop(own.at[:, 1 - row_y], y_recv, y_mate)

    def z_start(i, copy):
        own, y_recv, z_send, z_recv = buffers[i][3:7]
        copy.wait()
        copies = []
        for k in range(3):
            z_send[k] = (own[z_of[k], row_y].astype(FULL) + y_recv[z_of[k]].astype(FULL)).astype(LOW)
            copies.append(hop(z_send.at[k], z_recv.at[k], z_mates[k]))
        return copies

    def share_start(i, copies):
        own, y_recv, z_send, z_recv, gathered = buffers[i][3:8]
        total = own[row_z, row_y].astype(FULL) + y_recv[row_z].astype(FULL)
        for k in range(3):
            copies[k].wait()
            total = total + z_recv[k].astype(FULL)
        gathered[seq] = total.astype(LOW)
        mine = gathered.at[seq]
        return hop(mine, mine, x_mate), hop(mine, mine, mate)

    def share_pass(i, copies):
        gathered = buffers[i][7]
        copies[0].wait()
        theirs = gathered.at[far_seq]
        return hop(theirs, theirs, mate), copies[1]

    def share_finish(i, copies):
        gathered = buffers[i][7]
        for copy in copies:
            copy.wait()
        for s in range(4):
            share_outs[i][s * ROWS_PAD : (s + 1) * ROWS_PAD] = gathered[s].astype(FULL)

    def weight(i, left, right):
        term = dot(left, right, TN)
        share = width // SHARES
        for j in range(SHARES):
            rows = term[j * share : (j + 1) * share]
            if prev[i] is not None:
                rows = rows + prev[i][j, :share].astype(FULL)
            parts[i][j, :share] = rows.astype(LOW)

    low_grad = after_grad_ref[...].astype(LOW)
    mixed_back = dot(low_grad, w_out_ref[...], NT)
    lane = lax.broadcasted_iota(jnp.int32, (length, 128), 1)
    for pair in range((HEADS + 1) // 2):
        span = min(128, HEADS * HEAD_DIM - pair * 128)
        part = mixed_back[:, pair * 128 : pair * 128 + span]
        if span < 128:
            part = jnp.concatenate([part, part], axis=1)
        else:
            mixed_grad[2 * pair + 1] = jnp.where(lane >= HEAD_DIM, part, 0.0).astype(LOW)
        mixed_grad[2 * pair] = jnp.where(lane >= HEAD_DIM, pltpu.roll(part, 64, 1), 0.0).astype(LOW)
    product = mixed_back.astype(LOW).astype(FULL) * mixed_ref[...].astype(FULL)
    high = product.astype(LOW)
    rest_low = (product - high.astype(FULL)).astype(LOW)
    head = lax.broadcasted_iota(jnp.int32, (16, HEADS * HEAD_DIM), 0)
    column = lax.broadcasted_iota(jnp.int32, (16, HEADS * HEAD_DIM), 1)
    pick = jnp.where(lax.div(column, HEAD_DIM) == head, 1.0, 0.0).astype(LOW)
    sums = dot(pick, high, NT) + dot(pick, rest_low, NT)
    for g in range(KV_HEADS):
        delta[g] = jnp.concatenate([sums[3 * g + i : 3 * g + i + 1] for i in range(GROUP)], axis=1)
    query_grad[...] = jnp.zeros_like(query_grad)
    weight(0, mixed_ref[...], low_grad)
    if last:
        o_core = core_start(0)

    start, place = place_ref[0:1, :], place_ref[1:2, :]

    def attend(block, g, diagonal):
        columns = pl.ds(pl.multiple_of(g * 128, 128), 128)
        kv_g = kv_ref[block, :, columns]
        q_g = q_ref[pl.ds(3 * g, 3)].reshape(stacked, 128)
        out_g = mixed_grad[pl.ds(3 * g, 3)].reshape(stacked, 128)
        scores = dot(kv_g, q_g, NT)
        key = lax.broadcasted_iota(jnp.int32, (length, stacked), 0) + block * length
        allowed = key >= start
        if diagonal:
            allowed = allowed & (key <= place)
        weights = jnp.where(allowed, jnp.exp(scores - log_ref[g]), 0.0)
        probs_grad = dot(kv_g, out_g, NT)
        score_grad = (weights * (probs_grad - delta[g])).astype(LOW)
        kv_grad[block, :, columns] = dot(weights.astype(LOW), out_g) + dot(score_grad, q_g)
        query_grad[g] += dot(kv_g, score_grad, TN)[:HEAD_DIM]

    def attend_all(block, condition, diagonal=False):
        @pl.when(condition)
        def _():
            @pl.loop(0, KV_HEADS)
            def _(g):
                attend(block, g, diagonal)

        if not diagonal:
            @pl.when(jnp.logical_not(condition))
            def _():
                kv_grad[block] = jnp.zeros_like(kv_grad[block])

    right = chip_x == 1
    attend_all(far_mate, right)
    grad_send[0] = kv_grad[far_mate].astype(LOW)
    joint = hop(grad_send.at[0], grad_recv.at[0], mate)
    attend_all(far_seq, right)
    joint.wait()
    grad_send[1] = (kv_grad[far_seq] + grad_recv[0].astype(FULL)).astype(LOW)
    across = hop(grad_send.at[1], grad_recv.at[1], x_mate)
    if last:
        o_x = x_start(0, o_core)
        f_z = [f_z_start(0)]
    attend_all(mate_seq, core == 1)
    grad_send[2] = kv_grad[mate_seq].astype(LOW)
    beside = hop(grad_send.at[2], grad_recv.at[2], mate)
    attend_all(seq, seq >= 0, True)

    for g in range(KV_HEADS):
        heads = query_grad[g].T * SCALE
        for i in range(GROUP):
            h = GROUP * g + i
            part = heads[i * length : (i + 1) * length]
            part = jnp.concatenate([part, part], axis=1)
            turned = part * trig_ref[0] - swap_halves(part) * trig_ref[1]
            at = kv_width + h * HEAD_DIM
            back[:, at : at + HEAD_DIM] = turned[:, :HEAD_DIM].astype(LOW)
    weight(1, normed_ref[...], back[:, kv_width:])
    if last:
        q_core = core_start(1)
        o_y = y_start(0, o_x)
    normed_grad = dot(back[:, kv_width:], w_kvq_ref[:, kv_width:], NT)
    if last:
        q_x = x_start(1, q_core)

    across.wait()
    beside.wait()
    own = kv_grad[seq] + grad_recv[1].astype(FULL) + grad_recv[2].astype(FULL)
    for g in range(KV_HEADS):
        part = own[:, g * 128 : (g + 1) * 128]
        back[:, g * 128 : (g + 1) * 128] = (part * trig_ref[2] - swap_halves(part) * trig_ref[3]).astype(LOW)
    weight(2, normed_ref[...], back[:, :kv_width])
    if last:
        kv_core = core_start(2)
        f_z.append(f_z_start(1))
        kv_x = x_start(2, kv_core)
    normed_grad = normed_grad + dot(back[:, :kv_width], w_kvq_ref[:, :kv_width], NT)
    sent_back, gain_term = norm_back(res_ref[...], gains_ref[0:1, :], normed_grad)
    grad_out[...] = after_grad_ref[...] + sent_back
    if not last:
        gain_out[...] = jnp.broadcast_to(gain_term, gain_out.shape)
        return

    row = lax.broadcasted_iota(jnp.int32, gain_out.shape, 0)
    gain_out[...] = gain_ref[...] + jnp.where(row == 0, gain_term, 0.0)
    partners = [
        mate, x_mate, y_mate, device(seq, lax.rem(dp + 4, 8)), device(seq, dp + 2 - 4 * lax.rem(row_z, 2))
    ]
    gain_hop = lambda n: hop(gain_out, gain_recv.at[n], partners[n])

    def gain_add(n, copy):
        copy.wait()
        gain_out[...] += gain_recv[n]

    gain_copy = gain_hop(0)
    f_z.append(f_z_start(2))
    gain_add(0, gain_copy)
    gain_copy = gain_hop(1)
    q_y = y_start(1, q_x)
    o_z = z_start(0, o_y)
    gain_add(1, gain_copy)
    gain_copy = gain_hop(2)
    kv_y = y_start(2, kv_x)
    f_z_finish(0, f_z[0])
    gain_add(2, gain_copy)
    gain_copy = gain_hop(3)
    q_z = z_start(1, q_y)
    f_z_finish(1, f_z[1])
    gain_add(3, gain_copy)
    gain_copy = gain_hop(4)
    kv_z = z_start(2, kv_y)
    f_z_finish(2, f_z[2])
    o_s = share_start(0, o_z)
    o_s = share_pass(0, o_s)
    q_s = share_start(1, q_z)
    gain_add(4, gain_copy)
    kv_s = share_start(2, kv_z)
    q_s = share_pass(1, q_s)
    share_finish(0, o_s)
    kv_s = share_pass(2, kv_s)
    share_finish(1, q_s)
    share_finish(2, kv_s)


def attn_backward(after_grad, residual, normed, gains, q, kv, log_total, mixed, w_kvq, w_out, trig, place, final=None):
    length, width = residual.shape
    kv_width = 2 * KV_HEADS * HEAD_DIM
    last = final is not None
    args = (after_grad, residual, normed, gains, q, kv, log_total, mixed, w_kvq, w_out, trig, place)
    shapes = (((length, width), FULL), ((8, width), FULL))
    sizes = (width, width, kv_width)
    part_shapes = [((SHARES, 4 * ROWS_PAD, c), LOW) for c in sizes]
    scratch = [
        pltpu.VMEM((HEADS, length, 128), LOW),
        pltpu.VMEM((KV_HEADS, 1, GROUP * length), FULL),
        pltpu.VMEM((4, length, kv_width), FULL),
        pltpu.VMEM((KV_HEADS, HEAD_DIM, GROUP * length), FULL),
        pltpu.VMEM((length, kv_width + width), LOW),
        pltpu.VMEM((3, length, kv_width), LOW),
        pltpu.VMEM((3, length, kv_width), LOW),
    ]
    hops = 3
    if last:
        share, hidden = final[3].shape[3:]
        args = args + tuple(final)
        shapes = shapes + (((3, share, hidden), FULL),) + tuple(((4 * ROWS_PAD, c), FULL) for c in sizes)
        hops = 3 + 3 + 9 + 5 + 3 * (2 + 1 + 1 + 3 + 3)
        scratch += [pltpu.SemaphoreType.DMA((hops,))] * 2
        scratch += [pltpu.VMEM(*s) for s in part_shapes]
        scratch += [
            pltpu.VMEM((3, 4, share, hidden), LOW),
            pltpu.VMEM((3, 3, share, hidden), LOW),
            pltpu.VMEM((3, 3, share, hidden), LOW),
            pltpu.VMEM((5, 8, width), FULL),
        ]
        for c in sizes:
            scratch += [
                pltpu.VMEM((2, SHARES, ROWS_PAD, c), LOW),
                pltpu.VMEM((SHARES, ROWS_PAD, c), LOW),
                pltpu.VMEM((SHARES, ROWS_PAD, c), LOW),
                pltpu.VMEM((4, 2, ROWS_PAD, c), LOW),
                pltpu.VMEM((4, ROWS_PAD, c), LOW),
                pltpu.VMEM((3, ROWS_PAD, c), LOW),
                pltpu.VMEM((3, ROWS_PAD, c), LOW),
                pltpu.VMEM((4, ROWS_PAD, c), LOW),
            ]
    else:
        shapes = shapes + tuple(part_shapes)
        scratch += [pltpu.SemaphoreType.DMA((hops,))] * 2
    return pl.pallas_call(
        functools.partial(attn_backward_kernel, last),
        out_shape=tuple(jax.ShapeDtypeStruct(*s) for s in shapes),
        in_specs=[VMEM] * len(args),
        out_specs=(VMEM,) * len(shapes),
        scratch_shapes=scratch,
        compiler_params=pltpu.CompilerParams(
            collective_id=6 if last else 5, has_side_effects=True, vmem_limit_bytes=60 * 1024 * 1024
        ),
        cost_estimate=cost(95 if last else 40),
        name="attn_backward_last" if last else "attn_backward",
    )(*args)


def split_pairs(grads):
    rows = grads.shape[0]
    pairs = grads.reshape(rows, KV_HEADS, 2, HEAD_DIM)
    return pairs[:, :, 0].reshape(rows, -1), pairs[:, :, 1].reshape(rows, -1)


def on_device(
    tokens,
    seg_ids,
    positions,
    attn_gain,
    w_query,
    w_key,
    w_value,
    w_out,
    ffn_gain,
    w_gate,
    w_up,
    w_down,
    cotangent,
):
    width = tokens.shape[2]
    trig, w_kvq, place = prepare(positions[0], w_query, w_key, w_value)
    gains = jnp.pad(jnp.stack([attn_gain, ffn_gain]), ((0, 6), (0, 0)))
    whole = lax.axis_size("dp") != SHARES
    share = width // SHARES
    own_weights = (w_gate, w_up, w_down.T)

    def over_x(value):
        return lax.ppermute(value, "seq", [(s, (s + 2) % 4) for s in range(4)])

    def over_rows_piece(value, d):
        return lax.dynamic_slice_in_dim(value, jnp.minimum(d * PIECE, width - PIECE), PIECE, axis=0)

    if whole:
        theirs = [over_x(w) for w in own_weights]
        far = jnp.stack([jnp.concatenate([over_rows_piece(w, d) for w in theirs]) for d in range(SHARES)])
    else:
        piece = jnp.concatenate([over_rows_piece(w, lax.axis_index("dp")) for w in own_weights])
        far = lax.all_gather(over_x(piece), "dp", axis=0)

    tokens_full = tokens[0].astype(FULL)
    half = cotangent.shape[1] // 2
    first = attn_forward(tokens_full, gains, w_kvq, w_out, trig, place, cotangent[0, :half])
    residual, rows_all = ffn_forward(first[5], first[6], *own_weights)
    second = attn_forward(residual, gains, w_kvq, w_out, trig, place, cotangent[0, half:])
    output, after_grad, ffn_gain_term, ffn_grads = ffn_all(
        True, cotangent[0], second[5], gains, second[6], (first[7], second[7]), own_weights, far
    )

    def attn_args(after_grad, residual, kept):
        normed, q, kv, log_total, mixed = kept[:5]
        return (after_grad, residual, normed, gains, q, kv, log_total, mixed, w_kvq, w_out, trig, place)

    upstream, attn_gain_term, *parts = attn_backward(*attn_args(after_grad, residual, second))
    gain_grads = jnp.stack([attn_gain_term[0], ffn_gain_term[0]])
    after_grad, ffn_gain_term, ffn_grads = ffn_all(
        False, upstream, first[5], gains, upstream, (rows_all,), own_weights, far, ffn_grads
    )
    args = attn_args(after_grad, tokens_full, first)
    if whole:
        upstream, attn_gain_term, *terms = attn_backward(*args)
        gain_grads = gain_grads + jnp.stack([attn_gain_term[0], ffn_gain_term[0]])
        parts = [part.astype(FULL) + term.astype(FULL) for part, term in zip(parts, terms)]
    else:
        gain_grads = gain_grads + jnp.stack([jnp.zeros_like(attn_gain), ffn_gain_term[0]])
        final = (*parts, ffn_grads.reshape(3, SHARES // 2, 2, share, -1), jnp.pad(gain_grads, ((0, 6), (0, 0))))
        upstream, gain_all, ffn_share, *shares = attn_backward(*args, final)
    if whole:

        def over_rows(grads, dim):
            grads = lax.psum_scatter(grads.astype(LOW), "dp", scatter_dimension=dim, tiled=True)
            return grads.astype(FULL)

        def over_all(grads, dim):
            return lax.psum(over_rows(grads, dim).astype(LOW), "seq").astype(FULL)

        shares = [over_all(part[:, :share].reshape(width, -1), 0) for part in parts]
        ffn_share = over_rows(ffn_grads, 1)
        own_gains = over_all(gain_grads, 1)
    else:
        shares = [part[:share] for part in shares]
        own_gains = lax.dynamic_slice_in_dim(gain_all, lax.axis_index("dp") * share, share, axis=1)
    key_share, value_share = split_pairs(shares[2])
    return (
        output[None],
        upstream[None],
        own_gains[0],
        shares[1],
        key_share,
        value_share,
        shares[0],
        own_gains[1],
        ffn_share[0],
        ffn_share[1],
        ffn_share[2].T,
    )


def solution(mesh):
    in_specs = (
        P("dp", "seq", None),
        P("dp", "seq"),
        P("dp", "seq"),
        P(),
        P(),
        P(),
        P(),
        P(),
        P(),
        P(None, "seq"),
        P(None, "seq"),
        P("seq", None),
        P("dp", "seq", None),
    )
    out_specs = (
        P("dp", "seq", None),
        P("dp", "seq", None),
        P("dp"),
        P("dp", None),
        P("dp", None),
        P("dp", None),
        P("dp", None),
        P("dp"),
        P("dp", "seq"),
        P("dp", "seq"),
        P("seq", "dp"),
    )
    return jax.shard_map(
        on_device, mesh=mesh, in_specs=in_specs, out_specs=out_specs, check_vma=False
    )
```

```python
import functools

import jax
import jax.numpy as jnp
from jax import lax
from jax.experimental import pallas as pl
from jax.experimental.pallas import tpu as pltpu
from jax.sharding import PartitionSpec as P

MESH_ID = pl.DeviceIdType.MESH
HEADS = 15
KV_HEADS = 5
GROUP = 3
HEAD_DIM = 64
EPSILON = 1e-05
THETA = 10000.0
CHUNKS = 2
SHARES = 8
ROWS_PAD = 32
PIECE = 128
MASKED = -1e30
LOW = jnp.bfloat16
FULL = jnp.float32
SCALE = HEAD_DIM ** (-0.5)
NT = (((1,), (1,)), ((), ()))
TN = (((0,), (0,)), ((), ()))


def device(seq_pos, dp_pos):
    return {"seq": seq_pos, "dp": dp_pos}


def send(src, dst, send_sem, recv_sem, target):
    copy = pltpu.make_async_remote_copy(
        src_ref=src,
        dst_ref=dst,
        send_sem=send_sem,
        recv_sem=recv_sem,
        device_id=target,
        device_id_type=MESH_ID,
    )
    copy.start()
    return copy


class Hops:
    def __init__(self, send_sem, recv_sem):
        self.send_sem, self.recv_sem, self.used = send_sem, recv_sem, 0

    def __call__(self, src, dst, target):
        index, self.used = self.used, self.used + 1
        return send(src, dst, self.send_sem.at[index], self.recv_sem.at[index], target)


class Later:
    def __init__(self, src, dst, sem):
        self.copy, self.dst, self.waited = pltpu.make_async_copy(src, dst, sem), dst, False
        self.copy.start()

    def __call__(self):
        if not self.waited:
            self.copy.wait()
            self.waited = True
        return self.dst


class Early:
    def __init__(self, sem):
        self.sem, self.copies = sem, []

    def __call__(self, src, dst):
        self.copies.append(pltpu.make_async_copy(src, dst, self.sem.at[len(self.copies)]))
        self.copies[-1].start()

    def finish(self):
        for copy in self.copies:
            copy.wait()


class LaterPairs:
    def __init__(self, key_hbm, value_hbm, dst, sem):
        self.copies, self.dst = [], dst
        for h in range(2 * KV_HEADS):
            src = (key_hbm, value_hbm)[h % 2].at[pl.ds(h // 2 * HEAD_DIM, HEAD_DIM)]
            self.copies.append(pltpu.make_async_copy(src, dst.at[pl.ds(h * HEAD_DIM, HEAD_DIM)], sem.at[h]))
            self.copies[-1].start()

    def __call__(self):
        for copy in self.copies:
            copy.wait()
        self.copies = []
        return self.dst


def greet(targets):
    barrier = pltpu.get_barrier_semaphore()
    for target in targets:
        pl.semaphore_signal(barrier, inc=1, device_id=target, device_id_type=MESH_ID)
    pl.semaphore_wait(barrier, len(targets))


def dot(left, right, dims=None):
    if dims is None:
        return jnp.dot(left, right, preferred_element_type=FULL)
    return lax.dot_general(left, right, dims, preferred_element_type=FULL)


def cost(microseconds):
    return pl.CostEstimate(flops=int(microseconds * 1.15e9), bytes_accessed=1 << 20, transcendentals=0)


def inverse_rms(value):
    return lax.rsqrt(jnp.mean(value * value, axis=-1, keepdims=True) + EPSILON)


def swap_halves(value):
    lane = lax.broadcasted_iota(jnp.int32, value.shape, 1)
    first = (lane & (HEAD_DIM // 2)) == 0
    return jnp.where(first, pltpu.roll(value, 96, 1), pltpu.roll(value, 32, 1))


def attn_forward_kernel(
    extra, res_ref, gains_ref, w_key_hbm, w_value_hbm, w_query_hbm, w_out_hbm, trig_hbm, place_ref, *rest
):
    if extra:
        extra_ref, extra_out = rest[0], rest[8]
        rest = rest[1:8] + rest[9:]
    normed_hbm, q_hbm, kv_hbm, log_out, mixed_out, after_out, normed_two_out, *rest = rest
    w_kv_buf, w_query_buf, w_out_buf, trig_buf, normed_out, q_out, kv_out, pair_sem, late_sem, early_sem, *rest = rest
    peak, total, acc, send_sem, recv_sem, *rest = rest
    w_kv = LaterPairs(w_key_hbm, w_value_hbm, w_kv_buf, pair_sem)
    trig = Later(trig_hbm, trig_buf, late_sem.at[0])
    w_query = Later(w_query_hbm, w_query_buf, late_sem.at[1])
    w_out = Later(w_out_hbm, w_out_buf, late_sem.at[2])
    early = Early(early_sem)
    seq, dp = lax.axis_index("seq"), lax.axis_index("dp")
    core, chip_x = lax.rem(seq, 2), lax.div(seq, 2)
    mate_seq, far_seq = seq + 1 - 2 * core, lax.rem(seq + 2, 4)
    mate, x_mate = device(mate_seq, dp), device(far_seq, dp)
    length = res_ref.shape[0]
    stacked = GROUP * length
    residual = res_ref[...].astype(FULL)
    normed_out[...] = (residual * inverse_rms(residual) * gains_ref[0:1, :]).astype(LOW)
    early(normed_out, normed_hbm)
    kv_width = 2 * KV_HEADS * HEAD_DIM
    kv_pre = dot(normed_out[...], w_kv()[...], NT)
    trig_ref = trig()
    for g in range(KV_HEADS):
        part = kv_pre[:, g * 128 : (g + 1) * 128]
        turned = part * trig_ref[2] + swap_halves(part) * trig_ref[3]
        kv_out[seq, :, g * 128 : (g + 1) * 128] = turned.astype(LOW)
    greet([mate, x_mate])
    own_kv = kv_out.at[seq]
    to_mate = send(own_kv, own_kv, send_sem.at[0], recv_sem.at[0], mate)
    to_x = send(own_kv, own_kv, send_sem.at[1], recv_sem.at[1], x_mate)
    q_pre = dot(normed_out[...], w_query()[...])
    lane = lax.broadcasted_iota(jnp.int32, (length, 128), 1)
    for pair in range((HEADS + 1) // 2):
        width = min(128, HEADS * HEAD_DIM - pair * 128)
        part = q_pre[:, pair * 128 : pair * 128 + width]
        if width < 128:
            part = jnp.concatenate([part, part], axis=1)
        turned = (part * trig_ref[0] + swap_halves(part) * trig_ref[1]) * SCALE
        q_out[2 * pair] = jnp.where(lane < HEAD_DIM, turned, 0.0).astype(LOW)
        if width == 128:
            q_out[2 * pair + 1] = jnp.where(lane < HEAD_DIM, pltpu.roll(turned, 64, 1), 0.0).astype(LOW)

    early(q_out, q_hbm)
    start, place = place_ref[0:1, :], place_ref[1:2, :]

    def attend(block, g, first):
        kv_g = kv_out[block, :, pl.ds(pl.multiple_of(g * 128, 128), 128)]
        q_g = q_out[pl.ds(3 * g, 3)].reshape(stacked, 128)
        scores = dot(kv_g, q_g, NT)
        key = lax.broadcasted_iota(jnp.int32, (length, stacked), 0) + block * length
        allowed = key >= start
        if first:
            allowed = allowed & (key <= place)
        scores = jnp.where(allowed, scores, MASKED)
        here = jnp.max(scores, axis=0, keepdims=True)
        if first:
            new_peak = here
        else:
            new_peak = jnp.maximum(peak[g], here)
        weights = jnp.exp(scores - new_peak)
        row_total = jnp.sum(weights, axis=0, keepdims=True)
        mix = dot(kv_g, weights.astype(LOW), TN)[HEAD_DIM:]
        if not first:
            fade = jnp.exp(peak[g] - new_peak)
            row_total = row_total + fade * total[g]
            mix = mix + fade * acc[g]
        peak[g], total[g], acc[g] = new_peak, row_total, mix

    @pl.loop(0, KV_HEADS)
    def _(g):
        attend(seq, g, True)

    to_mate.wait()

    @pl.when(core == 1)
    def _():
        @pl.loop(0, KV_HEADS)
        def _(g):
            attend(mate_seq, g, False)

    to_x.wait()
    far_kv = kv_out.at[far_seq]
    onward = send(far_kv, far_kv, send_sem.at[2], recv_sem.at[2], mate)
    if extra:
        mine, theirs = extra_out.at[seq], extra_out.at[far_seq]
        early(extra_ref, mine)
        extra_x = send(extra_ref, mine, send_sem.at[3], recv_sem.at[3], x_mate)
        extra_mate = send(extra_ref, mine, send_sem.at[4], recv_sem.at[4], mate)

    @pl.when(chip_x == 1)
    def _():
        @pl.loop(0, KV_HEADS)
        def _(g):
            attend(far_seq, g, False)

    onward.wait()
    early(kv_out, kv_hbm)

    @pl.when(chip_x == 1)
    def _():
        @pl.loop(0, KV_HEADS)
        def _(g):
            attend(lax.rem(mate_seq + 2, 4), g, False)

    if extra:
        extra_x.wait()
        extra_onward = send(theirs, theirs, send_sem.at[5], recv_sem.at[5], mate)
    for g in range(KV_HEADS):
        heads = (acc[g] / total[g]).T.astype(LOW)
        log_out[g] = peak[g] + jnp.log(total[g])
        for i in range(GROUP):
            h = GROUP * g + i
            mixed_out[:, h * HEAD_DIM : (h + 1) * HEAD_DIM] = heads[i * length : (i + 1) * length]
    after = residual + dot(mixed_out[...], w_out()[...])
    after_out[...] = after
    normed_two_out[...] = (after * inverse_rms(after) * gains_ref[1:2, :]).astype(LOW)
    if extra:
        extra_mate.wait()
        extra_onward.wait()
    early.finish()


VMEM = pl.BlockSpec(memory_space=pltpu.VMEM)
ANYWHERE = pl.BlockSpec(memory_space=pl.ANY)


def attn_forward(residual, gains, attn_weights, trig, place, extra=None):
    length, width = residual.shape
    kv_width = 2 * KV_HEADS * HEAD_DIM
    shapes = (
        ((length, width), LOW),
        ((HEADS, length, 128), LOW),
        ((4, length, kv_width), LOW),
        ((KV_HEADS, 1, GROUP * length), FULL),
        ((length, HEADS * HEAD_DIM), LOW),
        ((length, width), FULL),
        ((length, width), LOW),
    )
    args = (residual, gains) + tuple(attn_weights) + (trig, place)
    in_specs, out_specs, hops = [VMEM] * 2 + [ANYWHERE] * 5 + [VMEM], (ANYWHERE,) * 3 + (VMEM,) * 4, 3
    if extra is not None:
        args, in_specs, out_specs = args + (extra,), in_specs + [ANYWHERE], out_specs + (ANYWHERE,)
        shapes = shapes + (((4,) + extra.shape, extra.dtype),)
        hops = 6
    return pl.pallas_call(
        functools.partial(attn_forward_kernel, extra is not None),
        out_shape=tuple(jax.ShapeDtypeStruct(*s) for s in shapes),
        in_specs=in_specs,
        out_specs=out_specs,
        scratch_shapes=[
            pltpu.VMEM((kv_width, width), LOW),
            pltpu.VMEM(attn_weights[2].shape, LOW),
            pltpu.VMEM(attn_weights[3].shape, LOW),
            pltpu.VMEM(trig.shape, FULL),
            pltpu.VMEM((length, width), LOW),
            pltpu.VMEM((HEADS, length, 128), LOW),
            pltpu.VMEM((4, length, kv_width), LOW),
            pltpu.SemaphoreType.DMA((2 * KV_HEADS,)),
            pltpu.SemaphoreType.DMA((3,)),
            pltpu.SemaphoreType.DMA((4,)),
            pltpu.VMEM((KV_HEADS, 1, GROUP * length), FULL),
            pltpu.VMEM((KV_HEADS, 1, GROUP * length), FULL),
            pltpu.VMEM((KV_HEADS, HEAD_DIM, GROUP * length), FULL),
            pltpu.SemaphoreType.DMA((hops,)),
            pltpu.SemaphoreType.DMA((hops,)),
        ],
        compiler_params=pltpu.CompilerParams(
            collective_id=1 if residual.dtype == FULL else 0, has_side_effects=True, vmem_limit_bytes=60 * 1024 * 1024
        ),
        cost_estimate=cost(25),
        name="attn_forward",
    )(*args)


def prepare(positions):
    length = positions.shape[0]
    frequency = THETA ** (-(jnp.arange(HEAD_DIM // 2, dtype=FULL) * 2.0 / HEAD_DIM))
    angles = positions.astype(FULL)[:, None] * frequency
    cos, sin = jnp.cos(angles), jnp.sin(angles)
    one, none = jnp.ones((length, HEAD_DIM), FULL), jnp.zeros((length, HEAD_DIM), FULL)
    trig = jnp.stack(
        [
            jnp.concatenate([cos, cos, cos, cos], 1),
            jnp.concatenate([-sin, sin, -sin, sin], 1),
            jnp.concatenate([cos, cos, one], 1),
            jnp.concatenate([-sin, sin, none], 1),
        ]
    )
    own = lax.axis_index("seq") * length + jnp.arange(length, dtype=jnp.int32)
    place = jnp.stack([jnp.tile(own - positions, GROUP), jnp.tile(own, GROUP)])
    place = jnp.pad(place, ((0, 6), (0, 0)))
    return trig, place


def ffn_forward_kernel(
    after_hbm, normed_ref, w_gate_hbm, w_up_hbm, w_down_hbm,
    res_out, rows_hbm, pre_hbm,
    after_buf, w_gate_buf, w_up_buf, w_down_buf, rows_out, pre_out, late_sem, early_sem,
    mate_send, mate_recv, x_send, x_recv, own_far,
    send_sem, recv_sem,
):
    weights = [
        Later(src, dst, late_sem.at[i])
        for i, (src, dst) in enumerate(
            ((w_gate_hbm, w_gate_buf), (w_up_hbm, w_up_buf), (w_down_hbm, w_down_buf), (after_hbm, after_buf))
        )
    ]
    early = Early(early_sem)
    seq, dp = lax.axis_index("seq"), lax.axis_index("dp")
    core = lax.rem(seq, 2)
    mate_seq, far_seq = seq + 1 - 2 * core, lax.rem(seq + 2, 4)
    far_mate = lax.rem(mate_seq + 2, 4)
    mate, x_mate = device(mate_seq, dp), device(far_seq, dp)
    length = after_hbm.shape[0]
    step = length // CHUNKS
    greet([mate, x_mate])
    part = lambda k: pl.ds(k * step, step)

    def hop(index, src, dst, target):
        return send(src, dst, send_sem.at[index], recv_sem.at[index], target)

    rows_out[seq] = normed_ref[...]
    own_rows = lambda k: rows_out.at[seq, part(k)]
    far_rows = lambda k: rows_out.at[far_seq, part(k)]
    to_x = [hop(k, own_rows(k), own_rows(k), x_mate) for k in range(CHUNKS)]
    to_mate = hop(CHUNKS, rows_out.at[seq], rows_out.at[seq], mate)
    base = CHUNKS + 1
    w_gate_ref, w_up_ref, w_down_ref, after_ref = (weight() for weight in weights)

    def ffn(quarter, rows):
        block = rows_out[quarter, rows]
        gate = dot(block, w_gate_ref[...])
        up = dot(block, w_up_ref[...])
        pre_out[quarter, rows, : gate.shape[1]] = gate.astype(LOW)
        pre_out[quarter, rows, gate.shape[1] :] = up.astype(LOW)
        hidden = (gate * jax.nn.sigmoid(gate) * up).astype(LOW)
        return dot(hidden, w_down_ref[...], NT)

    everything = pl.ds(0, length)
    res_out[...] = after_ref[...] + ffn(seq, everything)
    to_mate.wait()
    mate_send[0] = ffn(mate_seq, everything).astype(LOW)
    back = hop(base, mate_send.at[0], mate_recv.at[0], mate)
    onward = []
    for k in range(CHUNKS):
        to_x[k].wait()
        onward.append(hop(base + 1 + k, far_rows(k), far_rows(k), mate))
        own_far[part(k)] = ffn(far_seq, part(k))
        onward[k].wait()
        mate_send[1, part(k)] = ffn(far_mate, part(k)).astype(LOW)
        joint = hop(base + 1 + CHUNKS + k, mate_send.at[1, part(k)], mate_recv.at[1, part(k)], mate)
        joint.wait()
        x_send[part(k)] = (own_far[part(k)] + mate_recv[1, part(k)].astype(FULL)).astype(LOW)
        onward.append(
            hop(base + 1 + 2 * CHUNKS + k, x_send.at[part(k)], x_recv.at[part(k)], x_mate)
        )
        onward[k], onward[-1] = onward[-1], onward[k]
        onward.pop()
    early(rows_out, rows_hbm)
    early(pre_out, pre_hbm)
    back.wait()
    res_out[...] += mate_recv[0].astype(FULL)
    for k in range(CHUNKS):
        onward[k].wait()
        res_out[part(k)] += x_recv[part(k)].astype(FULL)
    early.finish()


def ffn_forward(after, normed_two, w_gate, w_up, w_down):
    length, width = after.shape
    shapes = (
        ((length, width), FULL),
        ((4, length, width), LOW),
        ((4, length, 2 * w_gate.shape[1]), LOW),
    )
    sems = 3 * CHUNKS + CHUNKS + 2
    return pl.pallas_call(
        ffn_forward_kernel,
        out_shape=tuple(jax.ShapeDtypeStruct(*s) for s in shapes),
        in_specs=[ANYWHERE, VMEM] + [ANYWHERE] * 3,
        out_specs=(VMEM, ANYWHERE, ANYWHERE),
        scratch_shapes=[
            pltpu.VMEM((length, width), FULL),
            pltpu.VMEM(w_gate.shape, LOW),
            pltpu.VMEM(w_up.shape, LOW),
            pltpu.VMEM(w_down.shape, LOW),
            pltpu.VMEM((4, length, width), LOW),
            pltpu.VMEM((4, length, 2 * w_gate.shape[1]), LOW),
            pltpu.SemaphoreType.DMA((4,)),
            pltpu.SemaphoreType.DMA((2,)),
            pltpu.VMEM((2, length, width), LOW),
            pltpu.VMEM((2, length, width), LOW),
            pltpu.VMEM((length, width), LOW),
            pltpu.VMEM((length, width), LOW),
            pltpu.VMEM((length, width), FULL),
            pltpu.SemaphoreType.DMA((sems,)),
            pltpu.SemaphoreType.DMA((sems,)),
        ],
        compiler_params=pltpu.CompilerParams(
            collective_id=2, has_side_effects=True, vmem_limit_bytes=60 * 1024 * 1024
        ),
        cost_estimate=cost(36),
        name="ffn_forward",
    )(after, normed_two, w_gate, w_up, w_down)


def norm_back(value, gain, grad):
    inverse = inverse_rms(value)
    weighted = grad * gain
    inner = jnp.mean(weighted * value, axis=-1, keepdims=True)
    back = inverse * weighted - value * (inverse * inverse * inverse) * inner
    return back, jnp.sum(grad * value * inverse, axis=0, keepdims=True)


def ffn_all_kernel(second, reduce, up_ref, own_ref, after_hbm, gains_ref, still_refs, gate_ref, upw_ref, down_ref, far_ref, *rest):
    y_part = prev_hbm = pre_hbm = None
    if second:
        result_out, rest = rest[0], rest[1:]
    else:
        prev_hbm, pre_hbm, *rest = rest
    grad_out, gain_out, weight_hbm, *rest = rest
    if reduce:
        y_part, *rest = rest
    (
        w_in, w_down, still_ref, moved, in_grad, in_temp, hidden, back, after_buf, prev_buf, pre_buf, weight_out,
        load_sem, late_sem, early_sem, send_sem, recv_sem,
    ) = rest
    early = Early(early_sem)
    after_ref = Later(after_hbm, after_buf, late_sem.at[0])
    prev_ref = None if second else Later(prev_hbm, prev_buf, late_sem.at[1])
    pre_ref = None if second else Later(pre_hbm, pre_buf, late_sem.at[2])
    hop = Hops(send_sem, recv_sem)
    seq, dp = lax.axis_index("seq"), lax.axis_index("dp")
    core = lax.rem(seq, 2)
    mate_seq, far_seq = seq + 1 - 2 * core, lax.rem(seq + 2, 4)
    far_mate = lax.rem(mate_seq + 2, 4)
    mate, x_mate = device(mate_seq, dp), device(far_seq, dp)
    length, width = up_ref.shape
    units = gate_ref.shape[1]
    whole = pl.ds(0, width)

    def slots(w, rows):
        return w_in.at[w, rows, :units], w_in.at[w, rows, units:], w_down.at[w, rows]

    loads = []

    def load(src, dst):
        loads.append(pltpu.make_async_copy(src, dst, load_sem.at[len(loads)]))
        loads[-1].start()

    for src, dst in zip((gate_ref, upw_ref, down_ref), slots(0, whole)):
        load(src, dst)
    moved[seq] = own_ref[...].astype(LOW)
    at = 0
    for ref in still_refs:
        load(ref, still_ref.at[:, pl.ds(at, ref.shape[1])])
        at += ref.shape[1]
    far_from = len(loads)
    for d in range(SHARES):
        at = min(d * PIECE, width - PIECE)
        rows = min(PIECE, width - PIECE - at) if d == SHARES - 2 else PIECE
        for i, dst in enumerate(slots(2, pl.ds(at, rows))):
            load(far_ref.at[d, pl.ds(i * PIECE, rows)], dst)
    y_mate = device(seq, dp + 1 - 2 * lax.rem(dp, 2))
    greet([mate, x_mate] + ([y_mate] if reduce else []))
    mine, theirs = moved.at[seq], moved.at[far_seq]
    to_x = hop(mine, mine, x_mate)
    to_mate = hop(mine, mine, mate)
    beside = [hop(src, dst, mate) for src, dst in zip((gate_ref, upw_ref, down_ref), slots(1, whole))]
    rows_ref, low_ref = (moved, still_ref) if second else (still_ref, moved)

    def halves(quarter, w, grads, known=False):
        both = pre_buf[quarter].astype(FULL) if known else dot(rows_ref[quarter], w_in[w])
        gate, up = both[:, :units], both[:, units:]
        bend = jax.nn.sigmoid(gate)
        silu = gate * bend
        hidden_grad = dot(low_ref[quarter], w_down[w])
        grads[:, :units] = (hidden_grad * up * bend * (1.0 + gate * (1.0 - bend))).astype(LOW)
        grads[:, units:] = (hidden_grad * silu).astype(LOW)
        return (silu * up).astype(LOW)

    def local(w):
        act = halves(seq, w, in_temp)
        back[...] += dot(in_temp[...], w_in[w], NT)
        if second:
            grad_out[...] += dot(act, w_down[w], NT)

    for copy in loads[:far_from]:
        copy.wait()
    if not second:
        pre_ref()
    hidden[seq] = halves(seq, 0, in_grad.at[seq], not second)
    if second:
        back[...] = dot(in_grad[seq], w_in[0], NT)
        grad_out[...] = after_ref()[...] + dot(hidden[seq], w_down[0], NT)
    for copy in loads[far_from:]:
        copy.wait()
    across = [hop(w_in.at[2], w_in.at[3], mate), hop(w_down.at[2], w_down.at[3], mate)]
    for copy in beside:
        copy.wait()

    if second:

        @pl.loop(1, 4)
        def _(w):
            @pl.when(w == 3)
            def _():
                for copy in across:
                    copy.wait()

            local(w)

    else:
        back[...] = jnp.zeros_like(back)
        local(1)

    to_mate.wait()
    to_x.wait()
    onward = hop(theirs, theirs, mate)

    @pl.loop(0, 3)
    def _(i):
        @pl.when(i == 2)
        def _():
            onward.wait()

        quarter = jnp.where(i == 0, mate_seq, jnp.where(i == 1, far_seq, far_mate))
        hidden[quarter] = halves(quarter, 0, in_grad.at[quarter], not second)

    flat = lambda ref: ref[...].reshape(4 * length, ref.shape[2])
    share = width // SHARES

    def finish(i, term):
        for j in range(SHARES):
            rows = term[j * share : (j + 1) * share]
            if prev_ref is not None:
                rows = rows + prev_ref()[i, j // 2, j % 2].astype(FULL)
            weight_out[i, j // 2, j % 2] = rows.astype(LOW)
        early(weight_out.at[i], weight_hbm.at[i])

    def half(columns):
        return in_grad[:, :, columns].reshape(4 * length, units)

    if second:
        both = dot(flat(rows_ref), flat(in_grad), TN)
        finish(0, both[:, :units])
        finish(1, both[:, units:])
    else:
        finish(0, dot(flat(rows_ref), half(slice(0, units)), TN))
        if reduce:
            first_y = hop(weight_out.at[0, :, 1 - lax.rem(dp, 2)], y_part, y_mate)
        finish(1, dot(flat(rows_ref), half(slice(units, 2 * units)), TN))
        back[...] += dot(in_grad[seq], w_in[0], NT)
        for copy in across:
            copy.wait()

        @pl.loop(2, 4)
        def _(w):
            local(w)

    finish(2, dot(flat(low_ref), flat(hidden), TN))
    if second:
        result_out[...] = grad_out[...].astype(LOW)
    sent_back, gain_term = norm_back(after_ref()[...], gains_ref[1:2, :], back[...])
    grad_out[...] = up_ref[...].astype(FULL) + sent_back
    gain_out[...] = jnp.broadcast_to(gain_term, gain_out.shape)
    if reduce:
        first_y.wait()
    early.finish()


def ffn_all_call(stills, second, reduce, *refs):
    refs = refs if second else refs[:1] + refs
    return ffn_all_kernel(second, reduce, *refs[:4], refs[4 : 4 + stills], *refs[4 + stills :])


def ffn_all(second, reduce, upstream, own, after, gains, stills, weights, far, prev=None, pre=None):
    length, width = after.shape
    units = weights[0].shape[1]
    share = width // SHARES
    grads = (3, SHARES // 2, 2, share, units)
    shapes = (
        ((length, width), FULL),
        ((8, width), FULL),
        (grads, LOW),
    )
    if second:
        shapes = (((length, width), LOW),) + shapes
    if reduce:
        shapes = shapes + (((SHARES // 2, share, units), LOW),)
    args = (after, gains) + tuple(stills) + tuple(weights) + (far,)
    specs = [ANYWHERE, VMEM] + [ANYWHERE] * (len(stills) + 4)
    if second:
        args, specs = (upstream, own) + args, [VMEM, VMEM] + specs
    else:
        args, specs = (upstream,) + args, [VMEM] + specs
        args, specs = args + (prev, pre), specs + [ANYWHERE] * 2
    return pl.pallas_call(
        functools.partial(ffn_all_call, len(stills), second, reduce),
        out_shape=tuple(jax.ShapeDtypeStruct(*s) for s in shapes),
        in_specs=specs,
        out_specs=tuple(ANYWHERE if s[0] == grads else VMEM for s in shapes),
        scratch_shapes=[
            pltpu.VMEM((4, width, 2 * units), LOW),
            pltpu.VMEM((4, width, units), LOW),
            pltpu.VMEM((4, length, width), LOW),
            pltpu.VMEM((4, length, width), LOW),
            pltpu.VMEM((4, length, 2 * units), LOW),
            pltpu.VMEM((length, 2 * units), LOW),
            pltpu.VMEM((4, length, units), LOW),
            pltpu.VMEM((length, width), FULL),
            pltpu.VMEM((length, width), FULL),
            pltpu.VMEM((1, 1, 2, 8, 128) if second else grads, LOW),
            pltpu.VMEM((1, 8, 128) if second else pre.shape, LOW),
            pltpu.VMEM(grads, LOW),
            pltpu.SemaphoreType.DMA((3 + len(stills) + 3 * SHARES,)),
            pltpu.SemaphoreType.DMA((3,)),
            pltpu.SemaphoreType.DMA((3,)),
            pltpu.SemaphoreType.DMA((9,)),
            pltpu.SemaphoreType.DMA((9,)),
        ],
        compiler_params=pltpu.CompilerParams(
            collective_id=3 if second else 4, has_side_effects=True, vmem_limit_bytes=60 * 1024 * 1024
        ),
        cost_estimate=cost(30),
        name="ffn_second" if second else "ffn_first_backward",
    )(*args)


def attn_backward_kernel(
    last, after_grad_ref, w_out_ref, mixed_ref, gains_ref, place_ref, log_ref, q_hbm, kv_hbm, trig_hbm,
    res_hbm, normed_hbm, w_key_hbm, w_value_hbm, w_query_hbm, *rest
):
    if last:
        prev, ffn_ref, first_hbm, gain_ref = rest[:3], rest[3], rest[4], rest[5]
        grad_out, gain_out, ffn_out, share_outs = rest[6], rest[7], rest[8], rest[9:12]
        rest = rest[12:]
    else:
        prev = (None, None, None)
        grad_out, gain_out = rest[:2]
        part_hbms = rest[2:5]
        rest = rest[5:]
    q_buf, kv_buf, trig_buf, res_buf, normed_buf, w_kv_buf, w_query_buf, pair_sem, late_sem, early_sem, *rest = rest
    late = iter(late_sem.at[i] for i in range(11))
    q_later, kv_later = Later(q_hbm, q_buf, next(late)), Later(kv_hbm, kv_buf, next(late))
    mixed_grad, delta, kv_grad, query_grad, back, grad_send, grad_recv, send_sem, recv_sem = rest[:9]
    hop = Hops(send_sem, recv_sem)
    seq, dp = lax.axis_index("seq"), lax.axis_index("dp")
    core, chip_x = lax.rem(seq, 2), lax.div(seq, 2)
    mate_seq, far_seq = seq + 1 - 2 * core, lax.rem(seq + 2, 4)
    far_mate = lax.rem(mate_seq + 2, 4)
    mate, x_mate = device(mate_seq, dp), device(far_seq, dp)
    length, width = res_hbm.shape
    stacked = GROUP * length
    kv_width = 2 * KV_HEADS * HEAD_DIM
    parts = rest[9:12]
    if last:
        f_own, f_y_recv, f_a_send, f_a_recv, f_b_send, f_b_recv, gain_recv = rest[12:19]
        prev_bufs = rest[19:22]
        buffers = [rest[22 + 10 * i : 32 + 10 * i] for i in range(3)]
        row_y, row_z = lax.rem(dp, 2), lax.div(dp, 2)
        low_z, high_z = lax.rem(row_z, 2), lax.div(row_z, 2)
        y_mate = device(seq, dp + 1 - 2 * row_y)
        near_z = device(seq, dp + 2 - 4 * low_z)
        far_z = device(seq, dp + 4 - 8 * high_z)
        greet([mate, x_mate, y_mate, near_z, far_z])
        f_y = [hop(ffn_ref.at[m, :, 1 - row_y], f_y_recv.at[m], y_mate) for m in (1, 2)]
        first_y = Later(first_hbm, f_y_recv.at[0], next(late))
        own_shares = Later(ffn_ref.at[:, :, row_y], f_own, next(late))
        prev = [Later(src, dst, next(late)) for src, dst in zip(prev, prev_bufs)]
    else:
        greet([mate, x_mate])
    early = Early(early_sem)
    trig = Later(trig_hbm, trig_buf, next(late))
    normed_ref = Later(normed_hbm, normed_buf, next(late))
    w_query = Later(w_query_hbm, w_query_buf, next(late))
    w_kv = LaterPairs(w_key_hbm, w_value_hbm, w_kv_buf, pair_sem)
    res_ref = Later(res_hbm, res_buf, next(late))

    def near_start(load, a_send, a_recv):
        for h in range(2):
            a_send[h] = load(2 * h + 1 - low_z).astype(LOW)
        return hop(a_send, a_recv, near_z)

    def far_start(load, a_recv, b_send, b_recv, copy):
        copy.wait()
        b_send[...] = (load(2 - 2 * high_z + low_z) + a_recv[1 - high_z].astype(FULL)).astype(LOW)
        return hop(b_send, b_recv, far_z)

    def z_total(load, a_recv, b_recv, copy):
        copy.wait()
        return load(row_z) + a_recv[high_z].astype(FULL) + b_recv[...].astype(FULL)

    def f_load(m):
        return lambda z: own_shares()[m, z].astype(FULL) + f_y_recv[m, z].astype(FULL)

    def f_near(m):
        own_shares()
        if m == 0:
            first_y()
        else:
            f_y[m - 1].wait()
        return near_start(f_load(m), f_a_send.at[m], f_a_recv.at[m])

    def f_far(m, copy):
        return far_start(f_load(m), f_a_recv.at[m], f_b_send.at[m], f_b_recv.at[m], copy)

    def f_finish(m, copy):
        ffn_out[m] = z_total(f_load(m), f_a_recv.at[m], f_b_recv.at[m], copy)

    quarter = lambda x, c: pl.ds(pl.multiple_of(64 * x + ROWS_PAD * c, ROWS_PAD), ROWS_PAD)

    def core_start(i):
        core_recv = buffers[i][0]
        return [hop(parts[i].at[:, quarter(x, 1 - core)], core_recv.at[x], mate) for x in range(2)]

    def x_start(i, copies):
        core_recv, x_send, x_recv = buffers[i][:3]
        for copy in copies:
            copy.wait()
        joint = parts[i][:, quarter(1 - chip_x, core)].astype(FULL) + core_recv[1 - chip_x].astype(FULL)
        x_send[...] = joint.astype(LOW)
        return hop(x_send, x_recv, x_mate)

    def y_start(i, copy):
        core_recv, x_send, x_recv, own, y_recv = buffers[i][:5]
        joint = parts[i][:, quarter(chip_x, core)].astype(FULL) + core_recv[chip_x].astype(FULL)
        copy.wait()
        own[...] = (joint + x_recv[...].astype(FULL)).astype(LOW).reshape(own.shape)
        return hop(own.at[:, 1 - row_y], y_recv, y_mate)

    def part_load(i):
        own, y_recv = buffers[i][3:5]
        return lambda z: own[z, row_y].astype(FULL) + y_recv[z].astype(FULL)

    def z_start(i, copy):
        copy.wait()
        return near_start(part_load(i), *buffers[i][5:7])

    def z_next(i, copy):
        return far_start(part_load(i), *buffers[i][6:9], copy)

    def share_start(i, copy):
        gathered = buffers[i][9]
        gathered[seq] = z_total(part_load(i), buffers[i][6], buffers[i][8], copy).astype(LOW)
        mine = gathered.at[seq]
        return hop(mine, mine, x_mate), hop(mine, mine, mate)

    def share_pass(i, copies):
        gathered = buffers[i][9]
        copies[0].wait()
        theirs = gathered.at[far_seq]
        return hop(theirs, theirs, mate), copies[1]

    def share_finish(i, copies):
        gathered = buffers[i][9]
        for copy in copies:
            copy.wait()
        for s in range(4):
            share_outs[i][s * ROWS_PAD : (s + 1) * ROWS_PAD] = gathered[s].astype(FULL)

    def weight(i, left, right):
        term = dot(left, right, TN)
        share = width // SHARES
        for j in range(SHARES):
            rows = term[j * share : (j + 1) * share]
            if prev[i] is not None:
                rows = rows + prev[i]()[j, :share].astype(FULL)
            parts[i][j, :share] = rows.astype(LOW)
        if not last:
            early(parts[i], part_hbms[i])

    low_grad = after_grad_ref[...].astype(LOW)
    mixed_back = dot(low_grad, w_out_ref[...], NT)
    lane = lax.broadcasted_iota(jnp.int32, (length, 128), 1)
    for pair in range((HEADS + 1) // 2):
        span = min(128, HEADS * HEAD_DIM - pair * 128)
        part = mixed_back[:, pair * 128 : pair * 128 + span]
        if span < 128:
            part = jnp.concatenate([part, part], axis=1)
        else:
            mixed_grad[2 * pair + 1] = jnp.where(lane >= HEAD_DIM, part, 0.0).astype(LOW)
        mixed_grad[2 * pair] = jnp.where(lane >= HEAD_DIM, pltpu.roll(part, 64, 1), 0.0).astype(LOW)
    product = mixed_back.astype(LOW).astype(FULL) * mixed_ref[...].astype(FULL)
    high = product.astype(LOW)
    rest_low = (product - high.astype(FULL)).astype(LOW)
    head = lax.broadcasted_iota(jnp.int32, (16, HEADS * HEAD_DIM), 0)
    column = lax.broadcasted_iota(jnp.int32, (16, HEADS * HEAD_DIM), 1)
    pick = jnp.where(lax.div(column, HEAD_DIM) == head, 1.0, 0.0).astype(LOW)
    sums = dot(pick, high, NT) + dot(pick, rest_low, NT)
    for g in range(KV_HEADS):
        delta[g] = jnp.concatenate([sums[3 * g + i : 3 * g + i + 1] for i in range(GROUP)], axis=1)
    query_grad[...] = jnp.zeros_like(query_grad)
    weight(0, mixed_ref[...], low_grad)
    if last:
        o_core = core_start(0)
        f_z = [f_near(0)]

    start, place = place_ref[0:1, :], place_ref[1:2, :]
    q_ref, kv_ref = q_later(), kv_later()

    def attend(block, g, diagonal):
        columns = pl.ds(pl.multiple_of(g * 128, 128), 128)
        kv_g = kv_ref[block, :, columns]
        q_g = q_ref[pl.ds(3 * g, 3)].reshape(stacked, 128)
        out_g = mixed_grad[pl.ds(3 * g, 3)].reshape(stacked, 128)
        scores = dot(kv_g, q_g, NT)
        key = lax.broadcasted_iota(jnp.int32, (length, stacked), 0) + block * length
        allowed = key >= start
        if diagonal:
            allowed = allowed & (key <= place)
        weights = jnp.where(allowed, jnp.exp(scores - log_ref[g]), 0.0)
        probs_grad = dot(kv_g, out_g, NT)
        score_grad = (weights * (probs_grad - delta[g])).astype(LOW)
        kv_grad[block, :, columns] = dot(weights.astype(LOW), out_g) + dot(score_grad, q_g)
        query_grad[g] += dot(kv_g, score_grad, TN)[:HEAD_DIM]

    def attend_all(block, condition, diagonal=False):
        @pl.when(condition)
        def _():
            @pl.loop(0, KV_HEADS)
            def _(g):
                attend(block, g, diagonal)

        if not diagonal:
            @pl.when(jnp.logical_not(condition))
            def _():
                kv_grad[block] = jnp.zeros_like(kv_grad[block])

    right = chip_x == 1
    attend_all(far_mate, right)
    grad_send[0] = kv_grad[far_mate].astype(LOW)
    joint = hop(grad_send.at[0], grad_recv.at[0], mate)
    attend_all(far_seq, right)
    joint.wait()
    grad_send[1] = (kv_grad[far_seq] + grad_recv[0].astype(FULL)).astype(LOW)
    across = hop(grad_send.at[1], grad_recv.at[1], x_mate)
    if last:
        o_x = x_start(0, o_core)
    attend_all(mate_seq, core == 1)
    grad_send[2] = kv_grad[mate_seq].astype(LOW)
    beside = hop(grad_send.at[2], grad_recv.at[2], mate)
    if last:
        f_z[0] = f_far(0, f_z[0])
        f_z.append(f_near(1))
    attend_all(seq, seq >= 0, True)

    trig_ref = trig()
    heads = []
    for g in range(KV_HEADS):
        turned = query_grad[g].T * SCALE
        heads += [turned[i * length : (i + 1) * length] for i in range(GROUP)]
    for pair in range((HEADS + 1) // 2):
        part = jnp.concatenate([heads[2 * pair], heads[min(2 * pair + 1, HEADS - 1)]], axis=1)
        turned = (part * trig_ref[0] - swap_halves(part) * trig_ref[1]).astype(LOW)
        at = kv_width + pair * 128
        stop = min(at + 128, kv_width + width)
        back[:, at:stop] = turned[:, : stop - at]
    weight(1, normed_ref()[...], back[:, kv_width:])
    if last:
        q_core = core_start(1)
        o_y = y_start(0, o_x)
    normed_grad = dot(back[:, kv_width:], w_query()[...], NT)
    if last:
        q_x = x_start(1, q_core)

    across.wait()
    beside.wait()
    own = kv_grad[seq] + grad_recv[1].astype(FULL) + grad_recv[2].astype(FULL)
    for g in range(KV_HEADS):
        part = own[:, g * 128 : (g + 1) * 128]
        back[:, g * 128 : (g + 1) * 128] = (part * trig_ref[2] - swap_halves(part) * trig_ref[3]).astype(LOW)
    weight(2, normed_ref()[...], back[:, :kv_width])
    if last:
        kv_core = core_start(2)
        f_z[1] = f_far(1, f_z[1])
        f_z.append(f_near(2))
        kv_x = x_start(2, kv_core)
    normed_grad = normed_grad + dot(back[:, :kv_width], w_kv()[...])
    sent_back, gain_term = norm_back(res_ref()[...].astype(FULL), gains_ref[0:1, :], normed_grad)
    grad_out[...] = after_grad_ref[...] + sent_back
    if not last:
        gain_out[...] = jnp.broadcast_to(gain_term, gain_out.shape)
        early.finish()
        return

    row = lax.broadcasted_iota(jnp.int32, gain_out.shape, 0)
    gain_out[...] = gain_ref[...] + jnp.where(row == 0, gain_term, 0.0)
    partners = [mate, x_mate, y_mate, near_z, far_z]
    gain_hop = lambda n: hop(gain_out, gain_recv.at[n], partners[n])

    def gain_add(n, copy):
        copy.wait()
        gain_out[...] += gain_recv[n]

    gain_copy = gain_hop(0)
    f_finish(0, f_z[0])
    o_z = z_start(0, o_y)
    gain_add(0, gain_copy)
    gain_copy = gain_hop(1)
    q_y = y_start(1, q_x)
    f_z[2] = f_far(2, f_z[2])
    f_finish(1, f_z[1])
    o_z = z_next(0, o_z)
    gain_add(1, gain_copy)
    gain_copy = gain_hop(2)
    kv_y = y_start(2, kv_x)
    q_z = z_start(1, q_y)
    gain_add(2, gain_copy)
    gain_copy = gain_hop(3)
    o_s = share_start(0, o_z)
    kv_z = z_start(2, kv_y)
    q_z = z_next(1, q_z)
    gain_add(3, gain_copy)
    gain_copy = gain_hop(4)
    f_finish(2, f_z[2])
    o_s = share_pass(0, o_s)
    kv_z = z_next(2, kv_z)
    q_s = share_start(1, q_z)
    gain_add(4, gain_copy)
    kv_s = share_start(2, kv_z)
    q_s = share_pass(1, q_s)
    share_finish(0, o_s)
    kv_s = share_pass(2, kv_s)
    share_finish(1, q_s)
    share_finish(2, kv_s)


def attn_backward(after_grad, residual, normed, gains, q, kv, log_total, mixed, attn_weights, trig, place, final=None):
    length, width = residual.shape
    kv_width = 2 * KV_HEADS * HEAD_DIM
    last = final is not None
    key_t, value_t, w_query, w_out = attn_weights
    args = (after_grad, w_out, mixed, gains, place, log_total, q, kv, trig, residual, normed, key_t, value_t, w_query)
    specs = [VMEM] * 6 + [ANYWHERE] * 8
    out_specs = (VMEM, VMEM)
    shapes = (((length, width), FULL), ((8, width), FULL))
    sizes = (width, width, kv_width)
    part_shapes = [((SHARES, 4 * ROWS_PAD, c), LOW) for c in sizes]
    scratch = [
        pltpu.VMEM(q.shape, LOW),
        pltpu.VMEM(kv.shape, LOW),
        pltpu.VMEM(trig.shape, FULL),
        pltpu.VMEM((length, width), residual.dtype),
        pltpu.VMEM((length, width), LOW),
        pltpu.VMEM((kv_width, width), LOW),
        pltpu.VMEM(w_query.shape, LOW),
        pltpu.SemaphoreType.DMA((2 * KV_HEADS,)),
        pltpu.SemaphoreType.DMA((11,)),
        pltpu.SemaphoreType.DMA((3,)),
        pltpu.VMEM((HEADS, length, 128), LOW),
        pltpu.VMEM((KV_HEADS, 1, GROUP * length), FULL),
        pltpu.VMEM((4, length, kv_width), FULL),
        pltpu.VMEM((KV_HEADS, HEAD_DIM, GROUP * length), FULL),
        pltpu.VMEM((length, kv_width + width), LOW),
        pltpu.VMEM((3, length, kv_width), LOW),
        pltpu.VMEM((3, length, kv_width), LOW),
    ]
    hops = 3
    if last:
        share, hidden = final[3].shape[3:]
        args = args + tuple(final)
        specs = specs + [ANYWHERE] * 5 + [VMEM]
        shapes = shapes + (((3, share, hidden), FULL),) + tuple(((4 * ROWS_PAD, c), FULL) for c in sizes)
        hops = 3 + 2 + 6 + 5 + 3 * (2 + 1 + 1 + 2 + 3)
        scratch += [pltpu.SemaphoreType.DMA((hops,))] * 2
        out_specs = (VMEM,) * len(shapes)
        scratch += [pltpu.VMEM(*s) for s in part_shapes]
        scratch += [
            pltpu.VMEM((3, 4, share, hidden), LOW),
            pltpu.VMEM((3, 4, share, hidden), LOW),
            pltpu.VMEM((3, 2, share, hidden), LOW),
            pltpu.VMEM((3, 2, share, hidden), LOW),
            pltpu.VMEM((3, share, hidden), LOW),
            pltpu.VMEM((3, share, hidden), LOW),
            pltpu.VMEM((5, 8, width), FULL),
        ]
        scratch += [pltpu.VMEM(*s) for s in part_shapes]
        for c in sizes:
            scratch += [
                pltpu.VMEM((2, SHARES, ROWS_PAD, c), LOW),
                pltpu.VMEM((SHARES, ROWS_PAD, c), LOW),
                pltpu.VMEM((SHARES, ROWS_PAD, c), LOW),
                pltpu.VMEM((4, 2, ROWS_PAD, c), LOW),
                pltpu.VMEM((4, ROWS_PAD, c), LOW),
                pltpu.VMEM((2, ROWS_PAD, c), LOW),
                pltpu.VMEM((2, ROWS_PAD, c), LOW),
                pltpu.VMEM((ROWS_PAD, c), LOW),
                pltpu.VMEM((ROWS_PAD, c), LOW),
                pltpu.VMEM((4, ROWS_PAD, c), LOW),
            ]
    else:
        shapes, out_specs = shapes + tuple(part_shapes), out_specs + (ANYWHERE,) * 3
        scratch += [pltpu.SemaphoreType.DMA((hops,))] * 2
        scratch += [pltpu.VMEM(*s) for s in part_shapes]
    return pl.pallas_call(
        functools.partial(attn_backward_kernel, last),
        out_shape=tuple(jax.ShapeDtypeStruct(*s) for s in shapes),
        in_specs=specs,
        out_specs=out_specs,
        scratch_shapes=scratch,
        compiler_params=pltpu.CompilerParams(
            collective_id=6 if last else 5, has_side_effects=True, vmem_limit_bytes=60 * 1024 * 1024
        ),
        cost_estimate=cost(95 if last else 40),
        name="attn_backward_last" if last else "attn_backward",
    )(*args)


def split_pairs(grads):
    rows = grads.shape[0]
    pairs = grads.reshape(rows, KV_HEADS, 2, HEAD_DIM)
    return pairs[:, :, 0].reshape(rows, -1), pairs[:, :, 1].reshape(rows, -1)


def on_device(
    tokens,
    seg_ids,
    positions,
    attn_gain,
    w_query,
    w_key,
    w_value,
    w_out,
    ffn_gain,
    w_gate,
    w_up,
    w_down,
    cotangent,
):
    width = tokens.shape[2]
    trig, place = prepare(positions[0])
    attn_weights = (w_key.T, w_value.T, w_query, w_out)
    gains = jnp.pad(jnp.stack([attn_gain, ffn_gain]), ((0, 6), (0, 0)))
    whole = lax.axis_size("dp") != SHARES
    share = width // SHARES
    own_weights = (w_gate, w_up, w_down.T)

    def over_x(value):
        return lax.ppermute(value, "seq", [(s, (s + 2) % 4) for s in range(4)])

    def over_rows_piece(value, d):
        return lax.dynamic_slice_in_dim(value, jnp.minimum(d * PIECE, width - PIECE), PIECE, axis=0)

    if whole:
        theirs = [over_x(w) for w in own_weights]
        far = jnp.stack([jnp.concatenate([over_rows_piece(w, d) for w in theirs]) for d in range(SHARES)])
    else:
        piece = jnp.concatenate([over_rows_piece(w, lax.axis_index("dp")) for w in own_weights])
        far = lax.all_gather(over_x(piece), "dp", axis=0)

    half = cotangent.shape[1] // 2
    first = attn_forward(tokens[0], gains, attn_weights, trig, place, cotangent[0, :half])
    residual, rows_all, pre_all = ffn_forward(first[5], first[6], *own_weights)
    second = attn_forward(residual, gains, attn_weights, trig, place, cotangent[0, half:])
    output, after_grad, ffn_gain_term, ffn_grads = ffn_all(
        True, False, cotangent[0], second[6], second[5], gains, (first[7], second[7]), own_weights, far
    )

    def attn_args(after_grad, residual, kept):
        normed, q, kv, log_total, mixed = kept[:5]
        return (after_grad, residual, normed, gains, q, kv, log_total, mixed, attn_weights, trig, place)

    upstream, attn_gain_term, *parts = attn_backward(*attn_args(after_grad, residual, second))
    gain_grads = jnp.stack([attn_gain_term[0], ffn_gain_term[0]])
    after_grad, ffn_gain_term, ffn_grads, *first_y = ffn_all(
        False, not whole, upstream, None, first[5], gains, (rows_all,), own_weights, far, ffn_grads, pre_all
    )
    args = attn_args(after_grad, tokens[0], first)
    if whole:
        upstream, attn_gain_term, *terms = attn_backward(*args)
        gain_grads = gain_grads + jnp.stack([attn_gain_term[0], ffn_gain_term[0]])
        parts = [part.astype(FULL) + term.astype(FULL) for part, term in zip(parts, terms)]
    else:
        gain_grads = gain_grads + jnp.stack([jnp.zeros_like(attn_gain), ffn_gain_term[0]])
        final = (*parts, ffn_grads, *first_y, jnp.pad(gain_grads, ((0, 6), (0, 0))))
        upstream, gain_all, ffn_share, *shares = attn_backward(*args, final)
    if whole:

        def over_rows(grads, dim):
            grads = lax.psum_scatter(grads.astype(LOW), "dp", scatter_dimension=dim, tiled=True)
            return grads.astype(FULL)

        def over_all(grads, dim):
            return lax.psum(over_rows(grads, dim).astype(LOW), "seq").astype(FULL)

        shares = [over_all(part[:, :share].reshape(width, -1), 0) for part in parts]
        ffn_share = over_rows(ffn_grads.reshape(3, width, -1), 1)
        own_gains = over_all(gain_grads, 1)
    else:
        shares = [part[:share] for part in shares]
        own_gains = lax.dynamic_slice_in_dim(gain_all, lax.axis_index("dp") * share, share, axis=1)
    key_share, value_share = split_pairs(shares[2])
    return (
        output[None],
        upstream[None],
        own_gains[0],
        shares[1],
        key_share,
        value_share,
        shares[0],
        own_gains[1],
        ffn_share[0],
        ffn_share[1],
        ffn_share[2].T,
    )


def solution(mesh):
    in_specs = (
        P("dp", "seq", None),
        P("dp", "seq"),
        P("dp", "seq"),
        P(),
        P(),
        P(),
        P(),
        P(),
        P(),
        P(None, "seq"),
        P(None, "seq"),
        P("seq", None),
        P("dp", "seq", None),
    )
    out_specs = (
        P("dp", "seq", None),
        P("dp", "seq", None),
        P("dp"),
        P("dp", None),
        P("dp", None),
        P("dp", None),
        P("dp", None),
        P("dp"),
        P("dp", "seq"),
        P("dp", "seq"),
        P("seq", "dp"),
    )
    return jax.shard_map(
        on_device, mesh=mesh, in_specs=in_specs, out_specs=out_specs, check_vma=False
    )
```

```python
import functools

import jax
import jax.numpy as jnp
from jax import lax
from jax.experimental import pallas as pl
from jax.experimental.pallas import tpu as pltpu
from jax.sharding import PartitionSpec as P

MESH_ID = pl.DeviceIdType.MESH
HEADS = 15
KV_HEADS = 5
GROUP = 3
HEAD_DIM = 64
EPSILON = 1e-05
THETA = 10000.0
CHUNKS = 2
SHARES = 8
ROWS_PAD = 32
PIECE = 128
MASKED = -1e30
LOW = jnp.bfloat16
FULL = jnp.float32
SCALE = HEAD_DIM ** (-0.5)
NT = (((1,), (1,)), ((), ()))
TN = (((0,), (0,)), ((), ()))


def device(seq_pos, dp_pos):
    return {"seq": seq_pos, "dp": dp_pos}


def send(src, dst, send_sem, recv_sem, target, start=True):
    copy = pltpu.make_async_remote_copy(
        src_ref=src,
        dst_ref=dst,
        send_sem=send_sem,
        recv_sem=recv_sem,
        device_id=target,
        device_id_type=MESH_ID,
    )
    if start:
        copy.start()
    return copy


class Hops:
    def __init__(self, send_sem, recv_sem):
        self.send_sem, self.recv_sem, self.used = send_sem, recv_sem, 0

    def __call__(self, src, dst, target, start=True):
        index, self.used = self.used, self.used + 1
        return send(src, dst, self.send_sem.at[index], self.recv_sem.at[index], target, start)


class Later:
    def __init__(self, src, dst, sem):
        self.copy, self.dst, self.waited = pltpu.make_async_copy(src, dst, sem), dst, False
        self.copy.start()

    def __call__(self):
        if not self.waited:
            self.copy.wait()
            self.waited = True
        return self.dst


class Early:
    def __init__(self, sem):
        self.sem, self.copies = sem, []

    def __call__(self, src, dst, start=True):
        self.copies.append(pltpu.make_async_copy(src, dst, self.sem.at[len(self.copies)]))
        if start:
            self.copies[-1].start()
        return self.copies[-1]

    def finish(self):
        for copy in self.copies:
            copy.wait()


class LaterPairs:
    def __init__(self, key_hbm, value_hbm, dst, sem):
        self.copies, self.dst = [], dst
        for h in range(2 * KV_HEADS):
            src = (key_hbm, value_hbm)[h % 2].at[pl.ds(h // 2 * HEAD_DIM, HEAD_DIM)]
            self.copies.append(pltpu.make_async_copy(src, dst.at[pl.ds(h * HEAD_DIM, HEAD_DIM)], sem.at[h]))
            self.copies[-1].start()

    def __call__(self):
        for copy in self.copies:
            copy.wait()
        self.copies = []
        return self.dst


def greet(targets):
    barrier = pltpu.get_barrier_semaphore()
    for target in targets:
        pl.semaphore_signal(barrier, inc=1, device_id=target, device_id_type=MESH_ID)
    pl.semaphore_wait(barrier, len(targets))


def dot(left, right, dims=None):
    if dims is None:
        return jnp.dot(left, right, preferred_element_type=FULL)
    return lax.dot_general(left, right, dims, preferred_element_type=FULL)


def cost(microseconds):
    return pl.CostEstimate(flops=int(microseconds * 1.15e9), bytes_accessed=1 << 20, transcendentals=0)


def inverse_rms(value):
    return lax.rsqrt(jnp.mean(value * value, axis=-1, keepdims=True) + EPSILON)


def swap_halves(value):
    lane = lax.broadcasted_iota(jnp.int32, value.shape, 1)
    first = (lane & (HEAD_DIM // 2)) == 0
    return jnp.where(first, pltpu.roll(value, 96, 1), pltpu.roll(value, 32, 1))


def attn_forward_kernel(
    extra, res_ref, gains_ref, w_key_hbm, w_value_hbm, w_query_hbm, w_out_hbm, trig_hbm, place_ref, *rest
):
    if extra:
        extra_ref, extra_out = rest[0], rest[8]
        rest = rest[1:8] + rest[9:]
    normed_hbm, q_hbm, kv_hbm, log_out, mixed_out, after_out, normed_two_out, *rest = rest
    w_kv_buf, w_query_buf, w_out_buf, trig_buf, normed_out, q_out, kv_out, pair_sem, late_sem, early_sem, *rest = rest
    peak, total, acc, send_sem, recv_sem, *rest = rest
    w_kv = LaterPairs(w_key_hbm, w_value_hbm, w_kv_buf, pair_sem)
    trig = Later(trig_hbm, trig_buf, late_sem.at[0])
    w_query = Later(w_query_hbm, w_query_buf, late_sem.at[1])
    w_out = Later(w_out_hbm, w_out_buf, late_sem.at[2])
    early = Early(early_sem)
    seq, dp = lax.axis_index("seq"), lax.axis_index("dp")
    core, chip_x = lax.rem(seq, 2), lax.div(seq, 2)
    mate_seq, far_seq = seq + 1 - 2 * core, lax.rem(seq + 2, 4)
    mate, x_mate = device(mate_seq, dp), device(far_seq, dp)
    length = res_ref.shape[0]
    stacked = GROUP * length
    residual = res_ref[...].astype(FULL)
    normed_out[...] = (residual * inverse_rms(residual) * gains_ref[0:1, :]).astype(LOW)
    early(normed_out, normed_hbm)
    kv_width = 2 * KV_HEADS * HEAD_DIM
    kv_pre = dot(normed_out[...], w_kv()[...], NT)
    trig_ref = trig()
    for g in range(KV_HEADS):
        part = kv_pre[:, g * 128 : (g + 1) * 128]
        turned = part * trig_ref[2] + swap_halves(part) * trig_ref[3]
        kv_out[seq, :, g * 128 : (g + 1) * 128] = turned.astype(LOW)
    greet([mate, x_mate])
    own_kv = kv_out.at[seq]
    to_mate = send(own_kv, own_kv, send_sem.at[0], recv_sem.at[0], mate)
    to_x = send(own_kv, own_kv, send_sem.at[1], recv_sem.at[1], x_mate)
    q_pre = dot(normed_out[...], w_query()[...])
    lane = lax.broadcasted_iota(jnp.int32, (length, 128), 1)
    for pair in range((HEADS + 1) // 2):
        width = min(128, HEADS * HEAD_DIM - pair * 128)
        part = q_pre[:, pair * 128 : pair * 128 + width]
        if width < 128:
            part = jnp.concatenate([part, part], axis=1)
        turned = (part * trig_ref[0] + swap_halves(part) * trig_ref[1]) * SCALE
        q_out[2 * pair] = jnp.where(lane < HEAD_DIM, turned, 0.0).astype(LOW)
        if width == 128:
            q_out[2 * pair + 1] = jnp.where(lane < HEAD_DIM, pltpu.roll(turned, 64, 1), 0.0).astype(LOW)

    early(q_out, q_hbm)
    start, place = place_ref[0:1, :], place_ref[1:2, :]

    def attend(block, g):
        kv_g = kv_out[block, :, pl.ds(pl.multiple_of(g * 128, 128), 128)]
        q_g = q_out[pl.ds(3 * g, 3)].reshape(stacked, 128)
        scores = dot(kv_g, q_g, NT)
        key = lax.broadcasted_iota(jnp.int32, (length, stacked), 0) + block * length
        scores = jnp.where((key >= start) & (key <= place), scores, MASKED)
        new_peak = jnp.maximum(peak[g], jnp.max(scores, axis=0, keepdims=True))
        weights = jnp.exp(scores - new_peak)
        fade = jnp.exp(peak[g] - new_peak)
        total[g] = jnp.sum(weights, axis=0, keepdims=True) + fade * total[g]
        acc[g] = dot(kv_g, weights.astype(LOW), TN)[HEAD_DIM:] + fade * acc[g]
        peak[g] = new_peak

    peak[...] = jnp.full_like(peak, MASKED)
    total[...] = jnp.zeros_like(total)
    acc[...] = jnp.zeros_like(acc)
    far_kv, far_mate = kv_out.at[far_seq], lax.rem(mate_seq + 2, 4)
    hops = functools.partial(send, start=False)
    kv_onward = hops(far_kv, far_kv, send_sem.at[2], recv_sem.at[2], mate)
    starts = [kv_onward]
    if extra:
        mine, theirs = extra_out.at[seq], extra_out.at[far_seq]
        extra_x = hops(extra_ref, mine, send_sem.at[3], recv_sem.at[3], x_mate)
        extra_mate = hops(extra_ref, mine, send_sem.at[4], recv_sem.at[4], mate)
        starts += [early(extra_ref, mine, start=False), extra_x, extra_mate]
    kv_keep = early(kv_out, kv_hbm, start=False)

    @pl.loop(0, 4)
    def _(step):
        @pl.when(step == 1)
        def _():
            to_mate.wait()

        @pl.when(step == 2)
        def _():
            to_x.wait()
            for copy in starts:
                copy.start()

        @pl.when(step == 3)
        def _():
            kv_onward.wait()
            kv_keep.start()

        block = jnp.where(
            step == 0, seq, jnp.where(step == 1, mate_seq, jnp.where(step == 2, far_seq, far_mate))
        )

        @pl.when(block <= seq)
        def _():
            @pl.loop(0, KV_HEADS)
            def _(g):
                attend(block, g)

    if extra:
        extra_x.wait()
        extra_onward = send(theirs, theirs, send_sem.at[5], recv_sem.at[5], mate)
    for g in range(KV_HEADS):
        heads = (acc[g] / total[g]).T.astype(LOW)
        log_out[g] = peak[g] + jnp.log(total[g])
        for i in range(GROUP):
            h = GROUP * g + i
            mixed_out[:, h * HEAD_DIM : (h + 1) * HEAD_DIM] = heads[i * length : (i + 1) * length]
    after = residual + dot(mixed_out[...], w_out()[...])
    after_out[...] = after
    normed_two_out[...] = (after * inverse_rms(after) * gains_ref[1:2, :]).astype(LOW)
    if extra:
        extra_mate.wait()
        extra_onward.wait()
    early.finish()


VMEM = pl.BlockSpec(memory_space=pltpu.VMEM)
ANYWHERE = pl.BlockSpec(memory_space=pl.ANY)


def attn_forward(residual, gains, attn_weights, trig, place, extra=None):
    length, width = residual.shape
    kv_width = 2 * KV_HEADS * HEAD_DIM
    shapes = (
        ((length, width), LOW),
        ((HEADS, length, 128), LOW),
        ((4, length, kv_width), LOW),
        ((KV_HEADS, 1, GROUP * length), FULL),
        ((length, HEADS * HEAD_DIM), LOW),
        ((length, width), FULL),
        ((length, width), LOW),
    )
    args = (residual, gains) + tuple(attn_weights) + (trig, place)
    in_specs, out_specs, hops = [VMEM] * 2 + [ANYWHERE] * 5 + [VMEM], (ANYWHERE,) * 3 + (VMEM,) * 4, 3
    if extra is not None:
        args, in_specs, out_specs = args + (extra,), in_specs + [ANYWHERE], out_specs + (ANYWHERE,)
        shapes = shapes + (((4,) + extra.shape, extra.dtype),)
        hops = 6
    return pl.pallas_call(
        functools.partial(attn_forward_kernel, extra is not None),
        out_shape=tuple(jax.ShapeDtypeStruct(*s) for s in shapes),
        in_specs=in_specs,
        out_specs=out_specs,
        scratch_shapes=[
            pltpu.VMEM((kv_width, width), LOW),
            pltpu.VMEM(attn_weights[2].shape, LOW),
            pltpu.VMEM(attn_weights[3].shape, LOW),
            pltpu.VMEM(trig.shape, FULL),
            pltpu.VMEM((length, width), LOW),
            pltpu.VMEM((HEADS, length, 128), LOW),
            pltpu.VMEM((4, length, kv_width), LOW),
            pltpu.SemaphoreType.DMA((2 * KV_HEADS,)),
            pltpu.SemaphoreType.DMA((3,)),
            pltpu.SemaphoreType.DMA((4,)),
            pltpu.VMEM((KV_HEADS, 1, GROUP * length), FULL),
            pltpu.VMEM((KV_HEADS, 1, GROUP * length), FULL),
            pltpu.VMEM((KV_HEADS, HEAD_DIM, GROUP * length), FULL),
            pltpu.SemaphoreType.DMA((hops,)),
            pltpu.SemaphoreType.DMA((hops,)),
        ],
        compiler_params=pltpu.CompilerParams(
            collective_id=1 if residual.dtype == FULL else 0, has_side_effects=True, vmem_limit_bytes=60 * 1024 * 1024
        ),
        cost_estimate=cost(25),
        name="attn_forward",
    )(*args)


def prepare(positions):
    length = positions.shape[0]
    frequency = THETA ** (-(jnp.arange(HEAD_DIM // 2, dtype=FULL) * 2.0 / HEAD_DIM))
    angles = positions.astype(FULL)[:, None] * frequency
    cos, sin = jnp.cos(angles), jnp.sin(angles)
    one, none = jnp.ones((length, HEAD_DIM), FULL), jnp.zeros((length, HEAD_DIM), FULL)
    trig = jnp.stack(
        [
            jnp.concatenate([cos, cos, cos, cos], 1),
            jnp.concatenate([-sin, sin, -sin, sin], 1),
            jnp.concatenate([cos, cos, one], 1),
            jnp.concatenate([-sin, sin, none], 1),
        ]
    )
    own = lax.axis_index("seq") * length + jnp.arange(length, dtype=jnp.int32)
    place = jnp.stack([jnp.tile(own - positions, GROUP), jnp.tile(own, GROUP)])
    place = jnp.pad(place, ((0, 6), (0, 0)))
    return trig, place


def ffn_forward_kernel(
    after_hbm, normed_ref, w_gate_hbm, w_up_hbm, w_down_hbm,
    res_out, rows_hbm, pre_hbm,
    after_buf, w_gate_buf, w_up_buf, w_down_buf, rows_out, pre_out, late_sem, early_sem,
    mate_send, mate_recv, x_send, x_recv, own_far,
    send_sem, recv_sem,
):
    weights = [
        Later(src, dst, late_sem.at[i])
        for i, (src, dst) in enumerate(
            ((w_gate_hbm, w_gate_buf), (w_up_hbm, w_up_buf), (w_down_hbm, w_down_buf), (after_hbm, after_buf))
        )
    ]
    early = Early(early_sem)
    seq, dp = lax.axis_index("seq"), lax.axis_index("dp")
    core = lax.rem(seq, 2)
    mate_seq, far_seq = seq + 1 - 2 * core, lax.rem(seq + 2, 4)
    far_mate = lax.rem(mate_seq + 2, 4)
    mate, x_mate = device(mate_seq, dp), device(far_seq, dp)
    length = after_hbm.shape[0]
    step = length // CHUNKS
    greet([mate, x_mate])
    part = lambda k: pl.ds(k * step, step)

    def hop(index, src, dst, target):
        return send(src, dst, send_sem.at[index], recv_sem.at[index], target)

    rows_out[seq] = normed_ref[...]
    own_rows = lambda k: rows_out.at[seq, part(k)]
    far_rows = lambda k: rows_out.at[far_seq, part(k)]
    to_x = [hop(k, own_rows(k), own_rows(k), x_mate) for k in range(CHUNKS)]
    to_mate = hop(CHUNKS, rows_out.at[seq], rows_out.at[seq], mate)
    base = CHUNKS + 1
    w_gate_ref, w_up_ref, w_down_ref, after_ref = (weight() for weight in weights)

    def ffn(quarter, rows):
        block = rows_out[quarter, rows]
        gate = dot(block, w_gate_ref[...])
        up = dot(block, w_up_ref[...])
        pre_out[quarter, rows, : gate.shape[1]] = gate.astype(LOW)
        pre_out[quarter, rows, gate.shape[1] :] = up.astype(LOW)
        hidden = (gate * jax.nn.sigmoid(gate) * up).astype(LOW)
        return dot(hidden, w_down_ref[...], NT)

    everything = pl.ds(0, length)
    res_out[...] = after_ref[...] + ffn(seq, everything)
    to_mate.wait()
    mate_send[0] = ffn(mate_seq, everything).astype(LOW)
    back = hop(base, mate_send.at[0], mate_recv.at[0], mate)
    onward = []
    for k in range(CHUNKS):
        to_x[k].wait()
        onward.append(hop(base + 1 + k, far_rows(k), far_rows(k), mate))
        own_far[part(k)] = ffn(far_seq, part(k))
        onward[k].wait()
        mate_send[1, part(k)] = ffn(far_mate, part(k)).astype(LOW)
        joint = hop(base + 1 + CHUNKS + k, mate_send.at[1, part(k)], mate_recv.at[1, part(k)], mate)
        joint.wait()
        x_send[part(k)] = (own_far[part(k)] + mate_recv[1, part(k)].astype(FULL)).astype(LOW)
        onward.append(
            hop(base + 1 + 2 * CHUNKS + k, x_send.at[part(k)], x_recv.at[part(k)], x_mate)
        )
        onward[k], onward[-1] = onward[-1], onward[k]
        onward.pop()
    early(rows_out, rows_hbm)
    early(pre_out, pre_hbm)
    back.wait()
    res_out[...] += mate_recv[0].astype(FULL)
    for k in range(CHUNKS):
        onward[k].wait()
        res_out[part(k)] += x_recv[part(k)].astype(FULL)
    early.finish()


def ffn_forward(after, normed_two, w_gate, w_up, w_down):
    length, width = after.shape
    shapes = (
        ((length, width), FULL),
        ((4, length, width), LOW),
        ((4, length, 2 * w_gate.shape[1]), LOW),
    )
    sems = 3 * CHUNKS + CHUNKS + 2
    return pl.pallas_call(
        ffn_forward_kernel,
        out_shape=tuple(jax.ShapeDtypeStruct(*s) for s in shapes),
        in_specs=[ANYWHERE, VMEM] + [ANYWHERE] * 3,
        out_specs=(VMEM, ANYWHERE, ANYWHERE),
        scratch_shapes=[
            pltpu.VMEM((length, width), FULL),
            pltpu.VMEM(w_gate.shape, LOW),
            pltpu.VMEM(w_up.shape, LOW),
            pltpu.VMEM(w_down.shape, LOW),
            pltpu.VMEM((4, length, width), LOW),
            pltpu.VMEM((4, length, 2 * w_gate.shape[1]), LOW),
            pltpu.SemaphoreType.DMA((4,)),
            pltpu.SemaphoreType.DMA((2,)),
            pltpu.VMEM((2, length, width), LOW),
            pltpu.VMEM((2, length, width), LOW),
            pltpu.VMEM((length, width), LOW),
            pltpu.VMEM((length, width), LOW),
            pltpu.VMEM((length, width), FULL),
            pltpu.SemaphoreType.DMA((sems,)),
            pltpu.SemaphoreType.DMA((sems,)),
        ],
        compiler_params=pltpu.CompilerParams(
            collective_id=2, has_side_effects=True, vmem_limit_bytes=60 * 1024 * 1024
        ),
        cost_estimate=cost(36),
        name="ffn_forward",
    )(after, normed_two, w_gate, w_up, w_down)


def norm_back(value, gain, grad):
    inverse = inverse_rms(value)
    weighted = grad * gain
    inner = jnp.mean(weighted * value, axis=-1, keepdims=True)
    back = inverse * weighted - value * (inverse * inverse * inverse) * inner
    return back, jnp.sum(grad * value * inverse, axis=0, keepdims=True)


def ffn_all_kernel(second, reduce, up_ref, own_ref, after_hbm, gains_ref, still_refs, gate_ref, upw_ref, down_ref, far_ref, *rest):
    y_part = prev_hbm = pre_hbm = None
    if second:
        result_out, rest = rest[0], rest[1:]
    else:
        prev_hbm, pre_hbm, *rest = rest
    grad_out, gain_out, weight_hbm, *rest = rest
    if reduce:
        y_part, *rest = rest
    (
        w_in, w_down, still_ref, moved, in_grad, in_temp, hidden, back, after_buf, prev_buf, pre_buf, weight_out,
        load_sem, late_sem, early_sem, send_sem, recv_sem,
    ) = rest
    early = Early(early_sem)
    after_ref = Later(after_hbm, after_buf, late_sem.at[0])
    prev_ref = None if second else Later(prev_hbm, prev_buf, late_sem.at[1])
    pre_ref = None if second else Later(pre_hbm, pre_buf, late_sem.at[2])
    hop = Hops(send_sem, recv_sem)
    seq, dp = lax.axis_index("seq"), lax.axis_index("dp")
    core = lax.rem(seq, 2)
    mate_seq, far_seq = seq + 1 - 2 * core, lax.rem(seq + 2, 4)
    far_mate = lax.rem(mate_seq + 2, 4)
    mate, x_mate = device(mate_seq, dp), device(far_seq, dp)
    length, width = up_ref.shape
    units = gate_ref.shape[1]
    whole = pl.ds(0, width)

    def slots(w, rows):
        return w_in.at[w, rows, :units], w_in.at[w, rows, units:], w_down.at[w, rows]

    loads = []

    def load(src, dst):
        loads.append(pltpu.make_async_copy(src, dst, load_sem.at[len(loads)]))
        loads[-1].start()

    for src, dst in zip((gate_ref, upw_ref, down_ref), slots(0, whole)):
        load(src, dst)
    moved[seq] = own_ref[...].astype(LOW)
    at = 0
    for ref in still_refs:
        load(ref, still_ref.at[:, pl.ds(at, ref.shape[1])])
        at += ref.shape[1]
    far_from = len(loads)
    for d in range(SHARES):
        at = min(d * PIECE, width - PIECE)
        rows = min(PIECE, width - PIECE - at) if d == SHARES - 2 else PIECE
        for i, dst in enumerate(slots(2, pl.ds(at, rows))):
            load(far_ref.at[d, pl.ds(i * PIECE, rows)], dst)
    y_mate = device(seq, dp + 1 - 2 * lax.rem(dp, 2))
    greet([mate, x_mate] + ([y_mate] if reduce else []))
    mine, theirs = moved.at[seq], moved.at[far_seq]
    to_x = hop(mine, mine, x_mate)
    to_mate = hop(mine, mine, mate)
    beside = [hop(src, dst, mate) for src, dst in zip((gate_ref, upw_ref, down_ref), slots(1, whole))]
    rows_ref, low_ref = (moved, still_ref) if second else (still_ref, moved)

    def halves(quarter, w, grads, known=False):
        both = pre_buf[quarter].astype(FULL) if known else dot(rows_ref[quarter], w_in[w])
        gate, up = both[:, :units], both[:, units:]
        bend = jax.nn.sigmoid(gate)
        silu = gate * bend
        hidden_grad = dot(low_ref[quarter], w_down[w])
        grads[:, :units] = (hidden_grad * up * bend * (1.0 + gate * (1.0 - bend))).astype(LOW)
        grads[:, units:] = (hidden_grad * silu).astype(LOW)
        return (silu * up).astype(LOW)

    def local(w):
        act = halves(seq, w, in_temp)
        back[...] += dot(in_temp[...], w_in[w], NT)
        if second:
            grad_out[...] += dot(act, w_down[w], NT)

    for copy in loads[:far_from]:
        copy.wait()
    if not second:
        pre_ref()
    hidden[seq] = halves(seq, 0, in_grad.at[seq], not second)
    if second:
        back[...] = dot(in_grad[seq], w_in[0], NT)
        grad_out[...] = after_ref()[...] + dot(hidden[seq], w_down[0], NT)
    for copy in loads[far_from:]:
        copy.wait()
    across = [hop(w_in.at[2], w_in.at[3], mate), hop(w_down.at[2], w_down.at[3], mate)]
    for copy in beside:
        copy.wait()

    if second:

        @pl.loop(1, 4)
        def _(w):
            @pl.when(w == 3)
            def _():
                for copy in across:
                    copy.wait()

            local(w)

    else:
        back[...] = jnp.zeros_like(back)
        local(1)

    to_mate.wait()
    to_x.wait()
    onward = hop(theirs, theirs, mate)

    @pl.loop(0, 3)
    def _(i):
        @pl.when(i == 2)
        def _():
            onward.wait()

        quarter = jnp.where(i == 0, mate_seq, jnp.where(i == 1, far_seq, far_mate))
        hidden[quarter] = halves(quarter, 0, in_grad.at[quarter], not second)

    flat = lambda ref: ref[...].reshape(4 * length, ref.shape[2])
    share = width // SHARES

    def finish(i, term):
        for j in range(SHARES):
            rows = term[j * share : (j + 1) * share]
            if prev_ref is not None:
                rows = rows + prev_ref()[i, j // 2, j % 2].astype(FULL)
            weight_out[i, j // 2, j % 2] = rows.astype(LOW)
        early(weight_out.at[i], weight_hbm.at[i])

    def half(columns):
        return in_grad[:, :, columns].reshape(4 * length, units)

    if second:
        both = dot(flat(rows_ref), flat(in_grad), TN)
        finish(0, both[:, :units])
        finish(1, both[:, units:])
    else:
        finish(0, dot(flat(rows_ref), half(slice(0, units)), TN))
        if reduce:
            first_y = hop(weight_out.at[0, :, 1 - lax.rem(dp, 2)], y_part, y_mate)
        finish(1, dot(flat(rows_ref), half(slice(units, 2 * units)), TN))
        back[...] += dot(in_grad[seq], w_in[0], NT)
        for copy in across:
            copy.wait()

        @pl.loop(2, 4)
        def _(w):
            local(w)

    finish(2, dot(flat(low_ref), flat(hidden), TN))
    if second:
        result_out[...] = grad_out[...].astype(LOW)
    sent_back, gain_term = norm_back(after_ref()[...], gains_ref[1:2, :], back[...])
    grad_out[...] = up_ref[...].astype(FULL) + sent_back
    gain_out[...] = jnp.broadcast_to(gain_term, gain_out.shape)
    if reduce:
        first_y.wait()
    early.finish()


def ffn_all_call(stills, second, reduce, *refs):
    refs = refs if second else refs[:1] + refs
    return ffn_all_kernel(second, reduce, *refs[:4], refs[4 : 4 + stills], *refs[4 + stills :])


def ffn_all(second, reduce, upstream, own, after, gains, stills, weights, far, prev=None, pre=None):
    length, width = after.shape
    units = weights[0].shape[1]
    share = width // SHARES
    grads = (3, SHARES // 2, 2, share, units)
    shapes = (
        ((length, width), FULL),
        ((8, width), FULL),
        (grads, LOW),
    )
    if second:
        shapes = (((length, width), LOW),) + shapes
    if reduce:
        shapes = shapes + (((SHARES // 2, share, units), LOW),)
    args = (after, gains) + tuple(stills) + tuple(weights) + (far,)
    specs = [ANYWHERE, VMEM] + [ANYWHERE] * (len(stills) + 4)
    if second:
        args, specs = (upstream, own) + args, [VMEM, VMEM] + specs
    else:
        args, specs = (upstream,) + args, [VMEM] + specs
        args, specs = args + (prev, pre), specs + [ANYWHERE] * 2
    return pl.pallas_call(
        functools.partial(ffn_all_call, len(stills), second, reduce),
        out_shape=tuple(jax.ShapeDtypeStruct(*s) for s in shapes),
        in_specs=specs,
        out_specs=tuple(ANYWHERE if s[0] == grads else VMEM for s in shapes),
        scratch_shapes=[
            pltpu.VMEM((4, width, 2 * units), LOW),
            pltpu.VMEM((4, width, units), LOW),
            pltpu.VMEM((4, length, width), LOW),
            pltpu.VMEM((4, length, width), LOW),
            pltpu.VMEM((4, length, 2 * units), LOW),
            pltpu.VMEM((length, 2 * units), LOW),
            pltpu.VMEM((4, length, units), LOW),
            pltpu.VMEM((length, width), FULL),
            pltpu.VMEM((length, width), FULL),
            pltpu.VMEM((1, 1, 2, 8, 128) if second else grads, LOW),
            pltpu.VMEM((1, 8, 128) if second else pre.shape, LOW),
            pltpu.VMEM(grads, LOW),
            pltpu.SemaphoreType.DMA((3 + len(stills) + 3 * SHARES,)),
            pltpu.SemaphoreType.DMA((3,)),
            pltpu.SemaphoreType.DMA((3,)),
            pltpu.SemaphoreType.DMA((9,)),
            pltpu.SemaphoreType.DMA((9,)),
        ],
        compiler_params=pltpu.CompilerParams(
            collective_id=3 if second else 4, has_side_effects=True, vmem_limit_bytes=60 * 1024 * 1024
        ),
        cost_estimate=cost(30),
        name="ffn_second" if second else "ffn_first_backward",
    )(*args)


def attn_backward_kernel(
    last, after_grad_ref, w_out_ref, mixed_ref, gains_ref, place_ref, log_ref, q_hbm, kv_hbm, trig_hbm,
    res_hbm, normed_hbm, w_key_hbm, w_value_hbm, w_query_hbm, *rest
):
    if last:
        prev, ffn_ref, first_hbm, gain_ref = rest[:3], rest[3], rest[4], rest[5]
        grad_out, gain_out, ffn_out, share_outs = rest[6], rest[7], rest[8], rest[9:12]
        rest = rest[12:]
    else:
        prev = (None, None, None)
        grad_out, gain_out = rest[:2]
        part_hbms = rest[2:5]
        rest = rest[5:]
    q_buf, kv_buf, trig_buf, res_buf, normed_buf, w_kv_buf, w_query_buf, pair_sem, late_sem, early_sem, *rest = rest
    late = iter(late_sem.at[i] for i in range(11))
    q_later, kv_later = Later(q_hbm, q_buf, next(late)), Later(kv_hbm, kv_buf, next(late))
    mixed_grad, delta, kv_grad, query_grad, back, grad_send, grad_recv, send_sem, recv_sem = rest[:9]
    hop = Hops(send_sem, recv_sem)
    seq, dp = lax.axis_index("seq"), lax.axis_index("dp")
    core, chip_x = lax.rem(seq, 2), lax.div(seq, 2)
    mate_seq, far_seq = seq + 1 - 2 * core, lax.rem(seq + 2, 4)
    far_mate = lax.rem(mate_seq + 2, 4)
    mate, x_mate = device(mate_seq, dp), device(far_seq, dp)
    length, width = res_hbm.shape
    stacked = GROUP * length
    kv_width = 2 * KV_HEADS * HEAD_DIM
    parts = rest[9:12]
    if last:
        f_own, f_y_recv, f_a_send, f_a_recv, f_b_send, f_b_recv, gain_recv = rest[12:19]
        prev_bufs = rest[19:22]
        buffers = [rest[22 + 10 * i : 32 + 10 * i] for i in range(3)]
        row_y, row_z = lax.rem(dp, 2), lax.div(dp, 2)
        low_z, high_z = lax.rem(row_z, 2), lax.div(row_z, 2)
        y_mate = device(seq, dp + 1 - 2 * row_y)
        near_z = device(seq, dp + 2 - 4 * low_z)
        far_z = device(seq, dp + 4 - 8 * high_z)
        greet([mate, x_mate, y_mate, near_z, far_z])
        f_y = [hop(ffn_ref.at[m, :, 1 - row_y], f_y_recv.at[m], y_mate) for m in (1, 2)]
        first_y = Later(first_hbm, f_y_recv.at[0], next(late))
        own_shares = Later(ffn_ref.at[:, :, row_y], f_own, next(late))
        prev = [Later(src, dst, next(late)) for src, dst in zip(prev, prev_bufs)]
    else:
        greet([mate, x_mate])
    early = Early(early_sem)
    trig = Later(trig_hbm, trig_buf, next(late))
    normed_ref = Later(normed_hbm, normed_buf, next(late))
    w_query = Later(w_query_hbm, w_query_buf, next(late))
    w_kv = LaterPairs(w_key_hbm, w_value_hbm, w_kv_buf, pair_sem)
    res_ref = Later(res_hbm, res_buf, next(late))

    def near_fill(load, a_send):
        for h in range(2):
            a_send[h] = load(2 * h + 1 - low_z).astype(LOW)

    def far_fill(load, a_recv, b_send):
        b_send[...] = (load(2 - 2 * high_z + low_z) + a_recv[1 - high_z].astype(FULL)).astype(LOW)

    def z_total(load, a_recv, b_recv):
        return load(row_z) + a_recv[high_z].astype(FULL) + b_recv[...].astype(FULL)

    def f_load(m):
        return lambda z: own_shares()[m, z].astype(FULL) + f_y_recv[m, z].astype(FULL)

    if last:
        f_nears = [hop(f_a_send.at[m], f_a_recv.at[m], near_z, start=False) for m in range(3)]
        f_fars = [hop(f_b_send.at[m], f_b_recv.at[m], far_z, start=False) for m in range(3)]

    def f_near(m):
        own_shares()
        if m == 0:
            first_y()
        else:
            f_y[m - 1].wait()
        near_fill(f_load(m), f_a_send.at[m])
        f_nears[m].start()

    def f_far(m):
        f_nears[m].wait()
        far_fill(f_load(m), f_a_recv.at[m], f_b_send.at[m])
        f_fars[m].start()

    def f_finish(m):
        f_fars[m].wait()
        ffn_out[m] = z_total(f_load(m), f_a_recv.at[m], f_b_recv.at[m])

    quarter = lambda x, c: pl.ds(pl.multiple_of(64 * x + ROWS_PAD * c, ROWS_PAD), ROWS_PAD)

    def core_start(i):
        core_recv = buffers[i][0]
        return [hop(parts[i].at[:, quarter(x, 1 - core)], core_recv.at[x], mate) for x in range(2)]

    def x_make(i):
        return hop(*buffers[i][1:3], x_mate, start=False)

    def x_start(i, copies, x_copy):
        core_recv, x_send, x_recv = buffers[i][:3]
        for copy in copies:
            copy.wait()
        joint = parts[i][:, quarter(1 - chip_x, core)].astype(FULL) + core_recv[1 - chip_x].astype(FULL)
        x_send[...] = joint.astype(LOW)
        x_copy.start()
        return x_copy

    def y_start(i, copy):
        core_recv, x_send, x_recv, own, y_recv = buffers[i][:5]
        joint = parts[i][:, quarter(chip_x, core)].astype(FULL) + core_recv[chip_x].astype(FULL)
        copy.wait()
        own[...] = (joint + x_recv[...].astype(FULL)).astype(LOW).reshape(own.shape)
        return hop(own.at[:, 1 - row_y], y_recv, y_mate)

    def part_load(i):
        own, y_recv = buffers[i][3:5]
        return lambda z: own[z, row_y].astype(FULL) + y_recv[z].astype(FULL)

    def z_start(i, copy):
        copy.wait()
        near_fill(part_load(i), buffers[i][5])
        return hop(*buffers[i][5:7], near_z)

    def z_next(i, copy):
        copy.wait()
        far_fill(part_load(i), *buffers[i][6:8])
        return hop(*buffers[i][7:9], far_z)

    def share_start(i, copy):
        gathered = buffers[i][9]
        copy.wait()
        gathered[seq] = z_total(part_load(i), buffers[i][6], buffers[i][8]).astype(LOW)
        mine = gathered.at[seq]
        return hop(mine, mine, x_mate), hop(mine, mine, mate)

    def share_pass(i, copies):
        gathered = buffers[i][9]
        copies[0].wait()
        theirs = gathered.at[far_seq]
        return hop(theirs, theirs, mate), copies[1]

    def share_finish(i, copies):
        gathered = buffers[i][9]
        for copy in copies:
            copy.wait()
        for s in range(4):
            share_outs[i][s * ROWS_PAD : (s + 1) * ROWS_PAD] = gathered[s].astype(FULL)

    def weight(i, left, right):
        term = dot(left, right, TN)
        share = width // SHARES
        for j in range(SHARES):
            rows = term[j * share : (j + 1) * share]
            if prev[i] is not None:
                rows = rows + prev[i]()[j, :share].astype(FULL)
            parts[i][j, :share] = rows.astype(LOW)
        if not last:
            early(parts[i], part_hbms[i])

    low_grad = after_grad_ref[...].astype(LOW)
    mixed_back = dot(low_grad, w_out_ref[...], NT)
    lane = lax.broadcasted_iota(jnp.int32, (length, 128), 1)
    for pair in range((HEADS + 1) // 2):
        span = min(128, HEADS * HEAD_DIM - pair * 128)
        part = mixed_back[:, pair * 128 : pair * 128 + span]
        if span < 128:
            part = jnp.concatenate([part, part], axis=1)
        else:
            mixed_grad[2 * pair + 1] = jnp.where(lane >= HEAD_DIM, part, 0.0).astype(LOW)
        mixed_grad[2 * pair] = jnp.where(lane >= HEAD_DIM, pltpu.roll(part, 64, 1), 0.0).astype(LOW)
    product = mixed_back.astype(LOW).astype(FULL) * mixed_ref[...].astype(FULL)
    high = product.astype(LOW)
    rest_low = (product - high.astype(FULL)).astype(LOW)
    head = lax.broadcasted_iota(jnp.int32, (16, HEADS * HEAD_DIM), 0)
    column = lax.broadcasted_iota(jnp.int32, (16, HEADS * HEAD_DIM), 1)
    pick = jnp.where(lax.div(column, HEAD_DIM) == head, 1.0, 0.0).astype(LOW)
    sums = dot(pick, high, NT) + dot(pick, rest_low, NT)
    for g in range(KV_HEADS):
        delta[g] = jnp.concatenate([sums[3 * g + i : 3 * g + i + 1] for i in range(GROUP)], axis=1)
    query_grad[...] = jnp.zeros_like(query_grad)
    weight(0, mixed_ref[...], low_grad)
    if last:
        o_core = core_start(0)
        f_near(0)
        o_x = x_make(0)

    start, place = place_ref[0:1, :], place_ref[1:2, :]
    q_ref, kv_ref = q_later(), kv_later()

    def attend(block, g):
        columns = pl.ds(pl.multiple_of(g * 128, 128), 128)
        kv_g = kv_ref[block, :, columns]
        q_g = q_ref[pl.ds(3 * g, 3)].reshape(stacked, 128)
        out_g = mixed_grad[pl.ds(3 * g, 3)].reshape(stacked, 128)
        scores = dot(kv_g, q_g, NT)
        key = lax.broadcasted_iota(jnp.int32, (length, stacked), 0) + block * length
        weights = jnp.where((key >= start) & (key <= place), jnp.exp(scores - log_ref[g]), 0.0)
        probs_grad = dot(kv_g, out_g, NT)
        score_grad = (weights * (probs_grad - delta[g])).astype(LOW)
        kv_grad[block, :, columns] = dot(weights.astype(LOW), out_g) + dot(score_grad, q_g)
        query_grad[g] += dot(kv_g, score_grad, TN)[:HEAD_DIM]

    joint = hop(grad_send.at[0], grad_recv.at[0], mate, start=False)
    across = hop(grad_send.at[1], grad_recv.at[1], x_mate, start=False)
    beside = hop(grad_send.at[2], grad_recv.at[2], mate, start=False)

    @pl.loop(0, 4)
    def _(step):
        block = jnp.where(
            step == 0, far_mate, jnp.where(step == 1, far_seq, jnp.where(step == 2, mate_seq, seq))
        )

        @pl.when(block <= seq)
        def _():
            @pl.loop(0, KV_HEADS)
            def _(g):
                attend(block, g)

        @pl.when(block > seq)
        def _():
            kv_grad[block] = jnp.zeros_like(kv_grad[block])

        @pl.when(step == 0)
        def _():
            grad_send[0] = kv_grad[far_mate].astype(LOW)
            joint.start()

        @pl.when(step == 1)
        def _():
            joint.wait()
            grad_send[1] = (kv_grad[far_seq] + grad_recv[0].astype(FULL)).astype(LOW)
            across.start()
            if last:
                x_start(0, o_core, o_x)

        @pl.when(step == 2)
        def _():
            grad_send[2] = kv_grad[mate_seq].astype(LOW)
            beside.start()
            if last:
                f_far(0)
                f_near(1)

    trig_ref = trig()
    heads = []
    for g in range(KV_HEADS):
        turned = query_grad[g].T * SCALE
        heads += [turned[i * length : (i + 1) * length] for i in range(GROUP)]
    for pair in range((HEADS + 1) // 2):
        part = jnp.concatenate([heads[2 * pair], heads[min(2 * pair + 1, HEADS - 1)]], axis=1)
        turned = (part * trig_ref[0] - swap_halves(part) * trig_ref[1]).astype(LOW)
        at = kv_width + pair * 128
        stop = min(at + 128, kv_width + width)
        back[:, at:stop] = turned[:, : stop - at]
    weight(1, normed_ref()[...], back[:, kv_width:])
    if last:
        q_core = core_start(1)
        o_y = y_start(0, o_x)
    normed_grad = dot(back[:, kv_width:], w_query()[...], NT)
    if last:
        q_x = x_start(1, q_core, x_make(1))

    across.wait()
    beside.wait()
    own = kv_grad[seq] + grad_recv[1].astype(FULL) + grad_recv[2].astype(FULL)
    for g in range(KV_HEADS):
        part = own[:, g * 128 : (g + 1) * 128]
        back[:, g * 128 : (g + 1) * 128] = (part * trig_ref[2] - swap_halves(part) * trig_ref[3]).astype(LOW)
    weight(2, normed_ref()[...], back[:, :kv_width])
    if last:
        kv_core = core_start(2)
        f_far(1)
        f_near(2)
        kv_x = x_start(2, kv_core, x_make(2))
    normed_grad = normed_grad + dot(back[:, :kv_width], w_kv()[...])
    sent_back, gain_term = norm_back(res_ref()[...].astype(FULL), gains_ref[0:1, :], normed_grad)
    grad_out[...] = after_grad_ref[...] + sent_back
    if not last:
        gain_out[...] = jnp.broadcast_to(gain_term, gain_out.shape)
        early.finish()
        return

    row = lax.broadcasted_iota(jnp.int32, gain_out.shape, 0)
    gain_out[...] = gain_ref[...] + jnp.where(row == 0, gain_term, 0.0)
    partners = [mate, x_mate, y_mate, near_z, far_z]
    gain_hop = lambda n: hop(gain_out, gain_recv.at[n], partners[n])

    def gain_add(n, copy):
        copy.wait()
        gain_out[...] += gain_recv[n]

    gain_copy = gain_hop(0)
    f_finish(0)
    o_z = z_start(0, o_y)
    gain_add(0, gain_copy)
    gain_copy = gain_hop(1)
    q_y = y_start(1, q_x)
    f_far(2)
    f_finish(1)
    o_z = z_next(0, o_z)
    gain_add(1, gain_copy)
    gain_copy = gain_hop(2)
    kv_y = y_start(2, kv_x)
    q_z = z_start(1, q_y)
    gain_add(2, gain_copy)
    gain_copy = gain_hop(3)
    o_s = share_start(0, o_z)
    kv_z = z_start(2, kv_y)
    q_z = z_next(1, q_z)
    gain_add(3, gain_copy)
    gain_copy = gain_hop(4)
    f_finish(2)
    o_s = share_pass(0, o_s)
    kv_z = z_next(2, kv_z)
    q_s = share_start(1, q_z)
    gain_add(4, gain_copy)
    kv_s = share_start(2, kv_z)
    q_s = share_pass(1, q_s)
    share_finish(0, o_s)
    kv_s = share_pass(2, kv_s)
    share_finish(1, q_s)
    share_finish(2, kv_s)


def attn_backward(after_grad, residual, normed, gains, q, kv, log_total, mixed, attn_weights, trig, place, final=None):
    length, width = residual.shape
    kv_width = 2 * KV_HEADS * HEAD_DIM
    last = final is not None
    key_t, value_t, w_query, w_out = attn_weights
    args = (after_grad, w_out, mixed, gains, place, log_total, q, kv, trig, residual, normed, key_t, value_t, w_query)
    specs = [VMEM] * 6 + [ANYWHERE] * 8
    out_specs = (VMEM, VMEM)
    shapes = (((length, width), FULL), ((8, width), FULL))
    sizes = (width, width, kv_width)
    part_shapes = [((SHARES, 4 * ROWS_PAD, c), LOW) for c in sizes]
    scratch = [
        pltpu.VMEM(q.shape, LOW),
        pltpu.VMEM(kv.shape, LOW),
        pltpu.VMEM(trig.shape, FULL),
        pltpu.VMEM((length, width), residual.dtype),
        pltpu.VMEM((length, width), LOW),
        pltpu.VMEM((kv_width, width), LOW),
        pltpu.VMEM(w_query.shape, LOW),
        pltpu.SemaphoreType.DMA((2 * KV_HEADS,)),
        pltpu.SemaphoreType.DMA((11,)),
        pltpu.SemaphoreType.DMA((3,)),
        pltpu.VMEM((HEADS, length, 128), LOW),
        pltpu.VMEM((KV_HEADS, 1, GROUP * length), FULL),
        pltpu.VMEM((4, length, kv_width), FULL),
        pltpu.VMEM((KV_HEADS, HEAD_DIM, GROUP * length), FULL),
        pltpu.VMEM((length, kv_width + width), LOW),
        pltpu.VMEM((3, length, kv_width), LOW),
        pltpu.VMEM((3, length, kv_width), LOW),
    ]
    hops = 3
    if last:
        share, hidden = final[3].shape[3:]
        args = args + tuple(final)
        specs = specs + [ANYWHERE] * 5 + [VMEM]
        shapes = shapes + (((3, share, hidden), FULL),) + tuple(((4 * ROWS_PAD, c), FULL) for c in sizes)
        hops = 3 + 2 + 6 + 5 + 3 * (2 + 1 + 1 + 2 + 3)
        scratch += [pltpu.SemaphoreType.DMA((hops,))] * 2
        out_specs = (VMEM,) * len(shapes)
        scratch += [pltpu.VMEM(*s) for s in part_shapes]
        scratch += [
            pltpu.VMEM((3, 4, share, hidden), LOW),
            pltpu.VMEM((3, 4, share, hidden), LOW),
            pltpu.VMEM((3, 2, share, hidden), LOW),
            pltpu.VMEM((3, 2, share, hidden), LOW),
            pltpu.VMEM((3, share, hidden), LOW),
            pltpu.VMEM((3, share, hidden), LOW),
            pltpu.VMEM((5, 8, width), FULL),
        ]
        scratch += [pltpu.VMEM(*s) for s in part_shapes]
        for c in sizes:
            scratch += [
                pltpu.VMEM((2, SHARES, ROWS_PAD, c), LOW),
                pltpu.VMEM((SHARES, ROWS_PAD, c), LOW),
                pltpu.VMEM((SHARES, ROWS_PAD, c), LOW),
                pltpu.VMEM((4, 2, ROWS_PAD, c), LOW),
                pltpu.VMEM((4, ROWS_PAD, c), LOW),
                pltpu.VMEM((2, ROWS_PAD, c), LOW),
                pltpu.VMEM((2, ROWS_PAD, c), LOW),
                pltpu.VMEM((ROWS_PAD, c), LOW),
                pltpu.VMEM((ROWS_PAD, c), LOW),
                pltpu.VMEM((4, ROWS_PAD, c), LOW),
            ]
    else:
        shapes, out_specs = shapes + tuple(part_shapes), out_specs + (ANYWHERE,) * 3
        scratch += [pltpu.SemaphoreType.DMA((hops,))] * 2
        scratch += [pltpu.VMEM(*s) for s in part_shapes]
    return pl.pallas_call(
        functools.partial(attn_backward_kernel, last),
        out_shape=tuple(jax.ShapeDtypeStruct(*s) for s in shapes),
        in_specs=specs,
        out_specs=out_specs,
        scratch_shapes=scratch,
        compiler_params=pltpu.CompilerParams(
            collective_id=6 if last else 5, has_side_effects=True, vmem_limit_bytes=60 * 1024 * 1024
        ),
        cost_estimate=cost(95 if last else 40),
        name="attn_backward_last" if last else "attn_backward",
    )(*args)


def split_pairs(grads):
    rows = grads.shape[0]
    pairs = grads.reshape(rows, KV_HEADS, 2, HEAD_DIM)
    return pairs[:, :, 0].reshape(rows, -1), pairs[:, :, 1].reshape(rows, -1)


def on_device(
    tokens,
    seg_ids,
    positions,
    attn_gain,
    w_query,
    w_key,
    w_value,
    w_out,
    ffn_gain,
    w_gate,
    w_up,
    w_down,
    cotangent,
):
    width = tokens.shape[2]
    trig, place = prepare(positions[0])
    attn_weights = (w_key.T, w_value.T, w_query, w_out)
    gains = jnp.pad(jnp.stack([attn_gain, ffn_gain]), ((0, 6), (0, 0)))
    whole = lax.axis_size("dp") != SHARES
    share = width // SHARES
    own_weights = (w_gate, w_up, w_down.T)

    def over_x(value):
        return lax.ppermute(value, "seq", [(s, (s + 2) % 4) for s in range(4)])

    def over_rows_piece(value, d):
        return lax.dynamic_slice_in_dim(value, jnp.minimum(d * PIECE, width - PIECE), PIECE, axis=0)

    if whole:
        theirs = [over_x(w) for w in own_weights]
        far = jnp.stack([jnp.concatenate([over_rows_piece(w, d) for w in theirs]) for d in range(SHARES)])
    else:
        piece = jnp.concatenate([over_rows_piece(w, lax.axis_index("dp")) for w in own_weights])
        far = lax.all_gather(over_x(piece), "dp", axis=0)

    half = cotangent.shape[1] // 2
    first = attn_forward(tokens[0], gains, attn_weights, trig, place, cotangent[0, :half])
    residual, rows_all, pre_all = ffn_forward(first[5], first[6], *own_weights)
    second = attn_forward(residual, gains, attn_weights, trig, place, cotangent[0, half:])
    output, after_grad, ffn_gain_term, ffn_grads = ffn_all(
        True, False, cotangent[0], second[6], second[5], gains, (first[7], second[7]), own_weights, far
    )

    def attn_args(after_grad, residual, kept):
        normed, q, kv, log_total, mixed = kept[:5]
        return (after_grad, residual, normed, gains, q, kv, log_total, mixed, attn_weights, trig, place)

    upstream, attn_gain_term, *parts = attn_backward(*attn_args(after_grad, residual, second))
    gain_grads = jnp.stack([attn_gain_term[0], ffn_gain_term[0]])
    after_grad, ffn_gain_term, ffn_grads, *first_y = ffn_all(
        False, not whole, upstream, None, first[5], gains, (rows_all,), own_weights, far, ffn_grads, pre_all
    )
    args = attn_args(after_grad, tokens[0], first)
    if whole:
        upstream, attn_gain_term, *terms = attn_backward(*args)
        gain_grads = gain_grads + jnp.stack([attn_gain_term[0], ffn_gain_term[0]])
        parts = [part.astype(FULL) + term.astype(FULL) for part, term in zip(parts, terms)]
    else:
        gain_grads = gain_grads + jnp.stack([jnp.zeros_like(attn_gain), ffn_gain_term[0]])
        final = (*parts, ffn_grads, *first_y, jnp.pad(gain_grads, ((0, 6), (0, 0))))
        upstream, gain_all, ffn_share, *shares = attn_backward(*args, final)
    if whole:

        def over_rows(grads, dim):
            grads = lax.psum_scatter(grads.astype(LOW), "dp", scatter_dimension=dim, tiled=True)
            return grads.astype(FULL)

        def over_all(grads, dim):
            return lax.psum(over_rows(grads, dim).astype(LOW), "seq").astype(FULL)

        shares = [over_all(part[:, :share].reshape(width, -1), 0) for part in parts]
        ffn_share = over_rows(ffn_grads.reshape(3, width, -1), 1)
        own_gains = over_all(gain_grads, 1)
    else:
        shares = [part[:share] for part in shares]
        own_gains = lax.dynamic_slice_in_dim(gain_all, lax.axis_index("dp") * share, share, axis=1)
    key_share, value_share = split_pairs(shares[2])
    return (
        output[None],
        upstream[None],
        own_gains[0],
        shares[1],
        key_share,
        value_share,
        shares[0],
        own_gains[1],
        ffn_share[0],
        ffn_share[1],
        ffn_share[2].T,
    )


def solution(mesh):
    in_specs = (
        P("dp", "seq", None),
        P("dp", "seq"),
        P("dp", "seq"),
        P(),
        P(),
        P(),
        P(),
        P(),
        P(),
        P(None, "seq"),
        P(None, "seq"),
        P("seq", None),
        P("dp", "seq", None),
    )
    out_specs = (
        P("dp", "seq", None),
        P("dp", "seq", None),
        P("dp"),
        P("dp", None),
        P("dp", None),
        P("dp", None),
        P("dp", None),
        P("dp"),
        P("dp", "seq"),
        P("dp", "seq"),
        P("seq", "dp"),
    )
    return jax.shard_map(
        on_device, mesh=mesh, in_specs=in_specs, out_specs=out_specs, check_vma=False
    )
```

```python
import functools

import jax
import jax.numpy as jnp
from jax import lax
from jax.experimental import pallas as pl
from jax.experimental.pallas import tpu as pltpu
from jax.sharding import PartitionSpec as P

MESH_ID = pl.DeviceIdType.MESH
HEADS = 15
KV_HEADS = 5
GROUP = 3
HEAD_DIM = 64
EPSILON = 1e-05
THETA = 10000.0
CHUNKS = 2
SHARES = 8
ROWS_PAD = 32
PIECE = 128
MASKED = -1e30
LOW = jnp.bfloat16
FULL = jnp.float32
SCALE = HEAD_DIM ** (-0.5)
NT = (((1,), (1,)), ((), ()))
TN = (((0,), (0,)), ((), ()))


def device(seq_pos, dp_pos):
    return {"seq": seq_pos, "dp": dp_pos}


def send(src, dst, send_sem, recv_sem, target, start=True):
    copy = pltpu.make_async_remote_copy(
        src_ref=src,
        dst_ref=dst,
        send_sem=send_sem,
        recv_sem=recv_sem,
        device_id=target,
        device_id_type=MESH_ID,
    )
    if start:
        copy.start()
    return copy


class Hops:
    def __init__(self, send_sem, recv_sem):
        self.send_sem, self.recv_sem, self.used = send_sem, recv_sem, 0

    def __call__(self, src, dst, target, start=True):
        index, self.used = self.used, self.used + 1
        return send(src, dst, self.send_sem.at[index], self.recv_sem.at[index], target, start)


class Later:
    def __init__(self, src, dst, sem):
        self.copy, self.dst, self.waited = pltpu.make_async_copy(src, dst, sem), dst, False
        self.copy.start()

    def __call__(self):
        if not self.waited:
            self.copy.wait()
            self.waited = True
        return self.dst


class Early:
    def __init__(self, sem):
        self.sem, self.copies = sem, []

    def __call__(self, src, dst, start=True):
        self.copies.append(pltpu.make_async_copy(src, dst, self.sem.at[len(self.copies)]))
        if start:
            self.copies[-1].start()
        return self.copies[-1]

    def finish(self):
        for copy in self.copies:
            copy.wait()


class LaterPairs:
    def __init__(self, key_hbm, value_hbm, dst, sem):
        self.copies, self.dst = [], dst
        for h in range(2 * KV_HEADS):
            src = (key_hbm, value_hbm)[h % 2].at[pl.ds(h // 2 * HEAD_DIM, HEAD_DIM)]
            self.copies.append(pltpu.make_async_copy(src, dst.at[pl.ds(h * HEAD_DIM, HEAD_DIM)], sem.at[h]))
            self.copies[-1].start()

    def __call__(self):
        for copy in self.copies:
            copy.wait()
        self.copies = []
        return self.dst


def greet(targets):
    barrier = pltpu.get_barrier_semaphore()
    for target in targets:
        pl.semaphore_signal(barrier, inc=1, device_id=target, device_id_type=MESH_ID)
    pl.semaphore_wait(barrier, len(targets))


def dot(left, right, dims=None):
    if dims is None:
        return jnp.dot(left, right, preferred_element_type=FULL)
    return lax.dot_general(left, right, dims, preferred_element_type=FULL)


def cost(microseconds):
    return pl.CostEstimate(flops=int(microseconds * 1.15e9), bytes_accessed=1 << 20, transcendentals=0)


def inverse_rms(value):
    return lax.rsqrt(jnp.mean(value * value, axis=-1, keepdims=True) + EPSILON)


def swap_halves(value):
    lane = lax.broadcasted_iota(jnp.int32, value.shape, 1)
    first = (lane & (HEAD_DIM // 2)) == 0
    return jnp.where(first, pltpu.roll(value, 96, 1), pltpu.roll(value, 32, 1))


VMEM = pl.BlockSpec(memory_space=pltpu.VMEM)
ANYWHERE = pl.BlockSpec(memory_space=pl.ANY)


def prepare(positions):
    length = positions.shape[0]
    frequency = THETA ** (-(jnp.arange(HEAD_DIM // 2, dtype=FULL) * 2.0 / HEAD_DIM))
    angles = positions.astype(FULL)[:, None] * frequency
    cos, sin = jnp.cos(angles), jnp.sin(angles)
    one, none = jnp.ones((length, HEAD_DIM), FULL), jnp.zeros((length, HEAD_DIM), FULL)
    trig = jnp.stack(
        [
            jnp.concatenate([cos, cos, cos, cos], 1),
            jnp.concatenate([-sin, sin, -sin, sin], 1),
            jnp.concatenate([cos, cos, one], 1),
            jnp.concatenate([-sin, sin, none], 1),
        ]
    )
    own = lax.axis_index("seq") * length + jnp.arange(length, dtype=jnp.int32)
    place = jnp.stack([jnp.tile(own - positions, GROUP), jnp.tile(own, GROUP)])
    place = jnp.pad(place, ((0, 6), (0, 0)))
    return trig, place


def norm_back(value, gain, grad):
    inverse = inverse_rms(value)
    weighted = grad * gain
    inner = jnp.mean(weighted * value, axis=-1, keepdims=True)
    back = inverse * weighted - value * (inverse * inverse * inverse) * inner
    return back, jnp.sum(grad * value * inverse, axis=0, keepdims=True)


KEPT = 6
CUT = 3


def forward_kernel(
    tokens_ref, gains_ref, place_ref, cotangent_hbm, w_key_hbm, w_value_hbm, w_query_hbm, w_out_hbm, trig_hbm,
    w_gate_hbm, w_up_hbm, w_down_hbm, *rest
):
    first_hbm, (rows_hbm, pre_hbm, res_hbm), rest = rest[:KEPT], rest[KEPT : KEPT + 3], rest[KEPT + 3 :]
    second_hbm, two_hbm, extra_outs, rest = rest[:KEPT], rest[KEPT], rest[KEPT + 1 : KEPT + 3], rest[KEPT + 3 :]
    first, second, rest = rest[:KEPT], rest[KEPT : 2 * KEPT], rest[2 * KEPT :]
    (
        w_kv_buf, w_query_buf, w_out_buf, trig_buf, w_gate_buf, w_up_buf, w_down_buf,
        two, rows, pre, res, peak, total, acc, mate_send, mate_recv, x_send, x_recv, own_far,
        pair_sem, late_sem, early_sem, send_sem, recv_sem,
    ) = rest
    w_kv = LaterPairs(w_key_hbm, w_value_hbm, w_kv_buf, pair_sem)
    trig, w_query, w_out, w_gate, w_up, w_down = [
        Later(src, dst, late_sem.at[i])
        for i, (src, dst) in enumerate(
            (
                (trig_hbm, trig_buf), (w_query_hbm, w_query_buf), (w_out_hbm, w_out_buf),
                (w_gate_hbm, w_gate_buf), (w_up_hbm, w_up_buf), (w_down_hbm, w_down_buf),
            )
        )
    ]
    early, hop = Early(early_sem), Hops(send_sem, recv_sem)
    seq, dp = lax.axis_index("seq"), lax.axis_index("dp")
    core = lax.rem(seq, 2)
    mate_seq, far_seq = seq + 1 - 2 * core, lax.rem(seq + 2, 4)
    far_mate = lax.rem(mate_seq + 2, 4)
    mate, x_mate = device(mate_seq, dp), device(far_seq, dp)
    length = tokens_ref.shape[0]
    stacked = GROUP * length
    start, place = place_ref[0:1, :], place_ref[1:2, :]
    step = length // CHUNKS
    part = lambda k: pl.ds(k * step, step)

    def attention(residual_ref, buffers, hbm, extra_ref, extra_out, meet):
        normed, q, kv, log_total, mixed, after = buffers
        residual = residual_ref[...].astype(FULL)
        normed[...] = (residual * inverse_rms(residual) * gains_ref[0:1, :]).astype(LOW)
        early(normed, hbm[0])
        kv_pre = dot(normed[...], w_kv()[...], NT)
        trig_ref = trig()
        for g in range(KV_HEADS):
            piece = kv_pre[:, g * 128 : (g + 1) * 128]
            turned = piece * trig_ref[2] + swap_halves(piece) * trig_ref[3]
            kv[seq, :, g * 128 : (g + 1) * 128] = turned.astype(LOW)
        if meet:
            greet([mate, x_mate])
        spans = (pl.ds(0, CUT * 128), pl.ds(CUT * 128, (KV_HEADS - CUT) * 128))
        to_x = [hop(kv.at[seq, :, s], kv.at[seq, :, s], x_mate) for s in spans]
        to_mate = hop(kv.at[seq], kv.at[seq], mate)
        onward = [hop(kv.at[far_seq, :, s], kv.at[far_seq, :, s], mate, start=False) for s in spans]
        mine, theirs = extra_out.at[seq], extra_out.at[far_seq]
        extra = [early(extra_ref, mine, start=False)]
        extra += [hop(extra_ref, mine, target, start=False) for target in (x_mate, mate)]
        kv_keep = early(kv, hbm[2], start=False)
        q_pre = dot(normed[...], w_query()[...])
        lane = lax.broadcasted_iota(jnp.int32, (length, 128), 1)
        for pair in range((HEADS + 1) // 2):
            width = min(128, HEADS * HEAD_DIM - pair * 128)
            piece = q_pre[:, pair * 128 : pair * 128 + width]
            if width < 128:
                piece = jnp.concatenate([piece, piece], axis=1)
            turned = (piece * trig_ref[0] + swap_halves(piece) * trig_ref[1]) * SCALE
            q[2 * pair] = jnp.where(lane < HEAD_DIM, turned, 0.0).astype(LOW)
            if width == 128:
                q[2 * pair + 1] = jnp.where(lane < HEAD_DIM, pltpu.roll(turned, 64, 1), 0.0).astype(LOW)
        early(q, hbm[1])

        def attend(block, g):
            kv_g = kv[block, :, pl.ds(pl.multiple_of(g * 128, 128), 128)]
            q_g = q[pl.ds(3 * g, 3)].reshape(stacked, 128)
            scores = dot(kv_g, q_g, NT)
            key = lax.broadcasted_iota(jnp.int32, (length, stacked), 0) + block * length
            scores = jnp.where((key >= start) & (key <= place), scores, MASKED)
            new_peak = jnp.maximum(peak[g], jnp.max(scores, axis=0, keepdims=True))
            weights = jnp.exp(scores - new_peak)
            fade = jnp.exp(peak[g] - new_peak)
            total[g] = jnp.sum(weights, axis=0, keepdims=True) + fade * total[g]
            acc[g] = dot(kv_g, weights.astype(LOW), TN)[HEAD_DIM:] + fade * acc[g]
            peak[g] = new_peak

        peak[...] = jnp.full_like(peak, MASKED)
        total[...] = jnp.zeros_like(total)
        acc[...] = jnp.zeros_like(acc)

        @pl.loop(0, 6)
        def _(turn):
            @pl.when(turn == 1)
            def _():
                to_mate.wait()

            @pl.when(turn == 2)
            def _():
                to_x[0].wait()
                onward[0].start()
                for copy in extra:
                    copy.start()

            @pl.when(turn == 3)
            def _():
                onward[0].wait()

            @pl.when(turn == 4)
            def _():
                to_x[1].wait()
                onward[1].start()

            @pl.when(turn == 5)
            def _():
                onward[1].wait()
                kv_keep.start()

            block = jnp.where(
                turn == 0, seq, jnp.where(turn == 1, mate_seq, jnp.where(lax.rem(turn, 2) == 0, far_seq, far_mate))
            )
            low = jnp.where(turn < 4, 0, CUT)
            high = jnp.where((turn == 2) | (turn == 3), CUT, KV_HEADS)

            @pl.when(block <= seq)
            def _():
                @pl.loop(low, high)
                def _(g):
                    attend(block, g)

        for g in range(KV_HEADS):
            heads = (acc[g] / total[g]).T.astype(LOW)
            log_total[g] = peak[g] + jnp.log(total[g])
            for i in range(GROUP):
                h = GROUP * g + i
                mixed[:, h * HEAD_DIM : (h + 1) * HEAD_DIM] = heads[i * length : (i + 1) * length]
        early(log_total, hbm[3])
        early(mixed, hbm[4])
        extra[1].wait()
        return hop(theirs, theirs, mate), extra[2]

    def project(residual_ref, buffers, rows_of, two_ref):
        mixed, after = buffers[4:]
        value = residual_ref[rows_of].astype(FULL) + dot(mixed[rows_of], w_out()[...])
        after[rows_of] = value
        two_ref[rows_of] = (value * inverse_rms(value) * gains_ref[1:2, :]).astype(LOW)

    waits = attention(tokens_ref, first, first_hbm, cotangent_hbm.at[pl.ds(0, step)], extra_outs[0], True)

    to_x = []
    for k in range(CHUNKS):
        project(tokens_ref, first, part(k), rows.at[seq])
        to_x.append(hop(rows.at[seq, part(k)], rows.at[seq, part(k)], x_mate))
    to_mate = hop(rows.at[seq], rows.at[seq], mate)
    early(first[5], first_hbm[5])
    for copy in waits:
        copy.wait()
    w_gate_ref, w_up_ref, w_down_ref = w_gate(), w_up(), w_down()
    units = w_gate_ref.shape[1]

    def ffn(quarter, rows_of):
        block = rows[quarter, rows_of]
        gate = dot(block, w_gate_ref[...])
        up = dot(block, w_up_ref[...])
        pre[quarter, rows_of, :units] = gate.astype(LOW)
        pre[quarter, rows_of, units:] = up.astype(LOW)
        hidden = (gate * jax.nn.sigmoid(gate) * up).astype(LOW)
        return dot(hidden, w_down_ref[...], NT)

    everything = pl.ds(0, length)
    res[...] = first[5][...] + ffn(seq, everything)
    to_mate.wait()
    mate_send[0] = ffn(mate_seq, everything).astype(LOW)
    back = hop(mate_send.at[0], mate_recv.at[0], mate)
    last = []
    for k in range(CHUNKS):
        to_x[k].wait()
        onward = hop(rows.at[far_seq, part(k)], rows.at[far_seq, part(k)], mate)
        own_far[part(k)] = ffn(far_seq, part(k))
        onward.wait()
        mate_send[1, part(k)] = ffn(far_mate, part(k)).astype(LOW)
        joint = hop(mate_send.at[1, part(k)], mate_recv.at[1, part(k)], mate)
        joint.wait()
        x_send[part(k)] = (own_far[part(k)] + mate_recv[1, part(k)].astype(FULL)).astype(LOW)
        last.append(hop(x_send.at[part(k)], x_recv.at[part(k)], x_mate))
    early(rows, rows_hbm)
    early(pre, pre_hbm)
    back.wait()
    res[...] += mate_recv[0].astype(FULL)
    for k in range(CHUNKS):
        last[k].wait()
        res[part(k)] += x_recv[part(k)].astype(FULL)
    early(res, res_hbm)

    waits = attention(res, second, second_hbm, cotangent_hbm.at[pl.ds(step, step)], extra_outs[1], False)
    project(res, second, everything, two)
    early(second[5], second_hbm[5])
    early(two, two_hbm)
    for copy in waits:
        copy.wait()
    early.finish()


def forward(tokens, gains, place, cotangent, attn_weights, trig, ffn_weights):
    length, width = tokens.shape
    kv_width = 2 * KV_HEADS * HEAD_DIM
    stats = (KV_HEADS, 1, GROUP * length)
    units = ffn_weights[0].shape[1]
    kept = (
        ((length, width), LOW),
        ((HEADS, length, 128), LOW),
        ((4, length, kv_width), LOW),
        (stats, FULL),
        ((length, HEADS * HEAD_DIM), LOW),
        ((length, width), FULL),
    )
    middle = (((4, length, width), LOW), ((4, length, 2 * units), LOW), ((length, width), FULL))
    extra = ((4, length // 2, width), LOW)
    shapes = kept + middle + kept + (((length, width), LOW), extra, extra)
    key_t, value_t, w_query, w_out = attn_weights
    return pl.pallas_call(
        forward_kernel,
        out_shape=tuple(jax.ShapeDtypeStruct(*s) for s in shapes),
        in_specs=[VMEM] * 3 + [ANYWHERE] * 9,
        out_specs=(ANYWHERE,) * len(shapes),
        scratch_shapes=[pltpu.VMEM(*s) for s in kept + kept]
        + [
            pltpu.VMEM((kv_width, width), LOW),
            pltpu.VMEM(w_query.shape, LOW),
            pltpu.VMEM(w_out.shape, LOW),
            pltpu.VMEM(trig.shape, FULL),
        ]
        + [pltpu.VMEM(w.shape, LOW) for w in ffn_weights]
        + [pltpu.VMEM((length, width), LOW)]
        + [pltpu.VMEM(*s) for s in middle]
        + [
            pltpu.VMEM(stats, FULL),
            pltpu.VMEM(stats, FULL),
            pltpu.VMEM((KV_HEADS, HEAD_DIM, GROUP * length), FULL),
            pltpu.VMEM((2, length, width), LOW),
            pltpu.VMEM((2, length, width), LOW),
            pltpu.VMEM((length, width), LOW),
            pltpu.VMEM((length, width), LOW),
            pltpu.VMEM((length, width), FULL),
            pltpu.SemaphoreType.DMA((2 * KV_HEADS,)),
            pltpu.SemaphoreType.DMA((6,)),
            pltpu.SemaphoreType.DMA((18,)),
            pltpu.SemaphoreType.DMA((26,)),
            pltpu.SemaphoreType.DMA((26,)),
        ],
        compiler_params=pltpu.CompilerParams(
            collective_id=0, has_side_effects=True, vmem_limit_bytes=60 * 1024 * 1024
        ),
        cost_estimate=cost(85),
        name="forward",
    )(tokens, gains, place, cotangent, *attn_weights, trig, *ffn_weights)


def ffn_all_kernel(second, reduce, up_ref, own_ref, after_hbm, gains_ref, still_refs, gate_ref, upw_ref, down_ref, far_ref, *rest):
    y_part = prev_hbm = pre_hbm = None
    if second:
        result_out, rest = rest[0], rest[1:]
    else:
        prev_hbm, pre_hbm, *rest = rest
    grad_out, gain_out, weight_hbm, *rest = rest
    if reduce:
        y_part, *rest = rest
    (
        w_in, w_down, still_ref, moved, in_grad, in_temp, hidden, back, after_buf, prev_buf, pre_buf, weight_out,
        load_sem, late_sem, early_sem, send_sem, recv_sem,
    ) = rest
    early = Early(early_sem)
    after_ref = Later(after_hbm, after_buf, late_sem.at[0])
    prev_ref = None if second else Later(prev_hbm, prev_buf, late_sem.at[1])
    pre_ref = None if second else Later(pre_hbm, pre_buf, late_sem.at[2])
    hop = Hops(send_sem, recv_sem)
    seq, dp = lax.axis_index("seq"), lax.axis_index("dp")
    core = lax.rem(seq, 2)
    mate_seq, far_seq = seq + 1 - 2 * core, lax.rem(seq + 2, 4)
    far_mate = lax.rem(mate_seq + 2, 4)
    mate, x_mate = device(mate_seq, dp), device(far_seq, dp)
    length, width = up_ref.shape
    units = gate_ref.shape[1]
    whole = pl.ds(0, width)

    def slots(w, rows):
        return w_in.at[w, rows, :units], w_in.at[w, rows, units:], w_down.at[w, rows]

    loads = []

    def load(src, dst):
        loads.append(pltpu.make_async_copy(src, dst, load_sem.at[len(loads)]))
        loads[-1].start()

    for src, dst in zip((gate_ref, upw_ref, down_ref), slots(0, whole)):
        load(src, dst)
    moved[seq] = own_ref[...].astype(LOW)
    at = 0
    for ref in still_refs:
        load(ref, still_ref.at[:, pl.ds(at, ref.shape[1])])
        at += ref.shape[1]
    far_from = len(loads)
    for d in range(SHARES):
        at = min(d * PIECE, width - PIECE)
        rows = min(PIECE, width - PIECE - at) if d == SHARES - 2 else PIECE
        for i, dst in enumerate(slots(2, pl.ds(at, rows))):
            load(far_ref.at[d, pl.ds(i * PIECE, rows)], dst)
    y_mate = device(seq, dp + 1 - 2 * lax.rem(dp, 2))
    greet([mate, x_mate] + ([y_mate] if reduce else []))
    mine, theirs = moved.at[seq], moved.at[far_seq]
    to_x = hop(mine, mine, x_mate)
    to_mate = hop(mine, mine, mate)
    beside = [hop(src, dst, mate) for src, dst in zip((gate_ref, upw_ref, down_ref), slots(1, whole))]
    rows_ref, low_ref = (moved, still_ref) if second else (still_ref, moved)

    def halves(quarter, w, grads, known=False):
        both = pre_buf[quarter].astype(FULL) if known else dot(rows_ref[quarter], w_in[w])
        gate, up = both[:, :units], both[:, units:]
        bend = jax.nn.sigmoid(gate)
        silu = gate * bend
        hidden_grad = dot(low_ref[quarter], w_down[w])
        grads[:, :units] = (hidden_grad * up * bend * (1.0 + gate * (1.0 - bend))).astype(LOW)
        grads[:, units:] = (hidden_grad * silu).astype(LOW)
        return (silu * up).astype(LOW)

    def local(w):
        act = halves(seq, w, in_temp)
        back[...] += dot(in_temp[...], w_in[w], NT)
        if second:
            grad_out[...] += dot(act, w_down[w], NT)

    for copy in loads[:far_from]:
        copy.wait()
    if not second:
        pre_ref()
    hidden[seq] = halves(seq, 0, in_grad.at[seq], not second)
    if second:
        back[...] = dot(in_grad[seq], w_in[0], NT)
        grad_out[...] = after_ref()[...] + dot(hidden[seq], w_down[0], NT)
    for copy in loads[far_from:]:
        copy.wait()
    across = [hop(w_in.at[2], w_in.at[3], mate), hop(w_down.at[2], w_down.at[3], mate)]
    for copy in beside:
        copy.wait()

    if second:

        @pl.loop(1, 4)
        def _(w):
            @pl.when(w == 3)
            def _():
                for copy in across:
                    copy.wait()

            local(w)

    else:
        back[...] = jnp.zeros_like(back)
        local(1)

    to_mate.wait()
    to_x.wait()
    onward = hop(theirs, theirs, mate)

    @pl.loop(0, 3)
    def _(i):
        @pl.when(i == 2)
        def _():
            onward.wait()

        quarter = jnp.where(i == 0, mate_seq, jnp.where(i == 1, far_seq, far_mate))
        hidden[quarter] = halves(quarter, 0, in_grad.at[quarter], not second)

    flat = lambda ref: ref[...].reshape(4 * length, ref.shape[2])
    share = width // SHARES

    def finish(i, term):
        for j in range(SHARES):
            rows = term[j * share : (j + 1) * share]
            if prev_ref is not None:
                rows = rows + prev_ref()[i, j // 2, j % 2].astype(FULL)
            weight_out[i, j // 2, j % 2] = rows.astype(LOW)
        early(weight_out.at[i], weight_hbm.at[i])

    def half(columns):
        return in_grad[:, :, columns].reshape(4 * length, units)

    if second:
        both = dot(flat(rows_ref), flat(in_grad), TN)
        finish(0, both[:, :units])
        finish(1, both[:, units:])
    else:
        finish(0, dot(flat(rows_ref), half(slice(0, units)), TN))
        if reduce:
            first_y = hop(weight_out.at[0, :, 1 - lax.rem(dp, 2)], y_part, y_mate)
        finish(1, dot(flat(rows_ref), half(slice(units, 2 * units)), TN))
        back[...] += dot(in_grad[seq], w_in[0], NT)
        for copy in across:
            copy.wait()

        @pl.loop(2, 4)
        def _(w):
            local(w)

    finish(2, dot(flat(low_ref), flat(hidden), TN))
    if second:
        result_out[...] = grad_out[...].astype(LOW)
    sent_back, gain_term = norm_back(after_ref()[...], gains_ref[1:2, :], back[...])
    grad_out[...] = up_ref[...].astype(FULL) + sent_back
    gain_out[...] = jnp.broadcast_to(gain_term, gain_out.shape)
    if reduce:
        first_y.wait()
    early.finish()


def ffn_all_call(stills, second, reduce, *refs):
    refs = refs if second else refs[:1] + refs
    return ffn_all_kernel(second, reduce, *refs[:4], refs[4 : 4 + stills], *refs[4 + stills :])


def ffn_all(second, reduce, upstream, own, after, gains, stills, weights, far, prev=None, pre=None):
    length, width = after.shape
    units = weights[0].shape[1]
    share = width // SHARES
    grads = (3, SHARES // 2, 2, share, units)
    shapes = (
        ((length, width), FULL),
        ((8, width), FULL),
        (grads, LOW),
    )
    if second:
        shapes = (((length, width), LOW),) + shapes
    if reduce:
        shapes = shapes + (((SHARES // 2, share, units), LOW),)
    args = (after, gains) + tuple(stills) + tuple(weights) + (far,)
    specs = [ANYWHERE, VMEM] + [ANYWHERE] * (len(stills) + 4)
    if second:
        args, specs = (upstream, own) + args, [VMEM, VMEM] + specs
    else:
        args, specs = (upstream,) + args, [VMEM] + specs
        args, specs = args + (prev, pre), specs + [ANYWHERE] * 2
    return pl.pallas_call(
        functools.partial(ffn_all_call, len(stills), second, reduce),
        out_shape=tuple(jax.ShapeDtypeStruct(*s) for s in shapes),
        in_specs=specs,
        out_specs=tuple(ANYWHERE if s[0] == grads else VMEM for s in shapes),
        scratch_shapes=[
            pltpu.VMEM((4, width, 2 * units), LOW),
            pltpu.VMEM((4, width, units), LOW),
            pltpu.VMEM((4, length, width), LOW),
            pltpu.VMEM((4, length, width), LOW),
            pltpu.VMEM((4, length, 2 * units), LOW),
            pltpu.VMEM((length, 2 * units), LOW),
            pltpu.VMEM((4, length, units), LOW),
            pltpu.VMEM((length, width), FULL),
            pltpu.VMEM((length, width), FULL),
            pltpu.VMEM((1, 1, 2, 8, 128) if second else grads, LOW),
            pltpu.VMEM((1, 8, 128) if second else pre.shape, LOW),
            pltpu.VMEM(grads, LOW),
            pltpu.SemaphoreType.DMA((3 + len(stills) + 3 * SHARES,)),
            pltpu.SemaphoreType.DMA((3,)),
            pltpu.SemaphoreType.DMA((3,)),
            pltpu.SemaphoreType.DMA((9,)),
            pltpu.SemaphoreType.DMA((9,)),
        ],
        compiler_params=pltpu.CompilerParams(
            collective_id=3 if second else 4, has_side_effects=True, vmem_limit_bytes=60 * 1024 * 1024
        ),
        cost_estimate=cost(30),
        name="ffn_second" if second else "ffn_first_backward",
    )(*args)


def attn_backward_kernel(
    last, after_grad_ref, w_out_ref, mixed_ref, gains_ref, place_ref, log_ref, q_hbm, kv_hbm, trig_hbm,
    res_hbm, normed_hbm, w_key_hbm, w_value_hbm, w_query_hbm, *rest
):
    if last:
        prev, ffn_ref, first_hbm, gain_ref = rest[:3], rest[3], rest[4], rest[5]
        grad_hbm, gain_out, ffn_hbm, share_hbms = rest[6], rest[7], rest[8], rest[9:12]
        rest = rest[12:]
    else:
        prev = (None, None, None)
        grad_hbm, gain_out = rest[:2]
        part_hbms = rest[2:5]
        rest = rest[5:]
    q_buf, kv_buf, trig_buf, res_buf, normed_buf, w_kv_buf, w_query_buf, grad_out, pair_sem, late_sem, early_sem, *rest = rest
    late = iter(late_sem.at[i] for i in range(11))
    q_later, kv_later = Later(q_hbm, q_buf, next(late)), Later(kv_hbm, kv_buf, next(late))
    mixed_grad, delta, kv_grad, query_grad, back, grad_send, grad_recv, send_sem, recv_sem = rest[:9]
    hop = Hops(send_sem, recv_sem)
    seq, dp = lax.axis_index("seq"), lax.axis_index("dp")
    core, chip_x = lax.rem(seq, 2), lax.div(seq, 2)
    mate_seq, far_seq = seq + 1 - 2 * core, lax.rem(seq + 2, 4)
    far_mate = lax.rem(mate_seq + 2, 4)
    mate, x_mate = device(mate_seq, dp), device(far_seq, dp)
    length, width = res_hbm.shape
    stacked = GROUP * length
    kv_width = 2 * KV_HEADS * HEAD_DIM
    parts = rest[9:12]
    if last:
        f_own, f_y_recv, f_a_send, f_a_recv, f_b_send, f_b_recv, gain_recv = rest[12:19]
        prev_bufs = rest[19:22]
        ffn_out, share_outs = rest[22], rest[23:26]
        buffers = [rest[26 + 10 * i : 36 + 10 * i] for i in range(3)]
        row_y, row_z = lax.rem(dp, 2), lax.div(dp, 2)
        low_z, high_z = lax.rem(row_z, 2), lax.div(row_z, 2)
        y_mate = device(seq, dp + 1 - 2 * row_y)
        near_z = device(seq, dp + 2 - 4 * low_z)
        far_z = device(seq, dp + 4 - 8 * high_z)
        cross = device(far_mate, dp)
        greet([mate, x_mate, cross, y_mate, near_z, far_z])
        f_y = [None]
        f_y += [hop(ffn_ref.at[m, :, 1 - row_y], f_y_recv.at[m], y_mate) for m in (1, 2)]
        first_y = Later(first_hbm, f_y_recv.at[0], next(late))
        own_shares = Later(ffn_ref.at[:, :, row_y], f_own, next(late))
        prev = [Later(src, dst, next(late)) for src, dst in zip(prev, prev_bufs)]
    else:
        greet([mate, x_mate])
    early = Early(early_sem)
    trig = Later(trig_hbm, trig_buf, next(late))
    normed_ref = Later(normed_hbm, normed_buf, next(late))
    w_query = Later(w_query_hbm, w_query_buf, next(late))
    w_kv = LaterPairs(w_key_hbm, w_value_hbm, w_kv_buf, pair_sem)
    res_ref = Later(res_hbm, res_buf, next(late))

    def near_fill(load, a_send):
        for h in range(2):
            a_send[h] = load(2 * h + 1 - low_z).astype(LOW)

    def far_fill(load, a_recv, b_send):
        b_send[...] = (load(2 - 2 * high_z + low_z) + a_recv[1 - high_z].astype(FULL)).astype(LOW)

    def z_total(load, a_recv, b_recv):
        return load(row_z) + a_recv[high_z].astype(FULL) + b_recv[...].astype(FULL)

    def f_load(m):
        return lambda z: own_shares()[m, z].astype(FULL) + f_y_recv[m, z].astype(FULL)

    if last:
        f_nears = [hop(f_a_send.at[m], f_a_recv.at[m], near_z, start=False) for m in range(3)]
        f_fars = [hop(f_b_send.at[m], f_b_recv.at[m], far_z, start=False) for m in range(3)]

    def f_near(m):
        own_shares()
        if m == 0:
            first_y()
        else:
            f_y[m].wait()
        near_fill(f_load(m), f_a_send.at[m])
        f_nears[m].start()

    def f_far(m):
        f_nears[m].wait()
        far_fill(f_load(m), f_a_recv.at[m], f_b_send.at[m])
        f_fars[m].start()

    def f_finish(m):
        f_fars[m].wait()
        ffn_out[m] = z_total(f_load(m), f_a_recv.at[m], f_b_recv.at[m])
        early(ffn_out.at[m], ffn_hbm.at[m])

    quarter = lambda x, c: pl.ds(pl.multiple_of(64 * x + ROWS_PAD * c, ROWS_PAD), ROWS_PAD)

    def core_start(i):
        core_recv = buffers[i][0]
        return [hop(parts[i].at[:, quarter(x, 1 - core)], core_recv.at[x], mate) for x in range(2)]

    def x_make(i):
        return hop(*buffers[i][1:3], x_mate, start=False)

    def x_start(i, copies, x_copy):
        core_recv, x_send, x_recv = buffers[i][:3]
        for copy in copies:
            copy.wait()
        joint = parts[i][:, quarter(1 - chip_x, core)].astype(FULL) + core_recv[1 - chip_x].astype(FULL)
        x_send[...] = joint.astype(LOW)
        x_copy.start()
        return x_copy

    def y_start(i, copy):
        core_recv, x_send, x_recv, own, y_recv = buffers[i][:5]
        joint = parts[i][:, quarter(chip_x, core)].astype(FULL) + core_recv[chip_x].astype(FULL)
        copy.wait()
        own[...] = (joint + x_recv[...].astype(FULL)).astype(LOW).reshape(own.shape)
        return hop(own.at[:, 1 - row_y], y_recv, y_mate)

    def part_load(i):
        own, y_recv = buffers[i][3:5]
        return lambda z: own[z, row_y].astype(FULL) + y_recv[z].astype(FULL)

    def z_start(i, copy):
        copy.wait()
        near_fill(part_load(i), buffers[i][5])
        return hop(*buffers[i][5:7], near_z)

    def z_next(i, copy):
        copy.wait()
        far_fill(part_load(i), *buffers[i][6:8])
        return hop(*buffers[i][7:9], far_z)

    def share_start(i, copy):
        gathered = buffers[i][9]
        copy.wait()
        gathered[seq] = z_total(part_load(i), buffers[i][6], buffers[i][8]).astype(LOW)
        mine = gathered.at[seq]
        return [hop(mine, mine, target) for target in (x_mate, cross, mate)]

    def share_finish(i, copies):
        gathered = buffers[i][9]
        for copy in copies:
            copy.wait()
        for s in range(4):
            share_outs[i][s * ROWS_PAD : (s + 1) * ROWS_PAD] = gathered[s].astype(FULL)
        early(share_outs[i], share_hbms[i])

    def weight(i, left, right):
        term = dot(left, right, TN)
        share = width // SHARES
        for j in range(SHARES):
            rows = term[j * share : (j + 1) * share]
            if prev[i] is not None:
                rows = rows + prev[i]()[j, :share].astype(FULL)
            parts[i][j, :share] = rows.astype(LOW)
        if not last:
            early(parts[i], part_hbms[i])

    low_grad = after_grad_ref[...].astype(LOW)
    mixed_back = dot(low_grad, w_out_ref[...], NT)
    lane = lax.broadcasted_iota(jnp.int32, (length, 128), 1)
    for pair in range((HEADS + 1) // 2):
        span = min(128, HEADS * HEAD_DIM - pair * 128)
        part = mixed_back[:, pair * 128 : pair * 128 + span]
        if span < 128:
            part = jnp.concatenate([part, part], axis=1)
        else:
            mixed_grad[2 * pair + 1] = jnp.where(lane >= HEAD_DIM, part, 0.0).astype(LOW)
        mixed_grad[2 * pair] = jnp.where(lane >= HEAD_DIM, pltpu.roll(part, 64, 1), 0.0).astype(LOW)
    product = mixed_back.astype(LOW).astype(FULL) * mixed_ref[...].astype(FULL)
    high = product.astype(LOW)
    rest_low = (product - high.astype(FULL)).astype(LOW)
    head = lax.broadcasted_iota(jnp.int32, (16, HEADS * HEAD_DIM), 0)
    column = lax.broadcasted_iota(jnp.int32, (16, HEADS * HEAD_DIM), 1)
    pick = jnp.where(lax.div(column, HEAD_DIM) == head, 1.0, 0.0).astype(LOW)
    sums = dot(pick, high, NT) + dot(pick, rest_low, NT)
    for g in range(KV_HEADS):
        delta[g] = jnp.concatenate([sums[3 * g + i : 3 * g + i + 1] for i in range(GROUP)], axis=1)
    query_grad[...] = jnp.zeros_like(query_grad)
    weight(0, mixed_ref[...], low_grad)
    if last:
        o_core = core_start(0)
        f_near(0)
        o_x = x_make(0)

    start, place = place_ref[0:1, :], place_ref[1:2, :]
    q_ref, kv_ref = q_later(), kv_later()

    def attend(block, g):
        columns = pl.ds(pl.multiple_of(g * 128, 128), 128)
        kv_g = kv_ref[block, :, columns]
        q_g = q_ref[pl.ds(3 * g, 3)].reshape(stacked, 128)
        out_g = mixed_grad[pl.ds(3 * g, 3)].reshape(stacked, 128)
        scores = dot(kv_g, q_g, NT)
        key = lax.broadcasted_iota(jnp.int32, (length, stacked), 0) + block * length
        weights = jnp.where((key >= start) & (key <= place), jnp.exp(scores - log_ref[g]), 0.0)
        probs_grad = dot(kv_g, out_g, NT)
        score_grad = (weights * (probs_grad - delta[g])).astype(LOW)
        kv_grad[block, :, columns] = dot(weights.astype(LOW), out_g) + dot(score_grad, q_g)
        query_grad[g] += dot(kv_g, score_grad, TN)[:HEAD_DIM]

    joint = hop(grad_send.at[0], grad_recv.at[0], mate, start=False)
    across = hop(grad_send.at[1], grad_recv.at[1], x_mate, start=False)
    beside = hop(grad_send.at[2], grad_recv.at[2], mate, start=False)

    @pl.loop(0, 4)
    def _(step):
        block = jnp.where(
            step == 0, far_mate, jnp.where(step == 1, far_seq, jnp.where(step == 2, mate_seq, seq))
        )

        @pl.when(block <= seq)
        def _():
            @pl.loop(0, KV_HEADS)
            def _(g):
                attend(block, g)

        @pl.when(block > seq)
        def _():
            kv_grad[block] = jnp.zeros_like(kv_grad[block])

        @pl.when(step == 0)
        def _():
            grad_send[0] = kv_grad[far_mate].astype(LOW)
            joint.start()
            if last:
                x_start(0, o_core, o_x)

        @pl.when(step == 1)
        def _():
            joint.wait()
            grad_send[1] = (kv_grad[far_seq] + grad_recv[0].astype(FULL)).astype(LOW)
            across.start()

        @pl.when(step == 2)
        def _():
            grad_send[2] = kv_grad[mate_seq].astype(LOW)
            beside.start()
            if last:
                f_far(0)
                f_near(1)

    trig_ref = trig()
    heads = []
    for g in range(KV_HEADS):
        turned = query_grad[g].T * SCALE
        heads += [turned[i * length : (i + 1) * length] for i in range(GROUP)]
    for pair in range((HEADS + 1) // 2):
        part = jnp.concatenate([heads[2 * pair], heads[min(2 * pair + 1, HEADS - 1)]], axis=1)
        turned = (part * trig_ref[0] - swap_halves(part) * trig_ref[1]).astype(LOW)
        at = kv_width + pair * 128
        stop = min(at + 128, kv_width + width)
        back[:, at:stop] = turned[:, : stop - at]
    weight(1, normed_ref()[...], back[:, kv_width:])
    if last:
        q_core = core_start(1)
        o_y = y_start(0, o_x)
    normed_grad = dot(back[:, kv_width:], w_query()[...], NT)
    if last:
        q_x = x_start(1, q_core, x_make(1))

    across.wait()
    beside.wait()
    own = kv_grad[seq] + grad_recv[1].astype(FULL) + grad_recv[2].astype(FULL)
    for g in range(KV_HEADS):
        part = own[:, g * 128 : (g + 1) * 128]
        back[:, g * 128 : (g + 1) * 128] = (part * trig_ref[2] - swap_halves(part) * trig_ref[3]).astype(LOW)
    weight(2, normed_ref()[...], back[:, :kv_width])
    if last:
        kv_core = core_start(2)
        f_far(1)
        f_near(2)
        kv_x = x_start(2, kv_core, x_make(2))
    normed_grad = normed_grad + dot(back[:, :kv_width], w_kv()[...])
    sent_back, gain_term = norm_back(res_ref()[...].astype(FULL), gains_ref[0:1, :], normed_grad)
    grad_out[...] = after_grad_ref[...] + sent_back
    early(grad_out, grad_hbm)
    if not last:
        gain_out[...] = jnp.broadcast_to(gain_term, gain_out.shape)
        early.finish()
        return

    row = lax.broadcasted_iota(jnp.int32, gain_out.shape, 0)
    gain_out[...] = gain_ref[...] + jnp.where(row == 0, gain_term, 0.0)
    partners = [mate, x_mate, y_mate, near_z, far_z]
    gain_hop = lambda n: hop(gain_out, gain_recv.at[n], partners[n])

    def gain_add(n, copy):
        copy.wait()
        gain_out[...] += gain_recv[n]

    gain_copy = gain_hop(0)
    f_finish(0)
    o_z = z_start(0, o_y)
    gain_add(0, gain_copy)
    gain_copy = gain_hop(1)
    q_y = y_start(1, q_x)
    f_far(2)
    f_finish(1)
    o_z = z_next(0, o_z)
    gain_add(1, gain_copy)
    gain_copy = gain_hop(2)
    kv_y = y_start(2, kv_x)
    q_z = z_start(1, q_y)
    gain_add(2, gain_copy)
    gain_copy = gain_hop(3)
    o_s = share_start(0, o_z)
    kv_z = z_start(2, kv_y)
    q_z = z_next(1, q_z)
    gain_add(3, gain_copy)
    gain_copy = gain_hop(4)
    f_finish(2)
    kv_z = z_next(2, kv_z)
    q_s = share_start(1, q_z)
    gain_add(4, gain_copy)
    kv_s = share_start(2, kv_z)
    share_finish(0, o_s)
    share_finish(1, q_s)
    share_finish(2, kv_s)
    early.finish()


def attn_backward(after_grad, residual, normed, gains, q, kv, log_total, mixed, attn_weights, trig, place, final=None):
    length, width = residual.shape
    kv_width = 2 * KV_HEADS * HEAD_DIM
    last = final is not None
    key_t, value_t, w_query, w_out = attn_weights
    args = (after_grad, w_out, mixed, gains, place, log_total, q, kv, trig, residual, normed, key_t, value_t, w_query)
    specs = [VMEM] * 6 + [ANYWHERE] * 8
    out_specs = (ANYWHERE, VMEM)
    shapes = (((length, width), FULL), ((8, width), FULL))
    sizes = (width, width, kv_width)
    part_shapes = [((SHARES, 4 * ROWS_PAD, c), LOW) for c in sizes]
    scratch = [
        pltpu.VMEM(q.shape, LOW),
        pltpu.VMEM(kv.shape, LOW),
        pltpu.VMEM(trig.shape, FULL),
        pltpu.VMEM((length, width), residual.dtype),
        pltpu.VMEM((length, width), LOW),
        pltpu.VMEM((kv_width, width), LOW),
        pltpu.VMEM(w_query.shape, LOW),
        pltpu.VMEM((length, width), FULL),
        pltpu.SemaphoreType.DMA((2 * KV_HEADS,)),
        pltpu.SemaphoreType.DMA((11,)),
        pltpu.SemaphoreType.DMA((7,)),
        pltpu.VMEM((HEADS, length, 128), LOW),
        pltpu.VMEM((KV_HEADS, 1, GROUP * length), FULL),
        pltpu.VMEM((4, length, kv_width), FULL),
        pltpu.VMEM((KV_HEADS, HEAD_DIM, GROUP * length), FULL),
        pltpu.VMEM((length, kv_width + width), LOW),
        pltpu.VMEM((3, length, kv_width), LOW),
        pltpu.VMEM((3, length, kv_width), LOW),
    ]
    hops = 3
    if last:
        share, hidden = final[3].shape[3:]
        args = args + tuple(final)
        specs = specs + [ANYWHERE] * 5 + [VMEM]
        shapes = shapes + (((3, share, hidden), FULL),) + tuple(((4 * ROWS_PAD, c), FULL) for c in sizes)
        hops = 3 + 2 + 6 + 5 + 3 * (2 + 1 + 1 + 2 + 3)
        scratch += [pltpu.SemaphoreType.DMA((hops,))] * 2
        out_specs = out_specs + (ANYWHERE,) * 4
        scratch += [pltpu.VMEM(*s) for s in part_shapes]
        scratch += [
            pltpu.VMEM((3, 4, share, hidden), LOW),
            pltpu.VMEM((3, 4, share, hidden), LOW),
            pltpu.VMEM((3, 2, share, hidden), LOW),
            pltpu.VMEM((3, 2, share, hidden), LOW),
            pltpu.VMEM((3, share, hidden), LOW),
            pltpu.VMEM((3, share, hidden), LOW),
            pltpu.VMEM((5, 8, width), FULL),
        ]
        scratch += [pltpu.VMEM(*s) for s in part_shapes]
        scratch += [pltpu.VMEM(*s) for s in shapes[2:]]
        for c in sizes:
            scratch += [
                pltpu.VMEM((2, SHARES, ROWS_PAD, c), LOW),
                pltpu.VMEM((SHARES, ROWS_PAD, c), LOW),
                pltpu.VMEM((SHARES, ROWS_PAD, c), LOW),
                pltpu.VMEM((4, 2, ROWS_PAD, c), LOW),
                pltpu.VMEM((4, ROWS_PAD, c), LOW),
                pltpu.VMEM((2, ROWS_PAD, c), LOW),
                pltpu.VMEM((2, ROWS_PAD, c), LOW),
                pltpu.VMEM((ROWS_PAD, c), LOW),
                pltpu.VMEM((ROWS_PAD, c), LOW),
                pltpu.VMEM((4, ROWS_PAD, c), LOW),
            ]
    else:
        shapes, out_specs = shapes + tuple(part_shapes), out_specs + (ANYWHERE,) * 3
        scratch += [pltpu.SemaphoreType.DMA((hops,))] * 2
        scratch += [pltpu.VMEM(*s) for s in part_shapes]
    return pl.pallas_call(
        functools.partial(attn_backward_kernel, last),
        out_shape=tuple(jax.ShapeDtypeStruct(*s) for s in shapes),
        in_specs=specs,
        out_specs=out_specs,
        scratch_shapes=scratch,
        compiler_params=pltpu.CompilerParams(
            collective_id=6 if last else 5, has_side_effects=True, vmem_limit_bytes=60 * 1024 * 1024
        ),
        cost_estimate=cost(95 if last else 40),
        name="attn_backward_last" if last else "attn_backward",
    )(*args)


def split_pairs(grads):
    rows = grads.shape[0]
    pairs = grads.reshape(rows, KV_HEADS, 2, HEAD_DIM)
    return pairs[:, :, 0].reshape(rows, -1), pairs[:, :, 1].reshape(rows, -1)


def on_device(
    tokens,
    seg_ids,
    positions,
    attn_gain,
    w_query,
    w_key,
    w_value,
    w_out,
    ffn_gain,
    w_gate,
    w_up,
    w_down,
    cotangent,
):
    width = tokens.shape[2]
    trig, place = prepare(positions[0])
    attn_weights = (w_key.T, w_value.T, w_query, w_out)
    gains = jnp.pad(jnp.stack([attn_gain, ffn_gain]), ((0, 6), (0, 0)))
    whole = lax.axis_size("dp") != SHARES
    share = width // SHARES
    own_weights = (w_gate, w_up, w_down.T)

    def over_x(value):
        return lax.ppermute(value, "seq", [(s, (s + 2) % 4) for s in range(4)])

    def over_rows_piece(value, d):
        return lax.dynamic_slice_in_dim(value, jnp.minimum(d * PIECE, width - PIECE), PIECE, axis=0)

    if whole:
        theirs = [over_x(w) for w in own_weights]
        far = jnp.stack([jnp.concatenate([over_rows_piece(w, d) for w in theirs]) for d in range(SHARES)])
    else:
        piece = jnp.concatenate([over_rows_piece(w, lax.axis_index("dp")) for w in own_weights])
        far = lax.all_gather(over_x(piece), "dp", axis=0)

    results = forward(tokens[0], gains, place, cotangent[0], attn_weights, trig, own_weights)
    first, (rows_all, pre_all, residual), results = results[:KEPT], results[KEPT : KEPT + 3], results[KEPT + 3 :]
    second, normed_two, low_halves = results[:KEPT], results[KEPT], results[KEPT + 1 :]
    output, after_grad, ffn_gain_term, ffn_grads = ffn_all(
        True, False, cotangent[0], normed_two, second[5], gains, low_halves, own_weights, far
    )

    def attn_args(after_grad, residual, kept):
        normed, q, kv, log_total, mixed = kept[:5]
        return (after_grad, residual, normed, gains, q, kv, log_total, mixed, attn_weights, trig, place)

    upstream, attn_gain_term, *parts = attn_backward(*attn_args(after_grad, residual, second))
    gain_grads = jnp.stack([attn_gain_term[0], ffn_gain_term[0]])
    after_grad, ffn_gain_term, ffn_grads, *first_y = ffn_all(
        False, not whole, upstream, None, first[5], gains, (rows_all,), own_weights, far, ffn_grads, pre_all
    )
    args = attn_args(after_grad, tokens[0], first)
    if whole:
        upstream, attn_gain_term, *terms = attn_backward(*args)
        gain_grads = gain_grads + jnp.stack([attn_gain_term[0], ffn_gain_term[0]])
        parts = [part.astype(FULL) + term.astype(FULL) for part, term in zip(parts, terms)]
    else:
        gain_grads = gain_grads + jnp.stack([jnp.zeros_like(attn_gain), ffn_gain_term[0]])
        final = (*parts, ffn_grads, *first_y, jnp.pad(gain_grads, ((0, 6), (0, 0))))
        upstream, gain_all, ffn_share, *shares = attn_backward(*args, final)
    if whole:

        def over_rows(grads, dim):
            grads = lax.psum_scatter(grads.astype(LOW), "dp", scatter_dimension=dim, tiled=True)
            return grads.astype(FULL)

        def over_all(grads, dim):
            return lax.psum(over_rows(grads, dim).astype(LOW), "seq").astype(FULL)

        shares = [over_all(part[:, :share].reshape(width, -1), 0) for part in parts]
        ffn_share = over_rows(ffn_grads.reshape(3, width, -1), 1)
        own_gains = over_all(gain_grads, 1)
    else:
        shares = [part[:share] for part in shares]
        own_gains = lax.dynamic_slice_in_dim(gain_all, lax.axis_index("dp") * share, share, axis=1)
    key_share, value_share = split_pairs(shares[2])
    return (
        output[None],
        upstream[None],
        own_gains[0],
        shares[1],
        key_share,
        value_share,
        shares[0],
        own_gains[1],
        ffn_share[0],
        ffn_share[1],
        ffn_share[2].T,
    )


def solution(mesh):
    in_specs = (
        P("dp", "seq", None),
        P("dp", "seq"),
        P("dp", "seq"),
        P(),
        P(),
        P(),
        P(),
        P(),
        P(),
        P(None, "seq"),
        P(None, "seq"),
        P("seq", None),
        P("dp", "seq", None),
    )
    out_specs = (
        P("dp", "seq", None),
        P("dp", "seq", None),
        P("dp"),
        P("dp", None),
        P("dp", None),
        P("dp", None),
        P("dp", None),
        P("dp"),
        P("dp", "seq"),
        P("dp", "seq"),
        P("seq", "dp"),
    )
    return jax.shard_map(
        on_device, mesh=mesh, in_specs=in_specs, out_specs=out_specs, check_vma=False
    )
```

```python
import functools

import jax
import jax.numpy as jnp
from jax import lax
from jax.experimental import pallas as pl
from jax.experimental.pallas import tpu as pltpu
from jax.sharding import PartitionSpec as P

MESH_ID = pl.DeviceIdType.MESH
HEADS = 15
KV_HEADS = 5
GROUP = 3
HEAD_DIM = 64
EPSILON = 1e-05
THETA = 10000.0
CHUNKS = 2
SHARES = 8
ROWS_PAD = 32
PIECE = 128
MASKED = -1e30
LOW = jnp.bfloat16
FULL = jnp.float32
SCALE = HEAD_DIM ** (-0.5)
NT = (((1,), (1,)), ((), ()))
TN = (((0,), (0,)), ((), ()))


def device(seq_pos, dp_pos):
    return {"seq": seq_pos, "dp": dp_pos}


def send(src, dst, send_sem, recv_sem, target, start=True):
    copy = pltpu.make_async_remote_copy(
        src_ref=src,
        dst_ref=dst,
        send_sem=send_sem,
        recv_sem=recv_sem,
        device_id=target,
        device_id_type=MESH_ID,
    )
    if start:
        copy.start()
    return copy


class Hops:
    def __init__(self, send_sem, recv_sem):
        self.send_sem, self.recv_sem, self.used = send_sem, recv_sem, 0

    def __call__(self, src, dst, target, start=True):
        index, self.used = self.used, self.used + 1
        return send(src, dst, self.send_sem.at[index], self.recv_sem.at[index], target, start)


class Later:
    def __init__(self, src, dst, sem):
        self.copy, self.dst, self.waited = pltpu.make_async_copy(src, dst, sem), dst, False
        self.copy.start()

    def __call__(self):
        if not self.waited:
            self.copy.wait()
            self.waited = True
        return self.dst


class Early:
    def __init__(self, sem):
        self.sem, self.copies = sem, []

    def __call__(self, src, dst, start=True):
        self.copies.append(pltpu.make_async_copy(src, dst, self.sem.at[len(self.copies)]))
        if start:
            self.copies[-1].start()
        return self.copies[-1]

    def finish(self):
        for copy in self.copies:
            copy.wait()


class LaterPairs:
    def __init__(self, key_hbm, value_hbm, dst, sem):
        self.copies, self.dst = [], dst
        for h in range(2 * KV_HEADS):
            src = (key_hbm, value_hbm)[h % 2].at[pl.ds(h // 2 * HEAD_DIM, HEAD_DIM)]
            self.copies.append(pltpu.make_async_copy(src, dst.at[pl.ds(h * HEAD_DIM, HEAD_DIM)], sem.at[h]))
            self.copies[-1].start()

    def __call__(self):
        for copy in self.copies:
            copy.wait()
        self.copies = []
        return self.dst


def greet(targets):
    barrier = pltpu.get_barrier_semaphore()
    for target in targets:
        pl.semaphore_signal(barrier, inc=1, device_id=target, device_id_type=MESH_ID)
    pl.semaphore_wait(barrier, len(targets))


def dot(left, right, dims=None):
    if dims is None:
        return jnp.dot(left, right, preferred_element_type=FULL)
    return lax.dot_general(left, right, dims, preferred_element_type=FULL)


def cost(microseconds):
    return pl.CostEstimate(flops=int(microseconds * 1.15e9), bytes_accessed=1 << 20, transcendentals=0)


def inverse_rms(value):
    return lax.rsqrt(jnp.mean(value * value, axis=-1, keepdims=True) + EPSILON)


def swap_halves(value):
    lane = lax.broadcasted_iota(jnp.int32, value.shape, 1)
    first = (lane & (HEAD_DIM // 2)) == 0
    return jnp.where(first, pltpu.roll(value, 96, 1), pltpu.roll(value, 32, 1))


VMEM = pl.BlockSpec(memory_space=pltpu.VMEM)
ANYWHERE = pl.BlockSpec(memory_space=pl.ANY)


def prepare(positions):
    length = positions.shape[0]
    frequency = THETA ** (-(jnp.arange(HEAD_DIM // 2, dtype=FULL) * 2.0 / HEAD_DIM))
    angles = positions.astype(FULL)[:, None] * frequency
    cos, sin = jnp.cos(angles), jnp.sin(angles)
    one, none = jnp.ones((length, HEAD_DIM), FULL), jnp.zeros((length, HEAD_DIM), FULL)
    trig = jnp.stack(
        [
            jnp.concatenate([cos, cos, cos, cos], 1),
            jnp.concatenate([-sin, sin, -sin, sin], 1),
            jnp.concatenate([cos, cos, one], 1),
            jnp.concatenate([-sin, sin, none], 1),
        ]
    )
    own = lax.axis_index("seq") * length + jnp.arange(length, dtype=jnp.int32)
    place = jnp.stack([jnp.tile(own - positions, GROUP), jnp.tile(own, GROUP)])
    place = jnp.pad(place, ((0, 6), (0, 0)))
    return trig, place


def norm_back(value, gain, grad):
    inverse = inverse_rms(value)
    weighted = grad * gain
    inner = jnp.mean(weighted * value, axis=-1, keepdims=True)
    back = inverse * weighted - value * (inverse * inverse * inverse) * inner
    return back, jnp.sum(grad * value * inverse, axis=0, keepdims=True)


KEPT = 6
CUT = 3


def forward_kernel(
    tokens_ref, gains_ref, place_ref, cotangent_hbm, w_key_hbm, w_value_hbm, w_query_hbm, w_out_hbm, trig_hbm,
    w_gate_hbm, w_up_hbm, w_down_hbm, *rest
):
    first_hbm, (rows_hbm, pre_hbm, res_hbm), rest = rest[:KEPT], rest[KEPT : KEPT + 3], rest[KEPT + 3 :]
    second_hbm, two_hbm, extra_outs, rest = rest[:KEPT], rest[KEPT], rest[KEPT + 1 : KEPT + 3], rest[KEPT + 3 :]
    first, second, rest = rest[:KEPT], rest[KEPT : 2 * KEPT], rest[2 * KEPT :]
    (
        w_kv_buf, w_query_buf, w_out_buf, trig_buf, w_gate_buf, w_up_buf, w_down_buf,
        two, rows, pre, res, peak, total, acc, mate_send, mate_recv, x_send, x_recv, own_far,
        pair_sem, late_sem, early_sem, send_sem, recv_sem,
    ) = rest
    w_kv = LaterPairs(w_key_hbm, w_value_hbm, w_kv_buf, pair_sem)
    trig, w_query, w_out, w_gate, w_up, w_down = [
        Later(src, dst, late_sem.at[i])
        for i, (src, dst) in enumerate(
            (
                (trig_hbm, trig_buf), (w_query_hbm, w_query_buf), (w_out_hbm, w_out_buf),
                (w_gate_hbm, w_gate_buf), (w_up_hbm, w_up_buf), (w_down_hbm, w_down_buf),
            )
        )
    ]
    early, hop = Early(early_sem), Hops(send_sem, recv_sem)
    seq, dp = lax.axis_index("seq"), lax.axis_index("dp")
    core = lax.rem(seq, 2)
    mate_seq, far_seq = seq + 1 - 2 * core, lax.rem(seq + 2, 4)
    far_mate = lax.rem(mate_seq + 2, 4)
    mate, x_mate = device(mate_seq, dp), device(far_seq, dp)
    length = tokens_ref.shape[0]
    stacked = GROUP * length
    start, place = place_ref[0:1, :], place_ref[1:2, :]
    step = length // CHUNKS
    part = lambda k: pl.ds(k * step, step)

    def attention(residual_ref, buffers, hbm, extra_ref, extra_out, meet):
        normed, q, kv, log_total, mixed, after = buffers
        residual = residual_ref[...].astype(FULL)
        normed[...] = (residual * inverse_rms(residual) * gains_ref[0:1, :]).astype(LOW)
        early(normed, hbm[0])
        kv_pre = dot(normed[...], w_kv()[...], NT)
        trig_ref = trig()
        for g in range(KV_HEADS):
            piece = kv_pre[:, g * 128 : (g + 1) * 128]
            turned = piece * trig_ref[2] + swap_halves(piece) * trig_ref[3]
            kv[seq, :, g * 128 : (g + 1) * 128] = turned.astype(LOW)
        if meet:
            greet([mate, x_mate])
        spans = (pl.ds(0, CUT * 128), pl.ds(CUT * 128, (KV_HEADS - CUT) * 128))
        to_x = [hop(kv.at[seq, :, s], kv.at[seq, :, s], x_mate) for s in spans]
        to_mate = hop(kv.at[seq], kv.at[seq], mate)
        onward = [hop(kv.at[far_seq, :, s], kv.at[far_seq, :, s], mate, start=False) for s in spans]
        mine, theirs = extra_out.at[seq], extra_out.at[far_seq]
        extra = [early(extra_ref, mine, start=False)]
        extra += [hop(extra_ref, mine, target, start=False) for target in (x_mate, mate)]
        kv_keep = early(kv, hbm[2], start=False)
        q_pre = dot(normed[...], w_query()[...])
        lane = lax.broadcasted_iota(jnp.int32, (length, 128), 1)
        for pair in range((HEADS + 1) // 2):
            width = min(128, HEADS * HEAD_DIM - pair * 128)
            piece = q_pre[:, pair * 128 : pair * 128 + width]
            if width < 128:
                piece = jnp.concatenate([piece, piece], axis=1)
            turned = (piece * trig_ref[0] + swap_halves(piece) * trig_ref[1]) * SCALE
            q[2 * pair] = jnp.where(lane < HEAD_DIM, turned, 0.0).astype(LOW)
            if width == 128:
                q[2 * pair + 1] = jnp.where(lane < HEAD_DIM, pltpu.roll(turned, 64, 1), 0.0).astype(LOW)
        early(q, hbm[1])

        def attend(block, g):
            kv_g = kv[block, :, pl.ds(pl.multiple_of(g * 128, 128), 128)]
            q_g = q[pl.ds(3 * g, 3)].reshape(stacked, 128)
            scores = dot(kv_g, q_g, NT)
            key = lax.broadcasted_iota(jnp.int32, (length, stacked), 0) + block * length
            scores = jnp.where((key >= start) & (key <= place), scores, MASKED)
            new_peak = jnp.maximum(peak[g], jnp.max(scores, axis=0, keepdims=True))
            weights = jnp.exp(scores - new_peak)
            fade = jnp.exp(peak[g] - new_peak)
            total[g] = jnp.sum(weights, axis=0, keepdims=True) + fade * total[g]
            acc[g] = dot(kv_g, weights.astype(LOW), TN)[HEAD_DIM:] + fade * acc[g]
            peak[g] = new_peak

        peak[...] = jnp.full_like(peak, MASKED)
        total[...] = jnp.zeros_like(total)
        acc[...] = jnp.zeros_like(acc)

        @pl.loop(0, 6)
        def _(turn):
            @pl.when(turn == 1)
            def _():
                to_mate.wait()

            @pl.when(turn == 2)
            def _():
                to_x[0].wait()
                onward[0].start()
                for copy in extra:
                    copy.start()

            @pl.when(turn == 3)
            def _():
                onward[0].wait()

            @pl.when(turn == 4)
            def _():
                to_x[1].wait()
                onward[1].start()

            @pl.when(turn == 5)
            def _():
                onward[1].wait()
                kv_keep.start()

            block = jnp.where(
                turn == 0, seq, jnp.where(turn == 1, mate_seq, jnp.where(lax.rem(turn, 2) == 0, far_seq, far_mate))
            )
            low = jnp.where(turn < 4, 0, CUT)
            high = jnp.where((turn == 2) | (turn == 3), CUT, KV_HEADS)

            @pl.when(block <= seq)
            def _():
                @pl.loop(low, high)
                def _(g):
                    attend(block, g)

        for g in range(KV_HEADS):
            heads = (acc[g] / total[g]).T.astype(LOW)
            log_total[g] = peak[g] + jnp.log(total[g])
            for i in range(GROUP):
                h = GROUP * g + i
                mixed[:, h * HEAD_DIM : (h + 1) * HEAD_DIM] = heads[i * length : (i + 1) * length]
        early(log_total, hbm[3])
        early(mixed, hbm[4])
        extra[1].wait()
        return hop(theirs, theirs, mate), extra[2]

    def project(residual_ref, buffers, rows_of, two_ref):
        mixed, after = buffers[4:]
        value = residual_ref[rows_of].astype(FULL) + dot(mixed[rows_of], w_out()[...])
        after[rows_of] = value
        two_ref[rows_of] = (value * inverse_rms(value) * gains_ref[1:2, :]).astype(LOW)

    waits = attention(tokens_ref, first, first_hbm, cotangent_hbm.at[pl.ds(0, step)], extra_outs[0], True)

    to_x = []
    for k in range(CHUNKS):
        project(tokens_ref, first, part(k), rows.at[seq])
        to_x.append(hop(rows.at[seq, part(k)], rows.at[seq, part(k)], x_mate))
    to_mate = hop(rows.at[seq], rows.at[seq], mate)
    early(first[5], first_hbm[5])
    for copy in waits:
        copy.wait()
    w_gate_ref, w_up_ref, w_down_ref = w_gate(), w_up(), w_down()
    units = w_gate_ref.shape[1]

    def ffn(quarter, rows_of):
        block = rows[quarter, rows_of]
        gate = dot(block, w_gate_ref[...])
        up = dot(block, w_up_ref[...])
        pre[quarter, rows_of, :units] = gate.astype(LOW)
        pre[quarter, rows_of, units:] = up.astype(LOW)
        hidden = (gate * jax.nn.sigmoid(gate) * up).astype(LOW)
        return dot(hidden, w_down_ref[...], NT)

    everything = pl.ds(0, length)
    res[...] = first[5][...] + ffn(seq, everything)
    to_mate.wait()
    mate_send[0] = ffn(mate_seq, everything).astype(LOW)
    back = hop(mate_send.at[0], mate_recv.at[0], mate)
    last = []
    for k in range(CHUNKS):
        to_x[k].wait()
        onward = hop(rows.at[far_seq, part(k)], rows.at[far_seq, part(k)], mate)
        own_far[part(k)] = ffn(far_seq, part(k))
        onward.wait()
        mate_send[1, part(k)] = ffn(far_mate, part(k)).astype(LOW)
        joint = hop(mate_send.at[1, part(k)], mate_recv.at[1, part(k)], mate)
        joint.wait()
        x_send[part(k)] = (own_far[part(k)] + mate_recv[1, part(k)].astype(FULL)).astype(LOW)
        last.append(hop(x_send.at[part(k)], x_recv.at[part(k)], x_mate))
    early(rows, rows_hbm)
    early(pre, pre_hbm)
    back.wait()
    res[...] += mate_recv[0].astype(FULL)
    for k in range(CHUNKS):
        last[k].wait()
        res[part(k)] += x_recv[part(k)].astype(FULL)
    early(res, res_hbm)

    waits = attention(res, second, second_hbm, cotangent_hbm.at[pl.ds(step, step)], extra_outs[1], False)
    project(res, second, everything, two)
    early(second[5], second_hbm[5])
    early(two, two_hbm)
    for copy in waits:
        copy.wait()
    early.finish()


def forward(tokens, gains, place, cotangent, attn_weights, trig, ffn_weights):
    length, width = tokens.shape
    kv_width = 2 * KV_HEADS * HEAD_DIM
    stats = (KV_HEADS, 1, GROUP * length)
    units = ffn_weights[0].shape[1]
    kept = (
        ((length, width), LOW),
        ((HEADS, length, 128), LOW),
        ((4, length, kv_width), LOW),
        (stats, FULL),
        ((length, HEADS * HEAD_DIM), LOW),
        ((length, width), FULL),
    )
    middle = (((4, length, width), LOW), ((4, length, 2 * units), LOW), ((length, width), FULL))
    extra = ((4, length // 2, width), LOW)
    shapes = kept + middle + kept + (((length, width), LOW), extra, extra)
    key_t, value_t, w_query, w_out = attn_weights
    return pl.pallas_call(
        forward_kernel,
        out_shape=tuple(jax.ShapeDtypeStruct(*s) for s in shapes),
        in_specs=[VMEM] * 3 + [ANYWHERE] * 9,
        out_specs=(ANYWHERE,) * len(shapes),
        scratch_shapes=[pltpu.VMEM(*s) for s in kept + kept]
        + [
            pltpu.VMEM((kv_width, width), LOW),
            pltpu.VMEM(w_query.shape, LOW),
            pltpu.VMEM(w_out.shape, LOW),
            pltpu.VMEM(trig.shape, FULL),
        ]
        + [pltpu.VMEM(w.shape, LOW) for w in ffn_weights]
        + [pltpu.VMEM((length, width), LOW)]
        + [pltpu.VMEM(*s) for s in middle]
        + [
            pltpu.VMEM(stats, FULL),
            pltpu.VMEM(stats, FULL),
            pltpu.VMEM((KV_HEADS, HEAD_DIM, GROUP * length), FULL),
            pltpu.VMEM((2, length, width), LOW),
            pltpu.VMEM((2, length, width), LOW),
            pltpu.VMEM((length, width), LOW),
            pltpu.VMEM((length, width), LOW),
            pltpu.VMEM((length, width), FULL),
            pltpu.SemaphoreType.DMA((2 * KV_HEADS,)),
            pltpu.SemaphoreType.DMA((6,)),
            pltpu.SemaphoreType.DMA((18,)),
            pltpu.SemaphoreType.DMA((26,)),
            pltpu.SemaphoreType.DMA((26,)),
        ],
        compiler_params=pltpu.CompilerParams(
            collective_id=0, has_side_effects=True, vmem_limit_bytes=60 * 1024 * 1024
        ),
        cost_estimate=cost(85),
        name="forward",
    )(tokens, gains, place, cotangent, *attn_weights, trig, *ffn_weights)


def ffn_all_kernel(second, reduce, up_ref, own_ref, after_hbm, gains_ref, still_refs, gate_ref, upw_ref, down_ref, far_ref, *rest):
    y_part = prev_hbm = pre_hbm = None
    if second:
        result_out, rest = rest[0], rest[1:]
    else:
        prev_hbm, pre_hbm, gain_ref, *rest = rest
    grad_out, gain_out, weight_hbm, *rest = rest
    if reduce:
        y_part, *rest = rest
    (
        w_in, w_down, still_ref, moved, in_grad, in_temp, hidden, back, after_buf, prev_buf, pre_buf, weight_out,
        load_sem, late_sem, early_sem, send_sem, recv_sem,
    ) = rest
    early = Early(early_sem)
    after_ref = Later(after_hbm, after_buf, late_sem.at[0])
    prev_ref = None if second else Later(prev_hbm, prev_buf, late_sem.at[1])
    pre_ref = None if second else Later(pre_hbm, pre_buf, late_sem.at[2])
    hop = Hops(send_sem, recv_sem)
    seq, dp = lax.axis_index("seq"), lax.axis_index("dp")
    core = lax.rem(seq, 2)
    mate_seq, far_seq = seq + 1 - 2 * core, lax.rem(seq + 2, 4)
    far_mate = lax.rem(mate_seq + 2, 4)
    mate, x_mate = device(mate_seq, dp), device(far_seq, dp)
    length, width = up_ref.shape
    units = gate_ref.shape[1]
    whole = pl.ds(0, width)

    def slots(w, rows):
        return w_in.at[w, rows, :units], w_in.at[w, rows, units:], w_down.at[w, rows]

    loads = []

    def load(src, dst):
        loads.append(pltpu.make_async_copy(src, dst, load_sem.at[len(loads)]))
        loads[-1].start()

    for src, dst in zip((gate_ref, upw_ref, down_ref), slots(0, whole)):
        load(src, dst)
    moved[seq] = own_ref[...].astype(LOW)
    at = 0
    for ref in still_refs:
        load(ref, still_ref.at[:, pl.ds(at, ref.shape[1])])
        at += ref.shape[1]
    far_from = len(loads)
    for d in range(SHARES):
        at = min(d * PIECE, width - PIECE)
        rows = min(PIECE, width - PIECE - at) if d == SHARES - 2 else PIECE
        for i, dst in enumerate(slots(2, pl.ds(at, rows))):
            load(far_ref.at[d, pl.ds(i * PIECE, rows)], dst)
    y_mate = device(seq, dp + 1 - 2 * lax.rem(dp, 2))
    greet([mate, x_mate] + ([y_mate] if reduce else []))
    mine, theirs = moved.at[seq], moved.at[far_seq]
    to_x = hop(mine, mine, x_mate)
    to_mate = hop(mine, mine, mate)
    beside = [hop(src, dst, mate) for src, dst in zip((gate_ref, upw_ref, down_ref), slots(1, whole))]
    rows_ref, low_ref = (moved, still_ref) if second else (still_ref, moved)

    def halves(quarter, w, grads, known=False):
        both = pre_buf[quarter].astype(FULL) if known else dot(rows_ref[quarter], w_in[w])
        gate, up = both[:, :units], both[:, units:]
        bend = jax.nn.sigmoid(gate)
        silu = gate * bend
        hidden_grad = dot(low_ref[quarter], w_down[w])
        grads[:, :units] = (hidden_grad * up * bend * (1.0 + gate * (1.0 - bend))).astype(LOW)
        grads[:, units:] = (hidden_grad * silu).astype(LOW)
        return (silu * up).astype(LOW)

    def local(w):
        act = halves(seq, w, in_temp)
        back[...] += dot(in_temp[...], w_in[w], NT)
        if second:
            grad_out[...] += dot(act, w_down[w], NT)

    for copy in loads[:far_from]:
        copy.wait()
    if not second:
        pre_ref()
    hidden[seq] = halves(seq, 0, in_grad.at[seq], not second)
    if second:
        back[...] = dot(in_grad[seq], w_in[0], NT)
        grad_out[...] = after_ref()[...] + dot(hidden[seq], w_down[0], NT)
    for copy in loads[far_from:]:
        copy.wait()
    across = [hop(w_in.at[2], w_in.at[3], mate), hop(w_down.at[2], w_down.at[3], mate)]
    for copy in beside:
        copy.wait()

    if second:

        @pl.loop(1, 4)
        def _(w):
            @pl.when(w == 3)
            def _():
                for copy in across:
                    copy.wait()

            local(w)

    else:
        back[...] = jnp.zeros_like(back)
        local(1)

    to_mate.wait()
    to_x.wait()
    onward = hop(theirs, theirs, mate)

    @pl.loop(0, 3)
    def _(i):
        @pl.when(i == 2)
        def _():
            onward.wait()

        quarter = jnp.where(i == 0, mate_seq, jnp.where(i == 1, far_seq, far_mate))
        hidden[quarter] = halves(quarter, 0, in_grad.at[quarter], not second)

    flat = lambda ref: ref[...].reshape(4 * length, ref.shape[2])
    share = width // SHARES

    def finish(i, term):
        for j in range(SHARES):
            rows = term[j * share : (j + 1) * share]
            if prev_ref is not None:
                rows = rows + prev_ref()[i, j // 2, j % 2].astype(FULL)
            weight_out[i, j // 2, j % 2] = rows.astype(LOW)
        early(weight_out.at[i], weight_hbm.at[i])

    def half(columns):
        return in_grad[:, :, columns].reshape(4 * length, units)

    if second:
        both = dot(flat(rows_ref), flat(in_grad), TN)
        finish(0, both[:, :units])
        finish(1, both[:, units:])
    else:
        finish(0, dot(flat(rows_ref), half(slice(0, units)), TN))
        if reduce:
            first_y = hop(weight_out.at[0, :, 1 - lax.rem(dp, 2)], y_part, y_mate)
        finish(1, dot(flat(rows_ref), half(slice(units, 2 * units)), TN))
        back[...] += dot(in_grad[seq], w_in[0], NT)
        for copy in across:
            copy.wait()

        @pl.loop(2, 4)
        def _(w):
            local(w)

    finish(2, dot(flat(low_ref), flat(hidden), TN))
    if second:
        result_out[...] = grad_out[...].astype(LOW)
    sent_back, gain_term = norm_back(after_ref()[...], gains_ref[1:2, :], back[...])
    grad_out[...] = up_ref[...].astype(FULL) + sent_back
    row = lax.broadcasted_iota(jnp.int32, gain_out.shape, 0)
    gain_term = jnp.where(row == 1, gain_term, 0.0)
    gain_out[...] = gain_term if second else gain_ref[...] + gain_term
    if reduce:
        first_y.wait()
    early.finish()


def ffn_all_call(stills, second, reduce, *refs):
    refs = refs if second else refs[:1] + refs
    return ffn_all_kernel(second, reduce, *refs[:4], refs[4 : 4 + stills], *refs[4 + stills :])


def ffn_all(second, reduce, upstream, own, after, gains, stills, weights, far, prev=None, pre=None, gain_grads=None):
    length, width = after.shape
    units = weights[0].shape[1]
    share = width // SHARES
    grads = (3, SHARES // 2, 2, share, units)
    shapes = (
        ((length, width), FULL),
        ((8, width), FULL),
        (grads, LOW),
    )
    if second:
        shapes = (((length, width), LOW),) + shapes
    if reduce:
        shapes = shapes + (((SHARES // 2, share, units), LOW),)
    args = (after, gains) + tuple(stills) + tuple(weights) + (far,)
    specs = [ANYWHERE, VMEM] + [ANYWHERE] * (len(stills) + 4)
    if second:
        args, specs = (upstream, own) + args, [VMEM, VMEM] + specs
    else:
        args, specs = (upstream,) + args, [VMEM] + specs
        args, specs = args + (prev, pre, gain_grads), specs + [ANYWHERE] * 2 + [VMEM]
    return pl.pallas_call(
        functools.partial(ffn_all_call, len(stills), second, reduce),
        out_shape=tuple(jax.ShapeDtypeStruct(*s) for s in shapes),
        in_specs=specs,
        out_specs=tuple(ANYWHERE if s[0] == grads else VMEM for s in shapes),
        scratch_shapes=[
            pltpu.VMEM((4, width, 2 * units), LOW),
            pltpu.VMEM((4, width, units), LOW),
            pltpu.VMEM((4, length, width), LOW),
            pltpu.VMEM((4, length, width), LOW),
            pltpu.VMEM((4, length, 2 * units), LOW),
            pltpu.VMEM((length, 2 * units), LOW),
            pltpu.VMEM((4, length, units), LOW),
            pltpu.VMEM((length, width), FULL),
            pltpu.VMEM((length, width), FULL),
            pltpu.VMEM((1, 1, 2, 8, 128) if second else grads, LOW),
            pltpu.VMEM((1, 8, 128) if second else pre.shape, LOW),
            pltpu.VMEM(grads, LOW),
            pltpu.SemaphoreType.DMA((3 + len(stills) + 3 * SHARES,)),
            pltpu.SemaphoreType.DMA((3,)),
            pltpu.SemaphoreType.DMA((3,)),
            pltpu.SemaphoreType.DMA((9,)),
            pltpu.SemaphoreType.DMA((9,)),
        ],
        compiler_params=pltpu.CompilerParams(
            collective_id=3 if second else 4, has_side_effects=True, vmem_limit_bytes=60 * 1024 * 1024
        ),
        cost_estimate=cost(30),
        name="ffn_second" if second else "ffn_first_backward",
    )(*args)


def attn_backward_kernel(
    last, gain_ref, gains_ref, place_ref, log_ref, after_grad_hbm, w_out_hbm, mixed_hbm, q_hbm, kv_hbm, trig_hbm,
    res_hbm, normed_hbm, w_key_hbm, w_value_hbm, w_query_hbm, *rest
):
    if last:
        prev, ffn_ref, first_hbm = rest[:3], rest[3], rest[4]
        grad_hbm, gain_out, ffn_hbm, share_hbms = rest[5], rest[6], rest[7], rest[8:11]
        rest = rest[11:]
    else:
        prev = (None, None, None)
        grad_hbm, gain_out = rest[:2]
        part_hbms = rest[2:5]
        rest = rest[5:]
    q_buf, kv_buf, trig_buf, res_buf, normed_buf, w_kv_buf, w_query_buf, grad_out, after_grad_buf, w_out_buf, mixed_buf, pair_sem, late_sem, early_sem, *rest = rest
    late = iter(late_sem.at[i] for i in range(14))
    after_grad_later = Later(after_grad_hbm, after_grad_buf, next(late))
    w_out_later = Later(w_out_hbm, w_out_buf, next(late))
    mixed_later = Later(mixed_hbm, mixed_buf, next(late))
    q_later, kv_later = Later(q_hbm, q_buf, next(late)), Later(kv_hbm, kv_buf, next(late))
    mixed_grad, delta, kv_grad, query_grad, back, grad_send, grad_recv, send_sem, recv_sem = rest[:9]
    hop = Hops(send_sem, recv_sem)
    seq, dp = lax.axis_index("seq"), lax.axis_index("dp")
    core, chip_x = lax.rem(seq, 2), lax.div(seq, 2)
    mate_seq, far_seq = seq + 1 - 2 * core, lax.rem(seq + 2, 4)
    far_mate = lax.rem(mate_seq + 2, 4)
    mate, x_mate = device(mate_seq, dp), device(far_seq, dp)
    length, width = res_hbm.shape
    stacked = GROUP * length
    kv_width = 2 * KV_HEADS * HEAD_DIM
    parts = rest[9:12]
    if last:
        f_own, f_y_recv, f_a_send, f_a_recv, f_b_send, f_b_recv, gain_recv = rest[12:19]
        prev_bufs = rest[19:22]
        ffn_out, share_outs = rest[22], rest[23:26]
        buffers = [rest[26 + 10 * i : 36 + 10 * i] for i in range(3)]
        row_y, row_z = lax.rem(dp, 2), lax.div(dp, 2)
        low_z, high_z = lax.rem(row_z, 2), lax.div(row_z, 2)
        y_mate = device(seq, dp + 1 - 2 * row_y)
        near_z = device(seq, dp + 2 - 4 * low_z)
        far_z = device(seq, dp + 4 - 8 * high_z)
        cross = device(far_mate, dp)
        greet([mate, x_mate, cross, y_mate, near_z, far_z])
        f_y = [None]
        f_y += [hop(ffn_ref.at[m, :, 1 - row_y], f_y_recv.at[m], y_mate) for m in (1, 2)]
        first_y = Later(first_hbm, f_y_recv.at[0], next(late))
        own_shares = Later(ffn_ref.at[:, :, row_y], f_own, next(late))
        prev = [Later(src, dst, next(late)) for src, dst in zip(prev, prev_bufs)]
    else:
        greet([mate, x_mate])
    early = Early(early_sem)
    trig = Later(trig_hbm, trig_buf, next(late))
    normed_ref = Later(normed_hbm, normed_buf, next(late))
    w_query = Later(w_query_hbm, w_query_buf, next(late))
    w_kv = LaterPairs(w_key_hbm, w_value_hbm, w_kv_buf, pair_sem)
    res_ref = Later(res_hbm, res_buf, next(late))

    def near_fill(load, a_send):
        for h in range(2):
            a_send[h] = load(2 * h + 1 - low_z).astype(LOW)

    def far_fill(load, a_recv, b_send):
        b_send[...] = (load(2 - 2 * high_z + low_z) + a_recv[1 - high_z].astype(FULL)).astype(LOW)

    def z_total(load, a_recv, b_recv):
        return load(row_z) + a_recv[high_z].astype(FULL) + b_recv[...].astype(FULL)

    def f_load(m):
        return lambda z: own_shares()[m, z].astype(FULL) + f_y_recv[m, z].astype(FULL)

    if last:
        f_nears = [hop(f_a_send.at[m], f_a_recv.at[m], near_z, start=False) for m in range(3)]
        f_fars = [hop(f_b_send.at[m], f_b_recv.at[m], far_z, start=False) for m in range(3)]

    def f_near(m):
        own_shares()
        if m == 0:
            first_y()
        else:
            f_y[m].wait()
        near_fill(f_load(m), f_a_send.at[m])
        f_nears[m].start()

    def f_far(m):
        f_nears[m].wait()
        far_fill(f_load(m), f_a_recv.at[m], f_b_send.at[m])
        f_fars[m].start()

    def f_finish(m):
        f_fars[m].wait()
        ffn_out[m] = z_total(f_load(m), f_a_recv.at[m], f_b_recv.at[m])
        early(ffn_out.at[m], ffn_hbm.at[m])

    quarter = lambda x, c: pl.ds(pl.multiple_of(64 * x + ROWS_PAD * c, ROWS_PAD), ROWS_PAD)

    def core_start(i):
        core_recv = buffers[i][0]
        return [hop(parts[i].at[:, quarter(x, 1 - core)], core_recv.at[x], mate) for x in range(2)]

    def x_make(i):
        return hop(*buffers[i][1:3], x_mate, start=False)

    def x_start(i, copies, x_copy):
        core_recv, x_send, x_recv = buffers[i][:3]
        for copy in copies:
            copy.wait()
        joint = parts[i][:, quarter(1 - chip_x, core)].astype(FULL) + core_recv[1 - chip_x].astype(FULL)
        x_send[...] = joint.astype(LOW)
        x_copy.start()
        return x_copy

    def y_start(i, copy):
        core_recv, x_send, x_recv, own, y_recv = buffers[i][:5]
        joint = parts[i][:, quarter(chip_x, core)].astype(FULL) + core_recv[chip_x].astype(FULL)
        copy.wait()
        own[...] = (joint + x_recv[...].astype(FULL)).astype(LOW).reshape(own.shape)
        return hop(own.at[:, 1 - row_y], y_recv, y_mate)

    def part_load(i):
        own, y_recv = buffers[i][3:5]
        return lambda z: own[z, row_y].astype(FULL) + y_recv[z].astype(FULL)

    def z_start(i, copy):
        copy.wait()
        near_fill(part_load(i), buffers[i][5])
        return hop(*buffers[i][5:7], near_z)

    def z_next(i, copy):
        copy.wait()
        far_fill(part_load(i), *buffers[i][6:8])
        return hop(*buffers[i][7:9], far_z)

    def share_start(i, copy):
        gathered = buffers[i][9]
        copy.wait()
        gathered[seq] = z_total(part_load(i), buffers[i][6], buffers[i][8]).astype(LOW)
        mine = gathered.at[seq]
        return [hop(mine, mine, target) for target in (x_mate, cross, mate)]

    def share_finish(i, copies):
        gathered = buffers[i][9]
        for copy in copies:
            copy.wait()
        for s in range(4):
            share_outs[i][s * ROWS_PAD : (s + 1) * ROWS_PAD] = gathered[s].astype(FULL)
        early(share_outs[i], share_hbms[i])

    def weight(i, left, right):
        term = dot(left, right, TN)
        share = width // SHARES
        for j in range(SHARES):
            rows = term[j * share : (j + 1) * share]
            if prev[i] is not None:
                rows = rows + prev[i]()[j, :share].astype(FULL)
            parts[i][j, :share] = rows.astype(LOW)
        if not last:
            early(parts[i], part_hbms[i])

    after_grad_ref, w_out_ref = after_grad_later(), w_out_later()
    low_grad = after_grad_ref[...].astype(LOW)
    mixed_back = dot(low_grad, w_out_ref[...], NT)
    lane = lax.broadcasted_iota(jnp.int32, (length, 128), 1)
    for pair in range((HEADS + 1) // 2):
        span = min(128, HEADS * HEAD_DIM - pair * 128)
        part = mixed_back[:, pair * 128 : pair * 128 + span]
        if span < 128:
            part = jnp.concatenate([part, part], axis=1)
        else:
            mixed_grad[2 * pair + 1] = jnp.where(lane >= HEAD_DIM, part, 0.0).astype(LOW)
        mixed_grad[2 * pair] = jnp.where(lane >= HEAD_DIM, pltpu.roll(part, 64, 1), 0.0).astype(LOW)
    mixed_ref = mixed_later()
    product = mixed_back.astype(LOW).astype(FULL) * mixed_ref[...].astype(FULL)
    high = product.astype(LOW)
    rest_low = (product - high.astype(FULL)).astype(LOW)
    head = lax.broadcasted_iota(jnp.int32, (16, HEADS * HEAD_DIM), 0)
    column = lax.broadcasted_iota(jnp.int32, (16, HEADS * HEAD_DIM), 1)
    pick = jnp.where(lax.div(column, HEAD_DIM) == head, 1.0, 0.0).astype(LOW)
    sums = dot(pick, high, NT) + dot(pick, rest_low, NT)
    for g in range(KV_HEADS):
        delta[g] = jnp.concatenate([sums[3 * g + i : 3 * g + i + 1] for i in range(GROUP)], axis=1)
    query_grad[...] = jnp.zeros_like(query_grad)
    weight(0, mixed_ref[...], low_grad)
    if last:
        o_core = core_start(0)
        f_near(0)
        o_x = x_make(0)

    start, place = place_ref[0:1, :], place_ref[1:2, :]
    q_ref, kv_ref = q_later(), kv_later()

    def attend(block, g):
        columns = pl.ds(pl.multiple_of(g * 128, 128), 128)
        kv_g = kv_ref[block, :, columns]
        q_g = q_ref[pl.ds(3 * g, 3)].reshape(stacked, 128)
        out_g = mixed_grad[pl.ds(3 * g, 3)].reshape(stacked, 128)
        scores = dot(kv_g, q_g, NT)
        key = lax.broadcasted_iota(jnp.int32, (length, stacked), 0) + block * length
        weights = jnp.where((key >= start) & (key <= place), jnp.exp(scores - log_ref[g]), 0.0)
        probs_grad = dot(kv_g, out_g, NT)
        score_grad = (weights * (probs_grad - delta[g])).astype(LOW)
        kv_grad[block, :, columns] = dot(weights.astype(LOW), out_g) + dot(score_grad, q_g)
        query_grad[g] += dot(kv_g, score_grad, TN)[:HEAD_DIM]

    joint = hop(grad_send.at[0], grad_recv.at[0], mate, start=False)
    across = hop(grad_send.at[1], grad_recv.at[1], x_mate, start=False)
    beside = hop(grad_send.at[2], grad_recv.at[2], mate, start=False)

    @pl.loop(0, 4)
    def _(step):
        block = jnp.where(
            step == 0, far_mate, jnp.where(step == 1, far_seq, jnp.where(step == 2, mate_seq, seq))
        )

        @pl.when(block <= seq)
        def _():
            @pl.loop(0, KV_HEADS)
            def _(g):
                attend(block, g)

        @pl.when(block > seq)
        def _():
            kv_grad[block] = jnp.zeros_like(kv_grad[block])

        @pl.when(step == 0)
        def _():
            grad_send[0] = kv_grad[far_mate].astype(LOW)
            joint.start()
            if last:
                x_start(0, o_core, o_x)

        @pl.when(step == 1)
        def _():
            joint.wait()
            grad_send[1] = (kv_grad[far_seq] + grad_recv[0].astype(FULL)).astype(LOW)
            across.start()

        @pl.when(step == 2)
        def _():
            grad_send[2] = kv_grad[mate_seq].astype(LOW)
            beside.start()
            if last:
                f_far(0)
                f_near(1)

    trig_ref = trig()
    heads = []
    for g in range(KV_HEADS):
        turned = query_grad[g].T * SCALE
        heads += [turned[i * length : (i + 1) * length] for i in range(GROUP)]
    for pair in range((HEADS + 1) // 2):
        part = jnp.concatenate([heads[2 * pair], heads[min(2 * pair + 1, HEADS - 1)]], axis=1)
        turned = (part * trig_ref[0] - swap_halves(part) * trig_ref[1]).astype(LOW)
        at = kv_width + pair * 128
        stop = min(at + 128, kv_width + width)
        back[:, at:stop] = turned[:, : stop - at]
    weight(1, normed_ref()[...], back[:, kv_width:])
    if last:
        q_core = core_start(1)
        o_y = y_start(0, o_x)
    normed_grad = dot(back[:, kv_width:], w_query()[...], NT)
    if last:
        q_x = x_start(1, q_core, x_make(1))

    across.wait()
    beside.wait()
    own = kv_grad[seq] + grad_recv[1].astype(FULL) + grad_recv[2].astype(FULL)
    for g in range(KV_HEADS):
        part = own[:, g * 128 : (g + 1) * 128]
        back[:, g * 128 : (g + 1) * 128] = (part * trig_ref[2] - swap_halves(part) * trig_ref[3]).astype(LOW)
    weight(2, normed_ref()[...], back[:, :kv_width])
    if last:
        kv_core = core_start(2)
        f_far(1)
        f_near(2)
        kv_x = x_start(2, kv_core, x_make(2))
    normed_grad = normed_grad + dot(back[:, :kv_width], w_kv()[...])
    sent_back, gain_term = norm_back(res_ref()[...].astype(FULL), gains_ref[0:1, :], normed_grad)
    grad_out[...] = after_grad_ref[...] + sent_back
    early(grad_out, grad_hbm)
    row = lax.broadcasted_iota(jnp.int32, gain_out.shape, 0)
    gain_out[...] = gain_ref[...] + jnp.where(row == 0, gain_term, 0.0)
    if not last:
        early.finish()
        return

    partners = [mate, x_mate, y_mate, near_z, far_z]
    gain_hop = lambda n: hop(gain_out, gain_recv.at[n], partners[n])

    def gain_add(n, copy):
        copy.wait()
        gain_out[...] += gain_recv[n]

    gain_copy = gain_hop(0)
    f_finish(0)
    o_z = z_start(0, o_y)
    gain_add(0, gain_copy)
    gain_copy = gain_hop(1)
    q_y = y_start(1, q_x)
    f_far(2)
    f_finish(1)
    o_z = z_next(0, o_z)
    gain_add(1, gain_copy)
    gain_copy = gain_hop(2)
    kv_y = y_start(2, kv_x)
    q_z = z_start(1, q_y)
    gain_add(2, gain_copy)
    gain_copy = gain_hop(3)
    o_s = share_start(0, o_z)
    kv_z = z_start(2, kv_y)
    q_z = z_next(1, q_z)
    gain_add(3, gain_copy)
    gain_copy = gain_hop(4)
    f_finish(2)
    kv_z = z_next(2, kv_z)
    q_s = share_start(1, q_z)
    gain_add(4, gain_copy)
    kv_s = share_start(2, kv_z)
    share_finish(0, o_s)
    share_finish(1, q_s)
    share_finish(2, kv_s)
    early.finish()


def attn_backward(after_grad, residual, normed, gains, q, kv, log_total, mixed, attn_weights, trig, place, gain_grads, final=None):
    length, width = residual.shape
    kv_width = 2 * KV_HEADS * HEAD_DIM
    last = final is not None
    key_t, value_t, w_query, w_out = attn_weights
    args = (gain_grads, gains, place, log_total, after_grad, w_out, mixed, q, kv, trig, residual, normed)
    args = args + (key_t, value_t, w_query)
    specs = [VMEM] * 4 + [ANYWHERE] * 11
    out_specs = (ANYWHERE, VMEM)
    shapes = (((length, width), FULL), ((8, width), FULL))
    sizes = (width, width, kv_width)
    part_shapes = [((SHARES, 4 * ROWS_PAD, c), LOW) for c in sizes]
    scratch = [
        pltpu.VMEM(q.shape, LOW),
        pltpu.VMEM(kv.shape, LOW),
        pltpu.VMEM(trig.shape, FULL),
        pltpu.VMEM((length, width), residual.dtype),
        pltpu.VMEM((length, width), LOW),
        pltpu.VMEM((kv_width, width), LOW),
        pltpu.VMEM(w_query.shape, LOW),
        pltpu.VMEM((length, width), FULL),
        pltpu.VMEM((length, width), FULL),
        pltpu.VMEM(w_out.shape, LOW),
        pltpu.VMEM(mixed.shape, LOW),
        pltpu.SemaphoreType.DMA((2 * KV_HEADS,)),
        pltpu.SemaphoreType.DMA((14,)),
        pltpu.SemaphoreType.DMA((7,)),
        pltpu.VMEM((HEADS, length, 128), LOW),
        pltpu.VMEM((KV_HEADS, 1, GROUP * length), FULL),
        pltpu.VMEM((4, length, kv_width), FULL),
        pltpu.VMEM((KV_HEADS, HEAD_DIM, GROUP * length), FULL),
        pltpu.VMEM((length, kv_width + width), LOW),
        pltpu.VMEM((3, length, kv_width), LOW),
        pltpu.VMEM((3, length, kv_width), LOW),
    ]
    hops = 3
    if last:
        share, hidden = final[3].shape[3:]
        args = args + tuple(final)
        specs = specs + [ANYWHERE] * 5
        shapes = shapes + (((3, share, hidden), FULL),) + tuple(((4 * ROWS_PAD, c), FULL) for c in sizes)
        hops = 3 + 2 + 6 + 5 + 3 * (2 + 1 + 1 + 2 + 3)
        scratch += [pltpu.SemaphoreType.DMA((hops,))] * 2
        out_specs = out_specs + (ANYWHERE,) * 4
        scratch += [pltpu.VMEM(*s) for s in part_shapes]
        scratch += [
            pltpu.VMEM((3, 4, share, hidden), LOW),
            pltpu.VMEM((3, 4, share, hidden), LOW),
            pltpu.VMEM((3, 2, share, hidden), LOW),
            pltpu.VMEM((3, 2, share, hidden), LOW),
            pltpu.VMEM((3, share, hidden), LOW),
            pltpu.VMEM((3, share, hidden), LOW),
            pltpu.VMEM((5, 8, width), FULL),
        ]
        scratch += [pltpu.VMEM(*s) for s in part_shapes]
        scratch += [pltpu.VMEM(*s) for s in shapes[2:]]
        for c in sizes:
            scratch += [
                pltpu.VMEM((2, SHARES, ROWS_PAD, c), LOW),
                pltpu.VMEM((SHARES, ROWS_PAD, c), LOW),
                pltpu.VMEM((SHARES, ROWS_PAD, c), LOW),
                pltpu.VMEM((4, 2, ROWS_PAD, c), LOW),
                pltpu.VMEM((4, ROWS_PAD, c), LOW),
                pltpu.VMEM((2, ROWS_PAD, c), LOW),
                pltpu.VMEM((2, ROWS_PAD, c), LOW),
                pltpu.VMEM((ROWS_PAD, c), LOW),
                pltpu.VMEM((ROWS_PAD, c), LOW),
                pltpu.VMEM((4, ROWS_PAD, c), LOW),
            ]
    else:
        shapes, out_specs = shapes + tuple(part_shapes), out_specs + (ANYWHERE,) * 3
        scratch += [pltpu.SemaphoreType.DMA((hops,))] * 2
        scratch += [pltpu.VMEM(*s) for s in part_shapes]
    return pl.pallas_call(
        functools.partial(attn_backward_kernel, last),
        out_shape=tuple(jax.ShapeDtypeStruct(*s) for s in shapes),
        in_specs=specs,
        out_specs=out_specs,
        scratch_shapes=scratch,
        compiler_params=pltpu.CompilerParams(
            collective_id=6 if last else 5, has_side_effects=True, vmem_limit_bytes=60 * 1024 * 1024
        ),
        cost_estimate=cost(95 if last else 40),
        name="attn_backward_last" if last else "attn_backward",
    )(*args)


def split_pairs(grads):
    rows = grads.shape[0]
    pairs = grads.reshape(rows, KV_HEADS, 2, HEAD_DIM)
    return pairs[:, :, 0].reshape(rows, -1), pairs[:, :, 1].reshape(rows, -1)


def on_device(
    tokens,
    seg_ids,
    positions,
    attn_gain,
    w_query,
    w_key,
    w_value,
    w_out,
    ffn_gain,
    w_gate,
    w_up,
    w_down,
    cotangent,
):
    width = tokens.shape[2]
    trig, place = prepare(positions[0])
    attn_weights = (w_key.T, w_value.T, w_query, w_out)
    gains = jnp.pad(jnp.stack([attn_gain, ffn_gain]), ((0, 6), (0, 0)))
    whole = lax.axis_size("dp") != SHARES
    share = width // SHARES
    own_weights = (w_gate, w_up, w_down.T)

    def over_x(value):
        return lax.ppermute(value, "seq", [(s, (s + 2) % 4) for s in range(4)])

    def over_rows_piece(value, d):
        return lax.dynamic_slice_in_dim(value, jnp.minimum(d * PIECE, width - PIECE), PIECE, axis=0)

    if whole:
        theirs = [over_x(w) for w in own_weights]
        far = jnp.stack([jnp.concatenate([over_rows_piece(w, d) for w in theirs]) for d in range(SHARES)])
    else:
        piece = jnp.concatenate([over_rows_piece(w, lax.axis_index("dp")) for w in own_weights])
        far = lax.all_gather(over_x(piece), "dp", axis=0)

    results = forward(tokens[0], gains, place, cotangent[0], attn_weights, trig, own_weights)
    first, (rows_all, pre_all, residual), results = results[:KEPT], results[KEPT : KEPT + 3], results[KEPT + 3 :]
    second, normed_two, low_halves = results[:KEPT], results[KEPT], results[KEPT + 1 :]
    output, after_grad, gain_grads, ffn_grads = ffn_all(
        True, False, cotangent[0], normed_two, second[5], gains, low_halves, own_weights, far
    )

    def attn_args(after_grad, residual, kept, gain_grads):
        normed, q, kv, log_total, mixed = kept[:5]
        return (after_grad, residual, normed, gains, q, kv, log_total, mixed, attn_weights, trig, place, gain_grads)

    upstream, gain_grads, *parts = attn_backward(*attn_args(after_grad, residual, second, gain_grads))
    after_grad, gain_grads, ffn_grads, *first_y = ffn_all(
        False, not whole, upstream, None, first[5], gains, (rows_all,), own_weights, far, ffn_grads, pre_all, gain_grads
    )
    args = attn_args(after_grad, tokens[0], first, gain_grads)
    if whole:
        upstream, gain_grads, *terms = attn_backward(*args)
        parts = [part.astype(FULL) + term.astype(FULL) for part, term in zip(parts, terms)]
    else:
        upstream, gain_all, ffn_share, *shares = attn_backward(*args, (*parts, ffn_grads, *first_y))
    if whole:

        def over_rows(grads, dim):
            grads = lax.psum_scatter(grads.astype(LOW), "dp", scatter_dimension=dim, tiled=True)
            return grads.astype(FULL)

        def over_all(grads, dim):
            return lax.psum(over_rows(grads, dim).astype(LOW), "seq").astype(FULL)

        shares = [over_all(part[:, :share].reshape(width, -1), 0) for part in parts]
        ffn_share = over_rows(ffn_grads.reshape(3, width, -1), 1)
        own_gains = over_all(gain_grads[:2], 1)
    else:
        shares = [part[:share] for part in shares]
        own_gains = lax.dynamic_slice_in_dim(gain_all, lax.axis_index("dp") * share, share, axis=1)
    key_share, value_share = split_pairs(shares[2])
    return (
        output[None],
        upstream[None],
        own_gains[0],
        shares[1],
        key_share,
        value_share,
        shares[0],
        own_gains[1],
        ffn_share[0],
        ffn_share[1],
        ffn_share[2].T,
    )


def solution(mesh):
    in_specs = (
        P("dp", "seq", None),
        P("dp", "seq"),
        P("dp", "seq"),
        P(),
        P(),
        P(),
        P(),
        P(),
        P(),
        P(None, "seq"),
        P(None, "seq"),
        P("seq", None),
        P("dp", "seq", None),
    )
    out_specs = (
        P("dp", "seq", None),
        P("dp", "seq", None),
        P("dp"),
        P("dp", None),
        P("dp", None),
        P("dp", None),
        P("dp", None),
        P("dp"),
        P("dp", "seq"),
        P("dp", "seq"),
        P("seq", "dp"),
    )
    return jax.shard_map(
        on_device, mesh=mesh, in_specs=in_specs, out_specs=out_specs, check_vma=False
    )
```

```python
import functools

import jax
import jax.numpy as jnp
from jax import lax
from jax.experimental import pallas as pl
from jax.experimental.pallas import tpu as pltpu
from jax.sharding import PartitionSpec as P

MESH_ID = pl.DeviceIdType.MESH
HEADS = 15
KV_HEADS = 5
GROUP = 3
HEAD_DIM = 64
EPSILON = 1e-05
THETA = 10000.0
CHUNKS = 2
SHARES = 8
ROWS_PAD = 32
PIECE = 128
MASKED = -1e30
LOW = jnp.bfloat16
FULL = jnp.float32
SCALE = HEAD_DIM ** (-0.5)
NT = (((1,), (1,)), ((), ()))
TN = (((0,), (0,)), ((), ()))


def device(seq_pos, dp_pos):
    return {"seq": seq_pos, "dp": dp_pos}


def send(src, dst, send_sem, recv_sem, target, start=True):
    copy = pltpu.make_async_remote_copy(
        src_ref=src,
        dst_ref=dst,
        send_sem=send_sem,
        recv_sem=recv_sem,
        device_id=target,
        device_id_type=MESH_ID,
    )
    if start:
        copy.start()
    return copy


class Hops:
    def __init__(self, send_sem, recv_sem):
        self.send_sem, self.recv_sem, self.used = send_sem, recv_sem, 0

    def __call__(self, src, dst, target, start=True):
        index, self.used = self.used, self.used + 1
        return send(src, dst, self.send_sem.at[index], self.recv_sem.at[index], target, start)


class Later:
    def __init__(self, src, dst, sem):
        self.copy, self.dst, self.waited = pltpu.make_async_copy(src, dst, sem), dst, False
        self.copy.start()

    def __call__(self):
        if not self.waited:
            self.copy.wait()
            self.waited = True
        return self.dst


class Early:
    def __init__(self, sem):
        self.sem, self.copies = sem, []

    def __call__(self, src, dst, start=True):
        self.copies.append(pltpu.make_async_copy(src, dst, self.sem.at[len(self.copies)]))
        if start:
            self.copies[-1].start()
        return self.copies[-1]

    def finish(self):
        for copy in self.copies:
            copy.wait()


class LaterPairs:
    def __init__(self, key_hbm, value_hbm, dst, sem):
        self.copies, self.dst = [], dst
        for h in range(2 * KV_HEADS):
            src = (key_hbm, value_hbm)[h % 2].at[pl.ds(h // 2 * HEAD_DIM, HEAD_DIM)]
            self.copies.append(pltpu.make_async_copy(src, dst.at[pl.ds(h * HEAD_DIM, HEAD_DIM)], sem.at[h]))
            self.copies[-1].start()

    def __call__(self):
        for copy in self.copies:
            copy.wait()
        self.copies = []
        return self.dst


def greet(targets):
    barrier = pltpu.get_barrier_semaphore()
    for target in targets:
        pl.semaphore_signal(barrier, inc=1, device_id=target, device_id_type=MESH_ID)
    pl.semaphore_wait(barrier, len(targets))


def dot(left, right, dims=None):
    if dims is None:
        return jnp.dot(left, right, preferred_element_type=FULL)
    return lax.dot_general(left, right, dims, preferred_element_type=FULL)


def cost(microseconds):
    return pl.CostEstimate(flops=int(microseconds * 1.15e9), bytes_accessed=1 << 20, transcendentals=0)


def inverse_rms(value):
    return lax.rsqrt(jnp.mean(value * value, axis=-1, keepdims=True) + EPSILON)


def swap_halves(value):
    lane = lax.broadcasted_iota(jnp.int32, value.shape, 1)
    first = (lane & (HEAD_DIM // 2)) == 0
    return jnp.where(first, pltpu.roll(value, 96, 1), pltpu.roll(value, 32, 1))


VMEM = pl.BlockSpec(memory_space=pltpu.VMEM)
ANYWHERE = pl.BlockSpec(memory_space=pl.ANY)


def prepare(positions):
    length = positions.shape[0]
    frequency = THETA ** (-(jnp.arange(HEAD_DIM // 2, dtype=FULL) * 2.0 / HEAD_DIM))
    angles = positions.astype(FULL)[:, None] * frequency
    cos, sin = jnp.cos(angles), jnp.sin(angles)
    one, none = jnp.ones((length, HEAD_DIM), FULL), jnp.zeros((length, HEAD_DIM), FULL)
    trig = jnp.stack(
        [
            jnp.concatenate([cos, cos, cos, cos], 1),
            jnp.concatenate([-sin, sin, -sin, sin], 1),
            jnp.concatenate([cos, cos, one], 1),
            jnp.concatenate([-sin, sin, none], 1),
        ]
    )
    own = lax.axis_index("seq") * length + jnp.arange(length, dtype=jnp.int32)
    place = jnp.stack([jnp.tile(own - positions, GROUP), jnp.tile(own, GROUP)])
    place = jnp.pad(place, ((0, 6), (0, 0)))
    return trig, place


def norm_back(value, gain, grad):
    inverse = inverse_rms(value)
    weighted = grad * gain
    inner = jnp.mean(weighted * value, axis=-1, keepdims=True)
    back = inverse * weighted - value * (inverse * inverse * inverse) * inner
    return back, jnp.sum(grad * value * inverse, axis=0, keepdims=True)


KEPT = 6
CUT = 3


def forward_kernel(
    tokens_ref, gains_ref, place_ref, cotangent_hbm, w_key_hbm, w_value_hbm, w_query_hbm, w_out_hbm, trig_hbm,
    w_gate_hbm, w_up_hbm, w_down_hbm, *rest
):
    first_hbm, (rows_hbm, pre_hbm, res_hbm), rest = rest[:KEPT], rest[KEPT : KEPT + 3], rest[KEPT + 3 :]
    second_hbm, two_hbm, extra_outs, rest = rest[:KEPT], rest[KEPT], rest[KEPT + 1 : KEPT + 3], rest[KEPT + 3 :]
    first, second, rest = rest[:KEPT], rest[KEPT : 2 * KEPT], rest[2 * KEPT :]
    (
        w_kv_buf, w_query_buf, w_out_buf, trig_buf, w_gate_buf, w_up_buf, w_down_buf,
        two, rows, pre, res, peak, total, acc, mate_send, mate_recv, x_send, x_recv, own_far,
        pair_sem, late_sem, early_sem, send_sem, recv_sem,
    ) = rest
    w_kv = LaterPairs(w_key_hbm, w_value_hbm, w_kv_buf, pair_sem)
    trig, w_query, w_out, w_gate, w_up, w_down = [
        Later(src, dst, late_sem.at[i])
        for i, (src, dst) in enumerate(
            (
                (trig_hbm, trig_buf), (w_query_hbm, w_query_buf), (w_out_hbm, w_out_buf),
                (w_gate_hbm, w_gate_buf), (w_up_hbm, w_up_buf), (w_down_hbm, w_down_buf),
            )
        )
    ]
    early, hop = Early(early_sem), Hops(send_sem, recv_sem)
    seq, dp = lax.axis_index("seq"), lax.axis_index("dp")
    core = lax.rem(seq, 2)
    mate_seq, far_seq = seq + 1 - 2 * core, lax.rem(seq + 2, 4)
    far_mate = lax.rem(mate_seq + 2, 4)
    mate, x_mate = device(mate_seq, dp), device(far_seq, dp)
    length = tokens_ref.shape[0]
    stacked = GROUP * length
    start, place = place_ref[0:1, :], place_ref[1:2, :]
    step = length // CHUNKS
    part = lambda k: pl.ds(k * step, step)

    def attention(residual_ref, buffers, hbm, extra_ref, extra_out, meet):
        normed, q, kv, log_total, mixed, after = buffers
        residual = residual_ref[...].astype(FULL)
        normed[...] = (residual * inverse_rms(residual) * gains_ref[0:1, :]).astype(LOW)
        early(normed, hbm[0])
        kv_pre = dot(normed[...], w_kv()[...], NT)
        trig_ref = trig()
        for g in range(KV_HEADS):
            piece = kv_pre[:, g * 128 : (g + 1) * 128]
            turned = piece * trig_ref[2] + swap_halves(piece) * trig_ref[3]
            kv[seq, :, g * 128 : (g + 1) * 128] = turned.astype(LOW)
        if meet:
            greet([mate, x_mate])
        spans = (pl.ds(0, CUT * 128), pl.ds(CUT * 128, (KV_HEADS - CUT) * 128))
        to_x = [hop(kv.at[seq, :, s], kv.at[seq, :, s], x_mate) for s in spans]
        to_mate = hop(kv.at[seq], kv.at[seq], mate)
        onward = [hop(kv.at[far_seq, :, s], kv.at[far_seq, :, s], mate, start=False) for s in spans]
        mine, theirs = extra_out.at[seq], extra_out.at[far_seq]
        extra = [early(extra_ref, mine, start=False)]
        extra += [hop(extra_ref, mine, target, start=False) for target in (x_mate, mate)]
        kv_keep = early(kv, hbm[2], start=False)
        q_pre = dot(normed[...], w_query()[...])
        lane = lax.broadcasted_iota(jnp.int32, (length, 128), 1)
        for pair in range((HEADS + 1) // 2):
            width = min(128, HEADS * HEAD_DIM - pair * 128)
            piece = q_pre[:, pair * 128 : pair * 128 + width]
            if width < 128:
                piece = jnp.concatenate([piece, piece], axis=1)
            turned = (piece * trig_ref[0] + swap_halves(piece) * trig_ref[1]) * SCALE
            q[2 * pair] = jnp.where(lane < HEAD_DIM, turned, 0.0).astype(LOW)
            if width == 128:
                q[2 * pair + 1] = jnp.where(lane < HEAD_DIM, pltpu.roll(turned, 64, 1), 0.0).astype(LOW)
        early(q, hbm[1])

        def attend(block, g):
            kv_g = kv[block, :, pl.ds(pl.multiple_of(g * 128, 128), 128)]
            q_g = q[pl.ds(3 * g, 3)].reshape(stacked, 128)
            scores = dot(kv_g, q_g, NT)
            key = lax.broadcasted_iota(jnp.int32, (length, stacked), 0) + block * length
            scores = jnp.where((key >= start) & (key <= place), scores, MASKED)
            new_peak = jnp.maximum(peak[g], jnp.max(scores, axis=0, keepdims=True))
            weights = jnp.exp(scores - new_peak)
            fade = jnp.exp(peak[g] - new_peak)
            total[g] = jnp.sum(weights, axis=0, keepdims=True) + fade * total[g]
            acc[g] = dot(kv_g, weights.astype(LOW), TN)[HEAD_DIM:] + fade * acc[g]
            peak[g] = new_peak

        peak[...] = jnp.full_like(peak, MASKED)
        total[...] = jnp.zeros_like(total)
        acc[...] = jnp.zeros_like(acc)

        @pl.loop(0, 6)
        def _(turn):
            @pl.when(turn == 1)
            def _():
                to_mate.wait()

            @pl.when(turn == 2)
            def _():
                to_x[0].wait()
                onward[0].start()
                for copy in extra:
                    copy.start()

            @pl.when(turn == 3)
            def _():
                onward[0].wait()

            @pl.when(turn == 4)
            def _():
                to_x[1].wait()
                onward[1].start()

            @pl.when(turn == 5)
            def _():
                onward[1].wait()
                kv_keep.start()

            block = jnp.where(
                turn == 0, seq, jnp.where(turn == 1, mate_seq, jnp.where(lax.rem(turn, 2) == 0, far_seq, far_mate))
            )
            low = jnp.where(turn < 4, 0, CUT)
            high = jnp.where((turn == 2) | (turn == 3), CUT, KV_HEADS)

            @pl.when(block <= seq)
            def _():
                @pl.loop(low, high)
                def _(g):
                    attend(block, g)

        for g in range(KV_HEADS):
            heads = (acc[g] / total[g]).T.astype(LOW)
            log_total[g] = peak[g] + jnp.log(total[g])
            for i in range(GROUP):
                h = GROUP * g + i
                mixed[:, h * HEAD_DIM : (h + 1) * HEAD_DIM] = heads[i * length : (i + 1) * length]
        early(log_total, hbm[3])
        early(mixed, hbm[4])
        extra[1].wait()
        return hop(theirs, theirs, mate), extra[2]

    def project(residual_ref, buffers, rows_of, two_ref):
        mixed, after = buffers[4:]
        value = residual_ref[rows_of].astype(FULL) + dot(mixed[rows_of], w_out()[...])
        after[rows_of] = value
        two_ref[rows_of] = (value * inverse_rms(value) * gains_ref[1:2, :]).astype(LOW)

    waits = attention(tokens_ref, first, first_hbm, cotangent_hbm.at[pl.ds(0, step)], extra_outs[0], True)

    to_x = []
    for k in range(CHUNKS):
        project(tokens_ref, first, part(k), rows.at[seq])
        to_x.append(hop(rows.at[seq, part(k)], rows.at[seq, part(k)], x_mate))
    to_mate = hop(rows.at[seq], rows.at[seq], mate)
    early(first[5], first_hbm[5])
    for copy in waits:
        copy.wait()
    w_gate_ref, w_up_ref, w_down_ref = w_gate(), w_up(), w_down()
    units = w_gate_ref.shape[1]

    def ffn(quarter, rows_of):
        block = rows[quarter, rows_of]
        gate = dot(block, w_gate_ref[...])
        up = dot(block, w_up_ref[...])
        pre[quarter, rows_of, :units] = gate.astype(LOW)
        pre[quarter, rows_of, units:] = up.astype(LOW)
        hidden = (gate * jax.nn.sigmoid(gate) * up).astype(LOW)
        return dot(hidden, w_down_ref[...], NT)

    everything = pl.ds(0, length)
    res[...] = first[5][...] + ffn(seq, everything)
    to_mate.wait()
    mate_send[0] = ffn(mate_seq, everything).astype(LOW)
    back = hop(mate_send.at[0], mate_recv.at[0], mate)
    last = []
    for k in range(CHUNKS):
        to_x[k].wait()
        onward = hop(rows.at[far_seq, part(k)], rows.at[far_seq, part(k)], mate)
        own_far[part(k)] = ffn(far_seq, part(k))
        onward.wait()
        mate_send[1, part(k)] = ffn(far_mate, part(k)).astype(LOW)
        joint = hop(mate_send.at[1, part(k)], mate_recv.at[1, part(k)], mate)
        joint.wait()
        x_send[part(k)] = (own_far[part(k)] + mate_recv[1, part(k)].astype(FULL)).astype(LOW)
        last.append(hop(x_send.at[part(k)], x_recv.at[part(k)], x_mate))
    early(rows, rows_hbm)
    early(pre, pre_hbm)
    back.wait()
    res[...] += mate_recv[0].astype(FULL)
    for k in range(CHUNKS):
        last[k].wait()
        res[part(k)] += x_recv[part(k)].astype(FULL)
    early(res, res_hbm)

    waits = attention(res, second, second_hbm, cotangent_hbm.at[pl.ds(step, step)], extra_outs[1], False)
    project(res, second, everything, two)
    early(second[5], second_hbm[5])
    early(two, two_hbm)
    for copy in waits:
        copy.wait()
    early.finish()


def forward(tokens, gains, place, cotangent, attn_weights, trig, ffn_weights):
    length, width = tokens.shape
    kv_width = 2 * KV_HEADS * HEAD_DIM
    stats = (KV_HEADS, 1, GROUP * length)
    units = ffn_weights[0].shape[1]
    kept = (
        ((length, width), LOW),
        ((HEADS, length, 128), LOW),
        ((4, length, kv_width), LOW),
        (stats, FULL),
        ((length, HEADS * HEAD_DIM), LOW),
        ((length, width), FULL),
    )
    middle = (((4, length, width), LOW), ((4, length, 2 * units), LOW), ((length, width), FULL))
    extra = ((4, length // 2, width), LOW)
    shapes = kept + middle + kept + (((length, width), LOW), extra, extra)
    key_t, value_t, w_query, w_out = attn_weights
    return pl.pallas_call(
        forward_kernel,
        out_shape=tuple(jax.ShapeDtypeStruct(*s) for s in shapes),
        in_specs=[VMEM] * 3 + [ANYWHERE] * 9,
        out_specs=(ANYWHERE,) * len(shapes),
        scratch_shapes=[pltpu.VMEM(*s) for s in kept + kept]
        + [
            pltpu.VMEM((kv_width, width), LOW),
            pltpu.VMEM(w_query.shape, LOW),
            pltpu.VMEM(w_out.shape, LOW),
            pltpu.VMEM(trig.shape, FULL),
        ]
        + [pltpu.VMEM(w.shape, LOW) for w in ffn_weights]
        + [pltpu.VMEM((length, width), LOW)]
        + [pltpu.VMEM(*s) for s in middle]
        + [
            pltpu.VMEM(stats, FULL),
            pltpu.VMEM(stats, FULL),
            pltpu.VMEM((KV_HEADS, HEAD_DIM, GROUP * length), FULL),
            pltpu.VMEM((2, length, width), LOW),
            pltpu.VMEM((2, length, width), LOW),
            pltpu.VMEM((length, width), LOW),
            pltpu.VMEM((length, width), LOW),
            pltpu.VMEM((length, width), FULL),
            pltpu.SemaphoreType.DMA((2 * KV_HEADS,)),
            pltpu.SemaphoreType.DMA((6,)),
            pltpu.SemaphoreType.DMA((18,)),
            pltpu.SemaphoreType.DMA((26,)),
            pltpu.SemaphoreType.DMA((26,)),
        ],
        compiler_params=pltpu.CompilerParams(
            collective_id=0, has_side_effects=True, vmem_limit_bytes=60 * 1024 * 1024
        ),
        cost_estimate=cost(85),
        name="forward",
    )(tokens, gains, place, cotangent, *attn_weights, trig, *ffn_weights)


def ffn_all_kernel(second, reduce, up_ref, own_ref, after_hbm, gains_ref, still_refs, gate_ref, upw_ref, down_ref, far_ref, *rest):
    y_part = prev_hbm = pre_hbm = None
    if second:
        result_out, rest = rest[0], rest[1:]
    else:
        prev_hbm, pre_hbm, gain_ref, *rest = rest
    grad_out, gain_out, weight_hbm, *rest = rest
    if reduce:
        y_part, *rest = rest
    (
        w_in, w_down, still_ref, moved, in_grad, in_temp, hidden, back, after_buf, prev_buf, pre_buf, weight_out,
        load_sem, late_sem, early_sem, send_sem, recv_sem,
    ) = rest
    early = Early(early_sem)
    after_ref = Later(after_hbm, after_buf, late_sem.at[0])
    pre_ref = None if second else Later(pre_hbm, pre_buf, late_sem.at[2])
    hop = Hops(send_sem, recv_sem)
    seq, dp = lax.axis_index("seq"), lax.axis_index("dp")
    core = lax.rem(seq, 2)
    mate_seq, far_seq = seq + 1 - 2 * core, lax.rem(seq + 2, 4)
    far_mate = lax.rem(mate_seq + 2, 4)
    mate, x_mate = device(mate_seq, dp), device(far_seq, dp)
    length, width = up_ref.shape
    units = gate_ref.shape[1]
    whole = pl.ds(0, width)

    def slots(w, rows):
        return w_in.at[w, rows, :units], w_in.at[w, rows, units:], w_down.at[w, rows]

    loads = []

    def load(src, dst):
        loads.append(pltpu.make_async_copy(src, dst, load_sem.at[len(loads)]))
        loads[-1].start()

    for src, dst in zip((gate_ref, upw_ref, down_ref), slots(0, whole)):
        load(src, dst)
    moved[seq] = own_ref[...].astype(LOW)
    at = 0
    for ref in still_refs:
        load(ref, still_ref.at[:, pl.ds(at, ref.shape[1])])
        at += ref.shape[1]
    far_from = len(loads)
    for d in range(SHARES):
        at = min(d * PIECE, width - PIECE)
        rows = min(PIECE, width - PIECE - at) if d == SHARES - 2 else PIECE
        for i, dst in enumerate(slots(2, pl.ds(at, rows))):
            load(far_ref.at[d, pl.ds(i * PIECE, rows)], dst)
    y_mate = device(seq, dp + 1 - 2 * lax.rem(dp, 2))
    greet([mate, x_mate] + ([y_mate] if reduce else []))
    mine, theirs = moved.at[seq], moved.at[far_seq]
    to_x = hop(mine, mine, x_mate)
    to_mate = hop(mine, mine, mate)
    beside = [hop(src, dst, mate) for src, dst in zip((gate_ref, upw_ref, down_ref), slots(1, whole))]
    rows_ref, low_ref = (moved, still_ref) if second else (still_ref, moved)

    def halves(quarter, w, grads, known=False):
        both = pre_buf[quarter].astype(FULL) if known else dot(rows_ref[quarter], w_in[w])
        gate, up = both[:, :units], both[:, units:]
        bend = jax.nn.sigmoid(gate)
        silu = gate * bend
        hidden_grad = dot(low_ref[quarter], w_down[w])
        grads[:, :units] = (hidden_grad * up * bend * (1.0 + gate * (1.0 - bend))).astype(LOW)
        grads[:, units:] = (hidden_grad * silu).astype(LOW)
        return (silu * up).astype(LOW)

    def local(w):
        act = halves(seq, w, in_temp)
        back[...] += dot(in_temp[...], w_in[w], NT)
        if second:
            grad_out[...] += dot(act, w_down[w], NT)

    for copy in loads[:far_from]:
        copy.wait()
    flat = lambda ref: ref[...].reshape(4 * length, ref.shape[2])
    share = width // SHARES

    def finish(i, term):
        for j in range(SHARES):
            rows = term[j * share : (j + 1) * share]
            if prev_ref is not None:
                rows = rows + prev_ref()[i, j // 2, j % 2].astype(FULL)
            weight_out[i, j // 2, j % 2] = rows.astype(LOW)
        early(weight_out.at[i], weight_hbm.at[i])

    if second:
        hidden[seq] = halves(seq, 0, in_grad.at[seq])
        back[...] = dot(in_grad[seq], w_in[0], NT)
        grad_out[...] = after_ref()[...] + dot(hidden[seq], w_down[0], NT)
    else:
        pre_ref()

        @pl.loop(0, 4)
        def _(quarter):
            both = pre_buf[quarter].astype(FULL)
            gate = both[:, :units]
            hidden[quarter] = (gate * jax.nn.sigmoid(gate) * both[:, units:]).astype(LOW)

        halves(seq, 0, in_grad.at[seq], True)
        back[...] = dot(in_grad[seq], w_in[0], NT)
    if not second:
        for copy in beside:
            copy.wait()
        local(1)
    for copy in loads[far_from:]:
        copy.wait()
    across = [hop(w_in.at[2], w_in.at[3], mate), hop(w_down.at[2], w_down.at[3], mate)]
    prev_ref = None if second else Later(prev_hbm, prev_buf, late_sem.at[1])
    if second:
        for copy in beside:
            copy.wait()

        @pl.loop(1, 4)
        def _(w):
            @pl.when(w == 3)
            def _():
                for copy in across:
                    copy.wait()

            local(w)

    else:
        local(2)

    to_mate.wait()
    if not second:
        halves(mate_seq, 0, in_grad.at[mate_seq], True)
    to_x.wait()
    onward = hop(theirs, theirs, mate)
    if second:

        @pl.loop(0, 3)
        def _(i):
            @pl.when(i == 2)
            def _():
                onward.wait()

            quarter = jnp.where(i == 0, mate_seq, jnp.where(i == 1, far_seq, far_mate))
            hidden[quarter] = halves(quarter, 0, in_grad.at[quarter])

        both = dot(flat(rows_ref), flat(in_grad), TN)
        finish(0, both[:, :units])
        finish(1, both[:, units:])
        finish(2, dot(flat(low_ref), flat(hidden), TN))
    else:
        onward.wait()
        finish(2, dot(flat(low_ref), flat(hidden), TN))
        if reduce:
            first_y = hop(weight_out.at[2, :, 1 - lax.rem(dp, 2)], y_part, y_mate)

        @pl.loop(0, 2)
        def _(i):
            quarter = jnp.where(i == 0, far_seq, far_mate)
            halves(quarter, 0, in_grad.at[quarter], True)

        both = dot(flat(rows_ref), flat(in_grad), TN)
        finish(0, both[:, :units])
        finish(1, both[:, units:])
        for copy in across:
            copy.wait()
        local(3)
    if second:
        result_out[...] = grad_out[...].astype(LOW)
    sent_back, gain_term = norm_back(after_ref()[...], gains_ref[1:2, :], back[...])
    grad_out[...] = up_ref[...].astype(FULL) + sent_back
    row = lax.broadcasted_iota(jnp.int32, gain_out.shape, 0)
    gain_term = jnp.where(row == 1, gain_term, 0.0)
    gain_out[...] = gain_term if second else gain_ref[...] + gain_term
    if reduce:
        first_y.wait()
    early.finish()


def ffn_all_call(stills, second, reduce, *refs):
    refs = refs if second else refs[:1] + refs
    return ffn_all_kernel(second, reduce, *refs[:4], refs[4 : 4 + stills], *refs[4 + stills :])


def ffn_all(second, reduce, upstream, own, after, gains, stills, weights, far, prev=None, pre=None, gain_grads=None):
    length, width = after.shape
    units = weights[0].shape[1]
    share = width // SHARES
    grads = (3, SHARES // 2, 2, share, units)
    shapes = (
        ((length, width), FULL),
        ((8, width), FULL),
        (grads, LOW),
    )
    if second:
        shapes = (((length, width), LOW),) + shapes
    if reduce:
        shapes = shapes + (((SHARES // 2, share, units), LOW),)
    args = (after, gains) + tuple(stills) + tuple(weights) + (far,)
    specs = [ANYWHERE, VMEM] + [ANYWHERE] * (len(stills) + 4)
    if second:
        args, specs = (upstream, own) + args, [VMEM, VMEM] + specs
    else:
        args, specs = (upstream,) + args, [VMEM] + specs
        args, specs = args + (prev, pre, gain_grads), specs + [ANYWHERE] * 2 + [VMEM]
    return pl.pallas_call(
        functools.partial(ffn_all_call, len(stills), second, reduce),
        out_shape=tuple(jax.ShapeDtypeStruct(*s) for s in shapes),
        in_specs=specs,
        out_specs=tuple(ANYWHERE if s[0] == grads else VMEM for s in shapes),
        scratch_shapes=[
            pltpu.VMEM((4, width, 2 * units), LOW),
            pltpu.VMEM((4, width, units), LOW),
            pltpu.VMEM((4, length, width), LOW),
            pltpu.VMEM((4, length, width), LOW),
            pltpu.VMEM((4, length, 2 * units), LOW),
            pltpu.VMEM((length, 2 * units), LOW),
            pltpu.VMEM((4, length, units), LOW),
            pltpu.VMEM((length, width), FULL),
            pltpu.VMEM((length, width), FULL),
            pltpu.VMEM((1, 1, 2, 8, 128) if second else grads, LOW),
            pltpu.VMEM((1, 8, 128) if second else pre.shape, LOW),
            pltpu.VMEM(grads, LOW),
            pltpu.SemaphoreType.DMA((3 + len(stills) + 3 * SHARES,)),
            pltpu.SemaphoreType.DMA((3,)),
            pltpu.SemaphoreType.DMA((3,)),
            pltpu.SemaphoreType.DMA((9,)),
            pltpu.SemaphoreType.DMA((9,)),
        ],
        compiler_params=pltpu.CompilerParams(
            collective_id=3 if second else 4, has_side_effects=True, vmem_limit_bytes=60 * 1024 * 1024
        ),
        cost_estimate=cost(30),
        name="ffn_second" if second else "ffn_first_backward",
    )(*args)


def attn_backward_kernel(
    last, gain_ref, gains_ref, place_ref, log_ref, after_grad_hbm, w_out_hbm, mixed_hbm, q_hbm, kv_hbm, trig_hbm,
    res_hbm, normed_hbm, w_key_hbm, w_value_hbm, w_query_hbm, *rest
):
    if last:
        prev, ffn_ref, first_hbm = rest[:3], rest[3], rest[4]
        grad_hbm, gain_out, ffn_hbm, share_hbms = rest[5], rest[6], rest[7], rest[8:11]
        rest = rest[11:]
    else:
        prev = (None, None, None)
        grad_hbm, gain_out = rest[:2]
        part_hbms = rest[2:5]
        rest = rest[5:]
    q_buf, kv_buf, trig_buf, res_buf, normed_buf, w_kv_buf, w_query_buf, grad_out, after_grad_buf, w_out_buf, mixed_buf, pair_sem, late_sem, early_sem, *rest = rest
    late = iter(late_sem.at[i] for i in range(14))
    after_grad_later = Later(after_grad_hbm, after_grad_buf, next(late))
    w_out_later = Later(w_out_hbm, w_out_buf, next(late))
    mixed_later = Later(mixed_hbm, mixed_buf, next(late))
    q_later, kv_later = Later(q_hbm, q_buf, next(late)), Later(kv_hbm, kv_buf, next(late))
    mixed_grad, delta, kv_grad, query_grad, back, grad_send, grad_recv, send_sem, recv_sem = rest[:9]
    hop = Hops(send_sem, recv_sem)
    seq, dp = lax.axis_index("seq"), lax.axis_index("dp")
    core, chip_x = lax.rem(seq, 2), lax.div(seq, 2)
    mate_seq, far_seq = seq + 1 - 2 * core, lax.rem(seq + 2, 4)
    far_mate = lax.rem(mate_seq + 2, 4)
    mate, x_mate = device(mate_seq, dp), device(far_seq, dp)
    length, width = res_hbm.shape
    stacked = GROUP * length
    kv_width = 2 * KV_HEADS * HEAD_DIM
    parts = rest[9:12]
    if last:
        f_own, f_y_recv, f_a_send, f_a_recv, f_b_send, f_b_recv, gain_recv = rest[12:19]
        prev_bufs = rest[19:22]
        ffn_out, share_outs = rest[22], rest[23:26]
        buffers = [rest[26 + 10 * i : 36 + 10 * i] for i in range(3)]
        row_y, row_z = lax.rem(dp, 2), lax.div(dp, 2)
        low_z, high_z = lax.rem(row_z, 2), lax.div(row_z, 2)
        y_mate = device(seq, dp + 1 - 2 * row_y)
        near_z = device(seq, dp + 2 - 4 * low_z)
        far_z = device(seq, dp + 4 - 8 * high_z)
        cross = device(far_mate, dp)
        greet([mate, x_mate, cross, y_mate, near_z, far_z])
        f_y = [hop(ffn_ref.at[m, :, 1 - row_y], f_y_recv.at[m], y_mate) for m in (0, 1)]
        first_y = Later(first_hbm, f_y_recv.at[2], next(late))
        own_shares = Later(ffn_ref.at[:, :, row_y], f_own, next(late))
        prev = [Later(src, dst, next(late)) for src, dst in zip(prev, prev_bufs)]
    else:
        greet([mate, x_mate])
    early = Early(early_sem)
    trig = Later(trig_hbm, trig_buf, next(late))
    normed_ref = Later(normed_hbm, normed_buf, next(late))
    w_query = Later(w_query_hbm, w_query_buf, next(late))
    w_kv = LaterPairs(w_key_hbm, w_value_hbm, w_kv_buf, pair_sem)
    res_ref = Later(res_hbm, res_buf, next(late))

    def near_fill(load, a_send):
        for h in range(2):
            a_send[h] = load(2 * h + 1 - low_z).astype(LOW)

    def far_fill(load, a_recv, b_send):
        b_send[...] = (load(2 - 2 * high_z + low_z) + a_recv[1 - high_z].astype(FULL)).astype(LOW)

    def z_total(load, a_recv, b_recv):
        return load(row_z) + a_recv[high_z].astype(FULL) + b_recv[...].astype(FULL)

    def f_load(m):
        return lambda z: own_shares()[m, z].astype(FULL) + f_y_recv[m, z].astype(FULL)

    if last:
        f_nears = [hop(f_a_send.at[m], f_a_recv.at[m], near_z, start=False) for m in range(3)]
        f_fars = [hop(f_b_send.at[m], f_b_recv.at[m], far_z, start=False) for m in range(3)]

    def f_near(m):
        own_shares()
        if m == 2:
            first_y()
        else:
            f_y[m].wait()
        near_fill(f_load(m), f_a_send.at[m])
        f_nears[m].start()

    def f_far(m):
        f_nears[m].wait()
        far_fill(f_load(m), f_a_recv.at[m], f_b_send.at[m])
        f_fars[m].start()

    def f_finish(m):
        f_fars[m].wait()
        ffn_out[m] = z_total(f_load(m), f_a_recv.at[m], f_b_recv.at[m])
        early(ffn_out.at[m], ffn_hbm.at[m])

    quarter = lambda x, c: pl.ds(pl.multiple_of(64 * x + ROWS_PAD * c, ROWS_PAD), ROWS_PAD)

    def core_start(i):
        core_recv = buffers[i][0]
        return [hop(parts[i].at[:, quarter(x, 1 - core)], core_recv.at[x], mate) for x in range(2)]

    def x_make(i):
        return hop(*buffers[i][1:3], x_mate, start=False)

    def x_start(i, copies, x_copy):
        core_recv, x_send, x_recv = buffers[i][:3]
        for copy in copies:
            copy.wait()
        joint = parts[i][:, quarter(1 - chip_x, core)].astype(FULL) + core_recv[1 - chip_x].astype(FULL)
        x_send[...] = joint.astype(LOW)
        x_copy.start()
        return x_copy

    def y_start(i, copy):
        core_recv, x_send, x_recv, own, y_recv = buffers[i][:5]
        joint = parts[i][:, quarter(chip_x, core)].astype(FULL) + core_recv[chip_x].astype(FULL)
        copy.wait()
        own[...] = (joint + x_recv[...].astype(FULL)).astype(LOW).reshape(own.shape)
        return hop(own.at[:, 1 - row_y], y_recv, y_mate)

    def part_load(i):
        own, y_recv = buffers[i][3:5]
        return lambda z: own[z, row_y].astype(FULL) + y_recv[z].astype(FULL)

    def z_start(i, copy):
        copy.wait()
        near_fill(part_load(i), buffers[i][5])
        return hop(*buffers[i][5:7], near_z)

    def z_next(i, copy):
        copy.wait()
        far_fill(part_load(i), *buffers[i][6:8])
        return hop(*buffers[i][7:9], far_z)

    def share_start(i, copy):
        gathered = buffers[i][9]
        copy.wait()
        gathered[seq] = z_total(part_load(i), buffers[i][6], buffers[i][8]).astype(LOW)
        mine = gathered.at[seq]
        return [hop(mine, mine, target) for target in (x_mate, cross, mate)]

    def share_finish(i, copies):
        gathered = buffers[i][9]
        for copy in copies:
            copy.wait()
        for s in range(4):
            share_outs[i][s * ROWS_PAD : (s + 1) * ROWS_PAD] = gathered[s].astype(FULL)
        early(share_outs[i], share_hbms[i])

    def weight(i, left, right):
        term = dot(left, right, TN)
        share = width // SHARES
        for j in range(SHARES):
            rows = term[j * share : (j + 1) * share]
            if prev[i] is not None:
                rows = rows + prev[i]()[j, :share].astype(FULL)
            parts[i][j, :share] = rows.astype(LOW)
        if not last:
            early(parts[i], part_hbms[i])

    after_grad_ref, w_out_ref = after_grad_later(), w_out_later()
    low_grad = after_grad_ref[...].astype(LOW)
    mixed_back = dot(low_grad, w_out_ref[...], NT)
    lane = lax.broadcasted_iota(jnp.int32, (length, 128), 1)
    for pair in range((HEADS + 1) // 2):
        span = min(128, HEADS * HEAD_DIM - pair * 128)
        part = mixed_back[:, pair * 128 : pair * 128 + span]
        if span < 128:
            part = jnp.concatenate([part, part], axis=1)
        else:
            mixed_grad[2 * pair + 1] = jnp.where(lane >= HEAD_DIM, part, 0.0).astype(LOW)
        mixed_grad[2 * pair] = jnp.where(lane >= HEAD_DIM, pltpu.roll(part, 64, 1), 0.0).astype(LOW)
    mixed_ref = mixed_later()
    product = mixed_back.astype(LOW).astype(FULL) * mixed_ref[...].astype(FULL)
    high = product.astype(LOW)
    rest_low = (product - high.astype(FULL)).astype(LOW)
    head = lax.broadcasted_iota(jnp.int32, (16, HEADS * HEAD_DIM), 0)
    column = lax.broadcasted_iota(jnp.int32, (16, HEADS * HEAD_DIM), 1)
    pick = jnp.where(lax.div(column, HEAD_DIM) == head, 1.0, 0.0).astype(LOW)
    sums = dot(pick, high, NT) + dot(pick, rest_low, NT)
    for g in range(KV_HEADS):
        delta[g] = jnp.concatenate([sums[3 * g + i : 3 * g + i + 1] for i in range(GROUP)], axis=1)
    query_grad[...] = jnp.zeros_like(query_grad)
    weight(0, mixed_ref[...], low_grad)
    if last:
        o_core = core_start(0)
        f_near(2)
        o_x = x_make(0)

    start, place = place_ref[0:1, :], place_ref[1:2, :]
    q_ref, kv_ref = q_later(), kv_later()

    def attend(block, g):
        columns = pl.ds(pl.multiple_of(g * 128, 128), 128)
        kv_g = kv_ref[block, :, columns]
        q_g = q_ref[pl.ds(3 * g, 3)].reshape(stacked, 128)
        out_g = mixed_grad[pl.ds(3 * g, 3)].reshape(stacked, 128)
        scores = dot(kv_g, q_g, NT)
        key = lax.broadcasted_iota(jnp.int32, (length, stacked), 0) + block * length
        weights = jnp.where((key >= start) & (key <= place), jnp.exp(scores - log_ref[g]), 0.0)
        probs_grad = dot(kv_g, out_g, NT)
        score_grad = (weights * (probs_grad - delta[g])).astype(LOW)
        kv_grad[block, :, columns] = dot(weights.astype(LOW), out_g) + dot(score_grad, q_g)
        query_grad[g] += dot(kv_g, score_grad, TN)[:HEAD_DIM]

    joint = hop(grad_send.at[0], grad_recv.at[0], mate, start=False)
    across = hop(grad_send.at[1], grad_recv.at[1], x_mate, start=False)
    beside = hop(grad_send.at[2], grad_recv.at[2], mate, start=False)

    @pl.loop(0, 4)
    def _(step):
        block = jnp.where(
            step == 0, far_mate, jnp.where(step == 1, far_seq, jnp.where(step == 2, mate_seq, seq))
        )

        @pl.when(block <= seq)
        def _():
            @pl.loop(0, KV_HEADS)
            def _(g):
                attend(block, g)

        @pl.when(block > seq)
        def _():
            kv_grad[block] = jnp.zeros_like(kv_grad[block])

        @pl.when(step == 0)
        def _():
            grad_send[0] = kv_grad[far_mate].astype(LOW)
            joint.start()
            if last:
                x_start(0, o_core, o_x)

        @pl.when(step == 1)
        def _():
            joint.wait()
            grad_send[1] = (kv_grad[far_seq] + grad_recv[0].astype(FULL)).astype(LOW)
            across.start()

        @pl.when(step == 2)
        def _():
            grad_send[2] = kv_grad[mate_seq].astype(LOW)
            beside.start()
            if last:
                f_far(2)
                f_near(0)

    trig_ref = trig()
    heads = []
    for g in range(KV_HEADS):
        turned = query_grad[g].T * SCALE
        heads += [turned[i * length : (i + 1) * length] for i in range(GROUP)]
    for pair in range((HEADS + 1) // 2):
        part = jnp.concatenate([heads[2 * pair], heads[min(2 * pair + 1, HEADS - 1)]], axis=1)
        turned = (part * trig_ref[0] - swap_halves(part) * trig_ref[1]).astype(LOW)
        at = kv_width + pair * 128
        stop = min(at + 128, kv_width + width)
        back[:, at:stop] = turned[:, : stop - at]
    weight(1, normed_ref()[...], back[:, kv_width:])
    if last:
        q_core = core_start(1)
        o_y = y_start(0, o_x)
    normed_grad = dot(back[:, kv_width:], w_query()[...], NT)
    if last:
        q_x = x_start(1, q_core, x_make(1))

    across.wait()
    beside.wait()
    own = kv_grad[seq] + grad_recv[1].astype(FULL) + grad_recv[2].astype(FULL)
    for g in range(KV_HEADS):
        part = own[:, g * 128 : (g + 1) * 128]
        back[:, g * 128 : (g + 1) * 128] = (part * trig_ref[2] - swap_halves(part) * trig_ref[3]).astype(LOW)
    weight(2, normed_ref()[...], back[:, :kv_width])
    if last:
        kv_core = core_start(2)
        f_far(0)
        f_near(1)
        kv_x = x_start(2, kv_core, x_make(2))
    normed_grad = normed_grad + dot(back[:, :kv_width], w_kv()[...])
    sent_back, gain_term = norm_back(res_ref()[...].astype(FULL), gains_ref[0:1, :], normed_grad)
    grad_out[...] = after_grad_ref[...] + sent_back
    early(grad_out, grad_hbm)
    row = lax.broadcasted_iota(jnp.int32, gain_out.shape, 0)
    gain_out[...] = gain_ref[...] + jnp.where(row == 0, gain_term, 0.0)
    if not last:
        early.finish()
        return

    partners = [mate, x_mate, y_mate, near_z, far_z]
    gain_hop = lambda n: hop(gain_out, gain_recv.at[n], partners[n])

    def gain_add(n, copy):
        copy.wait()
        gain_out[...] += gain_recv[n]

    gain_copy = gain_hop(0)
    f_finish(2)
    o_z = z_start(0, o_y)
    gain_add(0, gain_copy)
    gain_copy = gain_hop(1)
    q_y = y_start(1, q_x)
    f_far(1)
    f_finish(0)
    o_z = z_next(0, o_z)
    gain_add(1, gain_copy)
    gain_copy = gain_hop(2)
    kv_y = y_start(2, kv_x)
    q_z = z_start(1, q_y)
    gain_add(2, gain_copy)
    gain_copy = gain_hop(3)
    o_s = share_start(0, o_z)
    kv_z = z_start(2, kv_y)
    q_z = z_next(1, q_z)
    gain_add(3, gain_copy)
    gain_copy = gain_hop(4)
    f_finish(1)
    kv_z = z_next(2, kv_z)
    q_s = share_start(1, q_z)
    gain_add(4, gain_copy)
    kv_s = share_start(2, kv_z)
    share_finish(0, o_s)
    share_finish(1, q_s)
    share_finish(2, kv_s)
    early.finish()


def attn_backward(after_grad, residual, normed, gains, q, kv, log_total, mixed, attn_weights, trig, place, gain_grads, final=None):
    length, width = residual.shape
    kv_width = 2 * KV_HEADS * HEAD_DIM
    last = final is not None
    key_t, value_t, w_query, w_out = attn_weights
    args = (gain_grads, gains, place, log_total, after_grad, w_out, mixed, q, kv, trig, residual, normed)
    args = args + (key_t, value_t, w_query)
    specs = [VMEM] * 4 + [ANYWHERE] * 11
    out_specs = (ANYWHERE, VMEM)
    shapes = (((length, width), FULL), ((8, width), FULL))
    sizes = (width, width, kv_width)
    part_shapes = [((SHARES, 4 * ROWS_PAD, c), LOW) for c in sizes]
    scratch = [
        pltpu.VMEM(q.shape, LOW),
        pltpu.VMEM(kv.shape, LOW),
        pltpu.VMEM(trig.shape, FULL),
        pltpu.VMEM((length, width), residual.dtype),
        pltpu.VMEM((length, width), LOW),
        pltpu.VMEM((kv_width, width), LOW),
        pltpu.VMEM(w_query.shape, LOW),
        pltpu.VMEM((length, width), FULL),
        pltpu.VMEM((length, width), FULL),
        pltpu.VMEM(w_out.shape, LOW),
        pltpu.VMEM(mixed.shape, LOW),
        pltpu.SemaphoreType.DMA((2 * KV_HEADS,)),
        pltpu.SemaphoreType.DMA((14,)),
        pltpu.SemaphoreType.DMA((7,)),
        pltpu.VMEM((HEADS, length, 128), LOW),
        pltpu.VMEM((KV_HEADS, 1, GROUP * length), FULL),
        pltpu.VMEM((4, length, kv_width), FULL),
        pltpu.VMEM((KV_HEADS, HEAD_DIM, GROUP * length), FULL),
        pltpu.VMEM((length, kv_width + width), LOW),
        pltpu.VMEM((3, length, kv_width), LOW),
        pltpu.VMEM((3, length, kv_width), LOW),
    ]
    hops = 3
    if last:
        share, hidden = final[3].shape[3:]
        args = args + tuple(final)
        specs = specs + [ANYWHERE] * 5
        shapes = shapes + (((3, share, hidden), FULL),) + tuple(((4 * ROWS_PAD, c), FULL) for c in sizes)
        hops = 3 + 2 + 6 + 5 + 3 * (2 + 1 + 1 + 2 + 3)
        scratch += [pltpu.SemaphoreType.DMA((hops,))] * 2
        out_specs = out_specs + (ANYWHERE,) * 4
        scratch += [pltpu.VMEM(*s) for s in part_shapes]
        scratch += [
            pltpu.VMEM((3, 4, share, hidden), LOW),
            pltpu.VMEM((3, 4, share, hidden), LOW),
            pltpu.VMEM((3, 2, share, hidden), LOW),
            pltpu.VMEM((3, 2, share, hidden), LOW),
            pltpu.VMEM((3, share, hidden), LOW),
            pltpu.VMEM((3, share, hidden), LOW),
            pltpu.VMEM((5, 8, width), FULL),
        ]
        scratch += [pltpu.VMEM(*s) for s in part_shapes]
        scratch += [pltpu.VMEM(*s) for s in shapes[2:]]
        for c in sizes:
            scratch += [
                pltpu.VMEM((2, SHARES, ROWS_PAD, c), LOW),
                pltpu.VMEM((SHARES, ROWS_PAD, c), LOW),
                pltpu.VMEM((SHARES, ROWS_PAD, c), LOW),
                pltpu.VMEM((4, 2, ROWS_PAD, c), LOW),
                pltpu.VMEM((4, ROWS_PAD, c), LOW),
                pltpu.VMEM((2, ROWS_PAD, c), LOW),
                pltpu.VMEM((2, ROWS_PAD, c), LOW),
                pltpu.VMEM((ROWS_PAD, c), LOW),
                pltpu.VMEM((ROWS_PAD, c), LOW),
                pltpu.VMEM((4, ROWS_PAD, c), LOW),
            ]
    else:
        shapes, out_specs = shapes + tuple(part_shapes), out_specs + (ANYWHERE,) * 3
        scratch += [pltpu.SemaphoreType.DMA((hops,))] * 2
        scratch += [pltpu.VMEM(*s) for s in part_shapes]
    return pl.pallas_call(
        functools.partial(attn_backward_kernel, last),
        out_shape=tuple(jax.ShapeDtypeStruct(*s) for s in shapes),
        in_specs=specs,
        out_specs=out_specs,
        scratch_shapes=scratch,
        compiler_params=pltpu.CompilerParams(
            collective_id=6 if last else 5, has_side_effects=True, vmem_limit_bytes=60 * 1024 * 1024
        ),
        cost_estimate=cost(95 if last else 40),
        name="attn_backward_last" if last else "attn_backward",
    )(*args)


def split_pairs(grads):
    rows = grads.shape[0]
    pairs = grads.reshape(rows, KV_HEADS, 2, HEAD_DIM)
    return pairs[:, :, 0].reshape(rows, -1), pairs[:, :, 1].reshape(rows, -1)


def on_device(
    tokens,
    seg_ids,
    positions,
    attn_gain,
    w_query,
    w_key,
    w_value,
    w_out,
    ffn_gain,
    w_gate,
    w_up,
    w_down,
    cotangent,
):
    width = tokens.shape[2]
    trig, place = prepare(positions[0])
    attn_weights = (w_key.T, w_value.T, w_query, w_out)
    gains = jnp.pad(jnp.stack([attn_gain, ffn_gain]), ((0, 6), (0, 0)))
    whole = lax.axis_size("dp") != SHARES
    share = width // SHARES
    own_weights = (w_gate, w_up, w_down.T)

    def over_x(value):
        return lax.ppermute(value, "seq", [(s, (s + 2) % 4) for s in range(4)])

    def over_rows_piece(value, d):
        return lax.dynamic_slice_in_dim(value, jnp.minimum(d * PIECE, width - PIECE), PIECE, axis=0)

    if whole:
        theirs = [over_x(w) for w in own_weights]
        far = jnp.stack([jnp.concatenate([over_rows_piece(w, d) for w in theirs]) for d in range(SHARES)])
    else:
        piece = jnp.concatenate([over_rows_piece(w, lax.axis_index("dp")) for w in own_weights])
        far = lax.all_gather(over_x(piece), "dp", axis=0)

    results = forward(tokens[0], gains, place, cotangent[0], attn_weights, trig, own_weights)
    first, (rows_all, pre_all, residual), results = results[:KEPT], results[KEPT : KEPT + 3], results[KEPT + 3 :]
    second, normed_two, low_halves = results[:KEPT], results[KEPT], results[KEPT + 1 :]
    output, after_grad, gain_grads, ffn_grads = ffn_all(
        True, False, cotangent[0], normed_two, second[5], gains, low_halves, own_weights, far
    )

    def attn_args(after_grad, residual, kept, gain_grads):
        normed, q, kv, log_total, mixed = kept[:5]
        return (after_grad, residual, normed, gains, q, kv, log_total, mixed, attn_weights, trig, place, gain_grads)

    upstream, gain_grads, *parts = attn_backward(*attn_args(after_grad, residual, second, gain_grads))
    after_grad, gain_grads, ffn_grads, *first_y = ffn_all(
        False, not whole, upstream, None, first[5], gains, (rows_all,), own_weights, far, ffn_grads, pre_all, gain_grads
    )
    args = attn_args(after_grad, tokens[0], first, gain_grads)
    if whole:
        upstream, gain_grads, *terms = attn_backward(*args)
        parts = [part.astype(FULL) + term.astype(FULL) for part, term in zip(parts, terms)]
    else:
        upstream, gain_all, ffn_share, *shares = attn_backward(*args, (*parts, ffn_grads, *first_y))
    if whole:

        def over_rows(grads, dim):
            grads = lax.psum_scatter(grads.astype(LOW), "dp", scatter_dimension=dim, tiled=True)
            return grads.astype(FULL)

        def over_all(grads, dim):
            return lax.psum(over_rows(grads, dim).astype(LOW), "seq").astype(FULL)

        shares = [over_all(part[:, :share].reshape(width, -1), 0) for part in parts]
        ffn_share = over_rows(ffn_grads.reshape(3, width, -1), 1)
        own_gains = over_all(gain_grads[:2], 1)
    else:
        shares = [part[:share] for part in shares]
        own_gains = lax.dynamic_slice_in_dim(gain_all, lax.axis_index("dp") * share, share, axis=1)
    key_share, value_share = split_pairs(shares[2])
    return (
        output[None],
        upstream[None],
        own_gains[0],
        shares[1],
        key_share,
        value_share,
        shares[0],
        own_gains[1],
        ffn_share[0],
        ffn_share[1],
        ffn_share[2].T,
    )


def solution(mesh):
    in_specs = (
        P("dp", "seq", None),
        P("dp", "seq"),
        P("dp", "seq"),
        P(),
        P(),
        P(),
        P(),
        P(),
        P(),
        P(None, "seq"),
        P(None, "seq"),
        P("seq", None),
        P("dp", "seq", None),
    )
    out_specs = (
        P("dp", "seq", None),
        P("dp", "seq", None),
        P("dp"),
        P("dp", None),
        P("dp", None),
        P("dp", None),
        P("dp", None),
        P("dp"),
        P("dp", "seq"),
        P("dp", "seq"),
        P("seq", "dp"),
    )
    return jax.shard_map(
        on_device, mesh=mesh, in_specs=in_specs, out_specs=out_specs, check_vma=False
    )
```

```python
import functools

import jax
import jax.numpy as jnp
from jax import lax
from jax.experimental import pallas as pl
from jax.experimental.pallas import tpu as pltpu
from jax.sharding import PartitionSpec as P

MESH_ID = pl.DeviceIdType.MESH
HEADS = 15
KV_HEADS = 5
GROUP = 3
HEAD_DIM = 64
EPSILON = 1e-05
THETA = 10000.0
CHUNKS = 2
SHARES = 8
ROWS_PAD = 32
PIECE = 128
MASKED = -1e30
LOW = jnp.bfloat16
FULL = jnp.float32
SCALE = HEAD_DIM ** (-0.5)
NT = (((1,), (1,)), ((), ()))
TN = (((0,), (0,)), ((), ()))


def device(seq_pos, dp_pos):
    return {"seq": seq_pos, "dp": dp_pos}


def send(src, dst, send_sem, recv_sem, target, start=True):
    copy = pltpu.make_async_remote_copy(
        src_ref=src,
        dst_ref=dst,
        send_sem=send_sem,
        recv_sem=recv_sem,
        device_id=target,
        device_id_type=MESH_ID,
    )
    if start:
        copy.start()
    return copy


class Hops:
    def __init__(self, send_sem, recv_sem):
        self.send_sem, self.recv_sem, self.used = send_sem, recv_sem, 0

    def __call__(self, src, dst, target, start=True):
        index, self.used = self.used, self.used + 1
        return send(src, dst, self.send_sem.at[index], self.recv_sem.at[index], target, start)


class Later:
    def __init__(self, src, dst, sem):
        self.copy, self.dst, self.waited = pltpu.make_async_copy(src, dst, sem), dst, False
        self.copy.start()

    def __call__(self):
        if not self.waited:
            self.copy.wait()
            self.waited = True
        return self.dst


class Early:
    def __init__(self, sem):
        self.sem, self.copies = sem, []

    def __call__(self, src, dst, start=True):
        self.copies.append(pltpu.make_async_copy(src, dst, self.sem.at[len(self.copies)]))
        if start:
            self.copies[-1].start()
        return self.copies[-1]

    def finish(self):
        for copy in self.copies:
            copy.wait()


class LaterPairs:
    def __init__(self, key_hbm, value_hbm, dst, sem):
        self.copies, self.dst = [], dst
        for h in range(2 * KV_HEADS):
            src = (key_hbm, value_hbm)[h % 2].at[pl.ds(h // 2 * HEAD_DIM, HEAD_DIM)]
            self.copies.append(pltpu.make_async_copy(src, dst.at[pl.ds(h * HEAD_DIM, HEAD_DIM)], sem.at[h]))
            self.copies[-1].start()

    def __call__(self):
        for copy in self.copies:
            copy.wait()
        self.copies = []
        return self.dst


def greet(targets):
    barrier = pltpu.get_barrier_semaphore()
    for target in targets:
        pl.semaphore_signal(barrier, inc=1, device_id=target, device_id_type=MESH_ID)
    pl.semaphore_wait(barrier, len(targets))


def dot(left, right, dims=None):
    if dims is None:
        return jnp.dot(left, right, preferred_element_type=FULL)
    return lax.dot_general(left, right, dims, preferred_element_type=FULL)


def cost(microseconds):
    return pl.CostEstimate(flops=int(microseconds * 1.15e9), bytes_accessed=1 << 20, transcendentals=0)


def inverse_rms(value):
    return lax.rsqrt(jnp.mean(value * value, axis=-1, keepdims=True) + EPSILON)


def swap_halves(value):
    lane = lax.broadcasted_iota(jnp.int32, value.shape, 1)
    first = (lane & (HEAD_DIM // 2)) == 0
    return jnp.where(first, pltpu.roll(value, 96, 1), pltpu.roll(value, 32, 1))


VMEM = pl.BlockSpec(memory_space=pltpu.VMEM)
ANYWHERE = pl.BlockSpec(memory_space=pl.ANY)


def prepare(positions):
    length = positions.shape[0]
    frequency = THETA ** (-(jnp.arange(HEAD_DIM // 2, dtype=FULL) * 2.0 / HEAD_DIM))
    angles = positions.astype(FULL)[:, None] * frequency
    cos, sin = jnp.cos(angles), jnp.sin(angles)
    one, none = jnp.ones((length, HEAD_DIM), FULL), jnp.zeros((length, HEAD_DIM), FULL)
    trig = jnp.stack(
        [
            jnp.concatenate([cos, cos, cos, cos], 1),
            jnp.concatenate([-sin, sin, -sin, sin], 1),
            jnp.concatenate([cos, cos, one], 1),
            jnp.concatenate([-sin, sin, none], 1),
        ]
    )
    own = lax.axis_index("seq") * length + jnp.arange(length, dtype=jnp.int32)
    place = jnp.stack([jnp.tile(own - positions, GROUP), jnp.tile(own, GROUP)])
    place = jnp.pad(place, ((0, 6), (0, 0)))
    return trig, place


def norm_back(value, gain, grad):
    inverse = inverse_rms(value)
    weighted = grad * gain
    inner = jnp.mean(weighted * value, axis=-1, keepdims=True)
    back = inverse * weighted - value * (inverse * inverse * inverse) * inner
    return back, jnp.sum(grad * value * inverse, axis=0, keepdims=True)


KEPT = 6
CUT = 3


def forward_kernel(
    tokens_ref, gains_ref, place_ref, cotangent_hbm, w_key_hbm, w_value_hbm, w_query_hbm, w_out_hbm, trig_hbm,
    w_gate_hbm, w_up_hbm, w_down_hbm, *rest
):
    first_hbm, (rows_hbm, pre_hbm, res_hbm), rest = rest[:KEPT], rest[KEPT : KEPT + 3], rest[KEPT + 3 :]
    second_hbm, two_hbm, extra_outs, rest = rest[:KEPT], rest[KEPT], rest[KEPT + 1 : KEPT + 3], rest[KEPT + 3 :]
    first, second, rest = rest[:KEPT], rest[KEPT : 2 * KEPT], rest[2 * KEPT :]
    (
        w_kv_buf, w_query_buf, w_out_buf, trig_buf, w_gate_buf, w_up_buf, w_down_buf,
        two, rows, pre, res, peak, total, acc, mate_send, mate_recv, x_send, x_recv, own_far,
        pair_sem, late_sem, early_sem, send_sem, recv_sem,
    ) = rest
    w_kv = LaterPairs(w_key_hbm, w_value_hbm, w_kv_buf, pair_sem)
    trig, w_query, w_out, w_gate, w_up, w_down = [
        Later(src, dst, late_sem.at[i])
        for i, (src, dst) in enumerate(
            (
                (trig_hbm, trig_buf), (w_query_hbm, w_query_buf), (w_out_hbm, w_out_buf),
                (w_gate_hbm, w_gate_buf), (w_up_hbm, w_up_buf), (w_down_hbm, w_down_buf),
            )
        )
    ]
    early, hop = Early(early_sem), Hops(send_sem, recv_sem)
    seq, dp = lax.axis_index("seq"), lax.axis_index("dp")
    core = lax.rem(seq, 2)
    mate_seq, far_seq = seq + 1 - 2 * core, lax.rem(seq + 2, 4)
    far_mate = lax.rem(mate_seq + 2, 4)
    mate, x_mate = device(mate_seq, dp), device(far_seq, dp)
    length = tokens_ref.shape[0]
    stacked = GROUP * length
    start, place = place_ref[0:1, :], place_ref[1:2, :]
    step = length // CHUNKS
    part = lambda k: pl.ds(k * step, step)

    def attention(residual_ref, buffers, hbm, extra_ref, extra_out, meet):
        normed, q, kv, log_total, mixed, after = buffers
        residual = residual_ref[...].astype(FULL)
        normed[...] = (residual * inverse_rms(residual) * gains_ref[0:1, :]).astype(LOW)
        early(normed, hbm[0])
        kv_pre = dot(normed[...], w_kv()[...], NT)
        trig_ref = trig()
        for g in range(KV_HEADS):
            piece = kv_pre[:, g * 128 : (g + 1) * 128]
            turned = piece * trig_ref[2] + swap_halves(piece) * trig_ref[3]
            kv[seq, :, g * 128 : (g + 1) * 128] = turned.astype(LOW)
        if meet:
            greet([mate, x_mate])
        spans = (pl.ds(0, CUT * 128), pl.ds(CUT * 128, (KV_HEADS - CUT) * 128))
        to_x = [hop(kv.at[seq, :, s], kv.at[seq, :, s], x_mate) for s in spans]
        to_mate = hop(kv.at[seq], kv.at[seq], mate)
        onward = [hop(kv.at[far_seq, :, s], kv.at[far_seq, :, s], mate, start=False) for s in spans]
        mine, theirs = extra_out.at[seq], extra_out.at[far_seq]
        extra = [early(extra_ref, mine, start=False)]
        extra += [hop(extra_ref, mine, target, start=False) for target in (x_mate, mate)]
        kv_keep = early(kv, hbm[2], start=False)
        q_pre = dot(normed[...], w_query()[...])
        lane = lax.broadcasted_iota(jnp.int32, (length, 128), 1)
        for pair in range((HEADS + 1) // 2):
            width = min(128, HEADS * HEAD_DIM - pair * 128)
            piece = q_pre[:, pair * 128 : pair * 128 + width]
            if width < 128:
                piece = jnp.concatenate([piece, piece], axis=1)
            turned = (piece * trig_ref[0] + swap_halves(piece) * trig_ref[1]) * SCALE
            q[2 * pair] = jnp.where(lane < HEAD_DIM, turned, 0.0).astype(LOW)
            if width == 128:
                q[2 * pair + 1] = jnp.where(lane < HEAD_DIM, pltpu.roll(turned, 64, 1), 0.0).astype(LOW)
        early(q, hbm[1])

        def attend(block, g):
            kv_g = kv[block, :, pl.ds(pl.multiple_of(g * 128, 128), 128)]
            q_g = q[pl.ds(3 * g, 3)].reshape(stacked, 128)
            scores = dot(kv_g, q_g, NT)
            key = lax.broadcasted_iota(jnp.int32, (length, stacked), 0) + block * length
            scores = jnp.where((key >= start) & (key <= place), scores, MASKED)
            new_peak = jnp.maximum(peak[g], jnp.max(scores, axis=0, keepdims=True))
            weights = jnp.exp(scores - new_peak)
            fade = jnp.exp(peak[g] - new_peak)
            total[g] = jnp.sum(weights, axis=0, keepdims=True) + fade * total[g]
            acc[g] = dot(kv_g, weights.astype(LOW), TN)[HEAD_DIM:] + fade * acc[g]
            peak[g] = new_peak

        peak[...] = jnp.full_like(peak, MASKED)
        total[...] = jnp.zeros_like(total)
        acc[...] = jnp.zeros_like(acc)

        @pl.loop(0, 6)
        def _(turn):
            @pl.when(turn == 1)
            def _():
                to_mate.wait()

            @pl.when(turn == 2)
            def _():
                to_x[0].wait()
                onward[0].start()
                for copy in extra:
                    copy.start()

            @pl.when(turn == 3)
            def _():
                onward[0].wait()

            @pl.when(turn == 4)
            def _():
                to_x[1].wait()
                onward[1].start()

            @pl.when(turn == 5)
            def _():
                onward[1].wait()
                kv_keep.start()

            block = jnp.where(
                turn == 0, seq, jnp.where(turn == 1, mate_seq, jnp.where(lax.rem(turn, 2) == 0, far_seq, far_mate))
            )
            low = jnp.where(turn < 4, 0, CUT)
            high = jnp.where((turn == 2) | (turn == 3), CUT, KV_HEADS)

            @pl.when(block <= seq)
            def _():
                @pl.loop(low, high)
                def _(g):
                    attend(block, g)

        for g in range(KV_HEADS):
            heads = (acc[g] / total[g]).T.astype(LOW)
            log_total[g] = peak[g] + jnp.log(total[g])
            for i in range(GROUP):
                h = GROUP * g + i
                mixed[:, h * HEAD_DIM : (h + 1) * HEAD_DIM] = heads[i * length : (i + 1) * length]
        early(log_total, hbm[3])
        early(mixed, hbm[4])
        extra[1].wait()
        return hop(theirs, theirs, mate), extra[2]

    def project(residual_ref, buffers, rows_of, two_ref):
        mixed, after = buffers[4:]
        value = residual_ref[rows_of].astype(FULL) + dot(mixed[rows_of], w_out()[...])
        after[rows_of] = value
        two_ref[rows_of] = (value * inverse_rms(value) * gains_ref[1:2, :]).astype(LOW)

    waits = attention(tokens_ref, first, first_hbm, cotangent_hbm.at[pl.ds(0, step)], extra_outs[0], True)

    to_x = []
    for k in range(CHUNKS):
        project(tokens_ref, first, part(k), rows.at[seq])
        to_x.append(hop(rows.at[seq, part(k)], rows.at[seq, part(k)], x_mate))
    to_mate = hop(rows.at[seq], rows.at[seq], mate)
    early(first[5], first_hbm[5])
    for copy in waits:
        copy.wait()
    w_gate_ref, w_up_ref, w_down_ref = w_gate(), w_up(), w_down()
    units = w_gate_ref.shape[1]

    def ffn(quarter, rows_of):
        block = rows[quarter, rows_of]
        gate = dot(block, w_gate_ref[...])
        up = dot(block, w_up_ref[...])
        pre[quarter, rows_of, :units] = gate.astype(LOW)
        pre[quarter, rows_of, units:] = up.astype(LOW)
        hidden = (gate * jax.nn.sigmoid(gate) * up).astype(LOW)
        return dot(hidden, w_down_ref[...], NT)

    everything = pl.ds(0, length)
    res[...] = first[5][...] + ffn(seq, everything)
    to_mate.wait()
    mate_send[0] = ffn(mate_seq, everything).astype(LOW)
    back = hop(mate_send.at[0], mate_recv.at[0], mate)
    last = []
    for k in range(CHUNKS):
        to_x[k].wait()
        onward = hop(rows.at[far_seq, part(k)], rows.at[far_seq, part(k)], mate)
        own_far[part(k)] = ffn(far_seq, part(k))
        onward.wait()
        mate_send[1, part(k)] = ffn(far_mate, part(k)).astype(LOW)
        joint = hop(mate_send.at[1, part(k)], mate_recv.at[1, part(k)], mate)
        joint.wait()
        x_send[part(k)] = (own_far[part(k)] + mate_recv[1, part(k)].astype(FULL)).astype(LOW)
        last.append(hop(x_send.at[part(k)], x_recv.at[part(k)], x_mate))
    early(rows, rows_hbm)
    early(pre, pre_hbm)
    back.wait()
    res[...] += mate_recv[0].astype(FULL)
    for k in range(CHUNKS):
        last[k].wait()
        res[part(k)] += x_recv[part(k)].astype(FULL)
    early(res, res_hbm)

    waits = attention(res, second, second_hbm, cotangent_hbm.at[pl.ds(step, step)], extra_outs[1], False)
    project(res, second, everything, two)
    early(second[5], second_hbm[5])
    early(two, two_hbm)
    for copy in waits:
        copy.wait()
    early.finish()


def forward(tokens, gains, place, cotangent, attn_weights, trig, ffn_weights):
    length, width = tokens.shape
    kv_width = 2 * KV_HEADS * HEAD_DIM
    stats = (KV_HEADS, 1, GROUP * length)
    units = ffn_weights[0].shape[1]
    kept = (
        ((length, width), LOW),
        ((HEADS, length, 128), LOW),
        ((4, length, kv_width), LOW),
        (stats, FULL),
        ((length, HEADS * HEAD_DIM), LOW),
        ((length, width), FULL),
    )
    middle = (((4, length, width), LOW), ((4, length, 2 * units), LOW), ((length, width), FULL))
    extra = ((4, length // 2, width), LOW)
    shapes = kept + middle + kept + (((length, width), LOW), extra, extra)
    key_t, value_t, w_query, w_out = attn_weights
    return pl.pallas_call(
        forward_kernel,
        out_shape=tuple(jax.ShapeDtypeStruct(*s) for s in shapes),
        in_specs=[VMEM] * 3 + [ANYWHERE] * 9,
        out_specs=(ANYWHERE,) * len(shapes),
        scratch_shapes=[pltpu.VMEM(*s) for s in kept + kept]
        + [
            pltpu.VMEM((kv_width, width), LOW),
            pltpu.VMEM(w_query.shape, LOW),
            pltpu.VMEM(w_out.shape, LOW),
            pltpu.VMEM(trig.shape, FULL),
        ]
        + [pltpu.VMEM(w.shape, LOW) for w in ffn_weights]
        + [pltpu.VMEM((length, width), LOW)]
        + [pltpu.VMEM(*s) for s in middle]
        + [
            pltpu.VMEM(stats, FULL),
            pltpu.VMEM(stats, FULL),
            pltpu.VMEM((KV_HEADS, HEAD_DIM, GROUP * length), FULL),
            pltpu.VMEM((2, length, width), LOW),
            pltpu.VMEM((2, length, width), LOW),
            pltpu.VMEM((length, width), LOW),
            pltpu.VMEM((length, width), LOW),
            pltpu.VMEM((length, width), FULL),
            pltpu.SemaphoreType.DMA((2 * KV_HEADS,)),
            pltpu.SemaphoreType.DMA((6,)),
            pltpu.SemaphoreType.DMA((18,)),
            pltpu.SemaphoreType.DMA((26,)),
            pltpu.SemaphoreType.DMA((26,)),
        ],
        compiler_params=pltpu.CompilerParams(
            collective_id=0, has_side_effects=True, vmem_limit_bytes=60 * 1024 * 1024
        ),
        cost_estimate=cost(85),
        name="forward",
    )(tokens, gains, place, cotangent, *attn_weights, trig, *ffn_weights)


def ffn_all_kernel(second, reduce, up_ref, own_ref, after_hbm, gains_ref, still_refs, gate_ref, upw_ref, down_ref, far_ref, *rest):
    y_part = prev_hbm = pre_hbm = None
    if second:
        result_out, rest = rest[0], rest[1:]
    else:
        prev_hbm, pre_hbm, gain_ref, *rest = rest
    grad_out, gain_out, weight_hbm, *rest = rest
    if reduce:
        y_part, *rest = rest
    (
        w_in, w_down, still_ref, moved, in_grad, in_temp, hidden, back, after_buf, prev_buf, pre_buf, weight_out,
        load_sem, late_sem, early_sem, send_sem, recv_sem,
    ) = rest
    early = Early(early_sem)
    after_ref = Later(after_hbm, after_buf, late_sem.at[0])
    pre_ref = None if second else Later(pre_hbm, pre_buf, late_sem.at[2])
    hop = Hops(send_sem, recv_sem)
    seq, dp = lax.axis_index("seq"), lax.axis_index("dp")
    core = lax.rem(seq, 2)
    mate_seq, far_seq = seq + 1 - 2 * core, lax.rem(seq + 2, 4)
    far_mate = lax.rem(mate_seq + 2, 4)
    mate, x_mate = device(mate_seq, dp), device(far_seq, dp)
    length, width = up_ref.shape
    units = gate_ref.shape[1]
    whole = pl.ds(0, width)

    def slots(w, rows):
        return w_in.at[w, rows, :units], w_in.at[w, rows, units:], w_down.at[w, rows]

    loads = []

    def load(src, dst):
        loads.append(pltpu.make_async_copy(src, dst, load_sem.at[len(loads)]))
        loads[-1].start()

    for src, dst in zip((gate_ref, upw_ref, down_ref), slots(0, whole)):
        load(src, dst)
    moved[seq] = own_ref[...].astype(LOW)
    at = 0
    for ref in still_refs:
        load(ref, still_ref.at[:, pl.ds(at, ref.shape[1])])
        at += ref.shape[1]
    far_from = len(loads)
    for d in range(SHARES):
        at = min(d * PIECE, width - PIECE)
        rows = min(PIECE, width - PIECE - at) if d == SHARES - 2 else PIECE
        for i, dst in enumerate(slots(2, pl.ds(at, rows))):
            load(far_ref.at[d, pl.ds(i * PIECE, rows)], dst)
    y_mate = device(seq, dp + 1 - 2 * lax.rem(dp, 2))
    greet([mate, x_mate] + ([y_mate] if reduce else []))
    mine, theirs = moved.at[seq], moved.at[far_seq]
    to_x = hop(mine, mine, x_mate)
    to_mate = hop(mine, mine, mate)
    beside = [hop(src, dst, mate) for src, dst in zip((gate_ref, upw_ref, down_ref), slots(1, whole))]
    rows_ref, low_ref = (moved, still_ref) if second else (still_ref, moved)

    def halves(quarter, w, grads, known=False):
        both = pre_buf[quarter].astype(FULL) if known else dot(rows_ref[quarter], w_in[w])
        gate, up = both[:, :units], both[:, units:]
        bend = jax.nn.sigmoid(gate)
        silu = gate * bend
        hidden_grad = dot(low_ref[quarter], w_down[w])
        grads[:, :units] = (hidden_grad * up * bend * (1.0 + gate * (1.0 - bend))).astype(LOW)
        grads[:, units:] = (hidden_grad * silu).astype(LOW)
        return (silu * up).astype(LOW)

    def local(w):
        act = halves(seq, w, in_temp)
        back[...] += dot(in_temp[...], w_in[w], NT)
        if second:
            grad_out[...] += dot(act, w_down[w], NT)

    for copy in loads[:far_from]:
        copy.wait()
    flat = lambda ref: ref[...].reshape(4 * length, ref.shape[2])
    share = width // SHARES

    def finish(i, term):
        for j in range(SHARES):
            rows = term[j * share : (j + 1) * share]
            if prev_ref is not None:
                rows = rows + prev_ref()[i, j // 2, j % 2].astype(FULL)
            weight_out[i, j // 2, j % 2] = rows.astype(LOW)
        early(weight_out.at[i], weight_hbm.at[i])

    if second:
        hidden[seq] = halves(seq, 0, in_grad.at[seq])
        back[...] = dot(in_grad[seq], w_in[0], NT)
        grad_out[...] = after_ref()[...] + dot(hidden[seq], w_down[0], NT)
    else:
        pre_ref()

        @pl.loop(0, 4)
        def _(quarter):
            both = pre_buf[quarter].astype(FULL)
            gate = both[:, :units]
            hidden[quarter] = (gate * jax.nn.sigmoid(gate) * both[:, units:]).astype(LOW)

        halves(seq, 0, in_grad.at[seq], True)
        back[...] = dot(in_grad[seq], w_in[0], NT)
    if not second:
        for copy in beside:
            copy.wait()
        local(1)
    for copy in loads[far_from:]:
        copy.wait()
    across = [hop(w_in.at[2], w_in.at[3], mate), hop(w_down.at[2], w_down.at[3], mate)]
    prev_ref = None if second else Later(prev_hbm, prev_buf, late_sem.at[1])
    if second:
        for copy in beside:
            copy.wait()

        @pl.loop(1, 4)
        def _(w):
            @pl.when(w == 3)
            def _():
                for copy in across:
                    copy.wait()

            local(w)

    else:
        local(2)

    to_mate.wait()
    if not second:
        halves(mate_seq, 0, in_grad.at[mate_seq], True)
    to_x.wait()
    onward = hop(theirs, theirs, mate)
    if second:

        @pl.loop(0, 3)
        def _(i):
            @pl.when(i == 2)
            def _():
                onward.wait()

            quarter = jnp.where(i == 0, mate_seq, jnp.where(i == 1, far_seq, far_mate))
            hidden[quarter] = halves(quarter, 0, in_grad.at[quarter])

        both = dot(flat(rows_ref), flat(in_grad), TN)
        finish(0, both[:, :units])
        finish(1, both[:, units:])
        finish(2, dot(flat(low_ref), flat(hidden), TN))
    else:
        onward.wait()
        finish(2, dot(flat(low_ref), flat(hidden), TN))
        if reduce:
            first_y = hop(weight_out.at[2, :, 1 - lax.rem(dp, 2)], y_part, y_mate)

        @pl.loop(0, 2)
        def _(i):
            quarter = jnp.where(i == 0, far_seq, far_mate)
            halves(quarter, 0, in_grad.at[quarter], True)

        both = dot(flat(rows_ref), flat(in_grad), TN)
        finish(0, both[:, :units])
        finish(1, both[:, units:])
        for copy in across:
            copy.wait()
        local(3)
    if second:
        result_out[...] = grad_out[...].astype(LOW)
    sent_back, gain_term = norm_back(after_ref()[...], gains_ref[1:2, :], back[...])
    grad_out[...] = up_ref[...].astype(FULL) + sent_back
    row = lax.broadcasted_iota(jnp.int32, gain_out.shape, 0)
    gain_term = jnp.where(row == 1, gain_term, 0.0)
    gain_out[...] = gain_term if second else gain_ref[...] + gain_term
    if reduce:
        first_y.wait()
    early.finish()


def ffn_all_call(stills, second, reduce, *refs):
    refs = refs if second else refs[:1] + refs
    return ffn_all_kernel(second, reduce, *refs[:4], refs[4 : 4 + stills], *refs[4 + stills :])


def ffn_all(second, reduce, upstream, own, after, gains, stills, weights, far, prev=None, pre=None, gain_grads=None):
    length, width = after.shape
    units = weights[0].shape[1]
    share = width // SHARES
    grads = (3, SHARES // 2, 2, share, units)
    shapes = (
        ((length, width), FULL),
        ((8, width), FULL),
        (grads, LOW),
    )
    if second:
        shapes = (((length, width), LOW),) + shapes
    if reduce:
        shapes = shapes + (((SHARES // 2, share, units), LOW),)
    args = (after, gains) + tuple(stills) + tuple(weights) + (far,)
    specs = [ANYWHERE, VMEM] + [ANYWHERE] * (len(stills) + 4)
    if second:
        args, specs = (upstream, own) + args, [VMEM, VMEM] + specs
    else:
        args, specs = (upstream,) + args, [VMEM] + specs
        args, specs = args + (prev, pre, gain_grads), specs + [ANYWHERE] * 2 + [VMEM]
    return pl.pallas_call(
        functools.partial(ffn_all_call, len(stills), second, reduce),
        out_shape=tuple(jax.ShapeDtypeStruct(*s) for s in shapes),
        in_specs=specs,
        out_specs=tuple(ANYWHERE if s[0] == grads else VMEM for s in shapes),
        scratch_shapes=[
            pltpu.VMEM((4, width, 2 * units), LOW),
            pltpu.VMEM((4, width, units), LOW),
            pltpu.VMEM((4, length, width), LOW),
            pltpu.VMEM((4, length, width), LOW),
            pltpu.VMEM((4, length, 2 * units), LOW),
            pltpu.VMEM((length, 2 * units), LOW),
            pltpu.VMEM((4, length, units), LOW),
            pltpu.VMEM((length, width), FULL),
            pltpu.VMEM((length, width), FULL),
            pltpu.VMEM((1, 1, 2, 8, 128) if second else grads, LOW),
            pltpu.VMEM((1, 8, 128) if second else pre.shape, LOW),
            pltpu.VMEM(grads, LOW),
            pltpu.SemaphoreType.DMA((3 + len(stills) + 3 * SHARES,)),
            pltpu.SemaphoreType.DMA((3,)),
            pltpu.SemaphoreType.DMA((3,)),
            pltpu.SemaphoreType.DMA((9,)),
            pltpu.SemaphoreType.DMA((9,)),
        ],
        compiler_params=pltpu.CompilerParams(
            collective_id=3 if second else 4, has_side_effects=True, vmem_limit_bytes=60 * 1024 * 1024
        ),
        cost_estimate=cost(30),
        name="ffn_second" if second else "ffn_first_backward",
    )(*args)


def attn_backward_kernel(
    last, gain_ref, gains_ref, place_ref, log_ref, after_grad_hbm, w_out_hbm, mixed_hbm, q_hbm, kv_hbm, trig_hbm,
    res_hbm, normed_hbm, w_key_hbm, w_value_hbm, w_query_hbm, *rest
):
    if last:
        prev, ffn_ref, first_hbm = rest[:3], rest[3], rest[4]
        grad_hbm, gain_out, ffn_hbm, share_hbms = rest[5], rest[6], rest[7], rest[8:11]
        rest = rest[11:]
    else:
        prev = (None, None, None)
        grad_hbm, gain_out = rest[:2]
        part_hbms = rest[2:5]
        rest = rest[5:]
    q_buf, kv_buf, trig_buf, res_buf, normed_buf, w_kv_buf, w_query_buf, grad_out, after_grad_buf, w_out_buf, mixed_buf, pair_sem, late_sem, early_sem, *rest = rest
    late = iter(late_sem.at[i] for i in range(14))
    after_grad_later = Later(after_grad_hbm, after_grad_buf, next(late))
    w_out_later = Later(w_out_hbm, w_out_buf, next(late))
    mixed_later = Later(mixed_hbm, mixed_buf, next(late))
    q_later, kv_later = Later(q_hbm, q_buf, next(late)), Later(kv_hbm, kv_buf, next(late))
    mixed_grad, delta, kv_grad, query_grad, back, grad_send, grad_recv, send_sem, recv_sem = rest[:9]
    hop = Hops(send_sem, recv_sem)
    seq, dp = lax.axis_index("seq"), lax.axis_index("dp")
    core, chip_x = lax.rem(seq, 2), lax.div(seq, 2)
    mate_seq, far_seq = seq + 1 - 2 * core, lax.rem(seq + 2, 4)
    far_mate = lax.rem(mate_seq + 2, 4)
    mate, x_mate = device(mate_seq, dp), device(far_seq, dp)
    length, width = res_hbm.shape
    stacked = GROUP * length
    kv_width = 2 * KV_HEADS * HEAD_DIM
    parts = rest[9:12]
    if last:
        f_own, f_y_recv, f_a_send, f_a_recv, f_b_send, f_b_recv, gain_recv = rest[12:19]
        prev_bufs = rest[19:22]
        ffn_out, share_outs = rest[22], rest[23:26]
        buffers = [rest[26 + 10 * i : 36 + 10 * i] for i in range(3)]
        row_y, row_z = lax.rem(dp, 2), lax.div(dp, 2)
        low_z, high_z = lax.rem(row_z, 2), lax.div(row_z, 2)
        y_mate = device(seq, dp + 1 - 2 * row_y)
        near_z = device(seq, dp + 2 - 4 * low_z)
        far_z = device(seq, dp + 4 - 8 * high_z)
        cross = device(far_mate, dp)
        greet([mate, x_mate, cross, y_mate, near_z, far_z])
        f_y = [hop(ffn_ref.at[m, :, 1 - row_y], f_y_recv.at[m], y_mate) for m in (0, 1)]
        first_y = Later(first_hbm, f_y_recv.at[2], next(late))
        own_shares = Later(ffn_ref.at[:, :, row_y], f_own, next(late))
        prev = [Later(src, dst, next(late)) for src, dst in zip(prev, prev_bufs)]
    else:
        greet([mate, x_mate])
    early = Early(early_sem)
    trig = Later(trig_hbm, trig_buf, next(late))
    normed_ref = Later(normed_hbm, normed_buf, next(late))
    w_query = Later(w_query_hbm, w_query_buf, next(late))
    w_kv = LaterPairs(w_key_hbm, w_value_hbm, w_kv_buf, pair_sem)
    res_ref = Later(res_hbm, res_buf, next(late))

    def near_fill(load, a_send):
        for h in range(2):
            a_send[h] = load(2 * h + 1 - low_z).astype(LOW)

    def far_fill(load, a_recv, b_send):
        b_send[...] = (load(2 - 2 * high_z + low_z) + a_recv[1 - high_z].astype(FULL)).astype(LOW)

    def z_total(load, a_recv, b_recv):
        return load(row_z) + a_recv[high_z].astype(FULL) + b_recv[...].astype(FULL)

    def f_load(m):
        return lambda z: own_shares()[m, z].astype(FULL) + f_y_recv[m, z].astype(FULL)

    if last:
        f_nears = [hop(f_a_send.at[m], f_a_recv.at[m], near_z, start=False) for m in range(3)]
        f_fars = [hop(f_b_send.at[m], f_b_recv.at[m], far_z, start=False) for m in range(3)]

    def f_near(m):
        own_shares()
        if m == 2:
            first_y()
        else:
            f_y[m].wait()
        near_fill(f_load(m), f_a_send.at[m])
        f_nears[m].start()

    def f_far(m):
        f_nears[m].wait()
        far_fill(f_load(m), f_a_recv.at[m], f_b_send.at[m])
        f_fars[m].start()

    def f_finish(m):
        f_fars[m].wait()
        ffn_out[m] = z_total(f_load(m), f_a_recv.at[m], f_b_recv.at[m])
        early(ffn_out.at[m], ffn_hbm.at[m])

    quarter = lambda x, c: pl.ds(pl.multiple_of(64 * x + ROWS_PAD * c, ROWS_PAD), ROWS_PAD)

    def core_start(i):
        core_recv = buffers[i][0]
        return [hop(parts[i].at[:, quarter(x, 1 - core)], core_recv.at[x], mate) for x in range(2)]

    def x_make(i):
        return hop(*buffers[i][1:3], x_mate, start=False)

    def x_start(i, copies, x_copy):
        core_recv, x_send, x_recv = buffers[i][:3]
        for copy in copies:
            copy.wait()
        joint = parts[i][:, quarter(1 - chip_x, core)].astype(FULL) + core_recv[1 - chip_x].astype(FULL)
        x_send[...] = joint.astype(LOW)
        x_copy.start()
        return x_copy

    def y_start(i, copy):
        core_recv, x_send, x_recv, own, y_recv = buffers[i][:5]
        joint = parts[i][:, quarter(chip_x, core)].astype(FULL) + core_recv[chip_x].astype(FULL)
        copy.wait()
        own[...] = (joint + x_recv[...].astype(FULL)).astype(LOW).reshape(own.shape)
        return hop(own.at[:, 1 - row_y], y_recv, y_mate)

    def part_load(i):
        own, y_recv = buffers[i][3:5]
        return lambda z: own[z, row_y].astype(FULL) + y_recv[z].astype(FULL)

    def z_start(i, copy):
        copy.wait()
        near_fill(part_load(i), buffers[i][5])
        return hop(*buffers[i][5:7], near_z)

    def z_next(i, copy):
        copy.wait()
        far_fill(part_load(i), *buffers[i][6:8])
        return hop(*buffers[i][7:9], far_z)

    def share_start(i, copy):
        gathered = buffers[i][9]
        copy.wait()
        gathered[seq] = z_total(part_load(i), buffers[i][6], buffers[i][8]).astype(LOW)
        mine = gathered.at[seq]
        return [hop(mine, mine, target) for target in (x_mate, cross, mate)]

    def share_finish(i, copies):
        gathered = buffers[i][9]
        for copy in copies:
            copy.wait()
        for s in range(4):
            share_outs[i][s * ROWS_PAD : (s + 1) * ROWS_PAD] = gathered[s].astype(FULL)
        early(share_outs[i], share_hbms[i])

    def weight(i, left, right):
        term = dot(left, right, TN)
        share = width // SHARES
        for j in range(SHARES):
            rows = term[j * share : (j + 1) * share]
            if prev[i] is not None:
                rows = rows + prev[i]()[j, :share].astype(FULL)
            parts[i][j, :share] = rows.astype(LOW)
        if not last:
            early(parts[i], part_hbms[i])

    after_grad_ref, w_out_ref = after_grad_later(), w_out_later()
    low_grad = after_grad_ref[...].astype(LOW)
    mixed_back = dot(low_grad, w_out_ref[...], NT)
    lane = lax.broadcasted_iota(jnp.int32, (length, 128), 1)
    for pair in range((HEADS + 1) // 2):
        span = min(128, HEADS * HEAD_DIM - pair * 128)
        part = mixed_back[:, pair * 128 : pair * 128 + span]
        if span < 128:
            part = jnp.concatenate([part, part], axis=1)
        else:
            mixed_grad[2 * pair + 1] = jnp.where(lane >= HEAD_DIM, part, 0.0).astype(LOW)
        mixed_grad[2 * pair] = jnp.where(lane >= HEAD_DIM, pltpu.roll(part, 64, 1), 0.0).astype(LOW)
    mixed_ref = mixed_later()
    product = mixed_back.astype(LOW).astype(FULL) * mixed_ref[...].astype(FULL)
    high = product.astype(LOW)
    rest_low = (product - high.astype(FULL)).astype(LOW)
    head = lax.broadcasted_iota(jnp.int32, (16, HEADS * HEAD_DIM), 0)
    column = lax.broadcasted_iota(jnp.int32, (16, HEADS * HEAD_DIM), 1)
    pick = jnp.where(lax.div(column, HEAD_DIM) == head, 1.0, 0.0).astype(LOW)
    sums = dot(pick, high, NT) + dot(pick, rest_low, NT)
    for g in range(KV_HEADS):
        delta[g] = jnp.concatenate([sums[3 * g + i : 3 * g + i + 1] for i in range(GROUP)], axis=1)
    query_grad[...] = jnp.zeros_like(query_grad)
    weight(0, mixed_ref[...], low_grad)
    if last:
        o_core = core_start(0)
        f_near(2)
        o_x = x_make(0)

    start, place = place_ref[0:1, :], place_ref[1:2, :]
    q_ref, kv_ref = q_later(), kv_later()

    def attend(block, g):
        columns = pl.ds(pl.multiple_of(g * 128, 128), 128)
        kv_g = kv_ref[block, :, columns]
        q_g = q_ref[pl.ds(3 * g, 3)].reshape(stacked, 128)
        out_g = mixed_grad[pl.ds(3 * g, 3)].reshape(stacked, 128)
        scores = dot(kv_g, q_g, NT)
        key = lax.broadcasted_iota(jnp.int32, (length, stacked), 0) + block * length
        weights = jnp.where((key >= start) & (key <= place), jnp.exp(scores - log_ref[g]), 0.0)
        probs_grad = dot(kv_g, out_g, NT)
        score_grad = (weights * (probs_grad - delta[g])).astype(LOW)
        kv_grad[block, :, columns] = dot(weights.astype(LOW), out_g) + dot(score_grad, q_g)
        query_grad[g] += dot(kv_g, score_grad, TN)[:HEAD_DIM]

    joint = hop(grad_send.at[0], grad_recv.at[0], mate, start=False)
    across = hop(grad_send.at[1], grad_recv.at[1], x_mate, start=False)
    beside = hop(grad_send.at[2], grad_recv.at[2], mate, start=False)

    @pl.loop(0, 4)
    def _(step):
        block = jnp.where(
            step == 0, far_mate, jnp.where(step == 1, far_seq, jnp.where(step == 2, mate_seq, seq))
        )

        @pl.when(block <= seq)
        def _():
            @pl.loop(0, KV_HEADS)
            def _(g):
                attend(block, g)

        @pl.when(block > seq)
        def _():
            kv_grad[block] = jnp.zeros_like(kv_grad[block])

        @pl.when(step == 0)
        def _():
            grad_send[0] = kv_grad[far_mate].astype(LOW)
            joint.start()
            if last:
                x_start(0, o_core, o_x)

        @pl.when(step == 1)
        def _():
            joint.wait()
            grad_send[1] = (kv_grad[far_seq] + grad_recv[0].astype(FULL)).astype(LOW)
            across.start()

        @pl.when(step == 2)
        def _():
            grad_send[2] = kv_grad[mate_seq].astype(LOW)
            beside.start()
            if last:
                f_far(2)
                f_near(0)

    trig_ref = trig()
    heads = []
    for g in range(KV_HEADS):
        turned = query_grad[g].T * SCALE
        heads += [turned[i * length : (i + 1) * length] for i in range(GROUP)]
    for pair in range((HEADS + 1) // 2):
        part = jnp.concatenate([heads[2 * pair], heads[min(2 * pair + 1, HEADS - 1)]], axis=1)
        turned = (part * trig_ref[0] - swap_halves(part) * trig_ref[1]).astype(LOW)
        at = kv_width + pair * 128
        stop = min(at + 128, kv_width + width)
        back[:, at:stop] = turned[:, : stop - at]
    weight(1, normed_ref()[...], back[:, kv_width:])
    if last:
        q_core = core_start(1)
        o_y = y_start(0, o_x)
    normed_grad = dot(back[:, kv_width:], w_query()[...], NT)
    if last:
        q_x = x_start(1, q_core, x_make(1))

    across.wait()
    beside.wait()
    own = kv_grad[seq] + grad_recv[1].astype(FULL) + grad_recv[2].astype(FULL)
    for g in range(KV_HEADS):
        part = own[:, g * 128 : (g + 1) * 128]
        back[:, g * 128 : (g + 1) * 128] = (part * trig_ref[2] - swap_halves(part) * trig_ref[3]).astype(LOW)
    weight(2, normed_ref()[...], back[:, :kv_width])
    if last:
        kv_core = core_start(2)
        f_far(0)
        f_near(1)
        kv_x = x_start(2, kv_core, x_make(2))
    normed_grad = normed_grad + dot(back[:, :kv_width], w_kv()[...])
    sent_back, gain_term = norm_back(res_ref()[...].astype(FULL), gains_ref[0:1, :], normed_grad)
    grad_out[...] = after_grad_ref[...] + sent_back
    early(grad_out, grad_hbm)
    row = lax.broadcasted_iota(jnp.int32, gain_out.shape, 0)
    gain_out[...] = gain_ref[...] + jnp.where(row == 0, gain_term, 0.0)
    if not last:
        early.finish()
        return

    stages = [((0, mate), (1, x_mate), (2, cross)), ((3, y_mate),), ((4, near_z),), ((5, far_z),)]
    gain_hop = lambda n: [hop(gain_out, gain_recv.at[slot], target) for slot, target in stages[n]]

    def gain_add(n, copies):
        for copy in copies:
            copy.wait()
        for slot, _ in stages[n]:
            gain_out[...] += gain_recv[slot]

    gain_copy = gain_hop(0)
    f_finish(2)
    o_z = z_start(0, o_y)
    gain_add(0, gain_copy)
    gain_copy = gain_hop(1)
    q_y = y_start(1, q_x)
    f_far(1)
    f_finish(0)
    o_z = z_next(0, o_z)
    gain_add(1, gain_copy)
    gain_copy = gain_hop(2)
    kv_y = y_start(2, kv_x)
    q_z = z_start(1, q_y)
    gain_add(2, gain_copy)
    gain_copy = gain_hop(3)
    o_s = share_start(0, o_z)
    kv_z = z_start(2, kv_y)
    q_z = z_next(1, q_z)
    gain_add(3, gain_copy)
    f_finish(1)
    kv_z = z_next(2, kv_z)
    q_s = share_start(1, q_z)
    kv_s = share_start(2, kv_z)
    share_finish(0, o_s)
    share_finish(1, q_s)
    share_finish(2, kv_s)
    early.finish()


def attn_backward(after_grad, residual, normed, gains, q, kv, log_total, mixed, attn_weights, trig, place, gain_grads, final=None):
    length, width = residual.shape
    kv_width = 2 * KV_HEADS * HEAD_DIM
    last = final is not None
    key_t, value_t, w_query, w_out = attn_weights
    args = (gain_grads, gains, place, log_total, after_grad, w_out, mixed, q, kv, trig, residual, normed)
    args = args + (key_t, value_t, w_query)
    specs = [VMEM] * 4 + [ANYWHERE] * 11
    out_specs = (ANYWHERE, VMEM)
    shapes = (((length, width), FULL), ((8, width), FULL))
    sizes = (width, width, kv_width)
    part_shapes = [((SHARES, 4 * ROWS_PAD, c), LOW) for c in sizes]
    scratch = [
        pltpu.VMEM(q.shape, LOW),
        pltpu.VMEM(kv.shape, LOW),
        pltpu.VMEM(trig.shape, FULL),
        pltpu.VMEM((length, width), residual.dtype),
        pltpu.VMEM((length, width), LOW),
        pltpu.VMEM((kv_width, width), LOW),
        pltpu.VMEM(w_query.shape, LOW),
        pltpu.VMEM((length, width), FULL),
        pltpu.VMEM((length, width), FULL),
        pltpu.VMEM(w_out.shape, LOW),
        pltpu.VMEM(mixed.shape, LOW),
        pltpu.SemaphoreType.DMA((2 * KV_HEADS,)),
        pltpu.SemaphoreType.DMA((14,)),
        pltpu.SemaphoreType.DMA((7,)),
        pltpu.VMEM((HEADS, length, 128), LOW),
        pltpu.VMEM((KV_HEADS, 1, GROUP * length), FULL),
        pltpu.VMEM((4, length, kv_width), FULL),
        pltpu.VMEM((KV_HEADS, HEAD_DIM, GROUP * length), FULL),
        pltpu.VMEM((length, kv_width + width), LOW),
        pltpu.VMEM((3, length, kv_width), LOW),
        pltpu.VMEM((3, length, kv_width), LOW),
    ]
    hops = 3
    if last:
        share, hidden = final[3].shape[3:]
        args = args + tuple(final)
        specs = specs + [ANYWHERE] * 5
        shapes = shapes + (((3, share, hidden), FULL),) + tuple(((4 * ROWS_PAD, c), FULL) for c in sizes)
        hops = 3 + 2 + 6 + 6 + 3 * (2 + 1 + 1 + 2 + 3)
        scratch += [pltpu.SemaphoreType.DMA((hops,))] * 2
        out_specs = out_specs + (ANYWHERE,) * 4
        scratch += [pltpu.VMEM(*s) for s in part_shapes]
        scratch += [
            pltpu.VMEM((3, 4, share, hidden), LOW),
            pltpu.VMEM((3, 4, share, hidden), LOW),
            pltpu.VMEM((3, 2, share, hidden), LOW),
            pltpu.VMEM((3, 2, share, hidden), LOW),
            pltpu.VMEM((3, share, hidden), LOW),
            pltpu.VMEM((3, share, hidden), LOW),
            pltpu.VMEM((6, 8, width), FULL),
        ]
        scratch += [pltpu.VMEM(*s) for s in part_shapes]
        scratch += [pltpu.VMEM(*s) for s in shapes[2:]]
        for c in sizes:
            scratch += [
                pltpu.VMEM((2, SHARES, ROWS_PAD, c), LOW),
                pltpu.VMEM((SHARES, ROWS_PAD, c), LOW),
                pltpu.VMEM((SHARES, ROWS_PAD, c), LOW),
                pltpu.VMEM((4, 2, ROWS_PAD, c), LOW),
                pltpu.VMEM((4, ROWS_PAD, c), LOW),
                pltpu.VMEM((2, ROWS_PAD, c), LOW),
                pltpu.VMEM((2, ROWS_PAD, c), LOW),
                pltpu.VMEM((ROWS_PAD, c), LOW),
                pltpu.VMEM((ROWS_PAD, c), LOW),
                pltpu.VMEM((4, ROWS_PAD, c), LOW),
            ]
    else:
        shapes, out_specs = shapes + tuple(part_shapes), out_specs + (ANYWHERE,) * 3
        scratch += [pltpu.SemaphoreType.DMA((hops,))] * 2
        scratch += [pltpu.VMEM(*s) for s in part_shapes]
    return pl.pallas_call(
        functools.partial(attn_backward_kernel, last),
        out_shape=tuple(jax.ShapeDtypeStruct(*s) for s in shapes),
        in_specs=specs,
        out_specs=out_specs,
        scratch_shapes=scratch,
        compiler_params=pltpu.CompilerParams(
            collective_id=6 if last else 5, has_side_effects=True, vmem_limit_bytes=60 * 1024 * 1024
        ),
        cost_estimate=cost(95 if last else 40),
        name="attn_backward_last" if last else "attn_backward",
    )(*args)


def split_pairs(grads):
    rows = grads.shape[0]
    pairs = grads.reshape(rows, KV_HEADS, 2, HEAD_DIM)
    return pairs[:, :, 0].reshape(rows, -1), pairs[:, :, 1].reshape(rows, -1)


def on_device(
    tokens,
    seg_ids,
    positions,
    attn_gain,
    w_query,
    w_key,
    w_value,
    w_out,
    ffn_gain,
    w_gate,
    w_up,
    w_down,
    cotangent,
):
    width = tokens.shape[2]
    trig, place = prepare(positions[0])
    attn_weights = (w_key.T, w_value.T, w_query, w_out)
    gains = jnp.pad(jnp.stack([attn_gain, ffn_gain]), ((0, 6), (0, 0)))
    whole = lax.axis_size("dp") != SHARES
    share = width // SHARES
    own_weights = (w_gate, w_up, w_down.T)

    def over_x(value):
        return lax.ppermute(value, "seq", [(s, (s + 2) % 4) for s in range(4)])

    def over_rows_piece(value, d):
        return lax.dynamic_slice_in_dim(value, jnp.minimum(d * PIECE, width - PIECE), PIECE, axis=0)

    if whole:
        theirs = [over_x(w) for w in own_weights]
        far = jnp.stack([jnp.concatenate([over_rows_piece(w, d) for w in theirs]) for d in range(SHARES)])
    else:
        piece = jnp.concatenate([over_rows_piece(w, lax.axis_index("dp")) for w in own_weights])
        far = lax.all_gather(over_x(piece), "dp", axis=0)

    results = forward(tokens[0], gains, place, cotangent[0], attn_weights, trig, own_weights)
    first, (rows_all, pre_all, residual), results = results[:KEPT], results[KEPT : KEPT + 3], results[KEPT + 3 :]
    second, normed_two, low_halves = results[:KEPT], results[KEPT], results[KEPT + 1 :]
    output, after_grad, gain_grads, ffn_grads = ffn_all(
        True, False, cotangent[0], normed_two, second[5], gains, low_halves, own_weights, far
    )

    def attn_args(after_grad, residual, kept, gain_grads):
        normed, q, kv, log_total, mixed = kept[:5]
        return (after_grad, residual, normed, gains, q, kv, log_total, mixed, attn_weights, trig, place, gain_grads)

    upstream, gain_grads, *parts = attn_backward(*attn_args(after_grad, residual, second, gain_grads))
    after_grad, gain_grads, ffn_grads, *first_y = ffn_all(
        False, not whole, upstream, None, first[5], gains, (rows_all,), own_weights, far, ffn_grads, pre_all, gain_grads
    )
    args = attn_args(after_grad, tokens[0], first, gain_grads)
    if whole:
        upstream, gain_grads, *terms = attn_backward(*args)
        parts = [part.astype(FULL) + term.astype(FULL) for part, term in zip(parts, terms)]
    else:
        upstream, gain_all, ffn_share, *shares = attn_backward(*args, (*parts, ffn_grads, *first_y))
    if whole:

        def over_rows(grads, dim):
            grads = lax.psum_scatter(grads.astype(LOW), "dp", scatter_dimension=dim, tiled=True)
            return grads.astype(FULL)

        def over_all(grads, dim):
            return lax.psum(over_rows(grads, dim).astype(LOW), "seq").astype(FULL)

        shares = [over_all(part[:, :share].reshape(width, -1), 0) for part in parts]
        ffn_share = over_rows(ffn_grads.reshape(3, width, -1), 1)
        own_gains = over_all(gain_grads[:2], 1)
    else:
        shares = [part[:share] for part in shares]
        own_gains = lax.dynamic_slice_in_dim(gain_all, lax.axis_index("dp") * share, share, axis=1)
    key_share, value_share = split_pairs(shares[2])
    return (
        output[None],
        upstream[None],
        own_gains[0],
        shares[1],
        key_share,
        value_share,
        shares[0],
        own_gains[1],
        ffn_share[0],
        ffn_share[1],
        ffn_share[2].T,
    )


def solution(mesh):
    in_specs = (
        P("dp", "seq", None),
        P("dp", "seq"),
        P("dp", "seq"),
        P(),
        P(),
        P(),
        P(),
        P(),
        P(),
        P(None, "seq"),
        P(None, "seq"),
        P("seq", None),
        P("dp", "seq", None),
    )
    out_specs = (
        P("dp", "seq", None),
        P("dp", "seq", None),
        P("dp"),
        P("dp", None),
        P("dp", None),
        P("dp", None),
        P("dp", None),
        P("dp"),
        P("dp", "seq"),
        P("dp", "seq"),
        P("seq", "dp"),
    )
    return jax.shard_map(
        on_device, mesh=mesh, in_specs=in_specs, out_specs=out_specs, check_vma=False
    )
```
